32 devices in a mesh: date: 8 (over y, x, core), range: 4 (over z).
Axes of the slice: x: 2, y: 2, z: 4, core: 2. Of those that a mesh axis runs over, the one named last changes fastest.
Arguments:
- epoch_tiles_quadrature: bfloat16 [16, 2, 256, 1024], P('date', None, None, 'range'), may hold values from -6 to 6
- along_track_whole_displacement: int32 [16], replicated, may hold values from -8 to 8
- along_track_subpixel_weights: int32 [16], replicated, may hold values from 0 to 15
- slant_whole_displacement: int32 [16], replicated, may hold values from -12 to 12
- slant_subpixel_weights: int32 [16], replicated, may hold values from 0 to 15
- sweeps_each_epoch: int32 [16], replicated, may hold values from 1 to 4
- baseline_companion_gap: int32 [16, 2], replicated, may hold values from 2 to 3, as said below
- master_epoch_image: int32 [1], replicated, may hold values from 0 to 15
Outputs:
- interferograms: float32 [16, 6, 16, 256], P('date', None, None, 'range')
- coherence: float32 [16, 3, 16, 256], P('date', None, None, 'range')
The draws below stay inside these ranges and needn't reach their ends.
Inputs may be any that keep to these rules, and one draw needn't show every extreme that they name: `baseline_companion_gap`: the later gap is 3 for odd dates and 2 or 3 for even dates; the earlier gap is 3 for even dates and 2 or 3 for odd dates.
All inputs are finite; a program needn't handle non-finite values.
Results may differ from the reference program's by a relative error of at most 0.0061.
Values may be sent and summed in bfloat16 or wider, within the bound.
No kernel may reach another device: no remote copies, remote signals or barrier semaphores. Data moves between devices by JAX's collectives and lax.ppermute only.
A program may use at most 64 MiB of HBM per device.

```python
import jax
import jax.numpy as jnp
from jax import lax

ALONG_TRACK_SPAN = 256
MAX_SWEEPS = 4
TAPS = 8
FRACTIONS = 16
LINE_REACH = 8
COLUMN_REACH = 12
MARGIN = 16
LOOK_AZ = 16
LOOK_RG = 4
EPOCH_NUMBER = 16
COLS = 1024


def draw_baseline_companion_gap(key, part):
    picks = jax.random.randint(key, (EPOCH_NUMBER, 2), 2, 4).astype(jnp.int32)
    parity = jnp.arange(EPOCH_NUMBER, dtype=jnp.int32) % 2
    forward = jnp.where(parity == 1, 3, picks[:, 0])
    backward = jnp.where(parity == 0, 3, picks[:, 1])
    return jnp.stack([forward, backward], axis=1).astype(jnp.int32)


def place_ends(values, rng, smallest, high):
    longest = values.shape.index(max(values.shape))
    spots = []
    for shift in (0, 1):
        where = [jax.random.randint(jax.random.fold_in(rng, axis), (), 0, length) for axis, length in enumerate(values.shape)]
        where[longest] = (where[longest] + shift) % values.shape[longest]
        spots.append(tuple(where))
    return values.at[spots[0]].set(smallest).at[spots[1]].set(high)


def shard_levels(key, dims, cuts, smallest, top_value):
    loudness, own = 1.0, jax.random.fold_in(key, 6)
    for dim, blocks in cuts:
        draws = jnp.exp(jax.random.uniform(jax.random.fold_in(own, dim), (blocks,), jnp.float32, smallest / len(cuts), top_value / len(cuts)))
        loudness = loudness * jnp.repeat(draws, dims[dim] // blocks).reshape([-1 if axis == dim else 1 for axis in range(len(dims))])
    return loudness


def bell_draw(key, shape, spread, reach, pieces=(), held_as=jnp.bfloat16):
    gain = shard_levels(key, shape, pieces, -0.22, 0.18) if pieces else 1.0
    array = jax.random.normal(key, shape, jnp.float32) * spread * gain
    return jnp.minimum(jnp.maximum(array, -reach), reach).astype(held_as)


def setup_inputs(seed: int = 0) -> dict:
    key_of = jax.random.split(jax.random.key(seed), 9)
    epoch_tiles_quadrature = bell_draw(key_of[0], (EPOCH_NUMBER, 2, ALONG_TRACK_SPAN, COLS), 1.0, 6.0, ((0, 8), (3, 4)))
    along_track_whole_displacement = place_ends(jax.random.randint(key_of[1], (EPOCH_NUMBER,), 0 - LINE_REACH, LINE_REACH + 1), jax.random.fold_in(key_of[1], 1), 0 - LINE_REACH, LINE_REACH).astype(jnp.int32)
    along_track_subpixel_weights = place_ends(jax.random.randint(key_of[2], (EPOCH_NUMBER,), 0, FRACTIONS), jax.random.fold_in(key_of[2], 1), 0, FRACTIONS - 1).astype(jnp.int32)
    slant_whole_displacement = place_ends(jax.random.randint(key_of[3], (EPOCH_NUMBER,), 0 - COLUMN_REACH, COLUMN_REACH + 1), jax.random.fold_in(key_of[3], 1), 0 - COLUMN_REACH, COLUMN_REACH).astype(jnp.int32)
    slant_subpixel_weights = place_ends(jax.random.randint(key_of[4], (EPOCH_NUMBER,), 0, FRACTIONS), jax.random.fold_in(key_of[4], 1), 0, FRACTIONS - 1).astype(jnp.int32)
    sweeps_each_epoch = place_ends(jax.random.randint(key_of[5], (EPOCH_NUMBER,), 1, MAX_SWEEPS + 1), jax.random.fold_in(key_of[5], 1), 1, MAX_SWEEPS).astype(jnp.int32)
    baseline_companion_gap = draw_baseline_companion_gap(jax.random.fold_in(key_of[8], 71), 0)
    master_epoch_image = jax.random.randint(key_of[7], (1,), 0, EPOCH_NUMBER).astype(jnp.int32)
    return dict(epoch_tiles_quadrature=epoch_tiles_quadrature, along_track_whole_displacement=along_track_whole_displacement, along_track_subpixel_weights=along_track_subpixel_weights, slant_whole_displacement=slant_whole_displacement, slant_subpixel_weights=slant_subpixel_weights, sweeps_each_epoch=sweeps_each_epoch, baseline_companion_gap=baseline_companion_gap, master_epoch_image=master_epoch_image)


def kernel_weights():
    fraction = jnp.arange(FRACTIONS, dtype=jnp.float32)[:, None] / FRACTIONS
    spacing = jnp.arange(TAPS, dtype=jnp.float32)[None, :] - (TAPS // 2 - 1) - fraction
    window = jnp.cos(jnp.pi * spacing / (TAPS + 1)) ** 2
    weights = jnp.sinc(spacing) * window
    return (weights / lax.optimization_barrier(jnp.sum(weights, axis=1, keepdims=True))).astype(jnp.bfloat16)

def regrid_tile(input_scanlines, along_whole_displacement, along_subpixel_weights, across_whole_displacement, across_subpixel_weights, sweep_number, sinc_weight_table):
    values = input_scanlines.astype(jnp.float32)
    padded = jnp.pad(values, ((0, 0), (0, 0), (MARGIN, MARGIN)))
    taps_column = sinc_weight_table[across_subpixel_weights].astype(jnp.float32)
    ranged = jnp.zeros_like(values)
    for tap in range(TAPS):
        start = (MARGIN + across_whole_displacement + tap - (TAPS // 2 - 1)).astype(jnp.int32)
        ranged = ranged + taps_column[tap] * lax.dynamic_slice_in_dim(padded, start, COLS, axis=2)
    ranged = lax.optimization_barrier(ranged.astype(jnp.bfloat16)).astype(jnp.float32)
    reach_lines = LINE_REACH + TAPS // 2
    padded = jnp.pad(ranged, ((0, 0), (reach_lines, reach_lines), (0, 0)))
    taps_line = sinc_weight_table[along_subpixel_weights].astype(jnp.float32)
    shifted = jnp.zeros_like(values)
    for tap in range(TAPS):
        start = (reach_lines + along_whole_displacement + tap - (TAPS // 2 - 1)).astype(jnp.int32)
        shifted = shifted + taps_line[tap] * lax.dynamic_slice_in_dim(padded, start, ALONG_TRACK_SPAN, axis=1)
    usable_scanline_flags = (jnp.arange(ALONG_TRACK_SPAN, dtype=jnp.int32) < sweep_number * (ALONG_TRACK_SPAN // MAX_SWEEPS)).astype(jnp.float32)
    return (shifted * usable_scanline_flags[None, :, None]).astype(jnp.bfloat16)

def window_pool(values):
    return values.reshape(values.shape[0] // LOOK_AZ, LOOK_AZ, values.shape[1] // LOOK_RG, LOOK_RG).sum(axis=(1, 3))

def looks(first, second):
    left = first.astype(jnp.float32)
    right = second.astype(jnp.float32)
    real_part = window_pool(left[0] * right[0] + left[1] * right[1])
    imag_part = window_pool(left[1] * right[0] - left[0] * right[1])
    power_left = window_pool(left[0] * left[0] + left[1] * left[1])
    power_right = window_pool(right[0] * right[0] + right[1] * right[1])
    scale = 1.0 / jnp.sqrt(jnp.float32(LOOK_AZ * LOOK_RG))
    coherent = jnp.sqrt(real_part * real_part + imag_part * imag_part) / jnp.sqrt(power_left * power_right + 1e-06)
    return (jnp.stack([real_part * scale, imag_part * scale]), coherent)

def reference(epoch_tiles_quadrature, along_track_whole_displacement, along_track_subpixel_weights, slant_whole_displacement, slant_subpixel_weights, sweeps_each_epoch, baseline_companion_gap, master_epoch_image):
    sinc_weight_table = kernel_weights()

    def regrid_one_epoch(item):
        return regrid_tile(item[0], item[1], item[2], item[3], item[4], item[5], sinc_weight_table)
    regridded_tile = lax.map(regrid_one_epoch, (epoch_tiles_quadrature, along_track_whole_displacement, along_track_subpixel_weights, slant_whole_displacement, slant_subpixel_weights, sweeps_each_epoch))
    ref_block = regridded_tile[master_epoch_image[0]]
    date_ids = jnp.arange(EPOCH_NUMBER, dtype=jnp.int32)
    forward = date_ids + baseline_companion_gap[:, 0]
    later = jnp.where(forward < EPOCH_NUMBER, forward, date_ids - baseline_companion_gap[:, 0]).astype(jnp.int32)
    backward = date_ids - baseline_companion_gap[:, 1]
    earlier = jnp.where(backward >= 0, backward, date_ids + baseline_companion_gap[:, 1]).astype(jnp.int32)

    def per_date(item):
        ref_ifg, ref_coh = looks(item[0], ref_block)
        later_ifg, later_coh = looks(item[0], regridded_tile[item[1]])
        earlier_ifg, earlier_coh = looks(item[0], regridded_tile[item[2]])
        return (jnp.concatenate([ref_ifg, later_ifg, earlier_ifg], axis=0), jnp.stack([ref_coh, later_coh, earlier_coh]))
    interferograms, coherence = lax.map(per_date, (regridded_tile, later, earlier))
    return (interferograms, coherence)
```

```python
import functools

import jax
import jax.numpy as jnp
from jax import lax
from jax.experimental import pallas as pl
from jax.experimental.pallas import tpu as pltpu
from jax.sharding import PartitionSpec as P

MAX_SWEEPS = 4
TAPS = 8
FRACTIONS = 16
MARGIN = 16
LOOK_AZ = 16
LOOK_RG = 4
QUANTITIES = 8
KINDS = 3
CHANNELS = 9

SMEM = pl.BlockSpec(memory_space=pltpu.SMEM)
VMEM = pl.BlockSpec(memory_space=pltpu.VMEM)


def kernel_weights():
    fraction = jnp.arange(FRACTIONS, dtype=jnp.float32)[:, None] / FRACTIONS
    spacing = jnp.arange(TAPS, dtype=jnp.float32)[None, :] - (TAPS // 2 - 1) - fraction
    window = jnp.cos(jnp.pi * spacing / (TAPS + 1)) ** 2
    weights = jnp.sinc(spacing) * window
    return (weights / jnp.sum(weights, axis=1, keepdims=True)).astype(jnp.bfloat16)


def shifted(block, axis, distance):
    count = lax.axis_size(axis)
    return lax.ppermute(
        block, axis, [(i, i + distance) for i in range(count) if 0 <= i + distance < count]
    )


def banded(offsets, table_ref, row):
    result = jnp.zeros(offsets.shape, jnp.float32)
    for tap in range(TAPS):
        result = jnp.where(offsets == tap, table_ref[row, tap], result)
    return result


def taps_kernel(
    table_ref, az_whole, az_part, rg_whole, rg_part, sweeps, own_ref, edge_ref, line_ref
):
    dates, columns, _ = own_ref.shape
    lines = line_ref.shape[1]
    images, edge_rows, _ = edge_ref.shape
    first = lax.axis_index("date") * dates
    half = edge_rows // 2

    def grid(rows, cols):
        return (
            lax.broadcasted_iota(jnp.int32, (rows, cols), 0),
            lax.broadcasted_iota(jnp.int32, (rows, cols), 1),
        )

    for slot in range(dates):
        date = first + slot
        shift = TAPS // 2 - 1 - rg_whole[date]
        row, col = grid(columns, columns)
        own_ref[slot] = banded(row - col + shift, table_ref, rg_part[date]).astype(jnp.bfloat16)
        row, col = grid(edge_rows, columns)
        inner = row % MARGIN
        source = jnp.where(row < half, inner - MARGIN, columns + inner)
        edge = banded(source - col + shift, table_ref, rg_part[date])
        owner = (row % half) // MARGIN
        for image in range(images // dates):
            number = slot * (images // dates) + image
            edge_ref[number] = jnp.where(owner == number, edge, 0.0).astype(jnp.bfloat16)
        row, col = grid(lines, lines)
        band = banded(col - row - az_whole[date] + TAPS // 2 - 1, table_ref, az_part[date])
        usable = row < sweeps[date] * (lines // MAX_SWEEPS)
        line_ref[slot] = jnp.where(usable, band, 0.0).astype(jnp.bfloat16)


def resample_kernel(split, x_ref, low_ref, high_ref, own_ref, edge_ref, line_ref, out_ref):
    dates, parts = x_ref.shape[:2]
    line_groups, column_groups, tile_lines, tile_columns = split
    edges = jnp.concatenate([low_ref[...], high_ref[...]], axis=1)
    for slot in range(dates):
        for part in range(parts):
            ranged = jnp.dot(x_ref[slot, part], own_ref[slot], preferred_element_type=jnp.float32)
            ranged += jnp.dot(
                edges, edge_ref[slot * parts + part], preferred_element_type=jnp.float32
            )
            moved = jnp.dot(
                line_ref[slot], ranged.astype(jnp.bfloat16), preferred_element_type=jnp.float32
            ).astype(jnp.bfloat16)
            for i in range(line_groups):
                for j in range(column_groups):
                    out_ref[i * column_groups + j, slot, part] = moved[
                        i * tile_lines : (i + 1) * tile_lines,
                        j * tile_columns : (j + 1) * tile_columns,
                    ]


def partners(date, gap_ref, master_ref, total):
    ahead = date + gap_ref[date, 0]
    later = jnp.where(ahead < total, ahead, date - gap_ref[date, 0])
    back = date - gap_ref[date, 1]
    earlier = jnp.where(back >= 0, back, date + gap_ref[date, 1])
    return (master_ref[0], later, earlier)


def looks_kernel(gap_ref, master_ref, r_ref, out_ref, sums, pooled, powers):
    total, _, tile_lines, tile_columns = r_ref.shape
    owners, per_owner, lanes = out_ref.shape
    dates = per_owner // CHANNELS
    line_looks = tile_lines // LOOK_AZ
    unroll = total if total <= 16 else 1

    def collect(date, carry):
        left0 = r_ref[date, 0].astype(jnp.float32)
        left1 = r_ref[date, 1].astype(jnp.float32)
        values = []
        for partner in partners(date, gap_ref, master_ref, total):
            right0 = r_ref[partner, 0].astype(jnp.float32)
            right1 = r_ref[partner, 1].astype(jnp.float32)
            values += [left0 * right0 + left1 * right1, left1 * right0 - left0 * right1]
        values.append(left0 * left0 + left1 * left1)
        for number, value in enumerate(values):
            for look in range(line_looks):
                rows = value[look * LOOK_AZ : (look + 1) * LOOK_AZ]
                sums[
                    pl.ds(date * QUANTITIES + number, 1),
                    look * tile_columns : (look + 1) * tile_columns,
                ] = jnp.sum(rows, axis=0, keepdims=True)
        sums[pl.ds(date * QUANTITIES + len(values), 1), :] = jnp.zeros(
            (1, line_looks * tile_columns), jnp.float32
        )
        return carry

    lax.fori_loop(0, total, collect, 0, unroll=unroll)
    shape = (line_looks * tile_columns, lanes)
    row = lax.broadcasted_iota(jnp.int32, shape, 0)
    col = lax.broadcasted_iota(jnp.int32, shape, 1)
    pool = (row // LOOK_RG == col).astype(jnp.float32)
    pooled[...] = jnp.dot(
        sums[...], pool, preferred_element_type=jnp.float32, precision=lax.Precision.HIGHEST
    )

    def gather(date, carry):
        for kind, partner in enumerate(partners(date, gap_ref, master_ref, total)):
            powers[kind, pl.ds(date, 1), :] = pooled[
                pl.ds(partner * QUANTITIES + 2 * KINDS, 1), :
            ]
        return carry

    lax.fori_loop(0, total, gather, 0, unroll=unroll)
    scale = 1.0 / (LOOK_AZ * LOOK_RG) ** 0.5

    for slot in range(dates):

        def every(number):
            return pooled[pl.ds(slot * QUANTITIES + number, owners, stride=dates * QUANTITIES), :]

        power_left = every(2 * KINDS)
        for kind in range(KINDS):
            real, imag = every(2 * kind), every(2 * kind + 1)
            power_right = powers[kind, pl.ds(slot, owners, stride=dates), :]
            out_ref[:, slot * CHANNELS + 2 * kind, :] = real * scale
            out_ref[:, slot * CHANNELS + 2 * kind + 1, :] = imag * scale
            out_ref[:, slot * CHANNELS + 2 * KINDS + kind, :] = jnp.sqrt(
                real * real + imag * imag
            ) / jnp.sqrt(power_left * power_right + 1e-06)


def place_kernel(x_ref, ifg_ref, coh_ref):
    sources, rows, lanes = x_ref.shape
    dates, _, lines, columns = ifg_ref.shape
    looks = lanes // columns
    for slot in range(dates):
        for channel in range(CHANNELS):
            values = x_ref[:, slot * CHANNELS + channel, :]
            for look in range(looks):
                part = values[:, look * columns : (look + 1) * columns]
                where = pl.ds(look, sources, stride=looks)
                if channel < 2 * KINDS:
                    ifg_ref[slot, channel, where, :] = part
                else:
                    coh_ref[slot, channel - 2 * KINDS, where, :] = part


def body(
    epoch_tiles_quadrature,
    along_track_whole_displacement,
    along_track_subpixel_weights,
    slant_whole_displacement,
    slant_subpixel_weights,
    sweeps_each_epoch,
    baseline_companion_gap,
    master_epoch_image,
):
    block = epoch_tiles_quadrature
    dates, parts, lines, columns = block.shape
    owners = lax.axis_size("date")
    total = owners * dates
    images = dates * parts
    line_groups = min(owners, lines // LOOK_AZ)
    column_groups = owners // line_groups
    tile_lines, tile_columns = lines // line_groups, columns // column_groups
    line_looks, column_looks = tile_lines // LOOK_AZ, tile_columns // LOOK_RG
    lanes = line_looks * column_looks

    def edge(piece):
        return jnp.transpose(piece, (2, 0, 1, 3)).reshape(lines, images * MARGIN)

    low = shifted(edge(block[..., columns - MARGIN :]), "range", 1)
    high = shifted(edge(block[..., :MARGIN]), "range", -1)

    table = kernel_weights().astype(jnp.float32)
    own_taps, edge_taps, line_taps = pl.pallas_call(
        taps_kernel,
        out_shape=(
            jax.ShapeDtypeStruct((dates, columns, columns), jnp.bfloat16),
            jax.ShapeDtypeStruct((images, 2 * images * MARGIN, columns), jnp.bfloat16),
            jax.ShapeDtypeStruct((dates, lines, lines), jnp.bfloat16),
        ),
        in_specs=[SMEM] * 6,
        out_specs=(VMEM,) * 3,
        cost_estimate=pl.CostEstimate(flops=4000000, bytes_accessed=800000, transcendentals=0),
        name="taps",
    )(
        table,
        along_track_whole_displacement,
        along_track_subpixel_weights,
        slant_whole_displacement,
        slant_subpixel_weights,
        sweeps_each_epoch,
    )
    tiles = pl.pallas_call(
        functools.partial(
            resample_kernel, (line_groups, column_groups, tile_lines, tile_columns)
        ),
        out_shape=jax.ShapeDtypeStruct(
            (owners, dates, parts, tile_lines, tile_columns), jnp.bfloat16
        ),
        in_specs=[VMEM] * 6,
        out_specs=VMEM,
        name="resample",
    )(block, low, high, own_taps, edge_taps, line_taps)

    tiles = lax.all_to_all(tiles, "date", 0, 0)
    stack = tiles.reshape(total, parts, tile_lines, tile_columns)
    results = pl.pallas_call(
        looks_kernel,
        out_shape=jax.ShapeDtypeStruct((owners, dates * CHANNELS, lanes), jnp.float32),
        in_specs=[SMEM, SMEM, VMEM],
        out_specs=VMEM,
        scratch_shapes=[
            pltpu.VMEM((total * QUANTITIES, line_looks * tile_columns), jnp.float32),
            pltpu.VMEM((total * QUANTITIES, lanes), jnp.float32),
            pltpu.VMEM((KINDS, total, lanes), jnp.float32),
        ],
        name="looks",
    )(baseline_companion_gap, master_epoch_image, stack)
    results = lax.all_to_all(results, "date", 0, 0)

    rows, cols = lines // LOOK_AZ, columns // LOOK_RG
    if column_groups == 1:
        return pl.pallas_call(
            place_kernel,
            out_shape=(
                jax.ShapeDtypeStruct((dates, 2 * KINDS, rows, cols), jnp.float32),
                jax.ShapeDtypeStruct((dates, KINDS, rows, cols), jnp.float32),
            ),
            in_specs=[VMEM],
            out_specs=(VMEM, VMEM),
            name="place",
        )(results)
    whole = results.reshape(
        line_groups, column_groups, dates, CHANNELS, line_looks, column_looks
    )
    whole = jnp.transpose(whole, (2, 3, 0, 4, 1, 5)).reshape(dates, CHANNELS, rows, cols)
    return (whole[:, : 2 * KINDS], whole[:, 2 * KINDS :])


def solution(mesh):
    in_specs = (P("date", None, None, "range"), P(), P(), P(), P(), P(), P(), P())
    out_specs = (P("date", None, None, "range"), P("date", None, None, "range"))
    return jax.shard_map(body, mesh=mesh, in_specs=in_specs, out_specs=out_specs, check_vma=False)
```

```python
import functools

import jax
import jax.numpy as jnp
from jax import lax
from jax.experimental import pallas as pl
from jax.experimental.pallas import tpu as pltpu
from jax.sharding import PartitionSpec as P

MAX_SWEEPS = 4
TAPS = 8
FRACTIONS = 16
MARGIN = 16
LOOK_AZ = 16
LOOK_RG = 4
QUANTITIES = 8
KINDS = 3
CHANNELS = 9
LANES = 128
GRANT = 24 * 2**20

SMEM = pl.BlockSpec(memory_space=pltpu.SMEM)
VMEM = pl.BlockSpec(memory_space=pltpu.VMEM)


def shifted(block, axis, distance):
    count = lax.axis_size(axis)
    return lax.ppermute(
        block, axis, [(i, i + distance) for i in range(count) if 0 <= i + distance < count]
    )


def near(array):
    return pltpu.with_memory_space_constraint(array, pltpu.VMEM)


def iotas(rows, cols):
    return (
        lax.broadcasted_iota(jnp.int32, (rows, cols), 0),
        lax.broadcasted_iota(jnp.int32, (rows, cols), 1),
    )


def edges_kernel(x_ref, last_ref, first_ref):
    dates, parts, _, columns = x_ref.shape
    for slot in range(dates):
        for part in range(parts):
            spot = slice((slot * parts + part) * MARGIN, (slot * parts + part + 1) * MARGIN)
            last_ref[:, spot] = x_ref[slot, part, :, columns - MARGIN :]
            first_ref[:, spot] = x_ref[slot, part, :, :MARGIN]


def weight_rows(fractions):
    row, lane = iotas(8, LANES)
    spot = jnp.zeros((8, LANES), jnp.float32)
    for number, fraction in enumerate(fractions):
        spot = jnp.where(row == number, fraction.astype(jnp.float32), spot)
    spacing = (lane - 1 - (TAPS // 2 - 1)).astype(jnp.float32) - spot / FRACTIONS
    angle = jnp.pi * spacing
    sinc = jnp.where(spacing == 0.0, 1.0, jnp.sin(angle) / jnp.where(spacing == 0.0, 1.0, angle))
    weights = sinc * jnp.cos(angle / (TAPS + 1)) ** 2
    weights = jnp.where((lane >= 1) & (lane <= TAPS), weights, 0.0)
    weights = weights / jnp.sum(weights, axis=1, keepdims=True)
    return weights.astype(jnp.bfloat16).astype(jnp.float32)


def banded(offsets, weights):
    rows, cols = offsets.shape
    lanes = jnp.broadcast_to(weights, (rows, LANES))
    spots = jnp.clip(offsets + 1, 0, TAPS + 1)
    return jnp.concatenate(
        [
            jnp.take_along_axis(lanes, spots[:, start : start + LANES], axis=1)
            for start in range(0, cols, LANES)
        ],
        axis=1,
    )


def taps_kernel(az_whole, az_part, rg_whole, rg_part, sweeps, own_ref, low_ref, high_ref, line_ref):
    dates, columns, _ = own_ref.shape
    lines = line_ref.shape[1]
    edge_rows = low_ref.shape[0]
    parts = edge_rows // MARGIN // dates
    first = lax.axis_index("date") * dates
    centre = TAPS // 2 - 1
    present = [first + slot for slot in range(dates)]
    table = weight_rows([rg_part[d] for d in present] + [az_part[d] for d in present])
    for slot, date in enumerate(present):
        shift = centre - rg_whole[date]
        weights = table[slot : slot + 1]
        row, col = iotas(columns, columns)
        own_ref[slot] = banded(row - col + shift, weights).astype(jnp.bfloat16)
        row, col = iotas(edge_rows, LANES)
        low = banded(row % MARGIN - MARGIN - col + shift, weights)
        high = banded(row % MARGIN + LANES - col + shift, weights)
        for part in range(parts):
            image = slot * parts + part
            held = row // MARGIN == image
            spot = slice(image * LANES, (image + 1) * LANES)
            low_ref[:, spot] = jnp.where(held, low, 0.0).astype(jnp.bfloat16)
            high_ref[:, spot] = jnp.where(held, high, 0.0).astype(jnp.bfloat16)
        row, col = iotas(lines, lines)
        weights = table[dates + slot : dates + slot + 1]
        band = banded(col - row + (centre - az_whole[date]), weights)
        usable = row < sweeps[date] * (lines // MAX_SWEEPS)
        line_ref[slot] = jnp.where(usable, band, 0.0).astype(jnp.bfloat16)


def resample_kernel(
    split, x_ref, last_ref, first_ref, own_ref, low_ref, high_ref, line_ref, out_ref
):
    dates, parts, _, columns = x_ref.shape
    line_groups, column_groups, tile_lines, tile_columns = split
    low = jnp.dot(last_ref[...], low_ref[...], preferred_element_type=jnp.float32)
    high = jnp.dot(first_ref[...], high_ref[...], preferred_element_type=jnp.float32)
    for slot in range(dates):
        for part in range(parts):
            spot = slice((slot * parts + part) * LANES, (slot * parts + part + 1) * LANES)
            ranged = jnp.dot(x_ref[slot, part], own_ref[slot], preferred_element_type=jnp.float32)
            pieces = [ranged[:, start : start + LANES] for start in range(0, columns, LANES)]
            pieces[0] += low[:, spot]
            pieces[-1] += high[:, spot]
            ranged = jnp.concatenate(pieces, axis=1)
            moved = jnp.dot(
                line_ref[slot], ranged.astype(jnp.bfloat16), preferred_element_type=jnp.float32
            ).astype(jnp.bfloat16)
            for i in range(line_groups):
                for j in range(column_groups):
                    out_ref[i * column_groups + j, slot, part] = moved[
                        i * tile_lines : (i + 1) * tile_lines,
                        j * tile_columns : (j + 1) * tile_columns,
                    ]


def partners(date, gap_ref, master_ref, total):
    ahead = date + gap_ref[0, date]
    later = jnp.where(ahead < total, ahead, date - gap_ref[0, date])
    back = date - gap_ref[1, date]
    earlier = jnp.where(back >= 0, back, date + gap_ref[1, date])
    return (master_ref[0], later, earlier)


def row_sums(values):
    row = lax.broadcasted_iota(jnp.int32, values[0].shape, 0)
    order = (3, 2, 1, 0, 7, 6, 5, 4)
    values = [values[number] for number in order]
    upper = row < 4
    values = [
        jnp.where(upper, a, b) + pltpu.roll(jnp.where(upper, b, a), 4, 0)
        for a, b in zip(values[:4], values[4:])
    ]
    for step, kept in ((2, row % 4 >= 2), (1, row % 2 == 1)):
        values = [
            jnp.where(kept, a + pltpu.roll(a, step, 0), b + pltpu.roll(b, 8 - step, 0))
            for a, b in zip(values[:step], values[step:])
        ]
    return values[0]


def looks_kernel(gap_ref, master_ref, r_ref, out_ref, sums, pooled, powers):
    total, _, tile_lines, tile_columns = r_ref.shape
    owners, per_owner, lanes = out_ref.shape
    dates = per_owner // CHANNELS
    line_looks = tile_lines // LOOK_AZ
    unroll = total if total <= 16 else 1

    def collect(date, carry):
        left0 = r_ref[date, 0].astype(jnp.float32)
        left1 = r_ref[date, 1].astype(jnp.float32)
        values = []
        for partner in partners(date, gap_ref, master_ref, total):
            right0 = r_ref[partner, 0].astype(jnp.float32)
            right1 = r_ref[partner, 1].astype(jnp.float32)
            values += [left0 * right0 + left1 * right1, left1 * right0 - left0 * right1]
        values.append(left0 * left0 + left1 * left1)
        values.append(jnp.zeros_like(left0))
        rows = pl.ds(pl.multiple_of(date * QUANTITIES, QUANTITIES), QUANTITIES)
        for look in range(line_looks):
            start = look * LOOK_AZ
            sums[rows, look * tile_columns : (look + 1) * tile_columns] = row_sums(
                [value[start : start + 8] + value[start + 8 : start + 16] for value in values]
            )
        return carry

    lax.fori_loop(0, total, collect, 0, unroll=unroll)
    shape = (line_looks * tile_columns, lanes)
    row = lax.broadcasted_iota(jnp.int32, shape, 0)
    col = lax.broadcasted_iota(jnp.int32, shape, 1)
    pool = jnp.where(row // LOOK_RG == col, 1.0, 0.0).astype(jnp.bfloat16)
    whole = sums[...]
    coarse = whole.astype(jnp.bfloat16)
    fine = (whole - coarse.astype(jnp.float32)).astype(jnp.bfloat16)
    pooled[...] = jnp.dot(coarse, pool, preferred_element_type=jnp.float32) + jnp.dot(
        fine, pool, preferred_element_type=jnp.float32
    )

    def gather(date, carry):
        for kind, partner in enumerate(partners(date, gap_ref, master_ref, total)):
            powers[kind, pl.ds(date, 1), :] = pooled[
                pl.ds(partner * QUANTITIES + 2 * KINDS, 1), :
            ]
        return carry

    lax.fori_loop(0, total, gather, 0, unroll=unroll)
    scale = 1.0 / (LOOK_AZ * LOOK_RG) ** 0.5

    for slot in range(dates):

        def every(number):
            return pooled[pl.ds(slot * QUANTITIES + number, owners, stride=dates * QUANTITIES), :]

        power_left = every(2 * KINDS)
        for kind in range(KINDS):
            real, imag = every(2 * kind), every(2 * kind + 1)
            power_right = powers[kind, pl.ds(slot, owners, stride=dates), :]
            out_ref[:, slot * CHANNELS + 2 * kind, :] = real * scale
            out_ref[:, slot * CHANNELS + 2 * kind + 1, :] = imag * scale
            out_ref[:, slot * CHANNELS + 2 * KINDS + kind, :] = jnp.sqrt(
                real * real + imag * imag
            ) / jnp.sqrt(power_left * power_right + 1e-06)


def place_kernel(x_ref, ifg_ref, coh_ref):
    sources, rows, lanes = x_ref.shape
    dates, _, lines, columns = ifg_ref.shape
    looks = lanes // columns
    for slot in range(dates):
        for channel in range(CHANNELS):
            values = x_ref[:, slot * CHANNELS + channel, :]
            for look in range(looks):
                part = values[:, look * columns : (look + 1) * columns]
                where = pl.ds(look, sources, stride=looks)
                if channel < 2 * KINDS:
                    ifg_ref[slot, channel, where, :] = part
                else:
                    coh_ref[slot, channel - 2 * KINDS, where, :] = part


def body(
    epoch_tiles_quadrature,
    along_track_whole_displacement,
    along_track_subpixel_weights,
    slant_whole_displacement,
    slant_subpixel_weights,
    sweeps_each_epoch,
    baseline_companion_gap,
    master_epoch_image,
):
    block = epoch_tiles_quadrature
    dates, parts, lines, columns = block.shape
    owners = lax.axis_size("date")
    total = owners * dates
    images = dates * parts
    line_groups = min(owners, lines // LOOK_AZ)
    column_groups = owners // line_groups
    tile_lines, tile_columns = lines // line_groups, columns // column_groups
    line_looks, column_looks = tile_lines // LOOK_AZ, tile_columns // LOOK_RG
    lanes = line_looks * column_looks

    block = near(block)
    last, first = pl.pallas_call(
        edges_kernel,
        out_shape=(pltpu.VMEM((lines, images * MARGIN), jnp.bfloat16),) * 2,
        in_specs=[VMEM],
        out_specs=(VMEM, VMEM),
        name="edges",
        compiler_params=pltpu.CompilerParams(vmem_limit_bytes=GRANT),
    )(block)
    last = shifted(last, "range", 1)
    first = shifted(first, "range", -1)

    taps = pl.pallas_call(
        taps_kernel,
        out_shape=(
            pltpu.VMEM((dates, columns, columns), jnp.bfloat16),
            pltpu.VMEM((images * MARGIN, images * LANES), jnp.bfloat16),
            pltpu.VMEM((images * MARGIN, images * LANES), jnp.bfloat16),
            pltpu.VMEM((dates, lines, lines), jnp.bfloat16),
        ),
        in_specs=[SMEM] * 5,
        out_specs=(VMEM,) * 4,
        cost_estimate=pl.CostEstimate(flops=4000000, bytes_accessed=800000, transcendentals=0),
        name="taps",
        compiler_params=pltpu.CompilerParams(vmem_limit_bytes=GRANT),
    )(
        along_track_whole_displacement,
        along_track_subpixel_weights,
        slant_whole_displacement,
        slant_subpixel_weights,
        sweeps_each_epoch,
    )
    tiles = pl.pallas_call(
        functools.partial(
            resample_kernel, (line_groups, column_groups, tile_lines, tile_columns)
        ),
        out_shape=pltpu.VMEM((owners, dates, parts, tile_lines, tile_columns), jnp.bfloat16),
        in_specs=[VMEM] * 7,
        out_specs=VMEM,
        name="resample",
        compiler_params=pltpu.CompilerParams(vmem_limit_bytes=GRANT),
    )(block, near(last), near(first), *[near(tap) for tap in taps])

    tiles = lax.all_to_all(tiles, "date", 0, 0)
    stack = tiles.reshape(total, parts, tile_lines, tile_columns)
    results = pl.pallas_call(
        looks_kernel,
        out_shape=pltpu.VMEM((owners, dates * CHANNELS, lanes), jnp.float32),
        in_specs=[SMEM, SMEM, VMEM],
        out_specs=VMEM,
        scratch_shapes=[
            pltpu.VMEM((total * QUANTITIES, line_looks * tile_columns), jnp.float32),
            pltpu.VMEM((total * QUANTITIES, lanes), jnp.float32),
            pltpu.VMEM((KINDS, total, lanes), jnp.float32),
        ],
        name="looks",
        compiler_params=pltpu.CompilerParams(vmem_limit_bytes=GRANT),
    )(baseline_companion_gap.T, master_epoch_image, near(stack))
    results = lax.all_to_all(results, "date", 0, 0)

    rows, cols = lines // LOOK_AZ, columns // LOOK_RG
    if column_groups == 1:
        return pl.pallas_call(
            place_kernel,
            out_shape=(
                jax.ShapeDtypeStruct((dates, 2 * KINDS, rows, cols), jnp.float32),
                jax.ShapeDtypeStruct((dates, KINDS, rows, cols), jnp.float32),
            ),
            in_specs=[VMEM],
            out_specs=(VMEM, VMEM),
            name="place",
            compiler_params=pltpu.CompilerParams(vmem_limit_bytes=GRANT),
        )(near(results))
    whole = results.reshape(
        line_groups, column_groups, dates, CHANNELS, line_looks, column_looks
    )
    whole = jnp.transpose(whole, (2, 3, 0, 4, 1, 5)).reshape(dates, CHANNELS, rows, cols)
    return (whole[:, : 2 * KINDS], whole[:, 2 * KINDS :])


def solution(mesh):
    in_specs = (P("date", None, None, "range"), P(), P(), P(), P(), P(), P(), P())
    out_specs = (P("date", None, None, "range"), P("date", None, None, "range"))
    return jax.shard_map(body, mesh=mesh, in_specs=in_specs, out_specs=out_specs, check_vma=False)
```

```python
import functools

import jax
import jax.numpy as jnp
from jax import lax
from jax.experimental import pallas as pl
from jax.experimental.pallas import tpu as pltpu
from jax.sharding import PartitionSpec as P

MAX_SWEEPS = 4
TAPS = 8
FRACTIONS = 16
MARGIN = 16
LOOK_AZ = 16
LOOK_RG = 4
QUANTITIES = 8
KINDS = 3
CHANNELS = 9
LANES = 128
GRANT = 24 * 2**20

SMEM = pl.BlockSpec(memory_space=pltpu.SMEM)
VMEM = pl.BlockSpec(memory_space=pltpu.VMEM)


def exchanged(array, axis, pairs):
    return lax.ppermute(array, axis, [route for a, b in pairs for route in ((a, b), (b, a))])


def near(array):
    return pltpu.with_memory_space_constraint(array, pltpu.VMEM)


def iotas(rows, cols):
    return (
        lax.broadcasted_iota(jnp.int32, (rows, cols), 0),
        lax.broadcasted_iota(jnp.int32, (rows, cols), 1),
    )


def edges_kernel(x_ref, near_ref, even_ref, odd_ref, sems):
    dates, parts, _, columns = x_ref.shape
    forward = lax.axis_index("range") % 2 == 0
    images = [(slot, part) for slot in range(dates) for part in range(parts)]
    copies = [
        pltpu.make_async_copy(x_ref.at[image], near_ref.at[image], sems.at[number])
        for number, image in enumerate(images)
    ]
    for copy in copies:
        copy.start()
    for number, (slot, part) in enumerate(images):
        copies[number].wait()
        spot = slice(number * MARGIN, (number + 1) * MARGIN)
        last = near_ref[slot, part, :, columns - MARGIN :]
        first = near_ref[slot, part, :, :MARGIN]
        even_ref[:, spot] = jnp.where(forward, last, first)
        odd_ref[:, spot] = jnp.where(forward, first, last)


def weight_rows(fractions):
    row, lane = iotas(8, LANES)
    spot = jnp.zeros((8, LANES), jnp.float32)
    for number, fraction in enumerate(fractions):
        spot = jnp.where(row == number, fraction.astype(jnp.float32), spot)
    spacing = (lane - 1 - (TAPS // 2 - 1)).astype(jnp.float32) - spot / FRACTIONS
    angle = jnp.pi * spacing
    sinc = jnp.where(spacing == 0.0, 1.0, jnp.sin(angle) / jnp.where(spacing == 0.0, 1.0, angle))
    weights = sinc * jnp.cos(angle / (TAPS + 1)) ** 2
    weights = jnp.where((lane >= 1) & (lane <= TAPS), weights, 0.0)
    weights = weights / jnp.sum(weights, axis=1, keepdims=True)
    return weights.astype(jnp.bfloat16).astype(jnp.float32)


def by_pairs(owners):
    return owners in (2, 4, 8)


def tile_order(position):
    if by_pairs(lax.axis_size("date")):
        return position ^ lax.axis_index("date")
    return position


def banded(offsets, weights):
    rows, cols = offsets.shape
    lanes = jnp.broadcast_to(weights, (rows, LANES))
    spots = jnp.clip(offsets + 1, 0, TAPS + 1)
    return jnp.concatenate(
        [
            jnp.take_along_axis(lanes, spots[:, start : start + LANES], axis=1)
            for start in range(0, cols, LANES)
        ],
        axis=1,
    )


def taps_kernel(
    tile_lines,
    az_whole,
    az_part,
    rg_whole,
    rg_part,
    sweeps,
    gap_ref,
    master_ref,
    own_ref,
    low_ref,
    high_ref,
    line_ref,
    partner_ref,
):
    dates, columns, _ = own_ref.shape
    total = partner_ref.shape[1]
    lines = line_ref.shape[1]
    edge_rows = low_ref.shape[0]
    parts = edge_rows // MARGIN // dates
    first = lax.axis_index("date") * dates
    centre = TAPS // 2 - 1
    present = [first + slot for slot in range(dates)]
    table = weight_rows([rg_part[d] for d in present] + [az_part[d] for d in present])
    for slot, date in enumerate(present):
        shift = centre - rg_whole[date]
        weights = table[slot : slot + 1]
        row, col = iotas(columns, columns)
        own_ref[slot] = banded(row - col + shift, weights).astype(jnp.bfloat16)
        row, col = iotas(edge_rows, LANES)
        low = banded(row % MARGIN - MARGIN - col + shift, weights)
        high = banded(row % MARGIN + LANES - col + shift, weights)
        for part in range(parts):
            image = slot * parts + part
            held = row // MARGIN == image
            spot = slice(image * LANES, (image + 1) * LANES)
            low_ref[:, spot] = jnp.where(held, low, 0.0).astype(jnp.bfloat16)
            high_ref[:, spot] = jnp.where(held, high, 0.0).astype(jnp.bfloat16)
        row, col = iotas(lines, lines)
        row = tile_order(row // tile_lines) * tile_lines + row % tile_lines
        weights = table[dates + slot : dates + slot + 1]
        band = banded(col - row + (centre - az_whole[date]), weights)
        usable = row < sweeps[date] * (lines // MAX_SWEEPS)
        line_ref[slot] = jnp.where(usable, band, 0.0).astype(jnp.bfloat16)

    def find(date, carry):
        for kind, partner in enumerate(partners(date, gap_ref, master_ref, total)):
            partner_ref[kind, date] = partner
        return carry

    lax.fori_loop(0, total, find, 0)


def resample_kernel(split, x_ref, even_ref, odd_ref, own_ref, low_ref, high_ref, line_ref, *outs):
    dates, parts, _, columns = x_ref.shape
    line_groups, column_groups, tile_lines, tile_columns = split
    forward = lax.axis_index("range") % 2 == 0
    even, odd = even_ref[...], odd_ref[...]
    low = jnp.dot(
        jnp.where(forward, odd, even), low_ref[...], preferred_element_type=jnp.float32
    )
    high = jnp.dot(
        jnp.where(forward, even, odd), high_ref[...], preferred_element_type=jnp.float32
    )
    for slot in range(dates):
        for part in range(parts):
            spot = slice((slot * parts + part) * LANES, (slot * parts + part + 1) * LANES)
            ranged = jnp.dot(x_ref[slot, part], own_ref[slot], preferred_element_type=jnp.float32)
            pieces = [ranged[:, start : start + LANES] for start in range(0, columns, LANES)]
            pieces[0] += low[:, spot]
            pieces[-1] += high[:, spot]
            ranged = jnp.concatenate(pieces, axis=1)
            moved = jnp.dot(
                line_ref[slot], ranged.astype(jnp.bfloat16), preferred_element_type=jnp.float32
            ).astype(jnp.bfloat16)
            for i in range(line_groups):
                for j in range(column_groups):
                    tile = moved[
                        i * tile_lines : (i + 1) * tile_lines,
                        j * tile_columns : (j + 1) * tile_columns,
                    ]
                    if len(outs) == 1:
                        outs[0][i * column_groups + j, slot, part] = tile
                    else:
                        outs[i][slot, part] = tile


def partners(date, gap_ref, master_ref, total):
    ahead = date + gap_ref[0, date]
    later = jnp.where(ahead < total, ahead, date - gap_ref[0, date])
    back = date - gap_ref[1, date]
    earlier = jnp.where(back >= 0, back, date + gap_ref[1, date])
    return (master_ref[0], later, earlier)


def row_sums(values):
    row = lax.broadcasted_iota(jnp.int32, values[0].shape, 0)
    order = (3, 2, 1, 0, 7, 6, 5, 4)
    values = [values[number] for number in order]
    upper = row < 4
    values = [
        jnp.where(upper, a, b) + pltpu.roll(jnp.where(upper, b, a), 4, 0)
        for a, b in zip(values[:4], values[4:])
    ]
    for step, kept in ((2, row % 4 >= 2), (1, row % 2 == 1)):
        values = [
            jnp.where(kept, a + pltpu.roll(a, step, 0), b + pltpu.roll(b, 8 - step, 0))
            for a, b in zip(values[:step], values[step:])
        ]
    return values[0]


def looks_kernel(partner_ref, *refs):
    tiles, (out_ref, stack, sums, pooled, powers) = refs[:-5], refs[-5:]
    total, _, tile_lines, tile_columns = stack.shape
    owners, per_owner, lanes = out_ref.shape
    dates = per_owner // CHANNELS
    line_looks = tile_lines // LOOK_AZ
    unroll = total if total <= 16 else 1
    if len(tiles) > 1:
        for position, tile_ref in enumerate(tiles):
            stack[pl.ds(tile_order(position) * dates, dates)] = tile_ref[...].astype(jnp.float32)
    else:

        def widen(owner, carry):
            stack[pl.ds(owner * dates, dates)] = tiles[0][owner].astype(jnp.float32)
            return carry

        lax.fori_loop(0, owners, widen, 0)

    def collect(date, carry):
        left0, left1 = stack[date, 0], stack[date, 1]
        values = []
        for kind in range(KINDS):
            partner = partner_ref[kind, date]
            right0, right1 = stack[partner, 0], stack[partner, 1]
            values += [left0 * right0 + left1 * right1, left1 * right0 - left0 * right1]
        values.append(left0 * left0 + left1 * left1)
        values.append(jnp.zeros_like(left0))
        rows = pl.ds(pl.multiple_of(date * QUANTITIES, QUANTITIES), QUANTITIES)
        for look in range(line_looks):
            start = look * LOOK_AZ
            sums[rows, look * tile_columns : (look + 1) * tile_columns] = row_sums(
                [value[start : start + 8] + value[start + 8 : start + 16] for value in values]
            )
        return carry

    lax.fori_loop(0, total, collect, 0, unroll=unroll)
    shape = (line_looks * tile_columns, lanes)
    row = lax.broadcasted_iota(jnp.int32, shape, 0)
    col = lax.broadcasted_iota(jnp.int32, shape, 1)
    pool = jnp.where(row // LOOK_RG == col, 1.0, 0.0).astype(jnp.bfloat16)
    whole = sums[...]
    coarse = whole.astype(jnp.bfloat16)
    fine = (whole - coarse.astype(jnp.float32)).astype(jnp.bfloat16)
    pooled[...] = jnp.dot(coarse, pool, preferred_element_type=jnp.float32) + jnp.dot(
        fine, pool, preferred_element_type=jnp.float32
    )

    def gather(date, carry):
        for kind in range(KINDS):
            power = partner_ref[kind, date] * QUANTITIES + 2 * KINDS
            powers[kind, pl.ds(date, 1), :] = pooled[pl.ds(power, 1), :]
        return carry

    lax.fori_loop(0, total, gather, 0, unroll=unroll)
    scale = 1.0 / (LOOK_AZ * LOOK_RG) ** 0.5

    for slot in range(dates):

        def every(number):
            return pooled[pl.ds(slot * QUANTITIES + number, owners, stride=dates * QUANTITIES), :]

        power_left = every(2 * KINDS)
        for kind in range(KINDS):
            real, imag = every(2 * kind), every(2 * kind + 1)
            power_right = powers[kind, pl.ds(slot, owners, stride=dates), :]
            out_ref[:, slot * CHANNELS + 2 * kind, :] = real * scale
            out_ref[:, slot * CHANNELS + 2 * kind + 1, :] = imag * scale
            out_ref[:, slot * CHANNELS + 2 * KINDS + kind, :] = jnp.sqrt(
                real * real + imag * imag
            ) / jnp.sqrt(power_left * power_right + 1e-06)


def place_kernel(x_ref, ifg_ref, coh_ref):
    sources, rows, lanes = x_ref.shape
    dates, _, lines, columns = ifg_ref.shape
    looks = lanes // columns
    for slot in range(dates):
        for channel in range(CHANNELS):
            values = x_ref[:, slot * CHANNELS + channel, :]
            for look in range(looks):
                part = values[:, look * columns : (look + 1) * columns]
                where = pl.ds(look, sources, stride=looks)
                if channel < 2 * KINDS:
                    ifg_ref[slot, channel, where, :] = part
                else:
                    coh_ref[slot, channel - 2 * KINDS, where, :] = part


def body(
    epoch_tiles_quadrature,
    along_track_whole_displacement,
    along_track_subpixel_weights,
    slant_whole_displacement,
    slant_subpixel_weights,
    sweeps_each_epoch,
    baseline_companion_gap,
    master_epoch_image,
):
    block = epoch_tiles_quadrature
    dates, parts, lines, columns = block.shape
    owners = lax.axis_size("date")
    total = owners * dates
    images = dates * parts
    line_groups = min(owners, lines // LOOK_AZ)
    column_groups = owners // line_groups
    tile_lines, tile_columns = lines // line_groups, columns // column_groups
    line_looks, column_looks = tile_lines // LOOK_AZ, tile_columns // LOOK_RG
    lanes = line_looks * column_looks

    block, even, odd = pl.pallas_call(
        edges_kernel,
        out_shape=(
            pltpu.VMEM(block.shape, block.dtype),
            pltpu.VMEM((lines, images * MARGIN), jnp.bfloat16),
            pltpu.VMEM((lines, images * MARGIN), jnp.bfloat16),
        ),
        in_specs=[pl.BlockSpec(memory_space=pltpu.HBM)],
        out_specs=(VMEM,) * 3,
        scratch_shapes=[pltpu.SemaphoreType.DMA((images,))],
        name="edges",
        compiler_params=pltpu.CompilerParams(vmem_limit_bytes=GRANT),
    )(block)
    width = lax.axis_size("range")
    odd = exchanged(odd, "range", [(j, j + 1) for j in range(1, width - 1, 2)])
    even = exchanged(even, "range", [(j, j + 1) for j in range(0, width - 1, 2)])

    *taps, table = pl.pallas_call(
        functools.partial(taps_kernel, tile_lines),
        out_shape=(
            pltpu.VMEM((dates, columns, columns), jnp.bfloat16),
            pltpu.VMEM((images * MARGIN, images * LANES), jnp.bfloat16),
            pltpu.VMEM((images * MARGIN, images * LANES), jnp.bfloat16),
            pltpu.VMEM((dates, lines, lines), jnp.bfloat16),
            pltpu.SMEM((KINDS, total), jnp.int32),
        ),
        in_specs=[SMEM] * 7,
        out_specs=(VMEM,) * 4 + (SMEM,),
        cost_estimate=pl.CostEstimate(flops=4000000, bytes_accessed=800000, transcendentals=0),
        name="taps",
        compiler_params=pltpu.CompilerParams(vmem_limit_bytes=GRANT),
    )(
        along_track_whole_displacement,
        along_track_subpixel_weights,
        slant_whole_displacement,
        slant_subpixel_weights,
        sweeps_each_epoch,
        baseline_companion_gap.T,
        master_epoch_image,
    )
    tile = (dates, parts, tile_lines, tile_columns)
    if by_pairs(owners):
        out_shape = (pltpu.VMEM(tile, jnp.bfloat16),) * owners
    else:
        out_shape = (pltpu.VMEM((owners,) + tile, jnp.bfloat16),)
    tiles = pl.pallas_call(
        functools.partial(
            resample_kernel, (line_groups, column_groups, tile_lines, tile_columns)
        ),
        out_shape=out_shape,
        in_specs=[VMEM] * 7,
        out_specs=(VMEM,) * len(out_shape),
        name="resample",
        compiler_params=pltpu.CompilerParams(vmem_limit_bytes=GRANT),
    )(near(block), near(even), near(odd), *[near(tap) for tap in taps])

    if by_pairs(owners):
        tiles = [tiles[0]] + [
            exchanged(tiles[s], "date", [(i, i ^ s) for i in range(owners) if i < i ^ s])
            for s in range(1, owners)
        ]
    else:
        tiles = [lax.all_to_all(tiles[0], "date", 0, 0)]
    results = pl.pallas_call(
        looks_kernel,
        out_shape=pltpu.VMEM((owners, dates * CHANNELS, lanes), jnp.float32),
        in_specs=[SMEM] + [VMEM] * len(tiles),
        out_specs=VMEM,
        scratch_shapes=[
            pltpu.VMEM((total, parts, tile_lines, tile_columns), jnp.float32),
            pltpu.VMEM((total * QUANTITIES, line_looks * tile_columns), jnp.float32),
            pltpu.VMEM((total * QUANTITIES, lanes), jnp.float32),
            pltpu.VMEM((KINDS, total, lanes), jnp.float32),
        ],
        name="looks",
        compiler_params=pltpu.CompilerParams(vmem_limit_bytes=GRANT),
    )(
        pltpu.with_memory_space_constraint(table, pltpu.SMEM),
        *[near(tile) for tile in tiles],
    )
    results = lax.all_to_all(results, "date", 0, 0)

    rows, cols = lines // LOOK_AZ, columns // LOOK_RG
    if column_groups == 1:
        return pl.pallas_call(
            place_kernel,
            out_shape=(
                jax.ShapeDtypeStruct((dates, 2 * KINDS, rows, cols), jnp.float32),
                jax.ShapeDtypeStruct((dates, KINDS, rows, cols), jnp.float32),
            ),
            in_specs=[VMEM],
            out_specs=(VMEM, VMEM),
            name="place",
            compiler_params=pltpu.CompilerParams(vmem_limit_bytes=GRANT),
        )(near(results))
    whole = results.reshape(
        line_groups, column_groups, dates, CHANNELS, line_looks, column_looks
    )
    whole = jnp.transpose(whole, (2, 3, 0, 4, 1, 5)).reshape(dates, CHANNELS, rows, cols)
    return (whole[:, : 2 * KINDS], whole[:, 2 * KINDS :])


def solution(mesh):
    in_specs = (P("date", None, None, "range"), P(), P(), P(), P(), P(), P(), P())
    out_specs = (P("date", None, None, "range"), P("date", None, None, "range"))
    return jax.shard_map(body, mesh=mesh, in_specs=in_specs, out_specs=out_specs, check_vma=False)
```

```python
import functools

import jax
import jax.numpy as jnp
from jax import lax
from jax.experimental import pallas as pl
from jax.experimental.pallas import tpu as pltpu
from jax.sharding import PartitionSpec as P

MAX_SWEEPS = 4
TAPS = 8
FRACTIONS = 16
MARGIN = 16
LOOK_AZ = 16
LOOK_RG = 4
QUANTITIES = 8
KINDS = 3
CHANNELS = 9
LANES = 128
GRANT = 24 * 2**20

SMEM = pl.BlockSpec(memory_space=pltpu.SMEM)
VMEM = pl.BlockSpec(memory_space=pltpu.VMEM)


def exchanged(array, axis, pairs):
    return lax.ppermute(array, axis, [route for a, b in pairs for route in ((a, b), (b, a))])


def near(array):
    return pltpu.with_memory_space_constraint(array, pltpu.VMEM)


def iotas(rows, cols):
    return (
        lax.broadcasted_iota(jnp.int32, (rows, cols), 0),
        lax.broadcasted_iota(jnp.int32, (rows, cols), 1),
    )


def weight_rows(fractions):
    row, lane = iotas(8, LANES)
    spot = jnp.zeros((8, LANES), jnp.float32)
    for number, fraction in enumerate(fractions):
        spot = jnp.where(row == number, fraction.astype(jnp.float32), spot)
    spacing = (lane - 1 - (TAPS // 2 - 1)).astype(jnp.float32) - spot / FRACTIONS
    angle = jnp.pi * spacing
    sinc = jnp.where(spacing == 0.0, 1.0, jnp.sin(angle) / jnp.where(spacing == 0.0, 1.0, angle))
    weights = sinc * jnp.cos(angle / (TAPS + 1)) ** 2
    weights = jnp.where((lane >= 1) & (lane <= TAPS), weights, 0.0)
    weights = weights / jnp.sum(weights, axis=1, keepdims=True)
    return weights.astype(jnp.bfloat16).astype(jnp.float32)


def by_pairs(owners):
    return owners in (2, 4, 8)


def tile_order(position):
    if by_pairs(lax.axis_size("date")):
        return position ^ lax.axis_index("date")
    return position


def banded(offsets, weights):
    rows, cols = offsets.shape
    lanes = jnp.broadcast_to(weights, (rows, LANES))
    spots = jnp.clip(offsets + 1, 0, TAPS + 1)
    return jnp.concatenate(
        [
            jnp.take_along_axis(lanes, spots[:, start : start + LANES], axis=1)
            for start in range(0, cols, LANES)
        ],
        axis=1,
    )


def start_kernel(
    tile_lines,
    x_ref,
    az_whole_ref,
    az_part_ref,
    rg_whole_ref,
    rg_part_ref,
    sweeps_ref,
    gap_ref,
    near_ref,
    even_ref,
    odd_ref,
    line_ref,
    weights_ref,
    shift_ref,
    partner_ref,
    az_whole,
    az_part,
    rg_whole,
    rg_part,
    sweeps,
    gap,
    sems,
):
    dates, parts, lines, columns = x_ref.shape
    total = partner_ref.shape[1]
    images = [(slot, part) for slot in range(dates) for part in range(parts)]
    small = [
        (az_whole_ref, az_whole),
        (az_part_ref, az_part),
        (rg_whole_ref, rg_whole),
        (rg_part_ref, rg_part),
        (sweeps_ref, sweeps),
        (gap_ref, gap),
    ]
    copies = [
        pltpu.make_async_copy(source, target, sems.at[number])
        for number, (source, target) in enumerate(
            small + [(x_ref.at[image], near_ref.at[image]) for image in images]
        )
    ]
    for copy in copies:
        copy.start()
    for copy in copies[: len(small)]:
        copy.wait()

    present = [lax.axis_index("date") * dates + slot for slot in range(dates)]
    centre = TAPS // 2 - 1
    weights = weight_rows([rg_part[d] for d in present] + [az_part[d] for d in present])
    weights_ref[...] = weights
    for slot, date in enumerate(present):
        shift_ref[slot] = centre - rg_whole[date]
        row, col = iotas(lines, lines)
        row = tile_order(row // tile_lines) * tile_lines + row % tile_lines
        band = banded(col - row + (centre - az_whole[date]), weights[dates + slot : dates + slot + 1])
        usable = row < sweeps[date] * (lines // MAX_SWEEPS)
        line_ref[slot] = jnp.where(usable, band, 0.0).astype(jnp.bfloat16)

    def find(date, carry):
        for kind, partner in enumerate(partners(date, gap, total)):
            partner_ref[kind, date] = partner
        return carry

    lax.fori_loop(0, total, find, 0)

    forward = lax.axis_index("range") % 2 == 0
    for number, (slot, part) in enumerate(images):
        copies[len(small) + number].wait()
        spot = slice(number * MARGIN, (number + 1) * MARGIN)
        last = near_ref[slot, part, :, columns - MARGIN :]
        first = near_ref[slot, part, :, :MARGIN]
        even_ref[:, spot] = jnp.where(forward, last, first)
        odd_ref[:, spot] = jnp.where(forward, first, last)


def taps_kernel(shift_ref, master_ref, weights_ref, own_ref, low_ref, high_ref, root_ref):
    for number in range(root_ref.shape[0]):
        root_ref[number] = master_ref[0]
    dates, columns, _ = own_ref.shape
    edge_rows = low_ref.shape[0]
    parts = edge_rows // MARGIN // dates
    for slot in range(dates):
        shift = shift_ref[slot]
        weights = weights_ref[slot : slot + 1, :]
        row, col = iotas(columns, columns)
        own_ref[slot] = banded(row - col + shift, weights).astype(jnp.bfloat16)
        row, col = iotas(edge_rows, LANES)
        low = banded(row % MARGIN - MARGIN - col + shift, weights)
        high = banded(row % MARGIN + LANES - col + shift, weights)
        for part in range(parts):
            image = slot * parts + part
            held = row // MARGIN == image
            spot = slice(image * LANES, (image + 1) * LANES)
            low_ref[:, spot] = jnp.where(held, low, 0.0).astype(jnp.bfloat16)
            high_ref[:, spot] = jnp.where(held, high, 0.0).astype(jnp.bfloat16)


def resample_kernel(split, x_ref, even_ref, odd_ref, own_ref, low_ref, high_ref, line_ref, *outs):
    dates, parts, _, columns = x_ref.shape
    line_groups, column_groups, tile_lines, tile_columns = split
    forward = lax.axis_index("range") % 2 == 0
    even, odd = even_ref[...], odd_ref[...]
    low = jnp.dot(
        jnp.where(forward, odd, even), low_ref[...], preferred_element_type=jnp.float32
    )
    high = jnp.dot(
        jnp.where(forward, even, odd), high_ref[...], preferred_element_type=jnp.float32
    )
    for slot in range(dates):
        for part in range(parts):
            spot = slice((slot * parts + part) * LANES, (slot * parts + part + 1) * LANES)
            ranged = jnp.dot(x_ref[slot, part], own_ref[slot], preferred_element_type=jnp.float32)
            pieces = [ranged[:, start : start + LANES] for start in range(0, columns, LANES)]
            pieces[0] += low[:, spot]
            pieces[-1] += high[:, spot]
            ranged = jnp.concatenate(pieces, axis=1)
            moved = jnp.dot(
                line_ref[slot], ranged.astype(jnp.bfloat16), preferred_element_type=jnp.float32
            ).astype(jnp.bfloat16)
            for i in range(line_groups):
                for j in range(column_groups):
                    tile = moved[
                        i * tile_lines : (i + 1) * tile_lines,
                        j * tile_columns : (j + 1) * tile_columns,
                    ]
                    if len(outs) == 1:
                        outs[0][i * column_groups + j, slot, part] = tile
                    else:
                        outs[i][slot, part] = tile


def partners(date, gap_ref, total):
    ahead = date + gap_ref[0, date]
    later = jnp.where(ahead < total, ahead, date - gap_ref[0, date])
    back = date - gap_ref[1, date]
    earlier = jnp.where(back >= 0, back, date + gap_ref[1, date])
    return (later, earlier)


def row_sums(values):
    row = lax.broadcasted_iota(jnp.int32, values[0].shape, 0)
    order = (3, 2, 1, 0, 7, 6, 5, 4)
    values = [values[number] for number in order]
    upper = row < 4
    values = [
        jnp.where(upper, a, b) + pltpu.roll(jnp.where(upper, b, a), 4, 0)
        for a, b in zip(values[:4], values[4:])
    ]
    for step, kept in ((2, row % 4 >= 2), (1, row % 2 == 1)):
        values = [
            jnp.where(kept, a + pltpu.roll(a, step, 0), b + pltpu.roll(b, 8 - step, 0))
            for a, b in zip(values[:step], values[step:])
        ]
    return values[0]


def looks_kernel(root_ref, partner_ref, *refs):
    tiles, (out_ref, stack, sums, pooled, powers) = refs[:-5], refs[-5:]
    total, _, tile_lines, tile_columns = stack.shape
    owners, per_owner, lanes = out_ref.shape
    dates = per_owner // CHANNELS
    line_looks = tile_lines // LOOK_AZ
    unroll = total if total <= 16 else 1
    if len(tiles) > 1:
        for position, tile_ref in enumerate(tiles):
            stack[pl.ds(tile_order(position) * dates, dates)] = tile_ref[...].astype(jnp.float32)
    else:

        def widen(owner, carry):
            stack[pl.ds(owner * dates, dates)] = tiles[0][owner].astype(jnp.float32)
            return carry

        lax.fori_loop(0, owners, widen, 0)

    def partner_of(kind, date):
        return partner_ref[kind - 1, date] if kind else root_ref[0]

    def collect(date, carry):
        left0, left1 = stack[date, 0], stack[date, 1]
        values = []
        for kind in range(KINDS):
            partner = partner_of(kind, date)
            right0, right1 = stack[partner, 0], stack[partner, 1]
            values += [left0 * right0 + left1 * right1, left1 * right0 - left0 * right1]
        values.append(left0 * left0 + left1 * left1)
        values.append(jnp.zeros_like(left0))
        rows = pl.ds(pl.multiple_of(date * QUANTITIES, QUANTITIES), QUANTITIES)
        for look in range(line_looks):
            start = look * LOOK_AZ
            sums[rows, look * tile_columns : (look + 1) * tile_columns] = row_sums(
                [value[start : start + 8] + value[start + 8 : start + 16] for value in values]
            )
        return carry

    lax.fori_loop(0, total, collect, 0, unroll=unroll)
    shape = (line_looks * tile_columns, lanes)
    row = lax.broadcasted_iota(jnp.int32, shape, 0)
    col = lax.broadcasted_iota(jnp.int32, shape, 1)
    pool = jnp.where(row // LOOK_RG == col, 1.0, 0.0).astype(jnp.bfloat16)
    whole = sums[...]
    coarse = whole.astype(jnp.bfloat16)
    fine = (whole - coarse.astype(jnp.float32)).astype(jnp.bfloat16)
    pooled[...] = jnp.dot(coarse, pool, preferred_element_type=jnp.float32) + jnp.dot(
        fine, pool, preferred_element_type=jnp.float32
    )

    def gather(date, carry):
        for kind in range(KINDS):
            power = partner_of(kind, date) * QUANTITIES + 2 * KINDS
            powers[kind, pl.ds(date, 1), :] = pooled[pl.ds(power, 1), :]
        return carry

    lax.fori_loop(0, total, gather, 0, unroll=unroll)
    scale = 1.0 / (LOOK_AZ * LOOK_RG) ** 0.5

    for slot in range(dates):

        def every(number):
            return pooled[pl.ds(slot * QUANTITIES + number, owners, stride=dates * QUANTITIES), :]

        power_left = every(2 * KINDS)
        for kind in range(KINDS):
            real, imag = every(2 * kind), every(2 * kind + 1)
            power_right = powers[kind, pl.ds(slot, owners, stride=dates), :]
            out_ref[:, slot * CHANNELS + 2 * kind, :] = real * scale
            out_ref[:, slot * CHANNELS + 2 * kind + 1, :] = imag * scale
            out_ref[:, slot * CHANNELS + 2 * KINDS + kind, :] = jnp.sqrt(
                real * real + imag * imag
            ) / jnp.sqrt(power_left * power_right + 1e-06)


def place_kernel(x_ref, ifg_ref, coh_ref):
    sources, rows, lanes = x_ref.shape
    dates, _, lines, columns = ifg_ref.shape
    looks = lanes // columns
    for slot in range(dates):
        for channel in range(CHANNELS):
            values = x_ref[:, slot * CHANNELS + channel, :]
            for look in range(looks):
                part = values[:, look * columns : (look + 1) * columns]
                where = pl.ds(look, sources, stride=looks)
                if channel < 2 * KINDS:
                    ifg_ref[slot, channel, where, :] = part
                else:
                    coh_ref[slot, channel - 2 * KINDS, where, :] = part


def body(
    epoch_tiles_quadrature,
    along_track_whole_displacement,
    along_track_subpixel_weights,
    slant_whole_displacement,
    slant_subpixel_weights,
    sweeps_each_epoch,
    baseline_companion_gap,
    master_epoch_image,
):
    block = epoch_tiles_quadrature
    dates, parts, lines, columns = block.shape
    owners = lax.axis_size("date")
    total = owners * dates
    images = dates * parts
    line_groups = min(owners, lines // LOOK_AZ)
    column_groups = owners // line_groups
    tile_lines, tile_columns = lines // line_groups, columns // column_groups
    line_looks, column_looks = tile_lines // LOOK_AZ, tile_columns // LOOK_RG
    lanes = line_looks * column_looks

    arguments = (
        block,
        along_track_whole_displacement,
        along_track_subpixel_weights,
        slant_whole_displacement,
        slant_subpixel_weights,
        sweeps_each_epoch,
        baseline_companion_gap.T,
    )
    block, even, odd, line_taps, weights, shift, table = pl.pallas_call(
        functools.partial(start_kernel, tile_lines),
        out_shape=(
            pltpu.VMEM(block.shape, block.dtype),
            pltpu.VMEM((lines, images * MARGIN), jnp.bfloat16),
            pltpu.VMEM((lines, images * MARGIN), jnp.bfloat16),
            pltpu.VMEM((dates, lines, lines), jnp.bfloat16),
            pltpu.VMEM((8, LANES), jnp.float32),
            pltpu.SMEM((dates,), jnp.int32),
            pltpu.SMEM((KINDS - 1, total), jnp.int32),
        ),
        in_specs=[pl.BlockSpec(memory_space=pltpu.HBM)] * len(arguments),
        out_specs=(VMEM,) * 5 + (SMEM,) * 2,
        scratch_shapes=[pltpu.SMEM(array.shape, array.dtype) for array in arguments[1:]]
        + [pltpu.SemaphoreType.DMA((len(arguments) - 1 + images,))],
        name="start",
        compiler_params=pltpu.CompilerParams(vmem_limit_bytes=GRANT),
    )(*[pltpu.with_memory_space_constraint(array, pltpu.HBM) for array in arguments])
    width = lax.axis_size("range")
    odd = exchanged(odd, "range", [(j, j + 1) for j in range(1, width - 1, 2)])
    even = exchanged(even, "range", [(j, j + 1) for j in range(0, width - 1, 2)])

    own_taps, low_taps, high_taps, root = pl.pallas_call(
        taps_kernel,
        out_shape=(
            pltpu.VMEM((dates, columns, columns), jnp.bfloat16),
            pltpu.VMEM((images * MARGIN, images * LANES), jnp.bfloat16),
            pltpu.VMEM((images * MARGIN, images * LANES), jnp.bfloat16),
            pltpu.SMEM((8,), jnp.int32),
        ),
        in_specs=[SMEM, SMEM, VMEM],
        out_specs=(VMEM,) * 3 + (SMEM,),
        cost_estimate=pl.CostEstimate(flops=4000000, bytes_accessed=800000, transcendentals=0),
        name="taps",
        compiler_params=pltpu.CompilerParams(vmem_limit_bytes=GRANT),
    )(pltpu.with_memory_space_constraint(shift, pltpu.SMEM), master_epoch_image, near(weights))
    tile = (dates, parts, tile_lines, tile_columns)
    if by_pairs(owners):
        out_shape = (pltpu.VMEM(tile, jnp.bfloat16),) * owners
    else:
        out_shape = (pltpu.VMEM((owners,) + tile, jnp.bfloat16),)
    tiles = pl.pallas_call(
        functools.partial(
            resample_kernel, (line_groups, column_groups, tile_lines, tile_columns)
        ),
        out_shape=out_shape,
        in_specs=[VMEM] * 7,
        out_specs=(VMEM,) * len(out_shape),
        name="resample",
        compiler_params=pltpu.CompilerParams(vmem_limit_bytes=GRANT),
    )(*[near(array) for array in (block, even, odd, own_taps, low_taps, high_taps, line_taps)])

    if by_pairs(owners):
        tiles = [tiles[0]] + [
            exchanged(tiles[s], "date", [(i, i ^ s) for i in range(owners) if i < i ^ s])
            for s in range(1, owners)
        ]
    else:
        tiles = [lax.all_to_all(tiles[0], "date", 0, 0)]
    results = pl.pallas_call(
        looks_kernel,
        out_shape=pltpu.VMEM((owners, dates * CHANNELS, lanes), jnp.float32),
        in_specs=[SMEM] * 2 + [VMEM] * len(tiles),
        out_specs=VMEM,
        scratch_shapes=[
            pltpu.VMEM((total, parts, tile_lines, tile_columns), jnp.float32),
            pltpu.VMEM((total * QUANTITIES, line_looks * tile_columns), jnp.float32),
            pltpu.VMEM((total * QUANTITIES, lanes), jnp.float32),
            pltpu.VMEM((KINDS, total, lanes), jnp.float32),
        ],
        name="looks",
        compiler_params=pltpu.CompilerParams(vmem_limit_bytes=GRANT),
    )(
        pltpu.with_memory_space_constraint(root, pltpu.SMEM),
        pltpu.with_memory_space_constraint(table, pltpu.SMEM),
        *[near(tile) for tile in tiles],
    )
    results = lax.all_to_all(results, "date", 0, 0)

    rows, cols = lines // LOOK_AZ, columns // LOOK_RG
    if column_groups == 1:
        return pl.pallas_call(
            place_kernel,
            out_shape=(
                jax.ShapeDtypeStruct((dates, 2 * KINDS, rows, cols), jnp.float32),
                jax.ShapeDtypeStruct((dates, KINDS, rows, cols), jnp.float32),
            ),
            in_specs=[VMEM],
            out_specs=(VMEM, VMEM),
            name="place",
            compiler_params=pltpu.CompilerParams(vmem_limit_bytes=GRANT),
        )(near(results))
    whole = results.reshape(
        line_groups, column_groups, dates, CHANNELS, line_looks, column_looks
    )
    whole = jnp.transpose(whole, (2, 3, 0, 4, 1, 5)).reshape(dates, CHANNELS, rows, cols)
    return (whole[:, : 2 * KINDS], whole[:, 2 * KINDS :])


def solution(mesh):
    in_specs = (P("date", None, None, "range"), P(), P(), P(), P(), P(), P(), P())
    out_specs = (P("date", None, None, "range"), P("date", None, None, "range"))
    return jax.shard_map(body, mesh=mesh, in_specs=in_specs, out_specs=out_specs, check_vma=False)
```

```python
import functools

import jax
import jax.numpy as jnp
from jax import lax
from jax.experimental import pallas as pl
from jax.experimental.pallas import tpu as pltpu
from jax.sharding import PartitionSpec as P

MAX_SWEEPS = 4
TAPS = 8
FRACTIONS = 16
MARGIN = 16
LOOK_AZ = 16
LOOK_RG = 4
QUANTITIES = 8
KINDS = 3
CHANNELS = 9
LANES = 128
GRANT = 24 * 2**20

SMEM = pl.BlockSpec(memory_space=pltpu.SMEM)
VMEM = pl.BlockSpec(memory_space=pltpu.VMEM)


def exchanged(array, axis, pairs):
    return lax.ppermute(array, axis, [route for a, b in pairs for route in ((a, b), (b, a))])


def near(array):
    return pltpu.with_memory_space_constraint(array, pltpu.VMEM)


def iotas(rows, cols):
    return (
        lax.broadcasted_iota(jnp.int32, (rows, cols), 0),
        lax.broadcasted_iota(jnp.int32, (rows, cols), 1),
    )


def weight_rows(fractions):
    row, lane = iotas(8, LANES)
    spot = jnp.zeros((8, LANES), jnp.float32)
    for number, fraction in enumerate(fractions):
        spot = jnp.where(row == number, fraction.astype(jnp.float32), spot)
    spacing = (lane - 1 - (TAPS // 2 - 1)).astype(jnp.float32) - spot / FRACTIONS
    angle = jnp.pi * spacing
    sinc = jnp.where(spacing == 0.0, 1.0, jnp.sin(angle) / jnp.where(spacing == 0.0, 1.0, angle))
    weights = sinc * jnp.cos(angle / (TAPS + 1)) ** 2
    weights = jnp.where((lane >= 1) & (lane <= TAPS), weights, 0.0)
    weights = weights / jnp.sum(weights, axis=1, keepdims=True)
    return weights.astype(jnp.bfloat16).astype(jnp.float32)


def by_pairs(owners):
    return owners in (2, 4, 8)


def tile_order(position):
    if by_pairs(lax.axis_size("date")):
        return position ^ lax.axis_index("date")
    return position


def banded(offsets, weights):
    rows, cols = offsets.shape
    lanes = jnp.broadcast_to(weights, (rows, LANES))
    spots = jnp.clip(offsets + 1, 0, TAPS + 1)
    return jnp.concatenate(
        [
            jnp.take_along_axis(lanes, spots[:, start : start + LANES], axis=1)
            for start in range(0, cols, LANES)
        ],
        axis=1,
    )


def start_kernel(x_ref, *refs):
    dates, parts, _, columns = x_ref.shape
    images = [(slot, part) for slot in range(dates) for part in range(parts)]
    count = (len(refs) - 4) // 2
    near_ref, even_ref, odd_ref = refs[count : count + 3]
    sems = refs[-1]
    small = list(zip(refs[:count], refs[count + 3 : -1]))
    whole = [(x_ref.at[image], near_ref.at[image]) for image in images]
    copies = [
        pltpu.make_async_copy(source, target, sems.at[number])
        for number, (source, target) in enumerate(whole + small)
    ]
    for copy in copies:
        copy.start()
    forward = lax.axis_index("range") % 2 == 0
    for number, (slot, part) in enumerate(images):
        copies[number].wait()
        spot = slice(number * MARGIN, (number + 1) * MARGIN)
        last = near_ref[slot, part, :, columns - MARGIN :]
        first = near_ref[slot, part, :, :MARGIN]
        even_ref[:, spot] = jnp.where(forward, last, first)
        odd_ref[:, spot] = jnp.where(forward, first, last)
    for copy in copies[len(images) :]:
        copy.wait()


def taps_kernel(
    tile_lines,
    az_whole,
    az_part,
    rg_whole,
    rg_part,
    sweeps,
    master_ref,
    own_ref,
    low_ref,
    high_ref,
    line_ref,
    root_ref,
):
    dates, columns, _ = own_ref.shape
    lines = line_ref.shape[1]
    edge_rows = low_ref.shape[0]
    parts = edge_rows // MARGIN // dates
    centre = TAPS // 2 - 1
    for number in range(root_ref.shape[0]):
        root_ref[number] = master_ref[0]
    present = [lax.axis_index("date") * dates + slot for slot in range(dates)]
    table = weight_rows([rg_part[d] for d in present] + [az_part[d] for d in present])
    for slot, date in enumerate(present):
        shift = centre - rg_whole[date]
        weights = table[slot : slot + 1]
        row, col = iotas(columns, columns)
        own_ref[slot] = banded(row - col + shift, weights).astype(jnp.bfloat16)
        row, col = iotas(edge_rows, LANES)
        low = banded(row % MARGIN - MARGIN - col + shift, weights)
        high = banded(row % MARGIN + LANES - col + shift, weights)
        for part in range(parts):
            image = slot * parts + part
            held = row // MARGIN == image
            spot = slice(image * LANES, (image + 1) * LANES)
            low_ref[:, spot] = jnp.where(held, low, 0.0).astype(jnp.bfloat16)
            high_ref[:, spot] = jnp.where(held, high, 0.0).astype(jnp.bfloat16)
        row, col = iotas(lines, lines)
        row = tile_order(row // tile_lines) * tile_lines + row % tile_lines
        weights = table[dates + slot : dates + slot + 1]
        band = banded(col - row + (centre - az_whole[date]), weights)
        usable = row < sweeps[date] * (lines // MAX_SWEEPS)
        line_ref[slot] = jnp.where(usable, band, 0.0).astype(jnp.bfloat16)


def resample_kernel(split, x_ref, even_ref, odd_ref, own_ref, low_ref, high_ref, line_ref, *outs):
    dates, parts, _, columns = x_ref.shape
    line_groups, column_groups, tile_lines, tile_columns = split
    forward = lax.axis_index("range") % 2 == 0
    even, odd = even_ref[...], odd_ref[...]
    low = jnp.dot(
        jnp.where(forward, odd, even), low_ref[...], preferred_element_type=jnp.float32
    )
    high = jnp.dot(
        jnp.where(forward, even, odd), high_ref[...], preferred_element_type=jnp.float32
    )
    for slot in range(dates):
        for part in range(parts):
            spot = slice((slot * parts + part) * LANES, (slot * parts + part + 1) * LANES)
            ranged = jnp.dot(x_ref[slot, part], own_ref[slot], preferred_element_type=jnp.float32)
            pieces = [ranged[:, start : start + LANES] for start in range(0, columns, LANES)]
            pieces[0] += low[:, spot]
            pieces[-1] += high[:, spot]
            ranged = jnp.concatenate(pieces, axis=1)
            moved = jnp.dot(
                line_ref[slot], ranged.astype(jnp.bfloat16), preferred_element_type=jnp.float32
            ).astype(jnp.bfloat16)
            for i in range(line_groups):
                for j in range(column_groups):
                    tile = moved[
                        i * tile_lines : (i + 1) * tile_lines,
                        j * tile_columns : (j + 1) * tile_columns,
                    ]
                    if len(outs) == 1:
                        outs[0][i * column_groups + j, slot, part] = tile
                    else:
                        outs[i][slot, part] = tile


def partners(date, gap_ref, total):
    ahead = date + gap_ref[0, date]
    later = jnp.where(ahead < total, ahead, date - gap_ref[0, date])
    back = date - gap_ref[1, date]
    earlier = jnp.where(back >= 0, back, date + gap_ref[1, date])
    return (later, earlier)


def row_sums(values):
    row = lax.broadcasted_iota(jnp.int32, values[0].shape, 0)
    order = (3, 2, 1, 0, 7, 6, 5, 4)
    values = [values[number] for number in order]
    upper = row < 4
    values = [
        jnp.where(upper, a, b) + pltpu.roll(jnp.where(upper, b, a), 4, 0)
        for a, b in zip(values[:4], values[4:])
    ]
    for step, kept in ((2, row % 4 >= 2), (1, row % 2 == 1)):
        values = [
            jnp.where(kept, a + pltpu.roll(a, step, 0), b + pltpu.roll(b, 8 - step, 0))
            for a, b in zip(values[:step], values[step:])
        ]
    return values[0]


def looks_kernel(positions, root_ref, gap_ref, *refs):
    tiles, (out_ref, stack, sums, pooled, powers) = refs[:-5], refs[-5:]
    total, _, tile_lines, tile_columns = stack.shape
    owners, per_owner, lanes = out_ref.shape
    dates = per_owner // CHANNELS
    line_looks = tile_lines // LOOK_AZ
    unroll = total if total <= 16 else 1
    if len(tiles) > 1:
        for position, tile_ref in zip(positions, tiles):
            stack[pl.ds(tile_order(position) * dates, dates)] = tile_ref[...].astype(jnp.float32)
    else:

        def widen(owner, carry):
            stack[pl.ds(owner * dates, dates)] = tiles[0][owner].astype(jnp.float32)
            return carry

        lax.fori_loop(0, owners, widen, 0)

    def partner_of(kind, date):
        return partners(date, gap_ref, total)[kind - 1] if kind else root_ref[0]

    def collect(date, carry):
        left0, left1 = stack[date, 0], stack[date, 1]
        values = []
        for kind in range(KINDS):
            partner = partner_of(kind, date)
            right0, right1 = stack[partner, 0], stack[partner, 1]
            values += [left0 * right0 + left1 * right1, left1 * right0 - left0 * right1]
        values.append(left0 * left0 + left1 * left1)
        values.append(jnp.zeros_like(left0))
        rows = pl.ds(pl.multiple_of(date * QUANTITIES, QUANTITIES), QUANTITIES)
        for look in range(line_looks):
            start = look * LOOK_AZ
            sums[rows, look * tile_columns : (look + 1) * tile_columns] = row_sums(
                [value[start : start + 8] + value[start + 8 : start + 16] for value in values]
            )
        return carry

    lax.fori_loop(0, total, collect, 0, unroll=unroll)
    shape = (line_looks * tile_columns, lanes)
    row = lax.broadcasted_iota(jnp.int32, shape, 0)
    col = lax.broadcasted_iota(jnp.int32, shape, 1)
    pool = jnp.where(row // LOOK_RG == col, 1.0, 0.0).astype(jnp.bfloat16)
    whole = sums[...]
    coarse = whole.astype(jnp.bfloat16)
    fine = (whole - coarse.astype(jnp.float32)).astype(jnp.bfloat16)
    pooled[...] = jnp.dot(coarse, pool, preferred_element_type=jnp.float32) + jnp.dot(
        fine, pool, preferred_element_type=jnp.float32
    )

    def gather(date, carry):
        for kind in range(KINDS):
            power = partner_of(kind, date) * QUANTITIES + 2 * KINDS
            powers[kind, pl.ds(date, 1), :] = pooled[pl.ds(power, 1), :]
        return carry

    lax.fori_loop(0, total, gather, 0, unroll=unroll)
    scale = 1.0 / (LOOK_AZ * LOOK_RG) ** 0.5

    for slot in range(dates):

        def every(number):
            return pooled[pl.ds(slot * QUANTITIES + number, owners, stride=dates * QUANTITIES), :]

        power_left = every(2 * KINDS)
        for kind in range(KINDS):
            real, imag = every(2 * kind), every(2 * kind + 1)
            power_right = powers[kind, pl.ds(slot, owners, stride=dates), :]
            out_ref[:, slot * CHANNELS + 2 * kind, :] = real * scale
            out_ref[:, slot * CHANNELS + 2 * kind + 1, :] = imag * scale
            out_ref[:, slot * CHANNELS + 2 * KINDS + kind, :] = jnp.sqrt(
                real * real + imag * imag
            ) / jnp.sqrt(power_left * power_right + 1e-06)


def place_kernel(x_ref, ifg_ref, coh_ref):
    sources, rows, lanes = x_ref.shape
    dates, _, lines, columns = ifg_ref.shape
    looks = lanes // columns
    for slot in range(dates):
        for channel in range(CHANNELS):
            values = x_ref[:, slot * CHANNELS + channel, :]
            for look in range(looks):
                part = values[:, look * columns : (look + 1) * columns]
                where = pl.ds(look, sources, stride=looks)
                if channel < 2 * KINDS:
                    ifg_ref[slot, channel, where, :] = part
                else:
                    coh_ref[slot, channel - 2 * KINDS, where, :] = part


def body(
    epoch_tiles_quadrature,
    along_track_whole_displacement,
    along_track_subpixel_weights,
    slant_whole_displacement,
    slant_subpixel_weights,
    sweeps_each_epoch,
    baseline_companion_gap,
    master_epoch_image,
):
    block = epoch_tiles_quadrature
    dates, parts, lines, columns = block.shape
    owners = lax.axis_size("date")
    total = owners * dates
    images = dates * parts
    line_groups = min(owners, lines // LOOK_AZ)
    column_groups = owners // line_groups
    tile_lines, tile_columns = lines // line_groups, columns // column_groups
    line_looks, column_looks = tile_lines // LOOK_AZ, tile_columns // LOOK_RG
    lanes = line_looks * column_looks

    arguments = (
        block,
        along_track_whole_displacement,
        along_track_subpixel_weights,
        slant_whole_displacement,
        slant_subpixel_weights,
        sweeps_each_epoch,
        baseline_companion_gap.T,
    )
    block, even, odd, *small = pl.pallas_call(
        start_kernel,
        out_shape=(
            pltpu.VMEM(block.shape, block.dtype),
            pltpu.VMEM((lines, images * MARGIN), jnp.bfloat16),
            pltpu.VMEM((lines, images * MARGIN), jnp.bfloat16),
            *[pltpu.SMEM(array.shape, array.dtype) for array in arguments[1:]],
        ),
        in_specs=[pl.BlockSpec(memory_space=pltpu.HBM)] * len(arguments),
        out_specs=(VMEM,) * 3 + (SMEM,) * (len(arguments) - 1),
        scratch_shapes=[pltpu.SemaphoreType.DMA((images + len(arguments) - 1,))],
        name="start",
        compiler_params=pltpu.CompilerParams(vmem_limit_bytes=GRANT),
    )(*[pltpu.with_memory_space_constraint(array, pltpu.HBM) for array in arguments])
    *small, gap = [pltpu.with_memory_space_constraint(array, pltpu.SMEM) for array in small]
    width = lax.axis_size("range")
    odd = exchanged(odd, "range", [(j, j + 1) for j in range(1, width - 1, 2)])
    even = exchanged(even, "range", [(j, j + 1) for j in range(0, width - 1, 2)])

    own_taps, low_taps, high_taps, line_taps, root = pl.pallas_call(
        functools.partial(taps_kernel, tile_lines),
        out_shape=(
            pltpu.VMEM((dates, columns, columns), jnp.bfloat16),
            pltpu.VMEM((images * MARGIN, images * LANES), jnp.bfloat16),
            pltpu.VMEM((images * MARGIN, images * LANES), jnp.bfloat16),
            pltpu.VMEM((dates, lines, lines), jnp.bfloat16),
            pltpu.SMEM((8,), jnp.int32),
        ),
        in_specs=[SMEM] * (len(small) + 1),
        out_specs=(VMEM,) * 4 + (SMEM,),
        cost_estimate=pl.CostEstimate(flops=4000000, bytes_accessed=800000, transcendentals=0),
        name="taps",
        compiler_params=pltpu.CompilerParams(vmem_limit_bytes=GRANT),
    )(*small, master_epoch_image)
    tile = (dates, parts, tile_lines, tile_columns)
    if by_pairs(owners):
        out_shape = (pltpu.VMEM(tile, jnp.bfloat16),) * owners
    else:
        out_shape = (pltpu.VMEM((owners,) + tile, jnp.bfloat16),)
    tiles = pl.pallas_call(
        functools.partial(
            resample_kernel, (line_groups, column_groups, tile_lines, tile_columns)
        ),
        out_shape=out_shape,
        in_specs=[VMEM] * 7,
        out_specs=(VMEM,) * len(out_shape),
        name="resample",
        compiler_params=pltpu.CompilerParams(vmem_limit_bytes=GRANT),
    )(*[near(array) for array in (block, even, odd, own_taps, low_taps, high_taps, line_taps)])

    if by_pairs(owners):
        order = [*range(owners - 2, 0, -2), *range(owners - 1, 0, -2)]
        received = {
            s: exchanged(tiles[s], "date", [(i, i ^ s) for i in range(owners) if i < i ^ s])
            for s in order
        }
        positions = [0] + order
        tiles = [tiles[0]] + [received[s] for s in order]
    else:
        tiles = [lax.all_to_all(tiles[0], "date", 0, 0)]
        positions = None
    results = pl.pallas_call(
        functools.partial(looks_kernel, positions),
        out_shape=pltpu.VMEM((owners, dates * CHANNELS, lanes), jnp.float32),
        in_specs=[SMEM] * 2 + [VMEM] * len(tiles),
        out_specs=VMEM,
        scratch_shapes=[
            pltpu.VMEM((total, parts, tile_lines, tile_columns), jnp.float32),
            pltpu.VMEM((total * QUANTITIES, line_looks * tile_columns), jnp.float32),
            pltpu.VMEM((total * QUANTITIES, lanes), jnp.float32),
            pltpu.VMEM((KINDS, total, lanes), jnp.float32),
        ],
        name="looks",
        compiler_params=pltpu.CompilerParams(vmem_limit_bytes=GRANT),
    )(
        pltpu.with_memory_space_constraint(root, pltpu.SMEM),
        gap,
        *[near(tile) for tile in tiles],
    )
    results = lax.all_to_all(results, "date", 0, 0)

    rows, cols = lines // LOOK_AZ, columns // LOOK_RG
    if column_groups == 1:
        return pl.pallas_call(
            place_kernel,
            out_shape=(
                jax.ShapeDtypeStruct((dates, 2 * KINDS, rows, cols), jnp.float32),
                jax.ShapeDtypeStruct((dates, KINDS, rows, cols), jnp.float32),
            ),
            in_specs=[VMEM],
            out_specs=(VMEM, VMEM),
            name="place",
            compiler_params=pltpu.CompilerParams(vmem_limit_bytes=GRANT),
        )(near(results))
    whole = results.reshape(
        line_groups, column_groups, dates, CHANNELS, line_looks, column_looks
    )
    whole = jnp.transpose(whole, (2, 3, 0, 4, 1, 5)).reshape(dates, CHANNELS, rows, cols)
    return (whole[:, : 2 * KINDS], whole[:, 2 * KINDS :])


def solution(mesh):
    in_specs = (P("date", None, None, "range"), P(), P(), P(), P(), P(), P(), P())
    out_specs = (P("date", None, None, "range"), P("date", None, None, "range"))
    return jax.shard_map(body, mesh=mesh, in_specs=in_specs, out_specs=out_specs, check_vma=False)
```

```python
import functools

import jax
import jax.numpy as jnp
from jax import lax
from jax.experimental import pallas as pl
from jax.experimental.pallas import tpu as pltpu
from jax.sharding import PartitionSpec as P

MAX_SWEEPS = 4
TAPS = 8
FRACTIONS = 16
MARGIN = 16
LOOK_AZ = 16
LOOK_RG = 4
QUANTITIES = 8
KINDS = 3
CHANNELS = 9
LANES = 128
GRANT = 24 * 2**20

SMEM = pl.BlockSpec(memory_space=pltpu.SMEM)
VMEM = pl.BlockSpec(memory_space=pltpu.VMEM)


def exchanged(array, axis, pairs):
    return lax.ppermute(array, axis, [route for a, b in pairs for route in ((a, b), (b, a))])


def near(array):
    return pltpu.with_memory_space_constraint(array, pltpu.VMEM)


def iotas(rows, cols):
    return (
        lax.broadcasted_iota(jnp.int32, (rows, cols), 0),
        lax.broadcasted_iota(jnp.int32, (rows, cols), 1),
    )


def weight_rows(fractions):
    row, lane = iotas(8, LANES)
    spot = jnp.zeros((8, LANES), jnp.float32)
    for number, fraction in enumerate(fractions):
        spot = jnp.where(row == number, fraction.astype(jnp.float32), spot)
    spacing = (lane - 1 - (TAPS // 2 - 1)).astype(jnp.float32) - spot / FRACTIONS
    angle = jnp.pi * spacing
    sinc = jnp.where(spacing == 0.0, 1.0, jnp.sin(angle) / jnp.where(spacing == 0.0, 1.0, angle))
    weights = sinc * jnp.cos(angle / (TAPS + 1)) ** 2
    weights = jnp.where((lane >= 1) & (lane <= TAPS), weights, 0.0)
    weights = weights / jnp.sum(weights, axis=1, keepdims=True)
    return weights.astype(jnp.bfloat16).astype(jnp.float32)


def by_pairs(owners):
    return owners in (2, 4, 8)


def tile_order(position):
    if by_pairs(lax.axis_size("date")):
        return position ^ lax.axis_index("date")
    return position


def banded(offsets, weights):
    rows, cols = offsets.shape
    lanes = jnp.broadcast_to(weights, (rows, LANES))
    spots = jnp.clip(offsets + 1, 0, TAPS + 1)
    return jnp.concatenate(
        [
            jnp.take_along_axis(lanes, spots[:, start : start + LANES], axis=1)
            for start in range(0, cols, LANES)
        ],
        axis=1,
    )


def start_kernel(x_ref, *refs):
    dates, parts, _, columns = x_ref.shape
    images = [(slot, part) for slot in range(dates) for part in range(parts)]
    count = (len(refs) - 4) // 2
    near_ref, even_ref, odd_ref = refs[count : count + 3]
    sems = refs[-1]
    small = list(zip(refs[:count], refs[count + 3 : -1]))
    whole = [(x_ref.at[image], near_ref.at[image]) for image in images]
    copies = [
        pltpu.make_async_copy(source, target, sems.at[number])
        for number, (source, target) in enumerate(whole + small)
    ]
    for copy in copies:
        copy.start()
    forward = lax.axis_index("range") % 2 == 0
    for number, (slot, part) in enumerate(images):
        copies[number].wait()
        spot = slice(number * MARGIN, (number + 1) * MARGIN)
        for parity, last_ref, first_ref in (
            (forward, even_ref, odd_ref),
            (jnp.logical_not(forward), odd_ref, even_ref),
        ):

            @pl.when(parity)
            def _():
                last_ref[:, spot] = near_ref[slot, part, :, columns - MARGIN :]
                first_ref[:, spot] = near_ref[slot, part, :, :MARGIN]

    for copy in copies[len(images) :]:
        copy.wait()


def taps_kernel(
    tile_lines,
    az_whole,
    az_part,
    rg_whole,
    rg_part,
    sweeps,
    master_ref,
    own_ref,
    low_ref,
    high_ref,
    line_ref,
    root_ref,
):
    dates, columns, _ = own_ref.shape
    lines = line_ref.shape[1]
    edge_rows = low_ref.shape[0]
    parts = edge_rows // MARGIN // dates
    centre = TAPS // 2 - 1
    for number in range(root_ref.shape[0]):
        root_ref[number] = master_ref[0]
    present = [lax.axis_index("date") * dates + slot for slot in range(dates)]
    table = weight_rows([rg_part[d] for d in present] + [az_part[d] for d in present])
    for slot, date in enumerate(present):
        shift = centre - rg_whole[date]
        weights = table[slot : slot + 1]
        row, col = iotas(columns, columns)
        own_ref[slot] = banded(row - col + shift, weights).astype(jnp.bfloat16)
        row, col = iotas(edge_rows, LANES)
        low = banded(row % MARGIN - MARGIN - col + shift, weights)
        high = banded(row % MARGIN + LANES - col + shift, weights)
        for part in range(parts):
            image = slot * parts + part
            held = row // MARGIN == image
            spot = slice(image * LANES, (image + 1) * LANES)
            low_ref[:, spot] = jnp.where(held, low, 0.0).astype(jnp.bfloat16)
            high_ref[:, spot] = jnp.where(held, high, 0.0).astype(jnp.bfloat16)
        row, col = iotas(lines, lines)
        row = tile_order(row // tile_lines) * tile_lines + row % tile_lines
        weights = table[dates + slot : dates + slot + 1]
        band = banded(col - row + (centre - az_whole[date]), weights)
        usable = row < sweeps[date] * (lines // MAX_SWEEPS)
        line_ref[slot] = jnp.where(usable, band, 0.0).astype(jnp.bfloat16)


def resample_kernel(split, x_ref, even_ref, odd_ref, own_ref, low_ref, high_ref, line_ref, *refs):
    *outs, edges = refs
    dates, parts, _, columns = x_ref.shape
    line_groups, column_groups, tile_lines, tile_columns = split
    backward = lax.axis_index("range") % 2
    edges[1 - backward] = even_ref[...]
    edges[backward] = odd_ref[...]
    low = jnp.dot(edges[0], low_ref[...], preferred_element_type=jnp.float32)
    high = jnp.dot(edges[1], high_ref[...], preferred_element_type=jnp.float32)
    for slot in range(dates):
        for part in range(parts):
            spot = slice((slot * parts + part) * LANES, (slot * parts + part + 1) * LANES)
            ranged = jnp.dot(x_ref[slot, part], own_ref[slot], preferred_element_type=jnp.float32)
            pieces = [ranged[:, start : start + LANES] for start in range(0, columns, LANES)]
            pieces[0] += low[:, spot]
            pieces[-1] += high[:, spot]
            ranged = jnp.concatenate(pieces, axis=1)
            moved = jnp.dot(
                line_ref[slot], ranged.astype(jnp.bfloat16), preferred_element_type=jnp.float32
            ).astype(jnp.bfloat16)
            for i in range(line_groups):
                for j in range(column_groups):
                    tile = moved[
                        i * tile_lines : (i + 1) * tile_lines,
                        j * tile_columns : (j + 1) * tile_columns,
                    ]
                    if len(outs) == 1:
                        outs[0][i * column_groups + j, slot, part] = tile
                    else:
                        outs[i][slot, part] = tile


def partners(date, gap_ref, total):
    ahead = date + gap_ref[0, date]
    later = jnp.where(ahead < total, ahead, date - gap_ref[0, date])
    back = date - gap_ref[1, date]
    earlier = jnp.where(back >= 0, back, date + gap_ref[1, date])
    return (later, earlier)


def row_sums(values):
    row = lax.broadcasted_iota(jnp.int32, values[0].shape, 0)
    order = (3, 2, 1, 0, 7, 6, 5, 4)
    values = [values[number] for number in order]
    upper = row < 4
    values = [
        jnp.where(upper, a, b) + pltpu.roll(jnp.where(upper, b, a), 4, 0)
        for a, b in zip(values[:4], values[4:])
    ]
    for step, kept in ((2, row % 4 >= 2), (1, row % 2 == 1)):
        values = [
            jnp.where(kept, a + pltpu.roll(a, step, 0), b + pltpu.roll(b, 8 - step, 0))
            for a, b in zip(values[:step], values[step:])
        ]
    return values[0]


def looks_kernel(positions, root_ref, gap_ref, *refs):
    tiles, (out_ref, stack, sums, pooled, powers) = refs[:-5], refs[-5:]
    total, _, tile_lines, tile_columns = stack.shape
    owners, per_owner, lanes = out_ref.shape
    dates = per_owner // CHANNELS
    line_looks = tile_lines // LOOK_AZ
    unroll = total if total <= 16 else 1
    if len(tiles) > 1:
        for position, tile_ref in zip(positions, tiles):
            stack[pl.ds(tile_order(position) * dates, dates)] = tile_ref[...].astype(jnp.float32)
    else:

        def widen(owner, carry):
            stack[pl.ds(owner * dates, dates)] = tiles[0][owner].astype(jnp.float32)
            return carry

        lax.fori_loop(0, owners, widen, 0)

    def partner_of(kind, date):
        return partners(date, gap_ref, total)[kind - 1] if kind else root_ref[0]

    def collect(date, carry):
        left0, left1 = stack[date, 0], stack[date, 1]
        values = []
        for kind in range(KINDS):
            partner = partner_of(kind, date)
            right0, right1 = stack[partner, 0], stack[partner, 1]
            values += [left0 * right0 + left1 * right1, left1 * right0 - left0 * right1]
        values.append(left0 * left0 + left1 * left1)
        values.append(jnp.zeros_like(left0))
        rows = pl.ds(pl.multiple_of(date * QUANTITIES, QUANTITIES), QUANTITIES)
        for look in range(line_looks):
            start = look * LOOK_AZ
            sums[rows, look * tile_columns : (look + 1) * tile_columns] = row_sums(
                [value[start : start + 8] + value[start + 8 : start + 16] for value in values]
            )
        return carry

    lax.fori_loop(0, total, collect, 0, unroll=unroll)
    shape = (line_looks * tile_columns, lanes)
    row = lax.broadcasted_iota(jnp.int32, shape, 0)
    col = lax.broadcasted_iota(jnp.int32, shape, 1)
    pool = jnp.where(row // LOOK_RG == col, 1.0, 0.0).astype(jnp.bfloat16)
    whole = sums[...]
    coarse = whole.astype(jnp.bfloat16)
    fine = (whole - coarse.astype(jnp.float32)).astype(jnp.bfloat16)
    pooled[...] = jnp.dot(coarse, pool, preferred_element_type=jnp.float32) + jnp.dot(
        fine, pool, preferred_element_type=jnp.float32
    )

    def gather(date, carry):
        for kind in range(KINDS):
            power = partner_of(kind, date) * QUANTITIES + 2 * KINDS
            powers[kind, pl.ds(date, 1), :] = pooled[pl.ds(power, 1), :]
        return carry

    lax.fori_loop(0, total, gather, 0, unroll=unroll)
    scale = 1.0 / (LOOK_AZ * LOOK_RG) ** 0.5

    for slot in range(dates):

        def every(number):
            return pooled[pl.ds(slot * QUANTITIES + number, owners, stride=dates * QUANTITIES), :]

        power_left = every(2 * KINDS)
        for kind in range(KINDS):
            real, imag = every(2 * kind), every(2 * kind + 1)
            power_right = powers[kind, pl.ds(slot, owners, stride=dates), :]
            out_ref[:, slot * CHANNELS + 2 * kind, :] = real * scale
            out_ref[:, slot * CHANNELS + 2 * kind + 1, :] = imag * scale
            out_ref[:, slot * CHANNELS + 2 * KINDS + kind, :] = jnp.sqrt(
                real * real + imag * imag
            ) / jnp.sqrt(power_left * power_right + 1e-06)


def place_kernel(x_ref, ifg_ref, coh_ref):
    sources, rows, lanes = x_ref.shape
    dates, _, lines, columns = ifg_ref.shape
    looks = lanes // columns
    for slot in range(dates):
        for channel in range(CHANNELS):
            values = x_ref[:, slot * CHANNELS + channel, :]
            for look in range(looks):
                part = values[:, look * columns : (look + 1) * columns]
                where = pl.ds(look, sources, stride=looks)
                if channel < 2 * KINDS:
                    ifg_ref[slot, channel, where, :] = part
                else:
                    coh_ref[slot, channel - 2 * KINDS, where, :] = part


def body(
    epoch_tiles_quadrature,
    along_track_whole_displacement,
    along_track_subpixel_weights,
    slant_whole_displacement,
    slant_subpixel_weights,
    sweeps_each_epoch,
    baseline_companion_gap,
    master_epoch_image,
):
    block = epoch_tiles_quadrature
    dates, parts, lines, columns = block.shape
    owners = lax.axis_size("date")
    total = owners * dates
    images = dates * parts
    line_groups = min(owners, lines // LOOK_AZ)
    column_groups = owners // line_groups
    tile_lines, tile_columns = lines // line_groups, columns // column_groups
    line_looks, column_looks = tile_lines // LOOK_AZ, tile_columns // LOOK_RG
    lanes = line_looks * column_looks

    arguments = (
        block,
        along_track_whole_displacement,
        along_track_subpixel_weights,
        slant_whole_displacement,
        slant_subpixel_weights,
        sweeps_each_epoch,
        baseline_companion_gap.T,
    )
    block, even, odd, *small = pl.pallas_call(
        start_kernel,
        out_shape=(
            pltpu.VMEM(block.shape, block.dtype),
            pltpu.VMEM((lines, images * MARGIN), jnp.bfloat16),
            pltpu.VMEM((lines, images * MARGIN), jnp.bfloat16),
            *[pltpu.SMEM(array.shape, array.dtype) for array in arguments[1:]],
        ),
        in_specs=[pl.BlockSpec(memory_space=pltpu.HBM)] * len(arguments),
        out_specs=(VMEM,) * 3 + (SMEM,) * (len(arguments) - 1),
        scratch_shapes=[pltpu.SemaphoreType.DMA((images + len(arguments) - 1,))],
        name="start",
        compiler_params=pltpu.CompilerParams(vmem_limit_bytes=GRANT),
    )(*[pltpu.with_memory_space_constraint(array, pltpu.HBM) for array in arguments])
    *small, gap = [pltpu.with_memory_space_constraint(array, pltpu.SMEM) for array in small]
    width = lax.axis_size("range")
    odd = exchanged(odd, "range", [(j, j + 1) for j in range(1, width - 1, 2)])
    even = exchanged(even, "range", [(j, j + 1) for j in range(0, width - 1, 2)])

    own_taps, low_taps, high_taps, line_taps, root = pl.pallas_call(
        functools.partial(taps_kernel, tile_lines),
        out_shape=(
            pltpu.VMEM((dates, columns, columns), jnp.bfloat16),
            pltpu.VMEM((images * MARGIN, images * LANES), jnp.bfloat16),
            pltpu.VMEM((images * MARGIN, images * LANES), jnp.bfloat16),
            pltpu.VMEM((dates, lines, lines), jnp.bfloat16),
            pltpu.SMEM((8,), jnp.int32),
        ),
        in_specs=[SMEM] * (len(small) + 1),
        out_specs=(VMEM,) * 4 + (SMEM,),
        cost_estimate=pl.CostEstimate(flops=4000000, bytes_accessed=800000, transcendentals=0),
        name="taps",
        compiler_params=pltpu.CompilerParams(vmem_limit_bytes=GRANT),
    )(*small, master_epoch_image)
    tile = (dates, parts, tile_lines, tile_columns)
    if by_pairs(owners):
        out_shape = (pltpu.VMEM(tile, jnp.bfloat16),) * owners
    else:
        out_shape = (pltpu.VMEM((owners,) + tile, jnp.bfloat16),)
    tiles = pl.pallas_call(
        functools.partial(
            resample_kernel, (line_groups, column_groups, tile_lines, tile_columns)
        ),
        out_shape=out_shape,
        in_specs=[VMEM] * 7,
        out_specs=(VMEM,) * len(out_shape),
        scratch_shapes=[pltpu.VMEM((2,) + even.shape, even.dtype)],
        name="resample",
        compiler_params=pltpu.CompilerParams(vmem_limit_bytes=GRANT),
    )(*[near(array) for array in (block, even, odd, own_taps, low_taps, high_taps, line_taps)])

    if by_pairs(owners):
        order = [*range(owners - 2, 0, -2), *range(owners - 1, 0, -2)]
        received = {
            s: exchanged(tiles[s], "date", [(i, i ^ s) for i in range(owners) if i < i ^ s])
            for s in order
        }
        positions = [0] + order
        tiles = [tiles[0]] + [received[s] for s in order]
    else:
        tiles = [lax.all_to_all(tiles[0], "date", 0, 0)]
        positions = None
    results = pl.pallas_call(
        functools.partial(looks_kernel, positions),
        out_shape=pltpu.VMEM((owners, dates * CHANNELS, lanes), jnp.float32),
        in_specs=[SMEM] * 2 + [VMEM] * len(tiles),
        out_specs=VMEM,
        scratch_shapes=[
            pltpu.VMEM((total, parts, tile_lines, tile_columns), jnp.float32),
            pltpu.VMEM((total * QUANTITIES, line_looks * tile_columns), jnp.float32),
            pltpu.VMEM((total * QUANTITIES, lanes), jnp.float32),
            pltpu.VMEM((KINDS, total, lanes), jnp.float32),
        ],
        name="looks",
        compiler_params=pltpu.CompilerParams(vmem_limit_bytes=GRANT),
    )(
        pltpu.with_memory_space_constraint(root, pltpu.SMEM),
        gap,
        *[near(tile) for tile in tiles],
    )
    results = lax.all_to_all(results, "date", 0, 0)

    rows, cols = lines // LOOK_AZ, columns // LOOK_RG
    if column_groups == 1:
        return pl.pallas_call(
            place_kernel,
            out_shape=(
                jax.ShapeDtypeStruct((dates, 2 * KINDS, rows, cols), jnp.float32),
                jax.ShapeDtypeStruct((dates, KINDS, rows, cols), jnp.float32),
            ),
            in_specs=[VMEM],
            out_specs=(VMEM, VMEM),
            name="place",
            compiler_params=pltpu.CompilerParams(vmem_limit_bytes=GRANT),
        )(near(results))
    whole = results.reshape(
        line_groups, column_groups, dates, CHANNELS, line_looks, column_looks
    )
    whole = jnp.transpose(whole, (2, 3, 0, 4, 1, 5)).reshape(dates, CHANNELS, rows, cols)
    return (whole[:, : 2 * KINDS], whole[:, 2 * KINDS :])


def solution(mesh):
    in_specs = (P("date", None, None, "range"), P(), P(), P(), P(), P(), P(), P())
    out_specs = (P("date", None, None, "range"), P("date", None, None, "range"))
    return jax.shard_map(body, mesh=mesh, in_specs=in_specs, out_specs=out_specs, check_vma=False)
```

```python
import functools

import jax
import jax.numpy as jnp
from jax import lax
from jax.experimental import pallas as pl
from jax.experimental.pallas import tpu as pltpu
from jax.sharding import PartitionSpec as P

MAX_SWEEPS = 4
TAPS = 8
FRACTIONS = 16
MARGIN = 16
LOOK_AZ = 16
LOOK_RG = 4
QUANTITIES = 8
KINDS = 3
CHANNELS = 9
LANES = 128
GRANT = 24 * 2**20

SMEM = pl.BlockSpec(memory_space=pltpu.SMEM)
VMEM = pl.BlockSpec(memory_space=pltpu.VMEM)


def exchanged(array, axis, pairs):
    return lax.ppermute(array, axis, [route for a, b in pairs for route in ((a, b), (b, a))])


def near(array):
    return pltpu.with_memory_space_constraint(array, pltpu.VMEM)


def iotas(rows, cols):
    return (
        lax.broadcasted_iota(jnp.int32, (rows, cols), 0),
        lax.broadcasted_iota(jnp.int32, (rows, cols), 1),
    )


def weight_rows(fractions):
    row, lane = iotas(8, LANES)
    spot = jnp.zeros((8, LANES), jnp.float32)
    for number, fraction in enumerate(fractions):
        spot = jnp.where(row == number, fraction.astype(jnp.float32), spot)
    spacing = (lane - 1 - (TAPS // 2 - 1)).astype(jnp.float32) - spot / FRACTIONS
    angle = jnp.pi * spacing
    sinc = jnp.where(spacing == 0.0, 1.0, jnp.sin(angle) / jnp.where(spacing == 0.0, 1.0, angle))
    weights = sinc * jnp.cos(angle / (TAPS + 1)) ** 2
    weights = jnp.where((lane >= 1) & (lane <= TAPS), weights, 0.0)
    weights = weights / jnp.sum(weights, axis=1, keepdims=True)
    return weights.astype(jnp.bfloat16).astype(jnp.float32)


def by_pairs(owners):
    return owners in (2, 4, 8)


def tile_order(position):
    if by_pairs(lax.axis_size("date")):
        return position ^ lax.axis_index("date")
    return position


def banded(offsets, weights):
    rows, cols = offsets.shape
    lanes = jnp.broadcast_to(weights, (rows, LANES))
    spots = jnp.clip(offsets + 1, 0, TAPS + 1)
    return jnp.concatenate(
        [
            jnp.take_along_axis(lanes, spots[:, start : start + LANES], axis=1)
            for start in range(0, cols, LANES)
        ],
        axis=1,
    )


def start_kernel(x_ref, *refs):
    dates, parts, _, columns = x_ref.shape
    images = [(slot, part) for slot in range(dates) for part in range(parts)]
    count = (len(refs) - 4) // 2
    near_ref, even_ref, odd_ref = refs[count : count + 3]
    sems = refs[-1]
    small = list(zip(refs[:count], refs[count + 3 : -1]))
    whole = [(x_ref.at[image], near_ref.at[image]) for image in images]
    copies = [
        pltpu.make_async_copy(source, target, sems.at[number])
        for number, (source, target) in enumerate(whole + small)
    ]
    for copy in copies:
        copy.start()
    forward = lax.axis_index("range") % 2 == 0
    for number, (slot, part) in enumerate(images):
        copies[number].wait()
        spot = slice(number * MARGIN, (number + 1) * MARGIN)
        for parity, last_ref, first_ref in (
            (forward, even_ref, odd_ref),
            (jnp.logical_not(forward), odd_ref, even_ref),
        ):

            @pl.when(parity)
            def _():
                last_ref[:, spot] = near_ref[slot, part, :, columns - MARGIN :]
                first_ref[:, spot] = near_ref[slot, part, :, :MARGIN]

    for copy in copies[len(images) :]:
        copy.wait()


def taps_kernel(
    tile_lines,
    az_whole,
    az_part,
    rg_whole,
    rg_part,
    sweeps,
    master_ref,
    own_ref,
    low_ref,
    high_ref,
    line_ref,
    root_ref,
):
    dates, columns, _ = own_ref.shape
    lines = line_ref.shape[1]
    edge_rows = low_ref.shape[0]
    parts = edge_rows // MARGIN // dates
    centre = TAPS // 2 - 1
    for number in range(root_ref.shape[0]):
        root_ref[number] = master_ref[0]
    present = [lax.axis_index("date") * dates + slot for slot in range(dates)]
    table = weight_rows([rg_part[d] for d in present] + [az_part[d] for d in present])
    for slot, date in enumerate(present):
        shift = centre - rg_whole[date]
        weights = table[slot : slot + 1]
        row, col = iotas(columns, columns)
        own_ref[slot] = banded(row - col + shift, weights).astype(jnp.bfloat16)
        row, col = iotas(edge_rows, LANES)
        low = banded(row % MARGIN - MARGIN - col + shift, weights)
        high = banded(row % MARGIN + LANES - col + shift, weights)
        for part in range(parts):
            image = slot * parts + part
            held = row // MARGIN == image
            spot = slice(image * LANES, (image + 1) * LANES)
            low_ref[:, spot] = jnp.where(held, low, 0.0).astype(jnp.bfloat16)
            high_ref[:, spot] = jnp.where(held, high, 0.0).astype(jnp.bfloat16)
        row, col = iotas(lines, lines)
        row = tile_order(row // tile_lines) * tile_lines + row % tile_lines
        weights = table[dates + slot : dates + slot + 1]
        band = banded(col - row + (centre - az_whole[date]), weights)
        usable = row < sweeps[date] * (lines // MAX_SWEEPS)
        line_ref[slot] = jnp.where(usable, band, 0.0).astype(jnp.bfloat16)


def resample_kernel(split, x_ref, odd_ref, even_ref, own_ref, low_ref, high_ref, line_ref, *refs):
    *outs, edges = refs
    dates, parts, _, columns = x_ref.shape
    line_groups, column_groups, tile_lines, tile_columns = split
    backward = lax.axis_index("range") % 2
    edges[1 - backward] = even_ref[...]
    edges[backward] = odd_ref[...]
    low = jnp.dot(edges[0], low_ref[...], preferred_element_type=jnp.float32)
    high = jnp.dot(edges[1], high_ref[...], preferred_element_type=jnp.float32)
    for slot in range(dates):
        for part in range(parts):
            spot = slice((slot * parts + part) * LANES, (slot * parts + part + 1) * LANES)
            ranged = jnp.dot(x_ref[slot, part], own_ref[slot], preferred_element_type=jnp.float32)
            pieces = [ranged[:, start : start + LANES] for start in range(0, columns, LANES)]
            pieces[0] += low[:, spot]
            pieces[-1] += high[:, spot]
            ranged = jnp.concatenate(pieces, axis=1)
            moved = jnp.dot(
                line_ref[slot], ranged.astype(jnp.bfloat16), preferred_element_type=jnp.float32
            ).astype(jnp.bfloat16)
            for i in range(line_groups):
                for j in range(column_groups):
                    tile = moved[
                        i * tile_lines : (i + 1) * tile_lines,
                        j * tile_columns : (j + 1) * tile_columns,
                    ]
                    if len(outs) == 1:
                        outs[0][i * column_groups + j, slot, part] = tile
                    else:
                        outs[i][slot, part] = tile


def partners(date, gap_ref, total):
    ahead = date + gap_ref[0, date]
    later = jnp.where(ahead < total, ahead, date - gap_ref[0, date])
    back = date - gap_ref[1, date]
    earlier = jnp.where(back >= 0, back, date + gap_ref[1, date])
    return (later, earlier)


def row_sums(values):
    row = lax.broadcasted_iota(jnp.int32, values[0].shape, 0)
    order = (3, 2, 1, 0, 7, 6, 5, 4)
    values = [values[number] for number in order]
    upper = row < 4
    values = [
        jnp.where(upper, a, b) + pltpu.roll(jnp.where(upper, b, a), 4, 0)
        for a, b in zip(values[:4], values[4:])
    ]
    for step, kept in ((2, row % 4 >= 2), (1, row % 2 == 1)):
        values = [
            jnp.where(kept, a + pltpu.roll(a, step, 0), b + pltpu.roll(b, 8 - step, 0))
            for a, b in zip(values[:step], values[step:])
        ]
    return values[0]


def looks_kernel(positions, root_ref, gap_ref, *refs):
    tiles, (out_ref, stack, sums, pooled, powers) = refs[:-5], refs[-5:]
    total, _, tile_lines, tile_columns = stack.shape
    owners, per_owner, lanes = out_ref.shape
    dates = per_owner // CHANNELS
    line_looks = tile_lines // LOOK_AZ
    unroll = total if total <= 16 else 1
    if len(tiles) > 1:
        for position, tile_ref in zip(positions, tiles):
            stack[pl.ds(tile_order(position) * dates, dates)] = tile_ref[...].astype(jnp.float32)
    else:

        def widen(owner, carry):
            stack[pl.ds(owner * dates, dates)] = tiles[0][owner].astype(jnp.float32)
            return carry

        lax.fori_loop(0, owners, widen, 0)

    def partner_of(kind, date):
        return partners(date, gap_ref, total)[kind - 1] if kind else root_ref[0]

    def collect(date, carry):
        left0, left1 = stack[date, 0], stack[date, 1]
        values = []
        for kind in range(KINDS):
            partner = partner_of(kind, date)
            right0, right1 = stack[partner, 0], stack[partner, 1]
            values += [left0 * right0 + left1 * right1, left1 * right0 - left0 * right1]
        values.append(left0 * left0 + left1 * left1)
        values.append(jnp.zeros_like(left0))
        rows = pl.ds(pl.multiple_of(date * QUANTITIES, QUANTITIES), QUANTITIES)
        for look in range(line_looks):
            start = look * LOOK_AZ
            sums[rows, look * tile_columns : (look + 1) * tile_columns] = row_sums(
                [value[start : start + 8] + value[start + 8 : start + 16] for value in values]
            )
        return carry

    lax.fori_loop(0, total, collect, 0, unroll=unroll)
    shape = (line_looks * tile_columns, lanes)
    row = lax.broadcasted_iota(jnp.int32, shape, 0)
    col = lax.broadcasted_iota(jnp.int32, shape, 1)
    pool = jnp.where(row // LOOK_RG == col, 1.0, 0.0).astype(jnp.bfloat16)
    whole = sums[...]
    coarse = whole.astype(jnp.bfloat16)
    fine = (whole - coarse.astype(jnp.float32)).astype(jnp.bfloat16)
    pooled[...] = jnp.dot(coarse, pool, preferred_element_type=jnp.float32) + jnp.dot(
        fine, pool, preferred_element_type=jnp.float32
    )

    def gather(date, carry):
        for kind in range(KINDS):
            power = partner_of(kind, date) * QUANTITIES + 2 * KINDS
            powers[kind, pl.ds(date, 1), :] = pooled[pl.ds(power, 1), :]
        return carry

    lax.fori_loop(0, total, gather, 0, unroll=unroll)
    scale = 1.0 / (LOOK_AZ * LOOK_RG) ** 0.5

    for slot in range(dates):

        def every(number):
            return pooled[pl.ds(slot * QUANTITIES + number, owners, stride=dates * QUANTITIES), :]

        power_left = every(2 * KINDS)
        for kind in range(KINDS):
            real, imag = every(2 * kind), every(2 * kind + 1)
            power_right = powers[kind, pl.ds(slot, owners, stride=dates), :]
            out_ref[:, slot * CHANNELS + 2 * kind, :] = real * scale
            out_ref[:, slot * CHANNELS + 2 * kind + 1, :] = imag * scale
            out_ref[:, slot * CHANNELS + 2 * KINDS + kind, :] = jnp.sqrt(
                real * real + imag * imag
            ) / jnp.sqrt(power_left * power_right + 1e-06)


def place_kernel(x_ref, ifg_ref, coh_ref):
    sources, rows, lanes = x_ref.shape
    dates, _, lines, columns = ifg_ref.shape
    looks = lanes // columns
    for slot in range(dates):
        for channel in range(CHANNELS):
            values = x_ref[:, slot * CHANNELS + channel, :]
            for look in range(looks):
                part = values[:, look * columns : (look + 1) * columns]
                where = pl.ds(look, sources, stride=looks)
                if channel < 2 * KINDS:
                    ifg_ref[slot, channel, where, :] = part
                else:
                    coh_ref[slot, channel - 2 * KINDS, where, :] = part


def body(
    epoch_tiles_quadrature,
    along_track_whole_displacement,
    along_track_subpixel_weights,
    slant_whole_displacement,
    slant_subpixel_weights,
    sweeps_each_epoch,
    baseline_companion_gap,
    master_epoch_image,
):
    block = epoch_tiles_quadrature
    dates, parts, lines, columns = block.shape
    owners = lax.axis_size("date")
    total = owners * dates
    images = dates * parts
    line_groups = min(owners, lines // LOOK_AZ)
    column_groups = owners // line_groups
    tile_lines, tile_columns = lines // line_groups, columns // column_groups
    line_looks, column_looks = tile_lines // LOOK_AZ, tile_columns // LOOK_RG
    lanes = line_looks * column_looks

    arguments = (
        block,
        along_track_whole_displacement,
        along_track_subpixel_weights,
        slant_whole_displacement,
        slant_subpixel_weights,
        sweeps_each_epoch,
        baseline_companion_gap.T,
    )
    block, even, odd, *small = pl.pallas_call(
        start_kernel,
        out_shape=(
            pltpu.VMEM(block.shape, block.dtype),
            pltpu.VMEM((lines, images * MARGIN), jnp.bfloat16),
            pltpu.VMEM((lines, images * MARGIN), jnp.bfloat16),
            *[pltpu.SMEM(array.shape, array.dtype) for array in arguments[1:]],
        ),
        in_specs=[pl.BlockSpec(memory_space=pltpu.HBM)] * len(arguments),
        out_specs=(VMEM,) * 3 + (SMEM,) * (len(arguments) - 1),
        scratch_shapes=[pltpu.SemaphoreType.DMA((images + len(arguments) - 1,))],
        name="start",
        compiler_params=pltpu.CompilerParams(vmem_limit_bytes=GRANT),
    )(*[pltpu.with_memory_space_constraint(array, pltpu.HBM) for array in arguments])
    *small, gap = [pltpu.with_memory_space_constraint(array, pltpu.SMEM) for array in small]
    width = lax.axis_size("range")
    odd = exchanged(odd, "range", [(j, j + 1) for j in range(1, width - 1, 2)])
    even = exchanged(even, "range", [(j, j + 1) for j in range(0, width - 1, 2)])

    own_taps, low_taps, high_taps, line_taps, root = pl.pallas_call(
        functools.partial(taps_kernel, tile_lines),
        out_shape=(
            pltpu.VMEM((dates, columns, columns), jnp.bfloat16),
            pltpu.VMEM((images * MARGIN, images * LANES), jnp.bfloat16),
            pltpu.VMEM((images * MARGIN, images * LANES), jnp.bfloat16),
            pltpu.VMEM((dates, lines, lines), jnp.bfloat16),
            pltpu.SMEM((8,), jnp.int32),
        ),
        in_specs=[SMEM] * (len(small) + 1),
        out_specs=(VMEM,) * 4 + (SMEM,),
        cost_estimate=pl.CostEstimate(flops=4000000, bytes_accessed=800000, transcendentals=0),
        name="taps",
        compiler_params=pltpu.CompilerParams(vmem_limit_bytes=GRANT),
    )(*small, master_epoch_image)
    tile = (dates, parts, tile_lines, tile_columns)
    if by_pairs(owners):
        out_shape = (pltpu.VMEM(tile, jnp.bfloat16),) * owners
    else:
        out_shape = (pltpu.VMEM((owners,) + tile, jnp.bfloat16),)
    tiles = pl.pallas_call(
        functools.partial(
            resample_kernel, (line_groups, column_groups, tile_lines, tile_columns)
        ),
        out_shape=out_shape,
        in_specs=[VMEM] * 7,
        out_specs=(VMEM,) * len(out_shape),
        scratch_shapes=[pltpu.VMEM((2,) + even.shape, even.dtype)],
        name="resample",
        compiler_params=pltpu.CompilerParams(vmem_limit_bytes=GRANT),
    )(*[near(array) for array in (block, odd, even, own_taps, low_taps, high_taps, line_taps)])

    if by_pairs(owners):
        order = [*range(owners - 2, 0, -2), *range(owners - 1, 0, -2)]
        received = {
            s: exchanged(tiles[s], "date", [(i, i ^ s) for i in range(owners) if i < i ^ s])
            for s in order
        }
        positions = [0] + order
        tiles = [tiles[0]] + [received[s] for s in order]
    else:
        tiles = [lax.all_to_all(tiles[0], "date", 0, 0)]
        positions = None
    results = pl.pallas_call(
        functools.partial(looks_kernel, positions),
        out_shape=pltpu.VMEM((owners, dates * CHANNELS, lanes), jnp.float32),
        in_specs=[SMEM] * 2 + [VMEM] * len(tiles),
        out_specs=VMEM,
        scratch_shapes=[
            pltpu.VMEM((total, parts, tile_lines, tile_columns), jnp.float32),
            pltpu.VMEM((total * QUANTITIES, line_looks * tile_columns), jnp.float32),
            pltpu.VMEM((total * QUANTITIES, lanes), jnp.float32),
            pltpu.VMEM((KINDS, total, lanes), jnp.float32),
        ],
        name="looks",
        compiler_params=pltpu.CompilerParams(vmem_limit_bytes=GRANT),
    )(
        pltpu.with_memory_space_constraint(root, pltpu.SMEM),
        gap,
        *[near(tile) for tile in tiles],
    )
    results = lax.all_to_all(results, "date", 0, 0)

    rows, cols = lines // LOOK_AZ, columns // LOOK_RG
    if column_groups == 1:
        return pl.pallas_call(
            place_kernel,
            out_shape=(
                jax.ShapeDtypeStruct((dates, 2 * KINDS, rows, cols), jnp.float32),
                jax.ShapeDtypeStruct((dates, KINDS, rows, cols), jnp.float32),
            ),
            in_specs=[VMEM],
            out_specs=(VMEM, VMEM),
            name="place",
            compiler_params=pltpu.CompilerParams(vmem_limit_bytes=GRANT),
        )(near(results))
    whole = results.reshape(
        line_groups, column_groups, dates, CHANNELS, line_looks, column_looks
    )
    whole = jnp.transpose(whole, (2, 3, 0, 4, 1, 5)).reshape(dates, CHANNELS, rows, cols)
    return (whole[:, : 2 * KINDS], whole[:, 2 * KINDS :])


def solution(mesh):
    in_specs = (P("date", None, None, "range"), P(), P(), P(), P(), P(), P(), P())
    out_specs = (P("date", None, None, "range"), P("date", None, None, "range"))
    return jax.shard_map(body, mesh=mesh, in_specs=in_specs, out_specs=out_specs, check_vma=False)
```

```python
import functools

import jax
import jax.numpy as jnp
from jax import lax
from jax.experimental import pallas as pl
from jax.experimental.pallas import tpu as pltpu
from jax.sharding import PartitionSpec as P

MAX_SWEEPS = 4
TAPS = 8
FRACTIONS = 16
MARGIN = 16
LOOK_AZ = 16
LOOK_RG = 4
QUANTITIES = 8
KINDS = 3
CHANNELS = 9
LANES = 128
GRANT = 24 * 2**20
CORES = 2
CHIPS = 4
CHIP_LOOKS = 4

SMEM = pl.BlockSpec(memory_space=pltpu.SMEM)
VMEM = pl.BlockSpec(memory_space=pltpu.VMEM)


def exchanged(array, axis, pairs):
    return lax.ppermute(array, axis, [route for a, b in pairs for route in ((a, b), (b, a))])


def near(array):
    return pltpu.with_memory_space_constraint(array, pltpu.VMEM)


def iotas(rows, cols):
    return (
        lax.broadcasted_iota(jnp.int32, (rows, cols), 0),
        lax.broadcasted_iota(jnp.int32, (rows, cols), 1),
    )


def weight_rows(fractions):
    row, lane = iotas(8, LANES)
    spot = jnp.zeros((8, LANES), jnp.float32)
    for number, fraction in enumerate(fractions):
        spot = jnp.where(row == number, fraction.astype(jnp.float32), spot)
    spacing = (lane - 1 - (TAPS // 2 - 1)).astype(jnp.float32) - spot / FRACTIONS
    angle = jnp.pi * spacing
    sinc = jnp.where(spacing == 0.0, 1.0, jnp.sin(angle) / jnp.where(spacing == 0.0, 1.0, angle))
    weights = sinc * jnp.cos(angle / (TAPS + 1)) ** 2
    weights = jnp.where((lane >= 1) & (lane <= TAPS), weights, 0.0)
    weights = weights / jnp.sum(weights, axis=1, keepdims=True)
    return weights.astype(jnp.bfloat16).astype(jnp.float32)


def by_chips(block, owners):
    dates, parts, lines, columns = block.shape
    return (
        owners == CHIPS * CORES
        and (dates, parts) == (2, 2)
        and lines == CHIPS * CHIP_LOOKS * LOOK_AZ
        and columns == 2 * LANES
    )


def tile_order(position, chips):
    return position ^ (lax.axis_index("date") // CORES) if chips else position


def banded(offsets, weights):
    rows, cols = offsets.shape
    lanes = jnp.broadcast_to(weights, (rows, LANES))
    spots = jnp.clip(offsets + 1, 0, TAPS + 1)
    return jnp.concatenate(
        [
            jnp.take_along_axis(lanes, spots[:, start : start + LANES], axis=1)
            for start in range(0, cols, LANES)
        ],
        axis=1,
    )


def start_kernel(x_ref, *refs):
    dates, parts, _, columns = x_ref.shape
    images = [(slot, part) for slot in range(dates) for part in range(parts)]
    count = (len(refs) - 4) // 2
    near_ref, even_ref, odd_ref = refs[count : count + 3]
    sems = refs[-1]
    small = list(zip(refs[:count], refs[count + 3 : -1]))
    whole = [(x_ref.at[image], near_ref.at[image]) for image in images]
    copies = [
        pltpu.make_async_copy(source, target, sems.at[number])
        for number, (source, target) in enumerate(whole + small)
    ]
    for copy in copies:
        copy.start()
    forward = lax.axis_index("range") % 2 == 0
    for number, (slot, part) in enumerate(images):
        copies[number].wait()
        spot = slice(number * MARGIN, (number + 1) * MARGIN)
        for parity, last_ref, first_ref in (
            (forward, even_ref, odd_ref),
            (jnp.logical_not(forward), odd_ref, even_ref),
        ):

            @pl.when(parity)
            def _():
                last_ref[:, spot] = near_ref[slot, part, :, columns - MARGIN :]
                first_ref[:, spot] = near_ref[slot, part, :, :MARGIN]

    for copy in copies[len(images) :]:
        copy.wait()


def taps_kernel(
    chips,
    tile_lines,
    az_whole,
    az_part,
    rg_whole,
    rg_part,
    sweeps,
    master_ref,
    own_ref,
    low_ref,
    high_ref,
    line_ref,
    root_ref,
):
    dates, columns, _ = own_ref.shape
    lines = line_ref.shape[1]
    edge_rows = low_ref.shape[0]
    parts = edge_rows // MARGIN // dates
    centre = TAPS // 2 - 1
    for number in range(root_ref.shape[0]):
        root_ref[number] = master_ref[0]
    present = [lax.axis_index("date") * dates + slot for slot in range(dates)]
    table = weight_rows([rg_part[d] for d in present] + [az_part[d] for d in present])
    for slot, date in enumerate(present):
        shift = centre - rg_whole[date]
        weights = table[slot : slot + 1]
        row, col = iotas(columns, columns)
        own_ref[slot] = banded(row - col + shift, weights).astype(jnp.bfloat16)
        row, col = iotas(edge_rows, LANES)
        low = banded(row % MARGIN - MARGIN - col + shift, weights)
        high = banded(row % MARGIN + LANES - col + shift, weights)
        for part in range(parts):
            image = slot * parts + part
            held = row // MARGIN == image
            spot = slice(image * LANES, (image + 1) * LANES)
            low_ref[:, spot] = jnp.where(held, low, 0.0).astype(jnp.bfloat16)
            high_ref[:, spot] = jnp.where(held, high, 0.0).astype(jnp.bfloat16)
        row, col = iotas(lines, lines)
        row = tile_order(row // tile_lines, chips) * tile_lines + row % tile_lines
        weights = table[dates + slot : dates + slot + 1]
        band = banded(col - row + (centre - az_whole[date]), weights)
        usable = row < sweeps[date] * (lines // MAX_SWEEPS)
        line_ref[slot] = jnp.where(usable, band, 0.0).astype(jnp.bfloat16)


def resample_kernel(split, x_ref, even_ref, odd_ref, own_ref, low_ref, high_ref, line_ref, *refs):
    *outs, edges = refs
    dates, parts, _, columns = x_ref.shape
    line_groups, column_groups, tile_lines, tile_columns = split
    backward = lax.axis_index("range") % 2
    edges[1 - backward] = even_ref[...]
    edges[backward] = odd_ref[...]
    low = jnp.dot(edges[0], low_ref[...], preferred_element_type=jnp.float32)
    high = jnp.dot(edges[1], high_ref[...], preferred_element_type=jnp.float32)
    for slot in range(dates):
        for part in range(parts):
            spot = slice((slot * parts + part) * LANES, (slot * parts + part + 1) * LANES)
            ranged = jnp.dot(x_ref[slot, part], own_ref[slot], preferred_element_type=jnp.float32)
            pieces = [ranged[:, start : start + LANES] for start in range(0, columns, LANES)]
            pieces[0] += low[:, spot]
            pieces[-1] += high[:, spot]
            ranged = jnp.concatenate(pieces, axis=1)
            moved = jnp.dot(
                line_ref[slot], ranged.astype(jnp.bfloat16), preferred_element_type=jnp.float32
            ).astype(jnp.bfloat16)
            for i in range(line_groups):
                for j in range(column_groups):
                    tile = moved[
                        i * tile_lines : (i + 1) * tile_lines,
                        j * tile_columns : (j + 1) * tile_columns,
                    ]
                    if len(outs) == 1:
                        outs[0][i * column_groups + j, slot, part] = tile
                    else:
                        outs[i][slot, part] = tile


def partners(date, gap_ref, total):
    ahead = date + gap_ref[0, date]
    later = jnp.where(ahead < total, ahead, date - gap_ref[0, date])
    back = date - gap_ref[1, date]
    earlier = jnp.where(back >= 0, back, date + gap_ref[1, date])
    return (later, earlier)


def row_sums(values):
    row = lax.broadcasted_iota(jnp.int32, values[0].shape, 0)
    order = (3, 2, 1, 0, 7, 6, 5, 4)
    values = [values[number] for number in order]
    upper = row < 4
    values = [
        jnp.where(upper, a, b) + pltpu.roll(jnp.where(upper, b, a), 4, 0)
        for a, b in zip(values[:4], values[4:])
    ]
    for step, kept in ((2, row % 4 >= 2), (1, row % 2 == 1)):
        values = [
            jnp.where(kept, a + pltpu.roll(a, step, 0), b + pltpu.roll(b, 8 - step, 0))
            for a, b in zip(values[:step], values[step:])
        ]
    return values[0]


def pool_columns(sums, lanes):
    row, col = iotas(sums.shape[1], lanes)
    pool = jnp.where(row // LOOK_RG == col, 1.0, 0.0).astype(jnp.bfloat16)
    coarse = sums.astype(jnp.bfloat16)
    fine = (sums - coarse.astype(jnp.float32)).astype(jnp.bfloat16)
    return jnp.dot(coarse, pool, preferred_element_type=jnp.float32) + jnp.dot(
        fine, pool, preferred_element_type=jnp.float32
    )


def looks_kernel(root_ref, gap_ref, tiles_ref, out_ref, stack, sums, pooled, powers):
    total, _, tile_lines, tile_columns = stack.shape
    owners, per_owner, lanes = out_ref.shape
    dates = per_owner // CHANNELS
    line_looks = tile_lines // LOOK_AZ
    unroll = total if total <= 16 else 1

    def widen(owner, carry):
        stack[pl.ds(owner * dates, dates)] = tiles_ref[owner].astype(jnp.float32)
        return carry

    lax.fori_loop(0, owners, widen, 0)

    def partner_of(kind, date):
        return partners(date, gap_ref, total)[kind - 1] if kind else root_ref[0]

    def collect(date, carry):
        left0, left1 = stack[date, 0], stack[date, 1]
        values = []
        for kind in range(KINDS):
            partner = partner_of(kind, date)
            right0, right1 = stack[partner, 0], stack[partner, 1]
            values += [left0 * right0 + left1 * right1, left1 * right0 - left0 * right1]
        values.append(left0 * left0 + left1 * left1)
        values.append(jnp.zeros_like(left0))
        rows = pl.ds(pl.multiple_of(date * QUANTITIES, QUANTITIES), QUANTITIES)
        for look in range(line_looks):
            start = look * LOOK_AZ
            sums[rows, look * tile_columns : (look + 1) * tile_columns] = row_sums(
                [value[start : start + 8] + value[start + 8 : start + 16] for value in values]
            )
        return carry

    lax.fori_loop(0, total, collect, 0, unroll=unroll)
    pooled[...] = pool_columns(sums[...], lanes)

    def gather(date, carry):
        for kind in range(KINDS):
            power = partner_of(kind, date) * QUANTITIES + 2 * KINDS
            powers[kind, pl.ds(date, 1), :] = pooled[pl.ds(power, 1), :]
        return carry

    lax.fori_loop(0, total, gather, 0, unroll=unroll)
    scale = 1.0 / (LOOK_AZ * LOOK_RG) ** 0.5

    for slot in range(dates):

        def every(number):
            return pooled[pl.ds(slot * QUANTITIES + number, owners, stride=dates * QUANTITIES), :]

        power_left = every(2 * KINDS)
        for kind in range(KINDS):
            real, imag = every(2 * kind), every(2 * kind + 1)
            power_right = powers[kind, pl.ds(slot, owners, stride=dates), :]
            out_ref[:, slot * CHANNELS + 2 * kind, :] = real * scale
            out_ref[:, slot * CHANNELS + 2 * kind + 1, :] = imag * scale
            out_ref[:, slot * CHANNELS + 2 * KINDS + kind, :] = jnp.sqrt(
                real * real + imag * imag
            ) / jnp.sqrt(power_left * power_right + 1e-06)


def chip_looks_kernel(root_ref, gap_ref, *refs):
    tiles, outs, (stack, sums, pooled) = refs[: CHIPS * CORES], refs[CHIPS * CORES : -3], refs[-3:]
    dates, _, _, columns = tiles[0].shape
    me = lax.axis_index("date")
    total = len(tiles) * dates
    scale = 1.0 / (LOOK_AZ * LOOK_RG) ** 0.5
    for position, tile_ref in enumerate(tiles):
        stack[position * dates : (position + 1) * dates] = tile_ref[...].astype(jnp.float32)

    def partner_of(kind, date):
        partner = partners(date, gap_ref, total)[kind - 1] if kind else root_ref[0]
        return lax.div(partner, dates) ^ me, lax.rem(partner, dates)

    def part(spot, number, look):
        return stack[spot, number, look * LOOK_AZ : (look + 1) * LOOK_AZ, :]

    def folded(value):
        return value[: LOOK_AZ // 2] + value[LOOK_AZ // 2 :]

    block = QUANTITIES * CHIP_LOOKS
    for chip in range(CHIPS):
        for slot in range(dates):
            date = (me ^ (CORES * chip)) * dates + slot
            own = CORES * chip * dates + slot
            spot = slice(slot * columns, (slot + 1) * columns)
            for kind in range(KINDS):
                position, number = partner_of(kind, date)
                other = position * dates + number
                reals, imags = [], []
                for look in range(CHIP_LOOKS):
                    left0, left1 = part(own, 0, look), part(own, 1, look)
                    right0, right1 = part(other, 0, look), part(other, 1, look)
                    reals.append(folded(left0 * right0 + left1 * right1))
                    imags.append(folded(left1 * right0 - left0 * right1))
                start = chip * block + kind * 2 * CHIP_LOOKS
                sums[start : start + 2 * CHIP_LOOKS, spot] = row_sums(reals + imags)
            powers = []
            for core in range(CORES):
                for look in range(CHIP_LOOKS):
                    left0 = part(own + core * dates, 0, look)
                    left1 = part(own + core * dates, 1, look)
                    powers.append(folded(left0 * left0 + left1 * left1))
            start = chip * block + KINDS * 2 * CHIP_LOOKS
            sums[start : start + 2 * CHIP_LOOKS, spot] = row_sums(powers)
    pooled[...] = pool_columns(sums[...], LANES)

    row, lane = iotas(2 * CHIP_LOOKS, LANES)
    upper, first = row < CHIP_LOOKS, lane < LANES // 2
    for chip in range(CHIPS):
        base = chip * block
        views = [pooled[base + 8 * number : base + 8 * (number + 1), :] for number in range(4)]
        squares = [view * view for view in views[:KINDS]]
        squares = [square + pltpu.roll(square, CHIP_LOOKS, 0) for square in squares]
        power_left = jnp.where(upper, views[KINDS], pltpu.roll(views[KINDS], CHIP_LOOKS, 0))
        power_right = []
        for kind in range(KINDS):
            halves = []
            for slot in range(dates):
                position, number = partner_of(kind, (me ^ (CORES * chip)) * dates + slot)
                start = lax.div(position, CORES) * block + KINDS * 2 * CHIP_LOOKS
                power = pooled[pl.ds(pl.multiple_of(start, 8), 8), :]
                power = pltpu.roll(power, CHIP_LOOKS * (lax.rem(position, CORES) ^ (kind % 2)), 0)
                halves.append(pltpu.roll(power, LANES // 2 * (number ^ slot), 1))
            power_right.append(jnp.where(first, halves[0], halves[1]))
        outs[chip][: 2 * KINDS * CHIP_LOOKS, :] = (
            pooled[base : base + 2 * KINDS * CHIP_LOOKS, :] * scale
        )
        pairs = (
            (jnp.where(upper, squares[0], squares[1]), jnp.where(upper, *power_right[:2])),
            (squares[2], power_right[2]),
        )
        start = 2 * KINDS * CHIP_LOOKS
        for square, power in pairs:
            coherent = jnp.sqrt(square) / jnp.sqrt(power_left * power + 1e-06)
            rows = min(8, outs[chip].shape[0] - start)
            outs[chip][start : start + rows, :] = coherent[:rows]
            start += rows


def chip_place_kernel(*refs):
    pieces, (ifg_ref, coh_ref) = refs[:CHIPS], refs[CHIPS:]
    dates, _, _, columns = ifg_ref.shape
    mine = lax.axis_index("date") // CORES
    for chip in range(CHIPS):

        @pl.when(mine == chip)
        def _():
            for position, piece_ref in enumerate(pieces):
                start = (chip ^ position) * CHIP_LOOKS
                where = slice(start, start + CHIP_LOOKS)
                for channel in range(CHANNELS):
                    rows = piece_ref[channel * CHIP_LOOKS : (channel + 1) * CHIP_LOOKS, :]
                    for slot in range(dates):
                        part = rows[:, slot * columns : (slot + 1) * columns]
                        if channel < 2 * KINDS:
                            ifg_ref[slot, channel, where, :] = part
                        else:
                            coh_ref[slot, channel - 2 * KINDS, where, :] = part


def place_kernel(x_ref, ifg_ref, coh_ref):
    sources, rows, lanes = x_ref.shape
    dates, _, lines, columns = ifg_ref.shape
    looks = lanes // columns
    for slot in range(dates):
        for channel in range(CHANNELS):
            values = x_ref[:, slot * CHANNELS + channel, :]
            for look in range(looks):
                part = values[:, look * columns : (look + 1) * columns]
                where = pl.ds(look, sources, stride=looks)
                if channel < 2 * KINDS:
                    ifg_ref[slot, channel, where, :] = part
                else:
                    coh_ref[slot, channel - 2 * KINDS, where, :] = part


def body(
    epoch_tiles_quadrature,
    along_track_whole_displacement,
    along_track_subpixel_weights,
    slant_whole_displacement,
    slant_subpixel_weights,
    sweeps_each_epoch,
    baseline_companion_gap,
    master_epoch_image,
):
    block = epoch_tiles_quadrature
    dates, parts, lines, columns = block.shape
    owners = lax.axis_size("date")
    total = owners * dates
    images = dates * parts
    chips = by_chips(block, owners)
    line_groups = CHIPS if chips else min(owners, lines // LOOK_AZ)
    column_groups = 1 if chips else owners // line_groups
    tile_lines, tile_columns = lines // line_groups, columns // column_groups
    line_looks, column_looks = tile_lines // LOOK_AZ, tile_columns // LOOK_RG
    lanes = line_looks * column_looks

    arguments = (
        block,
        along_track_whole_displacement,
        along_track_subpixel_weights,
        slant_whole_displacement,
        slant_subpixel_weights,
        sweeps_each_epoch,
        baseline_companion_gap.T,
    )
    block, even, odd, *small = pl.pallas_call(
        start_kernel,
        out_shape=(
            pltpu.VMEM(block.shape, block.dtype),
            pltpu.VMEM((lines, images * MARGIN), jnp.bfloat16),
            pltpu.VMEM((lines, images * MARGIN), jnp.bfloat16),
            *[pltpu.SMEM(array.shape, array.dtype) for array in arguments[1:]],
        ),
        in_specs=[pl.BlockSpec(memory_space=pltpu.HBM)] * len(arguments),
        out_specs=(VMEM,) * 3 + (SMEM,) * (len(arguments) - 1),
        scratch_shapes=[pltpu.SemaphoreType.DMA((images + len(arguments) - 1,))],
        name="start",
        compiler_params=pltpu.CompilerParams(vmem_limit_bytes=GRANT),
    )(*[pltpu.with_memory_space_constraint(array, pltpu.HBM) for array in arguments])
    *small, gap = [pltpu.with_memory_space_constraint(array, pltpu.SMEM) for array in small]
    width = lax.axis_size("range")
    odd = exchanged(odd, "range", [(j, j + 1) for j in range(1, width - 1, 2)])
    even = exchanged(even, "range", [(j, j + 1) for j in range(0, width - 1, 2)])

    own_taps, low_taps, high_taps, line_taps, root = pl.pallas_call(
        functools.partial(taps_kernel, chips, tile_lines),
        out_shape=(
            pltpu.VMEM((dates, columns, columns), jnp.bfloat16),
            pltpu.VMEM((images * MARGIN, images * LANES), jnp.bfloat16),
            pltpu.VMEM((images * MARGIN, images * LANES), jnp.bfloat16),
            pltpu.VMEM((dates, lines, lines), jnp.bfloat16),
            pltpu.SMEM((8,), jnp.int32),
        ),
        in_specs=[SMEM] * (len(small) + 1),
        out_specs=(VMEM,) * 4 + (SMEM,),
        cost_estimate=pl.CostEstimate(flops=4000000, bytes_accessed=800000, transcendentals=0),
        name="taps",
        compiler_params=pltpu.CompilerParams(vmem_limit_bytes=GRANT),
    )(*small, master_epoch_image)
    tile = (dates, parts, tile_lines, tile_columns)
    if chips:
        out_shape = (pltpu.VMEM(tile, jnp.bfloat16),) * CHIPS
    else:
        out_shape = (pltpu.VMEM((owners,) + tile, jnp.bfloat16),)
    tiles = pl.pallas_call(
        functools.partial(
            resample_kernel, (line_groups, column_groups, tile_lines, tile_columns)
        ),
        out_shape=out_shape,
        in_specs=[VMEM] * 7,
        out_specs=(VMEM,) * len(out_shape),
        scratch_shapes=[pltpu.VMEM((2,) + even.shape, even.dtype)],
        name="resample",
        compiler_params=pltpu.CompilerParams(vmem_limit_bytes=GRANT),
    )(*[near(array) for array in (block, even, odd, own_taps, low_taps, high_taps, line_taps)])

    root = pltpu.with_memory_space_constraint(root, pltpu.SMEM)
    rows, cols = lines // LOOK_AZ, columns // LOOK_RG
    out_shape = (
        jax.ShapeDtypeStruct((dates, 2 * KINDS, rows, cols), jnp.float32),
        jax.ShapeDtypeStruct((dates, KINDS, rows, cols), jnp.float32),
    )
    if chips:

        def swapped(array, bits):
            pairs = [(i, i ^ bits) for i in range(owners) if i < i ^ bits]
            return exchanged(array, "date", pairs)

        order = [3, 2, 1]
        own = tiles[0]
        direct = {number: swapped(tiles[number], CORES * number) for number in order}
        other = swapped(own, 1)
        passed = {number: swapped(direct[number], 1) for number in order}
        held = [own, other]
        for number in range(1, CHIPS):
            held += [direct[number], passed[number]]
        results = pl.pallas_call(
            chip_looks_kernel,
            out_shape=(pltpu.VMEM((CHANNELS * CHIP_LOOKS, LANES), jnp.float32),) * CHIPS,
            in_specs=[SMEM] * 2 + [VMEM] * len(held),
            out_specs=(VMEM,) * CHIPS,
            scratch_shapes=[
                pltpu.VMEM((total, parts, tile_lines, tile_columns), jnp.float32),
                pltpu.VMEM((CHIPS * QUANTITIES * CHIP_LOOKS, dates * columns), jnp.float32),
                pltpu.VMEM((CHIPS * QUANTITIES * CHIP_LOOKS, LANES), jnp.float32),
            ],
            name="looks",
            compiler_params=pltpu.CompilerParams(vmem_limit_bytes=GRANT),
        )(root, gap, *[near(tile) for tile in held])
        back = {number: swapped(results[number], CORES * number) for number in order}
        pieces = [results[0]] + [back[number] for number in range(1, CHIPS)]
        return pl.pallas_call(
            chip_place_kernel,
            out_shape=out_shape,
            in_specs=[VMEM] * CHIPS,
            out_specs=(VMEM, VMEM),
            name="place",
            compiler_params=pltpu.CompilerParams(vmem_limit_bytes=GRANT),
        )(*[near(piece) for piece in pieces])

    tiles = lax.all_to_all(tiles[0], "date", 0, 0)
    results = pl.pallas_call(
        looks_kernel,
        out_shape=pltpu.VMEM((owners, dates * CHANNELS, lanes), jnp.float32),
        in_specs=[SMEM] * 2 + [VMEM],
        out_specs=VMEM,
        scratch_shapes=[
            pltpu.VMEM((total, parts, tile_lines, tile_columns), jnp.float32),
            pltpu.VMEM((total * QUANTITIES, line_looks * tile_columns), jnp.float32),
            pltpu.VMEM((total * QUANTITIES, lanes), jnp.float32),
            pltpu.VMEM((KINDS, total, lanes), jnp.float32),
        ],
        name="looks",
        compiler_params=pltpu.CompilerParams(vmem_limit_bytes=GRANT),
    )(root, gap, near(tiles))
    results = lax.all_to_all(results, "date", 0, 0)

    if column_groups == 1:
        return pl.pallas_call(
            place_kernel,
            out_shape=out_shape,
            in_specs=[VMEM],
            out_specs=(VMEM, VMEM),
            name="place",
            compiler_params=pltpu.CompilerParams(vmem_limit_bytes=GRANT),
        )(near(results))
    whole = results.reshape(
        line_groups, column_groups, dates, CHANNELS, line_looks, column_looks
    )
    whole = jnp.transpose(whole, (2, 3, 0, 4, 1, 5)).reshape(dates, CHANNELS, rows, cols)
    return (whole[:, : 2 * KINDS], whole[:, 2 * KINDS :])


def solution(mesh):
    in_specs = (P("date", None, None, "range"), P(), P(), P(), P(), P(), P(), P())
    out_specs = (P("date", None, None, "range"), P("date", None, None, "range"))
    return jax.shard_map(body, mesh=mesh, in_specs=in_specs, out_specs=out_specs, check_vma=False)
```

```python
import functools

import jax
import jax.numpy as jnp
from jax import lax
from jax.experimental import pallas as pl
from jax.experimental.pallas import tpu as pltpu
from jax.sharding import PartitionSpec as P

MAX_SWEEPS = 4
TAPS = 8
FRACTIONS = 16
MARGIN = 16
LOOK_AZ = 16
LOOK_RG = 4
QUANTITIES = 8
KINDS = 3
CHANNELS = 9
LANES = 128
GRANT = 24 * 2**20
CORES = 2
CHIPS = 4
CHIP_LOOKS = 4

SMEM = pl.BlockSpec(memory_space=pltpu.SMEM)
VMEM = pl.BlockSpec(memory_space=pltpu.VMEM)


def exchanged(array, axis, pairs):
    return lax.ppermute(array, axis, [route for a, b in pairs for route in ((a, b), (b, a))])


def near(array):
    return pltpu.with_memory_space_constraint(array, pltpu.VMEM)


def iotas(rows, cols):
    return (
        lax.broadcasted_iota(jnp.int32, (rows, cols), 0),
        lax.broadcasted_iota(jnp.int32, (rows, cols), 1),
    )


def weight_rows(fractions):
    row, lane = iotas(8, LANES)
    spot = jnp.zeros((8, LANES), jnp.float32)
    for number, fraction in enumerate(fractions):
        spot = jnp.where(row == number, fraction.astype(jnp.float32), spot)
    spacing = (lane - 1 - (TAPS // 2 - 1)).astype(jnp.float32) - spot / FRACTIONS
    angle = jnp.pi * spacing
    sinc = jnp.where(spacing == 0.0, 1.0, jnp.sin(angle) / jnp.where(spacing == 0.0, 1.0, angle))
    weights = sinc * jnp.cos(angle / (TAPS + 1)) ** 2
    weights = jnp.where((lane >= 1) & (lane <= TAPS), weights, 0.0)
    weights = weights / jnp.sum(weights, axis=1, keepdims=True)
    return weights.astype(jnp.bfloat16).astype(jnp.float32)


def by_chips(block, owners):
    dates, parts, lines, columns = block.shape
    return (
        owners == CHIPS * CORES
        and (dates, parts) == (2, 2)
        and lines == CHIPS * CHIP_LOOKS * LOOK_AZ
        and columns == 2 * LANES
    )


def tile_order(position, chips):
    return position ^ (lax.axis_index("date") // CORES) if chips else position


def banded(offsets, weights):
    rows, cols = offsets.shape
    lanes = jnp.broadcast_to(weights, (rows, LANES))
    spots = jnp.clip(offsets + 1, 0, TAPS + 1)
    return jnp.concatenate(
        [
            jnp.take_along_axis(lanes, spots[:, start : start + LANES], axis=1)
            for start in range(0, cols, LANES)
        ],
        axis=1,
    )


def start_kernel(x_ref, *refs):
    dates, parts, _, columns = x_ref.shape
    images = [(slot, part) for slot in range(dates) for part in range(parts)]
    count = (len(refs) - 4) // 2
    near_ref, even_ref, odd_ref = refs[count : count + 3]
    sems = refs[-1]
    small = list(zip(refs[:count], refs[count + 3 : -1]))
    whole = [(x_ref.at[image], near_ref.at[image]) for image in images]
    copies = [
        pltpu.make_async_copy(source, target, sems.at[number])
        for number, (source, target) in enumerate(whole + small)
    ]
    for copy in copies:
        copy.start()
    forward = lax.axis_index("range") % 2 == 0
    for number, (slot, part) in enumerate(images):
        copies[number].wait()
        spot = slice(number * MARGIN, (number + 1) * MARGIN)
        for parity, last_ref, first_ref in (
            (forward, even_ref, odd_ref),
            (jnp.logical_not(forward), odd_ref, even_ref),
        ):

            @pl.when(parity)
            def _():
                last_ref[:, spot] = near_ref[slot, part, :, columns - MARGIN :]
                first_ref[:, spot] = near_ref[slot, part, :, :MARGIN]

    for copy in copies[len(images) :]:
        copy.wait()


def taps_kernel(
    chips,
    tile_lines,
    az_whole,
    az_part,
    rg_whole,
    rg_part,
    sweeps,
    master_ref,
    own_ref,
    low_ref,
    high_ref,
    line_ref,
    root_ref,
):
    dates, columns, _ = own_ref.shape
    lines = line_ref.shape[1]
    edge_rows = low_ref.shape[0]
    parts = edge_rows // MARGIN // dates
    centre = TAPS // 2 - 1
    for number in range(root_ref.shape[0]):
        root_ref[number] = master_ref[0]
    present = [lax.axis_index("date") * dates + slot for slot in range(dates)]
    table = weight_rows([rg_part[d] for d in present] + [az_part[d] for d in present])
    for slot, date in enumerate(present):
        shift = centre - rg_whole[date]
        weights = table[slot : slot + 1]
        row, col = iotas(columns, columns)
        own_ref[slot] = banded(row - col + shift, weights).astype(jnp.bfloat16)
        row, col = iotas(edge_rows, LANES)
        low = banded(row % MARGIN - MARGIN - col + shift, weights)
        high = banded(row % MARGIN + LANES - col + shift, weights)
        for part in range(parts):
            image = slot * parts + part
            held = row // MARGIN == image
            spot = slice(image * LANES, (image + 1) * LANES)
            low_ref[:, spot] = jnp.where(held, low, 0.0).astype(jnp.bfloat16)
            high_ref[:, spot] = jnp.where(held, high, 0.0).astype(jnp.bfloat16)
        row, col = iotas(lines, lines)
        row = tile_order(row // tile_lines, chips) * tile_lines + row % tile_lines
        weights = table[dates + slot : dates + slot + 1]
        band = banded(col - row + (centre - az_whole[date]), weights)
        usable = row < sweeps[date] * (lines // MAX_SWEEPS)
        line_ref[slot] = jnp.where(usable, band, 0.0).astype(jnp.bfloat16)


def resample_kernel(split, x_ref, even_ref, odd_ref, own_ref, low_ref, high_ref, line_ref, *refs):
    *outs, edges = refs
    dates, parts, _, columns = x_ref.shape
    line_groups, column_groups, tile_lines, tile_columns = split
    backward = lax.axis_index("range") % 2
    edges[1 - backward] = even_ref[...]
    edges[backward] = odd_ref[...]
    low = jnp.dot(edges[0], low_ref[...], preferred_element_type=jnp.float32)
    high = jnp.dot(edges[1], high_ref[...], preferred_element_type=jnp.float32)
    for slot in range(dates):
        for part in range(parts):
            spot = slice((slot * parts + part) * LANES, (slot * parts + part + 1) * LANES)
            ranged = jnp.dot(x_ref[slot, part], own_ref[slot], preferred_element_type=jnp.float32)
            pieces = [ranged[:, start : start + LANES] for start in range(0, columns, LANES)]
            pieces[0] += low[:, spot]
            pieces[-1] += high[:, spot]
            ranged = jnp.concatenate(pieces, axis=1)
            moved = jnp.dot(
                line_ref[slot], ranged.astype(jnp.bfloat16), preferred_element_type=jnp.float32
            ).astype(jnp.bfloat16)
            for i in range(line_groups):
                for j in range(column_groups):
                    tile = moved[
                        i * tile_lines : (i + 1) * tile_lines,
                        j * tile_columns : (j + 1) * tile_columns,
                    ]
                    if len(outs) == 1:
                        outs[0][i * column_groups + j, slot, part] = tile
                    else:
                        outs[i][slot, part] = tile


def partners(date, gap_ref, total):
    ahead = date + gap_ref[0, date]
    later = jnp.where(ahead < total, ahead, date - gap_ref[0, date])
    back = date - gap_ref[1, date]
    earlier = jnp.where(back >= 0, back, date + gap_ref[1, date])
    return (later, earlier)


def row_sums(values):
    row = lax.broadcasted_iota(jnp.int32, values[0].shape, 0)
    order = (3, 2, 1, 0, 7, 6, 5, 4)
    values = [values[number] for number in order]
    upper = row < 4
    values = [
        jnp.where(upper, a, b) + pltpu.roll(jnp.where(upper, b, a), 4, 0)
        for a, b in zip(values[:4], values[4:])
    ]
    for step, kept in ((2, row % 4 >= 2), (1, row % 2 == 1)):
        values = [
            jnp.where(kept, a + pltpu.roll(a, step, 0), b + pltpu.roll(b, 8 - step, 0))
            for a, b in zip(values[:step], values[step:])
        ]
    return values[0]


def pool_columns(sums, lanes):
    row, col = iotas(sums.shape[1], lanes)
    pool = jnp.where(row // LOOK_RG == col, 1.0, 0.0).astype(jnp.bfloat16)
    coarse = sums.astype(jnp.bfloat16)
    fine = (sums - coarse.astype(jnp.float32)).astype(jnp.bfloat16)
    return jnp.dot(coarse, pool, preferred_element_type=jnp.float32) + jnp.dot(
        fine, pool, preferred_element_type=jnp.float32
    )


def looks_kernel(root_ref, gap_ref, tiles_ref, out_ref, stack, sums, pooled, powers):
    total, _, tile_lines, tile_columns = stack.shape
    owners, per_owner, lanes = out_ref.shape
    dates = per_owner // CHANNELS
    line_looks = tile_lines // LOOK_AZ
    unroll = total if total <= 16 else 1

    def widen(owner, carry):
        stack[pl.ds(owner * dates, dates)] = tiles_ref[owner].astype(jnp.float32)
        return carry

    lax.fori_loop(0, owners, widen, 0)

    def partner_of(kind, date):
        return partners(date, gap_ref, total)[kind - 1] if kind else root_ref[0]

    def collect(date, carry):
        left0, left1 = stack[date, 0], stack[date, 1]
        values = []
        for kind in range(KINDS):
            partner = partner_of(kind, date)
            right0, right1 = stack[partner, 0], stack[partner, 1]
            values += [left0 * right0 + left1 * right1, left1 * right0 - left0 * right1]
        values.append(left0 * left0 + left1 * left1)
        values.append(jnp.zeros_like(left0))
        rows = pl.ds(pl.multiple_of(date * QUANTITIES, QUANTITIES), QUANTITIES)
        for look in range(line_looks):
            start = look * LOOK_AZ
            sums[rows, look * tile_columns : (look + 1) * tile_columns] = row_sums(
                [value[start : start + 8] + value[start + 8 : start + 16] for value in values]
            )
        return carry

    lax.fori_loop(0, total, collect, 0, unroll=unroll)
    pooled[...] = pool_columns(sums[...], lanes)

    def gather(date, carry):
        for kind in range(KINDS):
            power = partner_of(kind, date) * QUANTITIES + 2 * KINDS
            powers[kind, pl.ds(date, 1), :] = pooled[pl.ds(power, 1), :]
        return carry

    lax.fori_loop(0, total, gather, 0, unroll=unroll)
    scale = 1.0 / (LOOK_AZ * LOOK_RG) ** 0.5

    for slot in range(dates):

        def every(number):
            return pooled[pl.ds(slot * QUANTITIES + number, owners, stride=dates * QUANTITIES), :]

        power_left = every(2 * KINDS)
        for kind in range(KINDS):
            real, imag = every(2 * kind), every(2 * kind + 1)
            power_right = powers[kind, pl.ds(slot, owners, stride=dates), :]
            out_ref[:, slot * CHANNELS + 2 * kind, :] = real * scale
            out_ref[:, slot * CHANNELS + 2 * kind + 1, :] = imag * scale
            out_ref[:, slot * CHANNELS + 2 * KINDS + kind, :] = jnp.sqrt(
                real * real + imag * imag
            ) / jnp.sqrt(power_left * power_right + 1e-06)


def chip_looks_kernel(positions, root_ref, gap_ref, *refs):
    tiles, outs, (stack, sums, pooled) = refs[: CHIPS * CORES], refs[CHIPS * CORES : -3], refs[-3:]
    dates, _, _, columns = tiles[0].shape
    me = lax.axis_index("date")
    total = len(tiles) * dates
    scale = 1.0 / (LOOK_AZ * LOOK_RG) ** 0.5
    for position, tile_ref in zip(positions, tiles):
        stack[position * dates : (position + 1) * dates] = tile_ref[...].astype(jnp.float32)

    def partner_of(kind, date):
        partner = partners(date, gap_ref, total)[kind - 1] if kind else root_ref[0]
        return lax.div(partner, dates) ^ me, lax.rem(partner, dates)

    def part(spot, number, look):
        return stack[spot, number, look * LOOK_AZ : (look + 1) * LOOK_AZ, :]

    def folded(value):
        return value[: LOOK_AZ // 2] + value[LOOK_AZ // 2 :]

    block = QUANTITIES * CHIP_LOOKS
    for chip in range(CHIPS):
        for slot in range(dates):
            date = (me ^ (CORES * chip)) * dates + slot
            own = CORES * chip * dates + slot
            spot = slice(slot * columns, (slot + 1) * columns)
            for kind in range(KINDS):
                position, number = partner_of(kind, date)
                other = position * dates + number
                reals, imags = [], []
                for look in range(CHIP_LOOKS):
                    left0, left1 = part(own, 0, look), part(own, 1, look)
                    right0, right1 = part(other, 0, look), part(other, 1, look)
                    reals.append(folded(left0 * right0 + left1 * right1))
                    imags.append(folded(left1 * right0 - left0 * right1))
                start = chip * block + kind * 2 * CHIP_LOOKS
                sums[start : start + 2 * CHIP_LOOKS, spot] = row_sums(reals + imags)
            powers = []
            for core in range(CORES):
                for look in range(CHIP_LOOKS):
                    left0 = part(own + core * dates, 0, look)
                    left1 = part(own + core * dates, 1, look)
                    powers.append(folded(left0 * left0 + left1 * left1))
            start = chip * block + KINDS * 2 * CHIP_LOOKS
            sums[start : start + 2 * CHIP_LOOKS, spot] = row_sums(powers)
    pooled[...] = pool_columns(sums[...], LANES)

    row, lane = iotas(2 * CHIP_LOOKS, LANES)
    upper, first = row < CHIP_LOOKS, lane < LANES // 2
    for chip in range(CHIPS):
        base = chip * block
        views = [pooled[base + 8 * number : base + 8 * (number + 1), :] for number in range(4)]
        squares = [view * view for view in views[:KINDS]]
        squares = [square + pltpu.roll(square, CHIP_LOOKS, 0) for square in squares]
        power_left = jnp.where(upper, views[KINDS], pltpu.roll(views[KINDS], CHIP_LOOKS, 0))
        power_right = []
        for kind in range(KINDS):
            halves = []
            for slot in range(dates):
                position, number = partner_of(kind, (me ^ (CORES * chip)) * dates + slot)
                start = lax.div(position, CORES) * block + KINDS * 2 * CHIP_LOOKS
                power = pooled[pl.ds(pl.multiple_of(start, 8), 8), :]
                power = pltpu.roll(power, CHIP_LOOKS * (lax.rem(position, CORES) ^ (kind % 2)), 0)
                halves.append(pltpu.roll(power, LANES // 2 * (number ^ slot), 1))
            power_right.append(jnp.where(first, halves[0], halves[1]))
        outs[chip][: 2 * KINDS * CHIP_LOOKS, :] = (
            pooled[base : base + 2 * KINDS * CHIP_LOOKS, :] * scale
        )
        pairs = (
            (jnp.where(upper, squares[0], squares[1]), jnp.where(upper, *power_right[:2])),
            (squares[2], power_right[2]),
        )
        start = 2 * KINDS * CHIP_LOOKS
        for square, power in pairs:
            coherent = jnp.sqrt(square) / jnp.sqrt(power_left * power + 1e-06)
            rows = min(8, outs[chip].shape[0] - start)
            outs[chip][start : start + rows, :] = coherent[:rows]
            start += rows


def chip_place_kernel(positions, *refs):
    pieces, (ifg_ref, coh_ref) = refs[:CHIPS], refs[CHIPS:]
    dates, _, _, columns = ifg_ref.shape
    mine = lax.axis_index("date") // CORES
    for chip in range(CHIPS):

        @pl.when(mine == chip)
        def _():
            for position, piece_ref in zip(positions, pieces):
                start = (chip ^ position) * CHIP_LOOKS
                where = slice(start, start + CHIP_LOOKS)
                for channel in range(CHANNELS):
                    rows = piece_ref[channel * CHIP_LOOKS : (channel + 1) * CHIP_LOOKS, :]
                    for slot in range(dates):
                        part = rows[:, slot * columns : (slot + 1) * columns]
                        if channel < 2 * KINDS:
                            ifg_ref[slot, channel, where, :] = part
                        else:
                            coh_ref[slot, channel - 2 * KINDS, where, :] = part


def place_kernel(x_ref, ifg_ref, coh_ref):
    sources, rows, lanes = x_ref.shape
    dates, _, lines, columns = ifg_ref.shape
    looks = lanes // columns
    for slot in range(dates):
        for channel in range(CHANNELS):
            values = x_ref[:, slot * CHANNELS + channel, :]
            for look in range(looks):
                part = values[:, look * columns : (look + 1) * columns]
                where = pl.ds(look, sources, stride=looks)
                if channel < 2 * KINDS:
                    ifg_ref[slot, channel, where, :] = part
                else:
                    coh_ref[slot, channel - 2 * KINDS, where, :] = part


def body(
    epoch_tiles_quadrature,
    along_track_whole_displacement,
    along_track_subpixel_weights,
    slant_whole_displacement,
    slant_subpixel_weights,
    sweeps_each_epoch,
    baseline_companion_gap,
    master_epoch_image,
):
    block = epoch_tiles_quadrature
    dates, parts, lines, columns = block.shape
    owners = lax.axis_size("date")
    total = owners * dates
    images = dates * parts
    chips = by_chips(block, owners)
    line_groups = CHIPS if chips else min(owners, lines // LOOK_AZ)
    column_groups = 1 if chips else owners // line_groups
    tile_lines, tile_columns = lines // line_groups, columns // column_groups
    line_looks, column_looks = tile_lines // LOOK_AZ, tile_columns // LOOK_RG
    lanes = line_looks * column_looks

    arguments = (
        block,
        along_track_whole_displacement,
        along_track_subpixel_weights,
        slant_whole_displacement,
        slant_subpixel_weights,
        sweeps_each_epoch,
        baseline_companion_gap.T,
    )
    block, even, odd, *small = pl.pallas_call(
        start_kernel,
        out_shape=(
            pltpu.VMEM(block.shape, block.dtype),
            pltpu.VMEM((lines, images * MARGIN), jnp.bfloat16),
            pltpu.VMEM((lines, images * MARGIN), jnp.bfloat16),
            *[pltpu.SMEM(array.shape, array.dtype) for array in arguments[1:]],
        ),
        in_specs=[pl.BlockSpec(memory_space=pltpu.HBM)] * len(arguments),
        out_specs=(VMEM,) * 3 + (SMEM,) * (len(arguments) - 1),
        scratch_shapes=[pltpu.SemaphoreType.DMA((images + len(arguments) - 1,))],
        name="start",
        compiler_params=pltpu.CompilerParams(vmem_limit_bytes=GRANT),
    )(*[pltpu.with_memory_space_constraint(array, pltpu.HBM) for array in arguments])
    *small, gap = [pltpu.with_memory_space_constraint(array, pltpu.SMEM) for array in small]
    width = lax.axis_size("range")
    odd = exchanged(odd, "range", [(j, j + 1) for j in range(1, width - 1, 2)])
    even = exchanged(even, "range", [(j, j + 1) for j in range(0, width - 1, 2)])

    own_taps, low_taps, high_taps, line_taps, root = pl.pallas_call(
        functools.partial(taps_kernel, chips, tile_lines),
        out_shape=(
            pltpu.VMEM((dates, columns, columns), jnp.bfloat16),
            pltpu.VMEM((images * MARGIN, images * LANES), jnp.bfloat16),
            pltpu.VMEM((images * MARGIN, images * LANES), jnp.bfloat16),
            pltpu.VMEM((dates, lines, lines), jnp.bfloat16),
            pltpu.SMEM((8,), jnp.int32),
        ),
        in_specs=[SMEM] * (len(small) + 1),
        out_specs=(VMEM,) * 4 + (SMEM,),
        cost_estimate=pl.CostEstimate(flops=4000000, bytes_accessed=800000, transcendentals=0),
        name="taps",
        compiler_params=pltpu.CompilerParams(vmem_limit_bytes=GRANT),
    )(*small, master_epoch_image)
    tile = (dates, parts, tile_lines, tile_columns)
    if chips:
        out_shape = (pltpu.VMEM(tile, jnp.bfloat16),) * CHIPS
    else:
        out_shape = (pltpu.VMEM((owners,) + tile, jnp.bfloat16),)
    tiles = pl.pallas_call(
        functools.partial(
            resample_kernel, (line_groups, column_groups, tile_lines, tile_columns)
        ),
        out_shape=out_shape,
        in_specs=[VMEM] * 7,
        out_specs=(VMEM,) * len(out_shape),
        scratch_shapes=[pltpu.VMEM((2,) + even.shape, even.dtype)],
        name="resample",
        compiler_params=pltpu.CompilerParams(vmem_limit_bytes=GRANT),
    )(*[near(array) for array in (block, even, odd, own_taps, low_taps, high_taps, line_taps)])

    root = pltpu.with_memory_space_constraint(root, pltpu.SMEM)
    rows, cols = lines // LOOK_AZ, columns // LOOK_RG
    out_shape = (
        jax.ShapeDtypeStruct((dates, 2 * KINDS, rows, cols), jnp.float32),
        jax.ShapeDtypeStruct((dates, KINDS, rows, cols), jnp.float32),
    )
    if chips:

        def swapped(array, bits):
            pairs = [(i, i ^ bits) for i in range(owners) if i < i ^ bits]
            return exchanged(array, "date", pairs)

        order = [3, 2, 1]
        own = tiles[0]
        direct = {number: swapped(tiles[number], CORES * number) for number in order}
        other = swapped(own, 1)
        passed = {number: swapped(direct[number], 1) for number in order}
        held, positions = [own, other], [0, 1]
        for number in order:
            held += [direct[number], passed[number]]
            positions += [CORES * number, CORES * number + 1]
        results = pl.pallas_call(
            functools.partial(chip_looks_kernel, positions),
            out_shape=(pltpu.VMEM((CHANNELS * CHIP_LOOKS, LANES), jnp.float32),) * CHIPS,
            in_specs=[SMEM] * 2 + [VMEM] * len(held),
            out_specs=(VMEM,) * CHIPS,
            scratch_shapes=[
                pltpu.VMEM((total, parts, tile_lines, tile_columns), jnp.float32),
                pltpu.VMEM((CHIPS * QUANTITIES * CHIP_LOOKS, dates * columns), jnp.float32),
                pltpu.VMEM((CHIPS * QUANTITIES * CHIP_LOOKS, LANES), jnp.float32),
            ],
            name="looks",
            compiler_params=pltpu.CompilerParams(vmem_limit_bytes=GRANT),
        )(root, gap, *[near(tile) for tile in held])
        back = {number: swapped(results[number], CORES * number) for number in order}
        pieces = [results[0]] + [back[number] for number in order]
        return pl.pallas_call(
            functools.partial(chip_place_kernel, [0] + order),
            out_shape=out_shape,
            in_specs=[VMEM] * CHIPS,
            out_specs=(VMEM, VMEM),
            name="place",
            compiler_params=pltpu.CompilerParams(vmem_limit_bytes=GRANT),
        )(*[near(piece) for piece in pieces])

    tiles = lax.all_to_all(tiles[0], "date", 0, 0)
    results = pl.pallas_call(
        looks_kernel,
        out_shape=pltpu.VMEM((owners, dates * CHANNELS, lanes), jnp.float32),
        in_specs=[SMEM] * 2 + [VMEM],
        out_specs=VMEM,
        scratch_shapes=[
            pltpu.VMEM((total, parts, tile_lines, tile_columns), jnp.float32),
            pltpu.VMEM((total * QUANTITIES, line_looks * tile_columns), jnp.float32),
            pltpu.VMEM((total * QUANTITIES, lanes), jnp.float32),
            pltpu.VMEM((KINDS, total, lanes), jnp.float32),
        ],
        name="looks",
        compiler_params=pltpu.CompilerParams(vmem_limit_bytes=GRANT),
    )(root, gap, near(tiles))
    results = lax.all_to_all(results, "date", 0, 0)

    if column_groups == 1:
        return pl.pallas_call(
            place_kernel,
            out_shape=out_shape,
            in_specs=[VMEM],
            out_specs=(VMEM, VMEM),
            name="place",
            compiler_params=pltpu.CompilerParams(vmem_limit_bytes=GRANT),
        )(near(results))
    whole = results.reshape(
        line_groups, column_groups, dates, CHANNELS, line_looks, column_looks
    )
    whole = jnp.transpose(whole, (2, 3, 0, 4, 1, 5)).reshape(dates, CHANNELS, rows, cols)
    return (whole[:, : 2 * KINDS], whole[:, 2 * KINDS :])


def solution(mesh):
    in_specs = (P("date", None, None, "range"), P(), P(), P(), P(), P(), P(), P())
    out_specs = (P("date", None, None, "range"), P("date", None, None, "range"))
    return jax.shard_map(body, mesh=mesh, in_specs=in_specs, out_specs=out_specs, check_vma=False)
```

```python
import functools

import jax
import jax.numpy as jnp
from jax import lax
from jax.experimental import pallas as pl
from jax.experimental.pallas import tpu as pltpu
from jax.sharding import PartitionSpec as P

MAX_SWEEPS = 4
TAPS = 8
FRACTIONS = 16
MARGIN = 16
LOOK_AZ = 16
LOOK_RG = 4
QUANTITIES = 8
KINDS = 3
CHANNELS = 9
LANES = 128
GRANT = 24 * 2**20
CORES = 2
CHIPS = 4
CHIP_LOOKS = 4

SMEM = pl.BlockSpec(memory_space=pltpu.SMEM)
VMEM = pl.BlockSpec(memory_space=pltpu.VMEM)


def exchanged(array, axis, pairs):
    return lax.ppermute(array, axis, [route for a, b in pairs for route in ((a, b), (b, a))])


def near(array):
    return pltpu.with_memory_space_constraint(array, pltpu.VMEM)


def iotas(rows, cols):
    return (
        lax.broadcasted_iota(jnp.int32, (rows, cols), 0),
        lax.broadcasted_iota(jnp.int32, (rows, cols), 1),
    )


def weight_rows(fractions):
    row, lane = iotas(8, LANES)
    spot = jnp.zeros((8, LANES), jnp.float32)
    for number, fraction in enumerate(fractions):
        spot = jnp.where(row == number, fraction.astype(jnp.float32), spot)
    spacing = (lane - 1 - (TAPS // 2 - 1)).astype(jnp.float32) - spot / FRACTIONS
    angle = jnp.pi * spacing
    sinc = jnp.where(spacing == 0.0, 1.0, jnp.sin(angle) / jnp.where(spacing == 0.0, 1.0, angle))
    weights = sinc * jnp.cos(angle / (TAPS + 1)) ** 2
    weights = jnp.where((lane >= 1) & (lane <= TAPS), weights, 0.0)
    weights = weights / jnp.sum(weights, axis=1, keepdims=True)
    return weights.astype(jnp.bfloat16).astype(jnp.float32)


def by_chips(block, owners):
    dates, parts, lines, columns = block.shape
    return (
        owners == CHIPS * CORES
        and (dates, parts) == (2, 2)
        and lines == CHIPS * CHIP_LOOKS * LOOK_AZ
        and columns == 2 * LANES
    )


def tile_order(position, chips):
    return position ^ (lax.axis_index("date") // CORES) if chips else position


def banded(offsets, weights):
    rows, cols = offsets.shape
    lanes = jnp.broadcast_to(weights, (rows, LANES))
    spots = jnp.clip(offsets + 1, 0, TAPS + 1)
    return jnp.concatenate(
        [
            jnp.take_along_axis(lanes, spots[:, start : start + LANES], axis=1)
            for start in range(0, cols, LANES)
        ],
        axis=1,
    )


def start_kernel(x_ref, *refs):
    dates, parts, _, columns = x_ref.shape
    images = [(slot, part) for slot in range(dates) for part in range(parts)]
    count = (len(refs) - 4) // 2
    near_ref, even_ref, odd_ref = refs[count : count + 3]
    sems = refs[-1]
    small = list(zip(refs[:count], refs[count + 3 : -1]))
    whole = [(x_ref.at[image], near_ref.at[image]) for image in images]
    copies = [
        pltpu.make_async_copy(source, target, sems.at[number])
        for number, (source, target) in enumerate(whole + small)
    ]
    for copy in copies:
        copy.start()
    forward = lax.axis_index("range") % 2 == 0
    for number, (slot, part) in enumerate(images):
        copies[number].wait()
        spot = slice(number * MARGIN, (number + 1) * MARGIN)
        for parity, last_ref, first_ref in (
            (forward, even_ref, odd_ref),
            (jnp.logical_not(forward), odd_ref, even_ref),
        ):

            @pl.when(parity)
            def _():
                last_ref[:, spot] = near_ref[slot, part, :, columns - MARGIN :]
                first_ref[:, spot] = near_ref[slot, part, :, :MARGIN]

    for copy in copies[len(images) :]:
        copy.wait()


def taps_kernel(
    chips,
    tile_lines,
    az_whole,
    az_part,
    rg_whole,
    rg_part,
    sweeps,
    x_ref,
    inner_ref,
    low_ref,
    high_ref,
    line_ref,
):
    dates, parts, lines, columns = x_ref.shape
    edge_rows = low_ref.shape[0]
    centre = TAPS // 2 - 1
    present = [lax.axis_index("date") * dates + slot for slot in range(dates)]
    table = weight_rows([rg_part[d] for d in present] + [az_part[d] for d in present])
    for slot, date in enumerate(present):
        shift = centre - rg_whole[date]
        weights = table[slot : slot + 1]
        row, col = iotas(columns, columns)
        own = banded(row - col + shift, weights).astype(jnp.bfloat16)
        for part in range(parts):
            inner_ref[slot, part] = jnp.dot(
                x_ref[slot, part], own, preferred_element_type=jnp.float32
            )
        row, col = iotas(edge_rows, LANES)
        low = banded(row % MARGIN - MARGIN - col + shift, weights)
        high = banded(row % MARGIN + LANES - col + shift, weights)
        for part in range(parts):
            image = slot * parts + part
            held = row // MARGIN == image
            spot = slice(image * LANES, (image + 1) * LANES)
            low_ref[:, spot] = jnp.where(held, low, 0.0).astype(jnp.bfloat16)
            high_ref[:, spot] = jnp.where(held, high, 0.0).astype(jnp.bfloat16)
        row, col = iotas(lines, lines)
        row = tile_order(row // tile_lines, chips) * tile_lines + row % tile_lines
        weights = table[dates + slot : dates + slot + 1]
        band = banded(col - row + (centre - az_whole[date]), weights)
        usable = row < sweeps[date] * (lines // MAX_SWEEPS)
        line_ref[slot] = jnp.where(usable, band, 0.0).astype(jnp.bfloat16)


def resample_kernel(split, inner_ref, even_ref, odd_ref, low_ref, high_ref, line_ref, *refs):
    *outs, edges = refs
    dates, parts, _, columns = inner_ref.shape
    line_groups, column_groups, tile_lines, tile_columns = split
    backward = lax.axis_index("range") % 2
    edges[1 - backward] = even_ref[...]
    edges[backward] = odd_ref[...]
    low = jnp.dot(edges[0], low_ref[...], preferred_element_type=jnp.float32)
    high = jnp.dot(edges[1], high_ref[...], preferred_element_type=jnp.float32)
    for slot in range(dates):
        for part in range(parts):
            spot = slice((slot * parts + part) * LANES, (slot * parts + part + 1) * LANES)
            pieces = [
                inner_ref[slot, part, :, start : start + LANES]
                for start in range(0, columns, LANES)
            ]
            pieces[0] += low[:, spot]
            pieces[-1] += high[:, spot]
            ranged = jnp.concatenate(pieces, axis=1)
            moved = jnp.dot(
                line_ref[slot], ranged.astype(jnp.bfloat16), preferred_element_type=jnp.float32
            ).astype(jnp.bfloat16)
            for i in range(line_groups):
                for j in range(column_groups):
                    tile = moved[
                        i * tile_lines : (i + 1) * tile_lines,
                        j * tile_columns : (j + 1) * tile_columns,
                    ]
                    if len(outs) == 1:
                        outs[0][i * column_groups + j, slot, part] = tile
                    else:
                        outs[i][slot, part] = tile


def partners(date, gap_ref, total):
    ahead = date + gap_ref[0, date]
    later = jnp.where(ahead < total, ahead, date - gap_ref[0, date])
    back = date - gap_ref[1, date]
    earlier = jnp.where(back >= 0, back, date + gap_ref[1, date])
    return (later, earlier)


def row_sums(values):
    row = lax.broadcasted_iota(jnp.int32, values[0].shape, 0)
    order = (3, 2, 1, 0, 7, 6, 5, 4)
    values = [values[number] for number in order]
    upper = row < 4
    values = [
        jnp.where(upper, a, b) + pltpu.roll(jnp.where(upper, b, a), 4, 0)
        for a, b in zip(values[:4], values[4:])
    ]
    for step, kept in ((2, row % 4 >= 2), (1, row % 2 == 1)):
        values = [
            jnp.where(kept, a + pltpu.roll(a, step, 0), b + pltpu.roll(b, 8 - step, 0))
            for a, b in zip(values[:step], values[step:])
        ]
    return values[0]


def pool_columns(sums, lanes):
    row, col = iotas(sums.shape[1], lanes)
    pool = jnp.where(row // LOOK_RG == col, 1.0, 0.0).astype(jnp.bfloat16)
    coarse = sums.astype(jnp.bfloat16)
    fine = (sums - coarse.astype(jnp.float32)).astype(jnp.bfloat16)
    return jnp.dot(coarse, pool, preferred_element_type=jnp.float32) + jnp.dot(
        fine, pool, preferred_element_type=jnp.float32
    )


def looks_kernel(root_ref, gap_ref, tiles_ref, out_ref, stack, sums, pooled, powers):
    total, _, tile_lines, tile_columns = stack.shape
    owners, per_owner, lanes = out_ref.shape
    dates = per_owner // CHANNELS
    line_looks = tile_lines // LOOK_AZ
    unroll = total if total <= 16 else 1

    def widen(owner, carry):
        stack[pl.ds(owner * dates, dates)] = tiles_ref[owner].astype(jnp.float32)
        return carry

    lax.fori_loop(0, owners, widen, 0)

    def partner_of(kind, date):
        return partners(date, gap_ref, total)[kind - 1] if kind else root_ref[0]

    def collect(date, carry):
        left0, left1 = stack[date, 0], stack[date, 1]
        values = []
        for kind in range(KINDS):
            partner = partner_of(kind, date)
            right0, right1 = stack[partner, 0], stack[partner, 1]
            values += [left0 * right0 + left1 * right1, left1 * right0 - left0 * right1]
        values.append(left0 * left0 + left1 * left1)
        values.append(jnp.zeros_like(left0))
        rows = pl.ds(pl.multiple_of(date * QUANTITIES, QUANTITIES), QUANTITIES)
        for look in range(line_looks):
            start = look * LOOK_AZ
            sums[rows, look * tile_columns : (look + 1) * tile_columns] = row_sums(
                [value[start : start + 8] + value[start + 8 : start + 16] for value in values]
            )
        return carry

    lax.fori_loop(0, total, collect, 0, unroll=unroll)
    pooled[...] = pool_columns(sums[...], lanes)

    def gather(date, carry):
        for kind in range(KINDS):
            power = partner_of(kind, date) * QUANTITIES + 2 * KINDS
            powers[kind, pl.ds(date, 1), :] = pooled[pl.ds(power, 1), :]
        return carry

    lax.fori_loop(0, total, gather, 0, unroll=unroll)
    scale = 1.0 / (LOOK_AZ * LOOK_RG) ** 0.5

    for slot in range(dates):

        def every(number):
            return pooled[pl.ds(slot * QUANTITIES + number, owners, stride=dates * QUANTITIES), :]

        power_left = every(2 * KINDS)
        for kind in range(KINDS):
            real, imag = every(2 * kind), every(2 * kind + 1)
            power_right = powers[kind, pl.ds(slot, owners, stride=dates), :]
            out_ref[:, slot * CHANNELS + 2 * kind, :] = real * scale
            out_ref[:, slot * CHANNELS + 2 * kind + 1, :] = imag * scale
            out_ref[:, slot * CHANNELS + 2 * KINDS + kind, :] = jnp.sqrt(
                real * real + imag * imag
            ) / jnp.sqrt(power_left * power_right + 1e-06)


def chip_looks_kernel(positions, root_ref, gap_ref, *refs):
    tiles, outs, (stack, sums, pooled) = refs[: CHIPS * CORES], refs[CHIPS * CORES : -3], refs[-3:]
    dates, _, _, columns = tiles[0].shape
    me = lax.axis_index("date")
    total = len(tiles) * dates
    scale = 1.0 / (LOOK_AZ * LOOK_RG) ** 0.5
    for position, tile_ref in zip(positions, tiles):
        stack[position * dates : (position + 1) * dates] = tile_ref[...].astype(jnp.float32)

    def partner_of(kind, date):
        partner = partners(date, gap_ref, total)[kind - 1] if kind else root_ref[0]
        return lax.div(partner, dates) ^ me, lax.rem(partner, dates)

    def part(spot, number, look):
        return stack[spot, number, look * LOOK_AZ : (look + 1) * LOOK_AZ, :]

    def folded(value):
        return value[: LOOK_AZ // 2] + value[LOOK_AZ // 2 :]

    block = QUANTITIES * CHIP_LOOKS
    for chip in range(CHIPS):
        for slot in range(dates):
            date = (me ^ (CORES * chip)) * dates + slot
            own = CORES * chip * dates + slot
            spot = slice(slot * columns, (slot + 1) * columns)
            for kind in range(KINDS):
                position, number = partner_of(kind, date)
                other = position * dates + number
                reals, imags = [], []
                for look in range(CHIP_LOOKS):
                    left0, left1 = part(own, 0, look), part(own, 1, look)
                    right0, right1 = part(other, 0, look), part(other, 1, look)
                    reals.append(folded(left0 * right0 + left1 * right1))
                    imags.append(folded(left1 * right0 - left0 * right1))
                start = chip * block + kind * 2 * CHIP_LOOKS
                sums[start : start + 2 * CHIP_LOOKS, spot] = row_sums(reals + imags)
            powers = []
            for core in range(CORES):
                for look in range(CHIP_LOOKS):
                    left0 = part(own + core * dates, 0, look)
                    left1 = part(own + core * dates, 1, look)
                    powers.append(folded(left0 * left0 + left1 * left1))
            start = chip * block + KINDS * 2 * CHIP_LOOKS
            sums[start : start + 2 * CHIP_LOOKS, spot] = row_sums(powers)
    pooled[...] = pool_columns(sums[...], LANES)

    row, lane = iotas(2 * CHIP_LOOKS, LANES)
    upper, first = row < CHIP_LOOKS, lane < LANES // 2
    for chip in range(CHIPS):
        base = chip * block
        views = [pooled[base + 8 * number : base + 8 * (number + 1), :] for number in range(4)]
        squares = [view * view for view in views[:KINDS]]
        squares = [square + pltpu.roll(square, CHIP_LOOKS, 0) for square in squares]
        power_left = jnp.where(upper, views[KINDS], pltpu.roll(views[KINDS], CHIP_LOOKS, 0))
        power_right = []
        for kind in range(KINDS):
            halves = []
            for slot in range(dates):
                position, number = partner_of(kind, (me ^ (CORES * chip)) * dates + slot)
                start = lax.div(position, CORES) * block + KINDS * 2 * CHIP_LOOKS
                power = pooled[pl.ds(pl.multiple_of(start, 8), 8), :]
                power = pltpu.roll(power, CHIP_LOOKS * (lax.rem(position, CORES) ^ (kind % 2)), 0)
                halves.append(pltpu.roll(power, LANES // 2 * (number ^ slot), 1))
            power_right.append(jnp.where(first, halves[0], halves[1]))
        outs[chip][: 2 * KINDS * CHIP_LOOKS, :] = (
            pooled[base : base + 2 * KINDS * CHIP_LOOKS, :] * scale
        )
        pairs = (
            (jnp.where(upper, squares[0], squares[1]), jnp.where(upper, *power_right[:2])),
            (squares[2], power_right[2]),
        )
        start = 2 * KINDS * CHIP_LOOKS
        for square, power in pairs:
            coherent = jnp.sqrt(square) / jnp.sqrt(power_left * power + 1e-06)
            rows = min(8, outs[chip].shape[0] - start)
            outs[chip][start : start + rows, :] = coherent[:rows]
            start += rows


def chip_place_kernel(positions, *refs):
    pieces, (ifg_ref, coh_ref) = refs[:CHIPS], refs[CHIPS:]
    dates, _, _, columns = ifg_ref.shape
    mine = lax.axis_index("date") // CORES
    for chip in range(CHIPS):

        @pl.when(mine == chip)
        def _():
            for position, piece_ref in zip(positions, pieces):
                start = (chip ^ position) * CHIP_LOOKS
                where = slice(start, start + CHIP_LOOKS)
                for channel in range(CHANNELS):
                    rows = piece_ref[channel * CHIP_LOOKS : (channel + 1) * CHIP_LOOKS, :]
                    for slot in range(dates):
                        part = rows[:, slot * columns : (slot + 1) * columns]
                        if channel < 2 * KINDS:
                            ifg_ref[slot, channel, where, :] = part
                        else:
                            coh_ref[slot, channel - 2 * KINDS, where, :] = part


def place_kernel(x_ref, ifg_ref, coh_ref):
    sources, rows, lanes = x_ref.shape
    dates, _, lines, columns = ifg_ref.shape
    looks = lanes // columns
    for slot in range(dates):
        for channel in range(CHANNELS):
            values = x_ref[:, slot * CHANNELS + channel, :]
            for look in range(looks):
                part = values[:, look * columns : (look + 1) * columns]
                where = pl.ds(look, sources, stride=looks)
                if channel < 2 * KINDS:
                    ifg_ref[slot, channel, where, :] = part
                else:
                    coh_ref[slot, channel - 2 * KINDS, where, :] = part


def body(
    epoch_tiles_quadrature,
    along_track_whole_displacement,
    along_track_subpixel_weights,
    slant_whole_displacement,
    slant_subpixel_weights,
    sweeps_each_epoch,
    baseline_companion_gap,
    master_epoch_image,
):
    block = epoch_tiles_quadrature
    dates, parts, lines, columns = block.shape
    owners = lax.axis_size("date")
    total = owners * dates
    images = dates * parts
    chips = by_chips(block, owners)
    line_groups = CHIPS if chips else min(owners, lines // LOOK_AZ)
    column_groups = 1 if chips else owners // line_groups
    tile_lines, tile_columns = lines // line_groups, columns // column_groups
    line_looks, column_looks = tile_lines // LOOK_AZ, tile_columns // LOOK_RG
    lanes = line_looks * column_looks

    arguments = (
        block,
        along_track_whole_displacement,
        along_track_subpixel_weights,
        slant_whole_displacement,
        slant_subpixel_weights,
        sweeps_each_epoch,
        baseline_companion_gap.T,
    )
    block, even, odd, *small = pl.pallas_call(
        start_kernel,
        out_shape=(
            pltpu.VMEM(block.shape, block.dtype),
            pltpu.VMEM((lines, images * MARGIN), jnp.bfloat16),
            pltpu.VMEM((lines, images * MARGIN), jnp.bfloat16),
            *[pltpu.SMEM(array.shape, array.dtype) for array in arguments[1:]],
        ),
        in_specs=[pl.BlockSpec(memory_space=pltpu.HBM)] * len(arguments),
        out_specs=(VMEM,) * 3 + (SMEM,) * (len(arguments) - 1),
        scratch_shapes=[pltpu.SemaphoreType.DMA((images + len(arguments) - 1,))],
        name="start",
        compiler_params=pltpu.CompilerParams(vmem_limit_bytes=GRANT),
    )(*[pltpu.with_memory_space_constraint(array, pltpu.HBM) for array in arguments])
    *small, gap = [pltpu.with_memory_space_constraint(array, pltpu.SMEM) for array in small]
    width = lax.axis_size("range")
    odd = exchanged(odd, "range", [(j, j + 1) for j in range(1, width - 1, 2)])
    even = exchanged(even, "range", [(j, j + 1) for j in range(0, width - 1, 2)])

    inner, low_taps, high_taps, line_taps = pl.pallas_call(
        functools.partial(taps_kernel, chips, tile_lines),
        out_shape=(
            pltpu.VMEM(block.shape, jnp.float32),
            pltpu.VMEM((images * MARGIN, images * LANES), jnp.bfloat16),
            pltpu.VMEM((images * MARGIN, images * LANES), jnp.bfloat16),
            pltpu.VMEM((dates, lines, lines), jnp.bfloat16),
        ),
        in_specs=[SMEM] * len(small) + [VMEM],
        out_specs=(VMEM,) * 4,
        cost_estimate=pl.CostEstimate(flops=4000000, bytes_accessed=800000, transcendentals=0),
        name="taps",
        compiler_params=pltpu.CompilerParams(vmem_limit_bytes=GRANT),
    )(*small, near(block))
    tile = (dates, parts, tile_lines, tile_columns)
    if chips:
        out_shape = (pltpu.VMEM(tile, jnp.bfloat16),) * CHIPS
    else:
        out_shape = (pltpu.VMEM((owners,) + tile, jnp.bfloat16),)
    tiles = pl.pallas_call(
        functools.partial(
            resample_kernel, (line_groups, column_groups, tile_lines, tile_columns)
        ),
        out_shape=out_shape,
        in_specs=[VMEM] * 6,
        out_specs=(VMEM,) * len(out_shape),
        scratch_shapes=[pltpu.VMEM((2,) + even.shape, even.dtype)],
        name="resample",
        compiler_params=pltpu.CompilerParams(vmem_limit_bytes=GRANT),
    )(*[near(array) for array in (inner, even, odd, low_taps, high_taps, line_taps)])

    rows, cols = lines // LOOK_AZ, columns // LOOK_RG
    out_shape = (
        jax.ShapeDtypeStruct((dates, 2 * KINDS, rows, cols), jnp.float32),
        jax.ShapeDtypeStruct((dates, KINDS, rows, cols), jnp.float32),
    )
    if chips:

        def swapped(array, bits):
            pairs = [(i, i ^ bits) for i in range(owners) if i < i ^ bits]
            return exchanged(array, "date", pairs)

        order = [3, 2, 1]
        own = tiles[0]
        direct = {number: swapped(tiles[number], CORES * number) for number in order}
        other = swapped(own, 1)
        passed = {number: swapped(direct[number], 1) for number in order}
        held, positions = [own, other], [0, 1]
        for number in order:
            held += [direct[number], passed[number]]
            positions += [CORES * number, CORES * number + 1]
        results = pl.pallas_call(
            functools.partial(chip_looks_kernel, positions),
            out_shape=(pltpu.VMEM((CHANNELS * CHIP_LOOKS, LANES), jnp.float32),) * CHIPS,
            in_specs=[SMEM] * 2 + [VMEM] * len(held),
            out_specs=(VMEM,) * CHIPS,
            scratch_shapes=[
                pltpu.VMEM((total, parts, tile_lines, tile_columns), jnp.float32),
                pltpu.VMEM((CHIPS * QUANTITIES * CHIP_LOOKS, dates * columns), jnp.float32),
                pltpu.VMEM((CHIPS * QUANTITIES * CHIP_LOOKS, LANES), jnp.float32),
            ],
            name="looks",
            compiler_params=pltpu.CompilerParams(vmem_limit_bytes=GRANT),
        )(master_epoch_image, gap, *[near(tile) for tile in held])
        back = {number: swapped(results[number], CORES * number) for number in order}
        pieces = [results[0]] + [back[number] for number in order]
        return pl.pallas_call(
            functools.partial(chip_place_kernel, [0] + order),
            out_shape=out_shape,
            in_specs=[VMEM] * CHIPS,
            out_specs=(VMEM, VMEM),
            name="place",
            compiler_params=pltpu.CompilerParams(vmem_limit_bytes=GRANT),
        )(*[near(piece) for piece in pieces])

    tiles = lax.all_to_all(tiles[0], "date", 0, 0)
    results = pl.pallas_call(
        looks_kernel,
        out_shape=pltpu.VMEM((owners, dates * CHANNELS, lanes), jnp.float32),
        in_specs=[SMEM] * 2 + [VMEM],
        out_specs=VMEM,
        scratch_shapes=[
            pltpu.VMEM((total, parts, tile_lines, tile_columns), jnp.float32),
            pltpu.VMEM((total * QUANTITIES, line_looks * tile_columns), jnp.float32),
            pltpu.VMEM((total * QUANTITIES, lanes), jnp.float32),
            pltpu.VMEM((KINDS, total, lanes), jnp.float32),
        ],
        name="looks",
        compiler_params=pltpu.CompilerParams(vmem_limit_bytes=GRANT),
    )(master_epoch_image, gap, near(tiles))
    results = lax.all_to_all(results, "date", 0, 0)

    if column_groups == 1:
        return pl.pallas_call(
            place_kernel,
            out_shape=out_shape,
            in_specs=[VMEM],
            out_specs=(VMEM, VMEM),
            name="place",
            compiler_params=pltpu.CompilerParams(vmem_limit_bytes=GRANT),
        )(near(results))
    whole = results.reshape(
        line_groups, column_groups, dates, CHANNELS, line_looks, column_looks
    )
    whole = jnp.transpose(whole, (2, 3, 0, 4, 1, 5)).reshape(dates, CHANNELS, rows, cols)
    return (whole[:, : 2 * KINDS], whole[:, 2 * KINDS :])


def solution(mesh):
    in_specs = (P("date", None, None, "range"), P(), P(), P(), P(), P(), P(), P())
    out_specs = (P("date", None, None, "range"), P("date", None, None, "range"))
    return jax.shard_map(body, mesh=mesh, in_specs=in_specs, out_specs=out_specs, check_vma=False)
```

```python
import functools

import jax
import jax.numpy as jnp
from jax import lax
from jax.experimental import pallas as pl
from jax.experimental.pallas import tpu as pltpu
from jax.sharding import PartitionSpec as P

MAX_SWEEPS = 4
TAPS = 8
FRACTIONS = 16
MARGIN = 16
LOOK_AZ = 16
LOOK_RG = 4
QUANTITIES = 8
KINDS = 3
CHANNELS = 9
LANES = 128
GRANT = 24 * 2**20
CORES = 2
CHIPS = 4
CHIP_LOOKS = 4

SMEM = pl.BlockSpec(memory_space=pltpu.SMEM)
VMEM = pl.BlockSpec(memory_space=pltpu.VMEM)


def exchanged(array, axis, pairs):
    return lax.ppermute(array, axis, [route for a, b in pairs for route in ((a, b), (b, a))])


def near(array):
    return pltpu.with_memory_space_constraint(array, pltpu.VMEM)


def iotas(rows, cols):
    return (
        lax.broadcasted_iota(jnp.int32, (rows, cols), 0),
        lax.broadcasted_iota(jnp.int32, (rows, cols), 1),
    )


def weight_rows(fractions):
    row, lane = iotas(8, LANES)
    spot = jnp.zeros((8, LANES), jnp.float32)
    for number, fraction in enumerate(fractions):
        spot = jnp.where(row == number, fraction.astype(jnp.float32), spot)
    spacing = (lane - 1 - (TAPS // 2 - 1)).astype(jnp.float32) - spot / FRACTIONS
    angle = jnp.pi * spacing
    sinc = jnp.where(spacing == 0.0, 1.0, jnp.sin(angle) / jnp.where(spacing == 0.0, 1.0, angle))
    weights = sinc * jnp.cos(angle / (TAPS + 1)) ** 2
    weights = jnp.where((lane >= 1) & (lane <= TAPS), weights, 0.0)
    weights = weights / jnp.sum(weights, axis=1, keepdims=True)
    return weights.astype(jnp.bfloat16).astype(jnp.float32)


def by_chips(block, owners):
    dates, parts, lines, columns = block.shape
    return (
        owners == CHIPS * CORES
        and (dates, parts) == (2, 2)
        and lines == CHIPS * CHIP_LOOKS * LOOK_AZ
        and columns == 2 * LANES
    )


def tile_order(position, chips):
    return position ^ (lax.axis_index("date") // CORES) if chips else position


def banded(offsets, weights):
    rows, cols = offsets.shape
    lanes = jnp.broadcast_to(weights, (rows, LANES))
    spots = jnp.clip(offsets + 1, 0, TAPS + 1)
    return jnp.concatenate(
        [
            jnp.take_along_axis(lanes, spots[:, start : start + LANES], axis=1)
            for start in range(0, cols, LANES)
        ],
        axis=1,
    )


def start_kernel(x_ref, *refs):
    dates, parts, lines, columns = x_ref.shape
    images = [(slot, part) for slot in range(dates) for part in range(parts)]
    count = (len(refs) - 4) // 2
    near_ref, even_ref, odd_ref = refs[count : count + 3]
    sems = refs[-1]
    small = list(zip(refs[:count], refs[count + 3 : -1]))
    whole = [(x_ref.at[image], near_ref.at[image]) for image in images]
    copies = [
        pltpu.make_async_copy(source, target, sems.at[number])
        for number, (source, target) in enumerate(whole + small)
    ]
    for copy in copies:
        copy.start()
    forward = lax.axis_index("range") % 2 == 0
    for number, (slot, part) in enumerate(images):
        copies[number].wait()
        for parity, last_ref, first_ref in (
            (forward, even_ref, odd_ref),
            (jnp.logical_not(forward), odd_ref, even_ref),
        ):

            @pl.when(parity)
            def _():
                for half in range(2):
                    rows = slice(half * (lines // 2), (half + 1) * (lines // 2))
                    start = (half * len(images) + number) * MARGIN
                    spot = slice(start, start + MARGIN)
                    last_ref[:, spot] = near_ref[slot, part, rows, columns - MARGIN :]
                    first_ref[:, spot] = near_ref[slot, part, rows, :MARGIN]

    for copy in copies[len(images) :]:
        copy.wait()


def taps_kernel(
    chips,
    tile_lines,
    az_whole,
    az_part,
    rg_whole,
    rg_part,
    sweeps,
    x_ref,
    inner_ref,
    low_ref,
    high_ref,
    line_ref,
):
    dates, parts, lines, columns = x_ref.shape
    edge_rows = low_ref.shape[0]
    centre = TAPS // 2 - 1
    present = [lax.axis_index("date") * dates + slot for slot in range(dates)]
    table = weight_rows([rg_part[d] for d in present] + [az_part[d] for d in present])
    for slot, date in enumerate(present):
        shift = centre - rg_whole[date]
        weights = table[slot : slot + 1]
        row, col = iotas(columns, columns)
        own = banded(row - col + shift, weights).astype(jnp.bfloat16)
        for part in range(parts):
            inner_ref[slot, part] = jnp.dot(
                x_ref[slot, part], own, preferred_element_type=jnp.float32
            )
        row, col = iotas(edge_rows, LANES)
        low = banded(row % MARGIN - MARGIN - col + shift, weights)
        high = banded(row % MARGIN + LANES - col + shift, weights)
        for part in range(parts):
            image = slot * parts + part
            held = row // MARGIN == image
            spot = slice(image * LANES, (image + 1) * LANES)
            low_ref[:, spot] = jnp.where(held, low, 0.0).astype(jnp.bfloat16)
            high_ref[:, spot] = jnp.where(held, high, 0.0).astype(jnp.bfloat16)
        row, col = iotas(lines, lines)
        row = tile_order(row // tile_lines, chips) * tile_lines + row % tile_lines
        weights = table[dates + slot : dates + slot + 1]
        band = banded(col - row + (centre - az_whole[date]), weights)
        usable = row < sweeps[date] * (lines // MAX_SWEEPS)
        line_ref[slot] = jnp.where(usable, band, 0.0).astype(jnp.bfloat16)


def resample_kernel(split, inner_ref, even_ref, odd_ref, low_ref, high_ref, line_ref, *refs):
    *outs, edges = refs
    dates, parts, _, columns = inner_ref.shape
    line_groups, column_groups, tile_lines, tile_columns = split
    backward = lax.axis_index("range") % 2
    height, width = even_ref.shape
    for half in range(2):
        rows = slice(half * height, (half + 1) * height)
        spot = slice(half * (width // 2), (half + 1) * (width // 2))
        edges[1 - backward, rows, :] = even_ref[:, spot]
        edges[backward, rows, :] = odd_ref[:, spot]
    low = jnp.dot(edges[0], low_ref[...], preferred_element_type=jnp.float32)
    high = jnp.dot(edges[1], high_ref[...], preferred_element_type=jnp.float32)
    for slot in range(dates):
        for part in range(parts):
            spot = slice((slot * parts + part) * LANES, (slot * parts + part + 1) * LANES)
            pieces = [
                inner_ref[slot, part, :, start : start + LANES]
                for start in range(0, columns, LANES)
            ]
            pieces[0] += low[:, spot]
            pieces[-1] += high[:, spot]
            ranged = jnp.concatenate(pieces, axis=1)
            moved = jnp.dot(
                line_ref[slot], ranged.astype(jnp.bfloat16), preferred_element_type=jnp.float32
            ).astype(jnp.bfloat16)
            for i in range(line_groups):
                for j in range(column_groups):
                    tile = moved[
                        i * tile_lines : (i + 1) * tile_lines,
                        j * tile_columns : (j + 1) * tile_columns,
                    ]
                    if len(outs) == 1:
                        outs[0][i * column_groups + j, slot, part] = tile
                    else:
                        outs[i][slot, part] = tile


def partners(date, gap_ref, total):
    ahead = date + gap_ref[0, date]
    later = jnp.where(ahead < total, ahead, date - gap_ref[0, date])
    back = date - gap_ref[1, date]
    earlier = jnp.where(back >= 0, back, date + gap_ref[1, date])
    return (later, earlier)


def row_sums(values):
    row = lax.broadcasted_iota(jnp.int32, values[0].shape, 0)
    order = (3, 2, 1, 0, 7, 6, 5, 4)
    values = [values[number] for number in order]
    upper = row < 4
    values = [
        jnp.where(upper, a, b) + pltpu.roll(jnp.where(upper, b, a), 4, 0)
        for a, b in zip(values[:4], values[4:])
    ]
    for step, kept in ((2, row % 4 >= 2), (1, row % 2 == 1)):
        values = [
            jnp.where(kept, a + pltpu.roll(a, step, 0), b + pltpu.roll(b, 8 - step, 0))
            for a, b in zip(values[:step], values[step:])
        ]
    return values[0]


def pool_columns(sums, lanes):
    row, col = iotas(sums.shape[1], lanes)
    pool = jnp.where(row // LOOK_RG == col, 1.0, 0.0).astype(jnp.bfloat16)
    coarse = sums.astype(jnp.bfloat16)
    fine = (sums - coarse.astype(jnp.float32)).astype(jnp.bfloat16)
    return jnp.dot(coarse, pool, preferred_element_type=jnp.float32) + jnp.dot(
        fine, pool, preferred_element_type=jnp.float32
    )


def looks_kernel(root_ref, gap_ref, tiles_ref, out_ref, stack, sums, pooled, powers):
    total, _, tile_lines, tile_columns = stack.shape
    owners, per_owner, lanes = out_ref.shape
    dates = per_owner // CHANNELS
    line_looks = tile_lines // LOOK_AZ
    unroll = total if total <= 16 else 1

    def widen(owner, carry):
        stack[pl.ds(owner * dates, dates)] = tiles_ref[owner].astype(jnp.float32)
        return carry

    lax.fori_loop(0, owners, widen, 0)

    def partner_of(kind, date):
        return partners(date, gap_ref, total)[kind - 1] if kind else root_ref[0]

    def collect(date, carry):
        left0, left1 = stack[date, 0], stack[date, 1]
        values = []
        for kind in range(KINDS):
            partner = partner_of(kind, date)
            right0, right1 = stack[partner, 0], stack[partner, 1]
            values += [left0 * right0 + left1 * right1, left1 * right0 - left0 * right1]
        values.append(left0 * left0 + left1 * left1)
        values.append(jnp.zeros_like(left0))
        rows = pl.ds(pl.multiple_of(date * QUANTITIES, QUANTITIES), QUANTITIES)
        for look in range(line_looks):
            start = look * LOOK_AZ
            sums[rows, look * tile_columns : (look + 1) * tile_columns] = row_sums(
                [value[start : start + 8] + value[start + 8 : start + 16] for value in values]
            )
        return carry

    lax.fori_loop(0, total, collect, 0, unroll=unroll)
    pooled[...] = pool_columns(sums[...], lanes)

    def gather(date, carry):
        for kind in range(KINDS):
            power = partner_of(kind, date) * QUANTITIES + 2 * KINDS
            powers[kind, pl.ds(date, 1), :] = pooled[pl.ds(power, 1), :]
        return carry

    lax.fori_loop(0, total, gather, 0, unroll=unroll)
    scale = 1.0 / (LOOK_AZ * LOOK_RG) ** 0.5

    for slot in range(dates):

        def every(number):
            return pooled[pl.ds(slot * QUANTITIES + number, owners, stride=dates * QUANTITIES), :]

        power_left = every(2 * KINDS)
        for kind in range(KINDS):
            real, imag = every(2 * kind), every(2 * kind + 1)
            power_right = powers[kind, pl.ds(slot, owners, stride=dates), :]
            out_ref[:, slot * CHANNELS + 2 * kind, :] = real * scale
            out_ref[:, slot * CHANNELS + 2 * kind + 1, :] = imag * scale
            out_ref[:, slot * CHANNELS + 2 * KINDS + kind, :] = jnp.sqrt(
                real * real + imag * imag
            ) / jnp.sqrt(power_left * power_right + 1e-06)


def chip_looks_kernel(positions, root_ref, gap_ref, *refs):
    tiles, outs, (stack, sums, pooled) = refs[: CHIPS * CORES], refs[CHIPS * CORES : -3], refs[-3:]
    dates, _, _, columns = tiles[0].shape
    me = lax.axis_index("date")
    total = len(tiles) * dates
    scale = 1.0 / (LOOK_AZ * LOOK_RG) ** 0.5
    for position, tile_ref in zip(positions, tiles):
        stack[position * dates : (position + 1) * dates] = tile_ref[...].astype(jnp.float32)

    def partner_of(kind, date):
        partner = partners(date, gap_ref, total)[kind - 1] if kind else root_ref[0]
        return lax.div(partner, dates) ^ me, lax.rem(partner, dates)

    def part(spot, number, look):
        return stack[spot, number, look * LOOK_AZ : (look + 1) * LOOK_AZ, :]

    def folded(value):
        return value[: LOOK_AZ // 2] + value[LOOK_AZ // 2 :]

    block = QUANTITIES * CHIP_LOOKS
    for chip in range(CHIPS):
        for slot in range(dates):
            date = (me ^ (CORES * chip)) * dates + slot
            own = CORES * chip * dates + slot
            spot = slice(slot * columns, (slot + 1) * columns)
            for kind in range(KINDS):
                position, number = partner_of(kind, date)
                other = position * dates + number
                reals, imags = [], []
                for look in range(CHIP_LOOKS):
                    left0, left1 = part(own, 0, look), part(own, 1, look)
                    right0, right1 = part(other, 0, look), part(other, 1, look)
                    reals.append(folded(left0 * right0 + left1 * right1))
                    imags.append(folded(left1 * right0 - left0 * right1))
                start = chip * block + kind * 2 * CHIP_LOOKS
                sums[start : start + 2 * CHIP_LOOKS, spot] = row_sums(reals + imags)
            powers = []
            for core in range(CORES):
                for look in range(CHIP_LOOKS):
                    left0 = part(own + core * dates, 0, look)
                    left1 = part(own + core * dates, 1, look)
                    powers.append(folded(left0 * left0 + left1 * left1))
            start = chip * block + KINDS * 2 * CHIP_LOOKS
            sums[start : start + 2 * CHIP_LOOKS, spot] = row_sums(powers)
    pooled[...] = pool_columns(sums[...], LANES)

    row, lane = iotas(2 * CHIP_LOOKS, LANES)
    upper, first = row < CHIP_LOOKS, lane < LANES // 2
    for chip in range(CHIPS):
        base = chip * block
        views = [pooled[base + 8 * number : base + 8 * (number + 1), :] for number in range(4)]
        squares = [view * view for view in views[:KINDS]]
        squares = [square + pltpu.roll(square, CHIP_LOOKS, 0) for square in squares]
        power_left = jnp.where(upper, views[KINDS], pltpu.roll(views[KINDS], CHIP_LOOKS, 0))
        power_right = []
        for kind in range(KINDS):
            halves = []
            for slot in range(dates):
                position, number = partner_of(kind, (me ^ (CORES * chip)) * dates + slot)
                start = lax.div(position, CORES) * block + KINDS * 2 * CHIP_LOOKS
                power = pooled[pl.ds(pl.multiple_of(start, 8), 8), :]
                power = pltpu.roll(power, CHIP_LOOKS * (lax.rem(position, CORES) ^ (kind % 2)), 0)
                halves.append(pltpu.roll(power, LANES // 2 * (number ^ slot), 1))
            power_right.append(jnp.where(first, halves[0], halves[1]))
        outs[chip][: 2 * KINDS * CHIP_LOOKS, :] = (
            pooled[base : base + 2 * KINDS * CHIP_LOOKS, :] * scale
        )
        pairs = (
            (jnp.where(upper, squares[0], squares[1]), jnp.where(upper, *power_right[:2])),
            (squares[2], power_right[2]),
        )
        start = 2 * KINDS * CHIP_LOOKS
        for square, power in pairs:
            coherent = jnp.sqrt(square) / jnp.sqrt(power_left * power + 1e-06)
            rows = min(8, outs[chip].shape[0] - start)
            outs[chip][start : start + rows, :] = coherent[:rows]
            start += rows


def chip_place_kernel(positions, *refs):
    pieces, (ifg_ref, coh_ref) = refs[:CHIPS], refs[CHIPS:]
    dates, _, _, columns = ifg_ref.shape
    mine = lax.axis_index("date") // CORES
    for chip in range(CHIPS):

        @pl.when(mine == chip)
        def _():
            for position, piece_ref in zip(positions, pieces):
                start = (chip ^ position) * CHIP_LOOKS
                where = slice(start, start + CHIP_LOOKS)
                for channel in range(CHANNELS):
                    rows = piece_ref[channel * CHIP_LOOKS : (channel + 1) * CHIP_LOOKS, :]
                    for slot in range(dates):
                        part = rows[:, slot * columns : (slot + 1) * columns]
                        if channel < 2 * KINDS:
                            ifg_ref[slot, channel, where, :] = part
                        else:
                            coh_ref[slot, channel - 2 * KINDS, where, :] = part


def place_kernel(x_ref, ifg_ref, coh_ref):
    sources, rows, lanes = x_ref.shape
    dates, _, lines, columns = ifg_ref.shape
    looks = lanes // columns
    for slot in range(dates):
        for channel in range(CHANNELS):
            values = x_ref[:, slot * CHANNELS + channel, :]
            for look in range(looks):
                part = values[:, look * columns : (look + 1) * columns]
                where = pl.ds(look, sources, stride=looks)
                if channel < 2 * KINDS:
                    ifg_ref[slot, channel, where, :] = part
                else:
                    coh_ref[slot, channel - 2 * KINDS, where, :] = part


def body(
    epoch_tiles_quadrature,
    along_track_whole_displacement,
    along_track_subpixel_weights,
    slant_whole_displacement,
    slant_subpixel_weights,
    sweeps_each_epoch,
    baseline_companion_gap,
    master_epoch_image,
):
    block = epoch_tiles_quadrature
    dates, parts, lines, columns = block.shape
    owners = lax.axis_size("date")
    total = owners * dates
    images = dates * parts
    chips = by_chips(block, owners)
    line_groups = CHIPS if chips else min(owners, lines // LOOK_AZ)
    column_groups = 1 if chips else owners // line_groups
    tile_lines, tile_columns = lines // line_groups, columns // column_groups
    line_looks, column_looks = tile_lines // LOOK_AZ, tile_columns // LOOK_RG
    lanes = line_looks * column_looks

    arguments = (
        block,
        along_track_whole_displacement,
        along_track_subpixel_weights,
        slant_whole_displacement,
        slant_subpixel_weights,
        sweeps_each_epoch,
        baseline_companion_gap.T,
    )
    block, even, odd, *small = pl.pallas_call(
        start_kernel,
        out_shape=(
            pltpu.VMEM(block.shape, block.dtype),
            pltpu.VMEM((lines // 2, 2 * images * MARGIN), jnp.bfloat16),
            pltpu.VMEM((lines // 2, 2 * images * MARGIN), jnp.bfloat16),
            *[pltpu.SMEM(array.shape, array.dtype) for array in arguments[1:]],
        ),
        in_specs=[pl.BlockSpec(memory_space=pltpu.HBM)] * len(arguments),
        out_specs=(VMEM,) * 3 + (SMEM,) * (len(arguments) - 1),
        scratch_shapes=[pltpu.SemaphoreType.DMA((images + len(arguments) - 1,))],
        name="start",
        compiler_params=pltpu.CompilerParams(vmem_limit_bytes=GRANT),
    )(*[pltpu.with_memory_space_constraint(array, pltpu.HBM) for array in arguments])
    *small, gap = [pltpu.with_memory_space_constraint(array, pltpu.SMEM) for array in small]
    width = lax.axis_size("range")
    odd = exchanged(odd, "range", [(j, j + 1) for j in range(1, width - 1, 2)])
    even = exchanged(even, "range", [(j, j + 1) for j in range(0, width - 1, 2)])

    inner, low_taps, high_taps, line_taps = pl.pallas_call(
        functools.partial(taps_kernel, chips, tile_lines),
        out_shape=(
            pltpu.VMEM(block.shape, jnp.float32),
            pltpu.VMEM((images * MARGIN, images * LANES), jnp.bfloat16),
            pltpu.VMEM((images * MARGIN, images * LANES), jnp.bfloat16),
            pltpu.VMEM((dates, lines, lines), jnp.bfloat16),
        ),
        in_specs=[SMEM] * len(small) + [VMEM],
        out_specs=(VMEM,) * 4,
        cost_estimate=pl.CostEstimate(flops=4000000, bytes_accessed=800000, transcendentals=0),
        name="taps",
        compiler_params=pltpu.CompilerParams(vmem_limit_bytes=GRANT),
    )(*small, near(block))
    tile = (dates, parts, tile_lines, tile_columns)
    if chips:
        out_shape = (pltpu.VMEM(tile, jnp.bfloat16),) * CHIPS
    else:
        out_shape = (pltpu.VMEM((owners,) + tile, jnp.bfloat16),)
    tiles = pl.pallas_call(
        functools.partial(
            resample_kernel, (line_groups, column_groups, tile_lines, tile_columns)
        ),
        out_shape=out_shape,
        in_specs=[VMEM] * 6,
        out_specs=(VMEM,) * len(out_shape),
        scratch_shapes=[pltpu.VMEM((2, lines, images * MARGIN), jnp.bfloat16)],
        name="resample",
        compiler_params=pltpu.CompilerParams(vmem_limit_bytes=GRANT),
    )(*[near(array) for array in (inner, even, odd, low_taps, high_taps, line_taps)])

    rows, cols = lines // LOOK_AZ, columns // LOOK_RG
    out_shape = (
        jax.ShapeDtypeStruct((dates, 2 * KINDS, rows, cols), jnp.float32),
        jax.ShapeDtypeStruct((dates, KINDS, rows, cols), jnp.float32),
    )
    if chips:

        def swapped(array, bits):
            pairs = [(i, i ^ bits) for i in range(owners) if i < i ^ bits]
            return exchanged(array, "date", pairs)

        order = [3, 2, 1]
        own = tiles[0]
        direct = {number: swapped(tiles[number], CORES * number) for number in order}
        other = swapped(own, 1)
        passed = {number: swapped(direct[number], 1) for number in order}
        held, positions = [own, other], [0, 1]
        for number in order:
            held += [direct[number], passed[number]]
            positions += [CORES * number, CORES * number + 1]
        results = pl.pallas_call(
            functools.partial(chip_looks_kernel, positions),
            out_shape=(pltpu.VMEM((CHANNELS * CHIP_LOOKS, LANES), jnp.float32),) * CHIPS,
            in_specs=[SMEM] * 2 + [VMEM] * len(held),
            out_specs=(VMEM,) * CHIPS,
            scratch_shapes=[
                pltpu.VMEM((total, parts, tile_lines, tile_columns), jnp.float32),
                pltpu.VMEM((CHIPS * QUANTITIES * CHIP_LOOKS, dates * columns), jnp.float32),
                pltpu.VMEM((CHIPS * QUANTITIES * CHIP_LOOKS, LANES), jnp.float32),
            ],
            name="looks",
            compiler_params=pltpu.CompilerParams(vmem_limit_bytes=GRANT),
        )(master_epoch_image, gap, *[near(tile) for tile in held])
        back = {number: swapped(results[number], CORES * number) for number in order}
        last = [1, 3, 2]
        pieces = [results[0]] + [back[number] for number in last]
        return pl.pallas_call(
            functools.partial(chip_place_kernel, [0] + last),
            out_shape=out_shape,
            in_specs=[VMEM] * CHIPS,
            out_specs=(VMEM, VMEM),
            name="place",
            compiler_params=pltpu.CompilerParams(vmem_limit_bytes=GRANT),
        )(*[near(piece) for piece in pieces])

    tiles = lax.all_to_all(tiles[0], "date", 0, 0)
    results = pl.pallas_call(
        looks_kernel,
        out_shape=pltpu.VMEM((owners, dates * CHANNELS, lanes), jnp.float32),
        in_specs=[SMEM] * 2 + [VMEM],
        out_specs=VMEM,
        scratch_shapes=[
            pltpu.VMEM((total, parts, tile_lines, tile_columns), jnp.float32),
            pltpu.VMEM((total * QUANTITIES, line_looks * tile_columns), jnp.float32),
            pltpu.VMEM((total * QUANTITIES, lanes), jnp.float32),
            pltpu.VMEM((KINDS, total, lanes), jnp.float32),
        ],
        name="looks",
        compiler_params=pltpu.CompilerParams(vmem_limit_bytes=GRANT),
    )(master_epoch_image, gap, near(tiles))
    results = lax.all_to_all(results, "date", 0, 0)

    if column_groups == 1:
        return pl.pallas_call(
            place_kernel,
            out_shape=out_shape,
            in_specs=[VMEM],
            out_specs=(VMEM, VMEM),
            name="place",
            compiler_params=pltpu.CompilerParams(vmem_limit_bytes=GRANT),
        )(near(results))
    whole = results.reshape(
        line_groups, column_groups, dates, CHANNELS, line_looks, column_looks
    )
    whole = jnp.transpose(whole, (2, 3, 0, 4, 1, 5)).reshape(dates, CHANNELS, rows, cols)
    return (whole[:, : 2 * KINDS], whole[:, 2 * KINDS :])


def solution(mesh):
    in_specs = (P("date", None, None, "range"), P(), P(), P(), P(), P(), P(), P())
    out_specs = (P("date", None, None, "range"), P("date", None, None, "range"))
    return jax.shard_map(body, mesh=mesh, in_specs=in_specs, out_specs=out_specs, check_vma=False)
```

```python
import functools

import jax
import jax.numpy as jnp
from jax import lax
from jax.experimental import pallas as pl
from jax.experimental.pallas import tpu as pltpu
from jax.sharding import PartitionSpec as P

MAX_SWEEPS = 4
TAPS = 8
FRACTIONS = 16
MARGIN = 16
LOOK_AZ = 16
LOOK_RG = 4
QUANTITIES = 8
KINDS = 3
CHANNELS = 9
LANES = 128
GRANT = 24 * 2**20
CORES = 2
CHIPS = 4
CHIP_LOOKS = 4

SMEM = pl.BlockSpec(memory_space=pltpu.SMEM)
VMEM = pl.BlockSpec(memory_space=pltpu.VMEM)


def exchanged(array, axis, pairs):
    return lax.ppermute(array, axis, [route for a, b in pairs for route in ((a, b), (b, a))])


def near(array):
    return pltpu.with_memory_space_constraint(array, pltpu.VMEM)


def iotas(rows, cols):
    return (
        lax.broadcasted_iota(jnp.int32, (rows, cols), 0),
        lax.broadcasted_iota(jnp.int32, (rows, cols), 1),
    )


def weight_rows(fractions):
    row, lane = iotas(8, LANES)
    spot = jnp.zeros((8, LANES), jnp.float32)
    for number, fraction in enumerate(fractions):
        spot = jnp.where(row == number, fraction.astype(jnp.float32), spot)
    spacing = (lane - 1 - (TAPS // 2 - 1)).astype(jnp.float32) - spot / FRACTIONS
    angle = jnp.pi * spacing
    sinc = jnp.where(spacing == 0.0, 1.0, jnp.sin(angle) / jnp.where(spacing == 0.0, 1.0, angle))
    weights = sinc * jnp.cos(angle / (TAPS + 1)) ** 2
    weights = jnp.where((lane >= 1) & (lane <= TAPS), weights, 0.0)
    weights = weights / jnp.sum(weights, axis=1, keepdims=True)
    return weights.astype(jnp.bfloat16).astype(jnp.float32)


def by_chips(block, owners):
    dates, parts, lines, columns = block.shape
    return (
        owners == CHIPS * CORES
        and (dates, parts) == (2, 2)
        and lines == CHIPS * CHIP_LOOKS * LOOK_AZ
        and columns == 2 * LANES
    )


def tile_order(position, chips):
    return position ^ (lax.axis_index("date") // CORES) if chips else position


def banded(offsets, weights):
    rows, cols = offsets.shape
    lanes = jnp.broadcast_to(weights, (rows, LANES))
    spots = jnp.clip(offsets + 1, 0, TAPS + 1)
    return jnp.concatenate(
        [
            jnp.take_along_axis(lanes, spots[:, start : start + LANES], axis=1)
            for start in range(0, cols, LANES)
        ],
        axis=1,
    )


def start_kernel(x_ref, *refs):
    dates, parts, lines, columns = x_ref.shape
    images = [(slot, part) for slot in range(dates) for part in range(parts)]
    count = (len(refs) - 4) // 2
    near_ref, even_ref, odd_ref = refs[count : count + 3]
    sems = refs[-1]
    small = list(zip(refs[:count], refs[count + 3 : -1]))
    whole = [(x_ref.at[image], near_ref.at[image]) for image in images]
    copies = [
        pltpu.make_async_copy(source, target, sems.at[number])
        for number, (source, target) in enumerate(whole + small)
    ]
    for copy in copies:
        copy.start()
    forward = lax.axis_index("range") % 2 == 0
    for number, (slot, part) in enumerate(images):
        copies[number].wait()
        for parity, last_ref, first_ref in (
            (forward, even_ref, odd_ref),
            (jnp.logical_not(forward), odd_ref, even_ref),
        ):

            @pl.when(parity)
            def _():
                for half in range(2):
                    rows = slice(half * (lines // 2), (half + 1) * (lines // 2))
                    start = (half * len(images) + number) * MARGIN
                    spot = slice(start, start + MARGIN)
                    last_ref[:, spot] = near_ref[slot, part, rows, columns - MARGIN :]
                    first_ref[:, spot] = near_ref[slot, part, rows, :MARGIN]

    for copy in copies[len(images) :]:
        copy.wait()


def taps_kernel(
    chips,
    tile_lines,
    az_whole,
    az_part,
    rg_whole,
    rg_part,
    sweeps,
    x_ref,
    inner_ref,
    low_ref,
    high_ref,
    line_ref,
):
    dates, parts, lines, columns = x_ref.shape
    edge_rows = low_ref.shape[0]
    centre = TAPS // 2 - 1
    present = [lax.axis_index("date") * dates + slot for slot in range(dates)]
    table = weight_rows([rg_part[d] for d in present] + [az_part[d] for d in present])
    for slot, date in enumerate(present):
        shift = centre - rg_whole[date]
        weights = table[slot : slot + 1]
        row, col = iotas(columns, columns)
        own = banded(row - col + shift, weights).astype(jnp.bfloat16)
        for part in range(parts):
            inner_ref[slot, part] = jnp.dot(
                x_ref[slot, part], own, preferred_element_type=jnp.float32
            )
        row, col = iotas(edge_rows, LANES)
        low = banded(row % MARGIN - MARGIN - col + shift, weights)
        high = banded(row % MARGIN + LANES - col + shift, weights)
        for part in range(parts):
            image = slot * parts + part
            held = row // MARGIN == image
            spot = slice(image * LANES, (image + 1) * LANES)
            low_ref[:, spot] = jnp.where(held, low, 0.0).astype(jnp.bfloat16)
            high_ref[:, spot] = jnp.where(held, high, 0.0).astype(jnp.bfloat16)
        row, col = iotas(lines, lines)
        row = tile_order(row // tile_lines, chips) * tile_lines + row % tile_lines
        weights = table[dates + slot : dates + slot + 1]
        band = banded(col - row + (centre - az_whole[date]), weights)
        usable = row < sweeps[date] * (lines // MAX_SWEEPS)
        line_ref[slot] = jnp.where(usable, band, 0.0).astype(jnp.bfloat16)


def resample_kernel(split, inner_ref, even_ref, odd_ref, low_ref, high_ref, line_ref, *refs):
    *outs, edges = refs
    dates, parts, _, columns = inner_ref.shape
    line_groups, column_groups, tile_lines, tile_columns = split
    backward = lax.axis_index("range") % 2
    height, width = even_ref.shape
    for half in range(2):
        rows = slice(half * height, (half + 1) * height)
        spot = slice(half * (width // 2), (half + 1) * (width // 2))
        edges[1 - backward, rows, :] = even_ref[:, spot]
        edges[backward, rows, :] = odd_ref[:, spot]
    low = jnp.dot(edges[0], low_ref[...], preferred_element_type=jnp.float32)
    high = jnp.dot(edges[1], high_ref[...], preferred_element_type=jnp.float32)
    for slot in range(dates):
        for part in range(parts):
            spot = slice((slot * parts + part) * LANES, (slot * parts + part + 1) * LANES)
            pieces = [
                inner_ref[slot, part, :, start : start + LANES]
                for start in range(0, columns, LANES)
            ]
            pieces[0] += low[:, spot]
            pieces[-1] += high[:, spot]
            ranged = jnp.concatenate(pieces, axis=1)
            moved = jnp.dot(
                line_ref[slot], ranged.astype(jnp.bfloat16), preferred_element_type=jnp.float32
            ).astype(jnp.bfloat16)
            for i in range(line_groups):
                for j in range(column_groups):
                    tile = moved[
                        i * tile_lines : (i + 1) * tile_lines,
                        j * tile_columns : (j + 1) * tile_columns,
                    ]
                    if len(outs) == 1:
                        outs[0][i * column_groups + j, slot, part] = tile
                    else:
                        outs[i][slot, part] = tile


def partners(date, gap_ref, total):
    ahead = date + gap_ref[0, date]
    later = jnp.where(ahead < total, ahead, date - gap_ref[0, date])
    back = date - gap_ref[1, date]
    earlier = jnp.where(back >= 0, back, date + gap_ref[1, date])
    return (later, earlier)


def row_sums(values):
    row = lax.broadcasted_iota(jnp.int32, values[0].shape, 0)
    order = (3, 2, 1, 0, 7, 6, 5, 4)
    values = [values[number] for number in order]
    upper = row < 4
    values = [
        jnp.where(upper, a, b) + pltpu.roll(jnp.where(upper, b, a), 4, 0)
        for a, b in zip(values[:4], values[4:])
    ]
    for step, kept in ((2, row % 4 >= 2), (1, row % 2 == 1)):
        values = [
            jnp.where(kept, a + pltpu.roll(a, step, 0), b + pltpu.roll(b, 8 - step, 0))
            for a, b in zip(values[:step], values[step:])
        ]
    return values[0]


def pool_columns(sums, lanes):
    row, col = iotas(sums.shape[1], lanes)
    pool = jnp.where(row // LOOK_RG == col, 1.0, 0.0).astype(jnp.bfloat16)
    coarse = sums.astype(jnp.bfloat16)
    fine = (sums - coarse.astype(jnp.float32)).astype(jnp.bfloat16)
    return jnp.dot(coarse, pool, preferred_element_type=jnp.float32) + jnp.dot(
        fine, pool, preferred_element_type=jnp.float32
    )


def looks_kernel(root_ref, gap_ref, tiles_ref, out_ref, stack, sums, pooled, powers):
    total, _, tile_lines, tile_columns = stack.shape
    owners, per_owner, lanes = out_ref.shape
    dates = per_owner // CHANNELS
    line_looks = tile_lines // LOOK_AZ
    unroll = total if total <= 16 else 1

    def widen(owner, carry):
        stack[pl.ds(owner * dates, dates)] = tiles_ref[owner].astype(jnp.float32)
        return carry

    lax.fori_loop(0, owners, widen, 0)

    def partner_of(kind, date):
        return partners(date, gap_ref, total)[kind - 1] if kind else root_ref[0]

    def collect(date, carry):
        left0, left1 = stack[date, 0], stack[date, 1]
        values = []
        for kind in range(KINDS):
            partner = partner_of(kind, date)
            right0, right1 = stack[partner, 0], stack[partner, 1]
            values += [left0 * right0 + left1 * right1, left1 * right0 - left0 * right1]
        values.append(left0 * left0 + left1 * left1)
        values.append(jnp.zeros_like(left0))
        rows = pl.ds(pl.multiple_of(date * QUANTITIES, QUANTITIES), QUANTITIES)
        for look in range(line_looks):
            start = look * LOOK_AZ
            sums[rows, look * tile_columns : (look + 1) * tile_columns] = row_sums(
                [value[start : start + 8] + value[start + 8 : start + 16] for value in values]
            )
        return carry

    lax.fori_loop(0, total, collect, 0, unroll=unroll)
    pooled[...] = pool_columns(sums[...], lanes)

    def gather(date, carry):
        for kind in range(KINDS):
            power = partner_of(kind, date) * QUANTITIES + 2 * KINDS
            powers[kind, pl.ds(date, 1), :] = pooled[pl.ds(power, 1), :]
        return carry

    lax.fori_loop(0, total, gather, 0, unroll=unroll)
    scale = 1.0 / (LOOK_AZ * LOOK_RG) ** 0.5

    for slot in range(dates):

        def every(number):
            return pooled[pl.ds(slot * QUANTITIES + number, owners, stride=dates * QUANTITIES), :]

        power_left = every(2 * KINDS)
        for kind in range(KINDS):
            real, imag = every(2 * kind), every(2 * kind + 1)
            power_right = powers[kind, pl.ds(slot, owners, stride=dates), :]
            out_ref[:, slot * CHANNELS + 2 * kind, :] = real * scale
            out_ref[:, slot * CHANNELS + 2 * kind + 1, :] = imag * scale
            out_ref[:, slot * CHANNELS + 2 * KINDS + kind, :] = jnp.sqrt(
                real * real + imag * imag
            ) / jnp.sqrt(power_left * power_right + 1e-06)


def chip_looks_kernel(positions, root_ref, gap_ref, *refs):
    tiles, outs, (stack, sums, pooled) = refs[: CHIPS * CORES], refs[CHIPS * CORES : -3], refs[-3:]
    dates, _, _, columns = tiles[0].shape
    me = lax.axis_index("date")
    total = len(tiles) * dates
    scale = 1.0 / (LOOK_AZ * LOOK_RG) ** 0.5
    for position, tile_ref in zip(positions, tiles):
        stack[position * dates : (position + 1) * dates] = tile_ref[...].astype(jnp.float32)

    def partner_of(kind, date):
        partner = partners(date, gap_ref, total)[kind - 1] if kind else root_ref[0]
        return lax.div(partner, dates) ^ me, lax.rem(partner, dates)

    def part(spot, number, look):
        return stack[spot, number, look * LOOK_AZ : (look + 1) * LOOK_AZ, :]

    def folded(value):
        return value[: LOOK_AZ // 2] + value[LOOK_AZ // 2 :]

    block = QUANTITIES * CHIP_LOOKS
    for chip in range(CHIPS):
        for slot in range(dates):
            own = CORES * chip * dates + slot
            others = []
            for kind in range(KINDS):
                position, number = partner_of(kind, (me ^ (CORES * chip)) * dates + slot)
                others.append(position * dates + number)
            for look in range(CHIP_LOOKS):
                left0, left1 = part(own, 0, look), part(own, 1, look)
                values = []
                for other in others:
                    right0, right1 = part(other, 0, look), part(other, 1, look)
                    values.append(folded(left0 * right0 + left1 * right1))
                    values.append(folded(left1 * right0 - left0 * right1))
                values.append(folded(left0 * left0 + left1 * left1))
                right0, right1 = part(own + dates, 0, look), part(own + dates, 1, look)
                values.append(folded(right0 * right0 + right1 * right1))
                start = chip * block + look * QUANTITIES
                sums[start : start + QUANTITIES, slot * columns : (slot + 1) * columns] = (
                    row_sums(values)
                )
    pooled[...] = pool_columns(sums[...], LANES)

    def every_look(start):
        return pooled[pl.ds(start, CHIP_LOOKS, stride=QUANTITIES), :]

    first = lax.broadcasted_iota(jnp.int32, (CHIP_LOOKS, LANES), 1) < LANES // 2
    for chip in range(CHIPS):
        base = chip * block
        power_left = every_look(base + 2 * KINDS)
        for kind in range(KINDS):
            halves = []
            for slot in range(dates):
                position, number = partner_of(kind, (me ^ (CORES * chip)) * dates + slot)
                start = lax.div(position, CORES) * block + 2 * KINDS + lax.rem(position, CORES)
                halves.append(pltpu.roll(every_look(start), LANES // 2 * (number ^ slot), 1))
            power = power_left * jnp.where(first, halves[0], halves[1])
            real, imag = every_look(base + 2 * kind), every_look(base + 2 * kind + 1)
            for channel, value in (
                (2 * kind, real * scale),
                (2 * kind + 1, imag * scale),
                (2 * KINDS + kind, jnp.sqrt(real * real + imag * imag) / jnp.sqrt(power + 1e-06)),
            ):
                outs[chip][channel * CHIP_LOOKS : (channel + 1) * CHIP_LOOKS, :] = value


def chip_place_kernel(positions, *refs):
    pieces, (ifg_ref, coh_ref) = refs[:CHIPS], refs[CHIPS:]
    dates, _, _, columns = ifg_ref.shape
    mine = lax.axis_index("date") // CORES
    for chip in range(CHIPS):

        @pl.when(mine == chip)
        def _():
            for position, piece_ref in zip(positions, pieces):
                start = (chip ^ position) * CHIP_LOOKS
                where = slice(start, start + CHIP_LOOKS)
                for channel in range(CHANNELS):
                    rows = piece_ref[channel * CHIP_LOOKS : (channel + 1) * CHIP_LOOKS, :]
                    for slot in range(dates):
                        part = rows[:, slot * columns : (slot + 1) * columns]
                        if channel < 2 * KINDS:
                            ifg_ref[slot, channel, where, :] = part
                        else:
                            coh_ref[slot, channel - 2 * KINDS, where, :] = part


def place_kernel(x_ref, ifg_ref, coh_ref):
    sources, rows, lanes = x_ref.shape
    dates, _, lines, columns = ifg_ref.shape
    looks = lanes // columns
    for slot in range(dates):
        for channel in range(CHANNELS):
            values = x_ref[:, slot * CHANNELS + channel, :]
            for look in range(looks):
                part = values[:, look * columns : (look + 1) * columns]
                where = pl.ds(look, sources, stride=looks)
                if channel < 2 * KINDS:
                    ifg_ref[slot, channel, where, :] = part
                else:
                    coh_ref[slot, channel - 2 * KINDS, where, :] = part


def body(
    epoch_tiles_quadrature,
    along_track_whole_displacement,
    along_track_subpixel_weights,
    slant_whole_displacement,
    slant_subpixel_weights,
    sweeps_each_epoch,
    baseline_companion_gap,
    master_epoch_image,
):
    block = epoch_tiles_quadrature
    dates, parts, lines, columns = block.shape
    owners = lax.axis_size("date")
    total = owners * dates
    images = dates * parts
    chips = by_chips(block, owners)
    line_groups = CHIPS if chips else min(owners, lines // LOOK_AZ)
    column_groups = 1 if chips else owners // line_groups
    tile_lines, tile_columns = lines // line_groups, columns // column_groups
    line_looks, column_looks = tile_lines // LOOK_AZ, tile_columns // LOOK_RG
    lanes = line_looks * column_looks

    arguments = (
        block,
        along_track_whole_displacement,
        along_track_subpixel_weights,
        slant_whole_displacement,
        slant_subpixel_weights,
        sweeps_each_epoch,
        baseline_companion_gap.T,
    )
    block, even, odd, *small = pl.pallas_call(
        start_kernel,
        out_shape=(
            pltpu.VMEM(block.shape, block.dtype),
            pltpu.VMEM((lines // 2, 2 * images * MARGIN), jnp.bfloat16),
            pltpu.VMEM((lines // 2, 2 * images * MARGIN), jnp.bfloat16),
            *[pltpu.SMEM(array.shape, array.dtype) for array in arguments[1:]],
        ),
        in_specs=[pl.BlockSpec(memory_space=pltpu.HBM)] * len(arguments),
        out_specs=(VMEM,) * 3 + (SMEM,) * (len(arguments) - 1),
        scratch_shapes=[pltpu.SemaphoreType.DMA((images + len(arguments) - 1,))],
        name="start",
        compiler_params=pltpu.CompilerParams(vmem_limit_bytes=GRANT),
    )(*[pltpu.with_memory_space_constraint(array, pltpu.HBM) for array in arguments])
    *small, gap = [pltpu.with_memory_space_constraint(array, pltpu.SMEM) for array in small]
    width = lax.axis_size("range")
    odd = exchanged(odd, "range", [(j, j + 1) for j in range(1, width - 1, 2)])
    even = exchanged(even, "range", [(j, j + 1) for j in range(0, width - 1, 2)])

    inner, low_taps, high_taps, line_taps = pl.pallas_call(
        functools.partial(taps_kernel, chips, tile_lines),
        out_shape=(
            pltpu.VMEM(block.shape, jnp.float32),
            pltpu.VMEM((images * MARGIN, images * LANES), jnp.bfloat16),
            pltpu.VMEM((images * MARGIN, images * LANES), jnp.bfloat16),
            pltpu.VMEM((dates, lines, lines), jnp.bfloat16),
        ),
        in_specs=[SMEM] * len(small) + [VMEM],
        out_specs=(VMEM,) * 4,
        cost_estimate=pl.CostEstimate(flops=4000000, bytes_accessed=800000, transcendentals=0),
        name="taps",
        compiler_params=pltpu.CompilerParams(vmem_limit_bytes=GRANT),
    )(*small, near(block))
    tile = (dates, parts, tile_lines, tile_columns)
    if chips:
        out_shape = (pltpu.VMEM(tile, jnp.bfloat16),) * CHIPS
    else:
        out_shape = (pltpu.VMEM((owners,) + tile, jnp.bfloat16),)
    tiles = pl.pallas_call(
        functools.partial(
            resample_kernel, (line_groups, column_groups, tile_lines, tile_columns)
        ),
        out_shape=out_shape,
        in_specs=[VMEM] * 6,
        out_specs=(VMEM,) * len(out_shape),
        scratch_shapes=[pltpu.VMEM((2, lines, images * MARGIN), jnp.bfloat16)],
        name="resample",
        compiler_params=pltpu.CompilerParams(vmem_limit_bytes=GRANT),
    )(*[near(array) for array in (inner, even, odd, low_taps, high_taps, line_taps)])

    rows, cols = lines // LOOK_AZ, columns // LOOK_RG
    out_shape = (
        jax.ShapeDtypeStruct((dates, 2 * KINDS, rows, cols), jnp.float32),
        jax.ShapeDtypeStruct((dates, KINDS, rows, cols), jnp.float32),
    )
    if chips:

        def swapped(array, bits):
            pairs = [(i, i ^ bits) for i in range(owners) if i < i ^ bits]
            return exchanged(array, "date", pairs)

        order = [3, 2, 1]
        own = tiles[0]
        direct = {number: swapped(tiles[number], CORES * number) for number in order}
        other = swapped(own, 1)
        passed = {number: swapped(direct[number], 1) for number in order}
        held, positions = [own, other], [0, 1]
        for number in order:
            held += [direct[number], passed[number]]
            positions += [CORES * number, CORES * number + 1]
        results = pl.pallas_call(
            functools.partial(chip_looks_kernel, positions),
            out_shape=(pltpu.VMEM((CHANNELS * CHIP_LOOKS, LANES), jnp.float32),) * CHIPS,
            in_specs=[SMEM] * 2 + [VMEM] * len(held),
            out_specs=(VMEM,) * CHIPS,
            scratch_shapes=[
                pltpu.VMEM((total, parts, tile_lines, tile_columns), jnp.float32),
                pltpu.VMEM((CHIPS * QUANTITIES * CHIP_LOOKS, dates * columns), jnp.float32),
                pltpu.VMEM((CHIPS * QUANTITIES * CHIP_LOOKS, LANES), jnp.float32),
            ],
            name="looks",
            compiler_params=pltpu.CompilerParams(vmem_limit_bytes=GRANT),
        )(master_epoch_image, gap, *[near(tile) for tile in held])
        back = {number: swapped(results[number], CORES * number) for number in order}
        last = [1, 3, 2]
        pieces = [results[0]] + [back[number] for number in last]
        return pl.pallas_call(
            functools.partial(chip_place_kernel, [0] + last),
            out_shape=out_shape,
            in_specs=[VMEM] * CHIPS,
            out_specs=(VMEM, VMEM),
            name="place",
            compiler_params=pltpu.CompilerParams(vmem_limit_bytes=GRANT),
        )(*[near(piece) for piece in pieces])

    tiles = lax.all_to_all(tiles[0], "date", 0, 0)
    results = pl.pallas_call(
        looks_kernel,
        out_shape=pltpu.VMEM((owners, dates * CHANNELS, lanes), jnp.float32),
        in_specs=[SMEM] * 2 + [VMEM],
        out_specs=VMEM,
        scratch_shapes=[
            pltpu.VMEM((total, parts, tile_lines, tile_columns), jnp.float32),
            pltpu.VMEM((total * QUANTITIES, line_looks * tile_columns), jnp.float32),
            pltpu.VMEM((total * QUANTITIES, lanes), jnp.float32),
            pltpu.VMEM((KINDS, total, lanes), jnp.float32),
        ],
        name="looks",
        compiler_params=pltpu.CompilerParams(vmem_limit_bytes=GRANT),
    )(master_epoch_image, gap, near(tiles))
    results = lax.all_to_all(results, "date", 0, 0)

    if column_groups == 1:
        return pl.pallas_call(
            place_kernel,
            out_shape=out_shape,
            in_specs=[VMEM],
            out_specs=(VMEM, VMEM),
            name="place",
            compiler_params=pltpu.CompilerParams(vmem_limit_bytes=GRANT),
        )(near(results))
    whole = results.reshape(
        line_groups, column_groups, dates, CHANNELS, line_looks, column_looks
    )
    whole = jnp.transpose(whole, (2, 3, 0, 4, 1, 5)).reshape(dates, CHANNELS, rows, cols)
    return (whole[:, : 2 * KINDS], whole[:, 2 * KINDS :])


def solution(mesh):
    in_specs = (P("date", None, None, "range"), P(), P(), P(), P(), P(), P(), P())
    out_specs = (P("date", None, None, "range"), P("date", None, None, "range"))
    return jax.shard_map(body, mesh=mesh, in_specs=in_specs, out_specs=out_specs, check_vma=False)
```

```python
import functools

import jax
import jax.numpy as jnp
from jax import lax
from jax.experimental import pallas as pl
from jax.experimental.pallas import tpu as pltpu
from jax.sharding import PartitionSpec as P

MAX_SWEEPS = 4
TAPS = 8
FRACTIONS = 16
MARGIN = 16
LOOK_AZ = 16
LOOK_RG = 4
QUANTITIES = 8
KINDS = 3
CHANNELS = 9
LANES = 128
GRANT = 24 * 2**20
CORES = 2
CHIPS = 4
CHIP_LOOKS = 4

SMEM = pl.BlockSpec(memory_space=pltpu.SMEM)
VMEM = pl.BlockSpec(memory_space=pltpu.VMEM)


def exchanged(array, axis, pairs):
    return lax.ppermute(array, axis, [route for a, b in pairs for route in ((a, b), (b, a))])


def near(array):
    return pltpu.with_memory_space_constraint(array, pltpu.VMEM)


def iotas(rows, cols):
    return (
        lax.broadcasted_iota(jnp.int32, (rows, cols), 0),
        lax.broadcasted_iota(jnp.int32, (rows, cols), 1),
    )


def weight_rows(fractions):
    row, lane = iotas(8, LANES)
    spot = jnp.zeros((8, LANES), jnp.float32)
    for number, fraction in enumerate(fractions):
        spot = jnp.where(row == number, fraction.astype(jnp.float32), spot)
    spacing = (lane - 1 - (TAPS // 2 - 1)).astype(jnp.float32) - spot / FRACTIONS
    angle = jnp.pi * spacing
    sinc = jnp.where(spacing == 0.0, 1.0, jnp.sin(angle) / jnp.where(spacing == 0.0, 1.0, angle))
    weights = sinc * jnp.cos(angle / (TAPS + 1)) ** 2
    weights = jnp.where((lane >= 1) & (lane <= TAPS), weights, 0.0)
    weights = weights / jnp.sum(weights, axis=1, keepdims=True)
    return weights.astype(jnp.bfloat16).astype(jnp.float32)


def by_chips(block, owners):
    dates, parts, lines, columns = block.shape
    return (
        owners == CHIPS * CORES
        and (dates, parts) == (2, 2)
        and lines == CHIPS * CHIP_LOOKS * LOOK_AZ
        and columns == 2 * LANES
    )


def tile_order(position, chips):
    return position ^ (lax.axis_index("date") // CORES) if chips else position


def banded(offsets, weights):
    rows, cols = offsets.shape
    lanes = jnp.broadcast_to(weights, (rows, LANES))
    spots = jnp.clip(offsets + 1, 0, TAPS + 1)
    return jnp.concatenate(
        [
            jnp.take_along_axis(lanes, spots[:, start : start + LANES], axis=1)
            for start in range(0, cols, LANES)
        ],
        axis=1,
    )


def start_kernel(x_ref, *refs):
    dates, parts, lines, columns = x_ref.shape
    images = [(slot, part) for slot in range(dates) for part in range(parts)]
    count = (len(refs) - 4) // 2
    near_ref, even_ref, odd_ref = refs[count : count + 3]
    sems = refs[-1]
    small = list(zip(refs[:count], refs[count + 3 : -1]))
    whole = [(x_ref.at[image], near_ref.at[image]) for image in images]
    copies = [
        pltpu.make_async_copy(source, target, sems.at[number])
        for number, (source, target) in enumerate(whole + small)
    ]
    for copy in copies:
        copy.start()
    forward = lax.axis_index("range") % 2 == 0
    for number, (slot, part) in enumerate(images):
        copies[number].wait()
        for parity, last_ref, first_ref in (
            (forward, even_ref, odd_ref),
            (jnp.logical_not(forward), odd_ref, even_ref),
        ):

            @pl.when(parity)
            def _():
                for half in range(2):
                    rows = slice(half * (lines // 2), (half + 1) * (lines // 2))
                    start = (half * len(images) + number) * MARGIN
                    spot = slice(start, start + MARGIN)
                    last_ref[:, spot] = near_ref[slot, part, rows, columns - MARGIN :]
                    first_ref[:, spot] = near_ref[slot, part, rows, :MARGIN]

    for copy in copies[len(images) :]:
        copy.wait()


def pool_matrix(columns, lanes):
    row, col = iotas(columns, lanes)
    return jnp.where(row // LOOK_RG == col, 1.0, 0.0).astype(jnp.bfloat16)


def taps_kernel(
    chips,
    tile_lines,
    az_whole,
    az_part,
    rg_whole,
    rg_part,
    sweeps,
    x_ref,
    inner_ref,
    low_ref,
    high_ref,
    line_ref,
    pool_ref,
):
    dates, parts, lines, columns = x_ref.shape
    pool_ref[...] = pool_matrix(*pool_ref.shape)
    edge_rows = low_ref.shape[0]
    centre = TAPS // 2 - 1
    present = [lax.axis_index("date") * dates + slot for slot in range(dates)]
    table = weight_rows([rg_part[d] for d in present] + [az_part[d] for d in present])
    for slot, date in enumerate(present):
        shift = centre - rg_whole[date]
        weights = table[slot : slot + 1]
        row, col = iotas(columns, columns)
        own = banded(row - col + shift, weights).astype(jnp.bfloat16)
        for part in range(parts):
            inner_ref[slot, part] = jnp.dot(
                x_ref[slot, part], own, preferred_element_type=jnp.float32
            )
        row, col = iotas(edge_rows, LANES)
        low = banded(row % MARGIN - MARGIN - col + shift, weights)
        high = banded(row % MARGIN + LANES - col + shift, weights)
        for part in range(parts):
            image = slot * parts + part
            held = row // MARGIN == image
            spot = slice(image * LANES, (image + 1) * LANES)
            low_ref[:, spot] = jnp.where(held, low, 0.0).astype(jnp.bfloat16)
            high_ref[:, spot] = jnp.where(held, high, 0.0).astype(jnp.bfloat16)
        row, col = iotas(lines, lines)
        row = tile_order(row // tile_lines, chips) * tile_lines + row % tile_lines
        weights = table[dates + slot : dates + slot + 1]
        band = banded(col - row + (centre - az_whole[date]), weights)
        usable = row < sweeps[date] * (lines // MAX_SWEEPS)
        line_ref[slot] = jnp.where(usable, band, 0.0).astype(jnp.bfloat16)


def resample_kernel(split, inner_ref, even_ref, odd_ref, low_ref, high_ref, line_ref, *refs):
    *outs, edges = refs
    dates, parts, _, columns = inner_ref.shape
    line_groups, column_groups, tile_lines, tile_columns = split
    backward = lax.axis_index("range") % 2
    height, width = even_ref.shape
    for half in range(2):
        rows = slice(half * height, (half + 1) * height)
        spot = slice(half * (width // 2), (half + 1) * (width // 2))
        edges[1 - backward, rows, :] = even_ref[:, spot]
        edges[backward, rows, :] = odd_ref[:, spot]
    low = jnp.dot(edges[0], low_ref[...], preferred_element_type=jnp.float32)
    high = jnp.dot(edges[1], high_ref[...], preferred_element_type=jnp.float32)
    for slot in range(dates):
        for part in range(parts):
            spot = slice((slot * parts + part) * LANES, (slot * parts + part + 1) * LANES)
            pieces = [
                inner_ref[slot, part, :, start : start + LANES]
                for start in range(0, columns, LANES)
            ]
            pieces[0] += low[:, spot]
            pieces[-1] += high[:, spot]
            ranged = jnp.concatenate(pieces, axis=1)
            moved = jnp.dot(
                line_ref[slot], ranged.astype(jnp.bfloat16), preferred_element_type=jnp.float32
            ).astype(jnp.bfloat16)
            for i in range(line_groups):
                for j in range(column_groups):
                    tile = moved[
                        i * tile_lines : (i + 1) * tile_lines,
                        j * tile_columns : (j + 1) * tile_columns,
                    ]
                    if len(outs) == 1:
                        outs[0][i * column_groups + j, slot, part] = tile
                    else:
                        outs[i][slot, part] = tile


def partners(date, gap_ref, total):
    ahead = date + gap_ref[0, date]
    later = jnp.where(ahead < total, ahead, date - gap_ref[0, date])
    back = date - gap_ref[1, date]
    earlier = jnp.where(back >= 0, back, date + gap_ref[1, date])
    return (later, earlier)


def row_sums(values):
    row = lax.broadcasted_iota(jnp.int32, values[0].shape, 0)
    order = (3, 2, 1, 0, 7, 6, 5, 4)
    values = [values[number] for number in order]
    upper = row < 4
    values = [
        jnp.where(upper, a, b) + pltpu.roll(jnp.where(upper, b, a), 4, 0)
        for a, b in zip(values[:4], values[4:])
    ]
    for step, kept in ((2, row % 4 >= 2), (1, row % 2 == 1)):
        values = [
            jnp.where(kept, a + pltpu.roll(a, step, 0), b + pltpu.roll(b, 8 - step, 0))
            for a, b in zip(values[:step], values[step:])
        ]
    return values[0]


def pool_columns(sums, pool):
    coarse = sums.astype(jnp.bfloat16)
    fine = (sums - coarse.astype(jnp.float32)).astype(jnp.bfloat16)
    return jnp.dot(coarse, pool, preferred_element_type=jnp.float32) + jnp.dot(
        fine, pool, preferred_element_type=jnp.float32
    )


def looks_kernel(root_ref, gap_ref, tiles_ref, out_ref, stack, sums, pooled, powers):
    total, _, tile_lines, tile_columns = stack.shape
    owners, per_owner, lanes = out_ref.shape
    dates = per_owner // CHANNELS
    line_looks = tile_lines // LOOK_AZ
    unroll = total if total <= 16 else 1

    def widen(owner, carry):
        stack[pl.ds(owner * dates, dates)] = tiles_ref[owner].astype(jnp.float32)
        return carry

    lax.fori_loop(0, owners, widen, 0)

    def partner_of(kind, date):
        return partners(date, gap_ref, total)[kind - 1] if kind else root_ref[0]

    def collect(date, carry):
        left0, left1 = stack[date, 0], stack[date, 1]
        values = []
        for kind in range(KINDS):
            partner = partner_of(kind, date)
            right0, right1 = stack[partner, 0], stack[partner, 1]
            values += [left0 * right0 + left1 * right1, left1 * right0 - left0 * right1]
        values.append(left0 * left0 + left1 * left1)
        values.append(jnp.zeros_like(left0))
        rows = pl.ds(pl.multiple_of(date * QUANTITIES, QUANTITIES), QUANTITIES)
        for look in range(line_looks):
            start = look * LOOK_AZ
            sums[rows, look * tile_columns : (look + 1) * tile_columns] = row_sums(
                [value[start : start + 8] + value[start + 8 : start + 16] for value in values]
            )
        return carry

    lax.fori_loop(0, total, collect, 0, unroll=unroll)
    pooled[...] = pool_columns(sums[...], pool_matrix(sums.shape[1], lanes))

    def gather(date, carry):
        for kind in range(KINDS):
            power = partner_of(kind, date) * QUANTITIES + 2 * KINDS
            powers[kind, pl.ds(date, 1), :] = pooled[pl.ds(power, 1), :]
        return carry

    lax.fori_loop(0, total, gather, 0, unroll=unroll)
    scale = 1.0 / (LOOK_AZ * LOOK_RG) ** 0.5

    for slot in range(dates):

        def every(number):
            return pooled[pl.ds(slot * QUANTITIES + number, owners, stride=dates * QUANTITIES), :]

        power_left = every(2 * KINDS)
        for kind in range(KINDS):
            real, imag = every(2 * kind), every(2 * kind + 1)
            power_right = powers[kind, pl.ds(slot, owners, stride=dates), :]
            out_ref[:, slot * CHANNELS + 2 * kind, :] = real * scale
            out_ref[:, slot * CHANNELS + 2 * kind + 1, :] = imag * scale
            out_ref[:, slot * CHANNELS + 2 * KINDS + kind, :] = jnp.sqrt(
                real * real + imag * imag
            ) / jnp.sqrt(power_left * power_right + 1e-06)


def chip_looks_kernel(positions, root_ref, gap_ref, pool_ref, *refs):
    tiles, outs, (stack, sums, pooled) = refs[: CHIPS * CORES], refs[CHIPS * CORES : -3], refs[-3:]
    dates, _, _, columns = tiles[0].shape
    me = lax.axis_index("date")
    total = len(tiles) * dates
    scale = 1.0 / (LOOK_AZ * LOOK_RG) ** 0.5
    for position, tile_ref in zip(positions, tiles):
        stack[position * dates : (position + 1) * dates] = tile_ref[...].astype(jnp.float32)

    def partner_of(kind, date):
        partner = partners(date, gap_ref, total)[kind - 1] if kind else root_ref[0]
        return lax.div(partner, dates) ^ me, lax.rem(partner, dates)

    def part(spot, number, look):
        return stack[spot, number, look * LOOK_AZ : (look + 1) * LOOK_AZ, :]

    def folded(value):
        return value[: LOOK_AZ // 2] + value[LOOK_AZ // 2 :]

    block = QUANTITIES * CHIP_LOOKS
    for chip in range(CHIPS):
        for slot in range(dates):
            own = CORES * chip * dates + slot
            others = []
            for kind in range(KINDS):
                position, number = partner_of(kind, (me ^ (CORES * chip)) * dates + slot)
                others.append(position * dates + number)
            for look in range(CHIP_LOOKS):
                left0, left1 = part(own, 0, look), part(own, 1, look)
                values = []
                for other in others:
                    right0, right1 = part(other, 0, look), part(other, 1, look)
                    values.append(folded(left0 * right0 + left1 * right1))
                    values.append(folded(left1 * right0 - left0 * right1))
                values.append(folded(left0 * left0 + left1 * left1))
                right0, right1 = part(own + dates, 0, look), part(own + dates, 1, look)
                values.append(folded(right0 * right0 + right1 * right1))
                start = chip * block + look * QUANTITIES
                sums[start : start + QUANTITIES, slot * columns : (slot + 1) * columns] = (
                    row_sums(values)
                )
        rows = slice(chip * block, (chip + 1) * block)
        pooled[rows] = pool_columns(sums[rows], pool_ref[...])

    def every_look(start):
        return pooled[pl.ds(start, CHIP_LOOKS, stride=QUANTITIES), :]

    first = lax.broadcasted_iota(jnp.int32, (CHIP_LOOKS, LANES), 1) < LANES // 2
    for chip in range(CHIPS):
        base = chip * block
        power_left = every_look(base + 2 * KINDS)
        for kind in range(KINDS):
            halves = []
            for slot in range(dates):
                position, number = partner_of(kind, (me ^ (CORES * chip)) * dates + slot)
                start = lax.div(position, CORES) * block + 2 * KINDS + lax.rem(position, CORES)
                halves.append(pltpu.roll(every_look(start), LANES // 2 * (number ^ slot), 1))
            power = power_left * jnp.where(first, halves[0], halves[1])
            real, imag = every_look(base + 2 * kind), every_look(base + 2 * kind + 1)
            for channel, value in (
                (2 * kind, real * scale),
                (2 * kind + 1, imag * scale),
                (2 * KINDS + kind, jnp.sqrt(real * real + imag * imag) / jnp.sqrt(power + 1e-06)),
            ):
                outs[chip][channel * CHIP_LOOKS : (channel + 1) * CHIP_LOOKS, :] = value


def chip_place_kernel(positions, *refs):
    pieces, (ifg_ref, coh_ref) = refs[:CHIPS], refs[CHIPS:]
    dates, _, _, columns = ifg_ref.shape
    mine = lax.axis_index("date") // CORES
    for chip in range(CHIPS):

        @pl.when(mine == chip)
        def _():
            for position, piece_ref in zip(positions, pieces):
                start = (chip ^ position) * CHIP_LOOKS
                where = slice(start, start + CHIP_LOOKS)
                for channel in range(CHANNELS):
                    rows = piece_ref[channel * CHIP_LOOKS : (channel + 1) * CHIP_LOOKS, :]
                    for slot in range(dates):
                        part = rows[:, slot * columns : (slot + 1) * columns]
                        if channel < 2 * KINDS:
                            ifg_ref[slot, channel, where, :] = part
                        else:
                            coh_ref[slot, channel - 2 * KINDS, where, :] = part


def place_kernel(x_ref, ifg_ref, coh_ref):
    sources, rows, lanes = x_ref.shape
    dates, _, lines, columns = ifg_ref.shape
    looks = lanes // columns
    for slot in range(dates):
        for channel in range(CHANNELS):
            values = x_ref[:, slot * CHANNELS + channel, :]
            for look in range(looks):
                part = values[:, look * columns : (look + 1) * columns]
                where = pl.ds(look, sources, stride=looks)
                if channel < 2 * KINDS:
                    ifg_ref[slot, channel, where, :] = part
                else:
                    coh_ref[slot, channel - 2 * KINDS, where, :] = part


def body(
    epoch_tiles_quadrature,
    along_track_whole_displacement,
    along_track_subpixel_weights,
    slant_whole_displacement,
    slant_subpixel_weights,
    sweeps_each_epoch,
    baseline_companion_gap,
    master_epoch_image,
):
    block = epoch_tiles_quadrature
    dates, parts, lines, columns = block.shape
    owners = lax.axis_size("date")
    total = owners * dates
    images = dates * parts
    chips = by_chips(block, owners)
    line_groups = CHIPS if chips else min(owners, lines // LOOK_AZ)
    column_groups = 1 if chips else owners // line_groups
    tile_lines, tile_columns = lines // line_groups, columns // column_groups
    line_looks, column_looks = tile_lines // LOOK_AZ, tile_columns // LOOK_RG
    lanes = line_looks * column_looks

    arguments = (
        block,
        along_track_whole_displacement,
        along_track_subpixel_weights,
        slant_whole_displacement,
        slant_subpixel_weights,
        sweeps_each_epoch,
        baseline_companion_gap.T,
    )
    block, even, odd, *small = pl.pallas_call(
        start_kernel,
        out_shape=(
            pltpu.VMEM(block.shape, block.dtype),
            pltpu.VMEM((lines // 2, 2 * images * MARGIN), jnp.bfloat16),
            pltpu.VMEM((lines // 2, 2 * images * MARGIN), jnp.bfloat16),
            *[pltpu.SMEM(array.shape, array.dtype) for array in arguments[1:]],
        ),
        in_specs=[pl.BlockSpec(memory_space=pltpu.HBM)] * len(arguments),
        out_specs=(VMEM,) * 3 + (SMEM,) * (len(arguments) - 1),
        scratch_shapes=[pltpu.SemaphoreType.DMA((images + len(arguments) - 1,))],
        name="start",
        compiler_params=pltpu.CompilerParams(vmem_limit_bytes=GRANT),
    )(*[pltpu.with_memory_space_constraint(array, pltpu.HBM) for array in arguments])
    *small, gap = [pltpu.with_memory_space_constraint(array, pltpu.SMEM) for array in small]
    width = lax.axis_size("range")
    odd = exchanged(odd, "range", [(j, j + 1) for j in range(1, width - 1, 2)])
    even = exchanged(even, "range", [(j, j + 1) for j in range(0, width - 1, 2)])

    inner, low_taps, high_taps, line_taps, pool = pl.pallas_call(
        functools.partial(taps_kernel, chips, tile_lines),
        out_shape=(
            pltpu.VMEM(block.shape, jnp.float32),
            pltpu.VMEM((images * MARGIN, images * LANES), jnp.bfloat16),
            pltpu.VMEM((images * MARGIN, images * LANES), jnp.bfloat16),
            pltpu.VMEM((dates, lines, lines), jnp.bfloat16),
            pltpu.VMEM((dates * columns, LANES), jnp.bfloat16),
        ),
        in_specs=[SMEM] * len(small) + [VMEM],
        out_specs=(VMEM,) * 5,
        cost_estimate=pl.CostEstimate(flops=4000000, bytes_accessed=800000, transcendentals=0),
        name="taps",
        compiler_params=pltpu.CompilerParams(vmem_limit_bytes=GRANT),
    )(*small, near(block))
    tile = (dates, parts, tile_lines, tile_columns)
    if chips:
        out_shape = (pltpu.VMEM(tile, jnp.bfloat16),) * CHIPS
    else:
        out_shape = (pltpu.VMEM((owners,) + tile, jnp.bfloat16),)
    tiles = pl.pallas_call(
        functools.partial(
            resample_kernel, (line_groups, column_groups, tile_lines, tile_columns)
        ),
        out_shape=out_shape,
        in_specs=[VMEM] * 6,
        out_specs=(VMEM,) * len(out_shape),
        scratch_shapes=[pltpu.VMEM((2, lines, images * MARGIN), jnp.bfloat16)],
        name="resample",
        compiler_params=pltpu.CompilerParams(vmem_limit_bytes=GRANT),
    )(*[near(array) for array in (inner, even, odd, low_taps, high_taps, line_taps)])

    rows, cols = lines // LOOK_AZ, columns // LOOK_RG
    out_shape = (
        jax.ShapeDtypeStruct((dates, 2 * KINDS, rows, cols), jnp.float32),
        jax.ShapeDtypeStruct((dates, KINDS, rows, cols), jnp.float32),
    )
    if chips:

        def swapped(array, bits):
            pairs = [(i, i ^ bits) for i in range(owners) if i < i ^ bits]
            return exchanged(array, "date", pairs)

        order = [3, 2, 1]
        own = tiles[0]
        direct = {number: swapped(tiles[number], CORES * number) for number in order}
        other = swapped(own, 1)
        passed = {number: swapped(direct[number], 1) for number in order}
        held, positions = [own, other], [0, 1]
        for number in order:
            held += [direct[number], passed[number]]
            positions += [CORES * number, CORES * number + 1]
        results = pl.pallas_call(
            functools.partial(chip_looks_kernel, positions),
            out_shape=(pltpu.VMEM((CHANNELS * CHIP_LOOKS, LANES), jnp.float32),) * CHIPS,
            in_specs=[SMEM] * 2 + [VMEM] * (1 + len(held)),
            out_specs=(VMEM,) * CHIPS,
            scratch_shapes=[
                pltpu.VMEM((total, parts, tile_lines, tile_columns), jnp.float32),
                pltpu.VMEM((CHIPS * QUANTITIES * CHIP_LOOKS, dates * columns), jnp.float32),
                pltpu.VMEM((CHIPS * QUANTITIES * CHIP_LOOKS, LANES), jnp.float32),
            ],
            name="looks",
            compiler_params=pltpu.CompilerParams(vmem_limit_bytes=GRANT),
        )(master_epoch_image, gap, near(pool), *[near(tile) for tile in held])
        back = {number: swapped(results[number], CORES * number) for number in order}
        last = [1, 3, 2]
        pieces = [results[0]] + [back[number] for number in last]
        return pl.pallas_call(
            functools.partial(chip_place_kernel, [0] + last),
            out_shape=out_shape,
            in_specs=[VMEM] * CHIPS,
            out_specs=(VMEM, VMEM),
            name="place",
            compiler_params=pltpu.CompilerParams(vmem_limit_bytes=GRANT),
        )(*[near(piece) for piece in pieces])

    tiles = lax.all_to_all(tiles[0], "date", 0, 0)
    results = pl.pallas_call(
        looks_kernel,
        out_shape=pltpu.VMEM((owners, dates * CHANNELS, lanes), jnp.float32),
        in_specs=[SMEM] * 2 + [VMEM],
        out_specs=VMEM,
        scratch_shapes=[
            pltpu.VMEM((total, parts, tile_lines, tile_columns), jnp.float32),
            pltpu.VMEM((total * QUANTITIES, line_looks * tile_columns), jnp.float32),
            pltpu.VMEM((total * QUANTITIES, lanes), jnp.float32),
            pltpu.VMEM((KINDS, total, lanes), jnp.float32),
        ],
        name="looks",
        compiler_params=pltpu.CompilerParams(vmem_limit_bytes=GRANT),
    )(master_epoch_image, gap, near(tiles))
    results = lax.all_to_all(results, "date", 0, 0)

    if column_groups == 1:
        return pl.pallas_call(
            place_kernel,
            out_shape=out_shape,
            in_specs=[VMEM],
            out_specs=(VMEM, VMEM),
            name="place",
            compiler_params=pltpu.CompilerParams(vmem_limit_bytes=GRANT),
        )(near(results))
    whole = results.reshape(
        line_groups, column_groups, dates, CHANNELS, line_looks, column_looks
    )
    whole = jnp.transpose(whole, (2, 3, 0, 4, 1, 5)).reshape(dates, CHANNELS, rows, cols)
    return (whole[:, : 2 * KINDS], whole[:, 2 * KINDS :])


def solution(mesh):
    in_specs = (P("date", None, None, "range"), P(), P(), P(), P(), P(), P(), P())
    out_specs = (P("date", None, None, "range"), P("date", None, None, "range"))
    return jax.shard_map(body, mesh=mesh, in_specs=in_specs, out_specs=out_specs, check_vma=False)
```

```python
import functools

import jax
import jax.numpy as jnp
from jax import lax
from jax.experimental import pallas as pl
from jax.experimental.pallas import tpu as pltpu
from jax.sharding import PartitionSpec as P

MAX_SWEEPS = 4
TAPS = 8
FRACTIONS = 16
MARGIN = 16
LOOK_AZ = 16
LOOK_RG = 4
QUANTITIES = 8
KINDS = 3
CHANNELS = 9
LANES = 128
GRANT = 24 * 2**20
CORES = 2
CHIPS = 4
CHIP_LOOKS = 4

SMEM = pl.BlockSpec(memory_space=pltpu.SMEM)
VMEM = pl.BlockSpec(memory_space=pltpu.VMEM)


def exchanged(array, axis, pairs):
    return lax.ppermute(array, axis, [route for a, b in pairs for route in ((a, b), (b, a))])


def near(array):
    return pltpu.with_memory_space_constraint(array, pltpu.VMEM)


def iotas(rows, cols):
    return (
        lax.broadcasted_iota(jnp.int32, (rows, cols), 0),
        lax.broadcasted_iota(jnp.int32, (rows, cols), 1),
    )


def weight_rows(fractions):
    row, lane = iotas(8, LANES)
    spot = jnp.zeros((8, LANES), jnp.float32)
    for number, fraction in enumerate(fractions):
        spot = jnp.where(row == number, fraction.astype(jnp.float32), spot)
    spacing = (lane - 1 - (TAPS // 2 - 1)).astype(jnp.float32) - spot / FRACTIONS
    angle = jnp.pi * spacing
    sinc = jnp.where(spacing == 0.0, 1.0, jnp.sin(angle) / jnp.where(spacing == 0.0, 1.0, angle))
    weights = sinc * jnp.cos(angle / (TAPS + 1)) ** 2
    weights = jnp.where((lane >= 1) & (lane <= TAPS), weights, 0.0)
    weights = weights / jnp.sum(weights, axis=1, keepdims=True)
    return weights.astype(jnp.bfloat16).astype(jnp.float32)


def by_chips(block, owners):
    dates, parts, lines, columns = block.shape
    return (
        owners == CHIPS * CORES
        and (dates, parts) == (2, 2)
        and lines == CHIPS * CHIP_LOOKS * LOOK_AZ
        and columns == 2 * LANES
    )


def tile_order(position):
    return position ^ (lax.axis_index("date") // CORES)


def banded(offsets, weights):
    rows, cols = offsets.shape
    lanes = jnp.broadcast_to(weights, (rows, LANES))
    spots = jnp.clip(offsets + 1, 0, TAPS + 1)
    return jnp.concatenate(
        [
            jnp.take_along_axis(lanes, spots[:, start : start + LANES], axis=1)
            for start in range(0, cols, LANES)
        ],
        axis=1,
    )


def start_kernel(x_ref, *refs):
    dates, parts, lines, columns = x_ref.shape
    images = [(slot, part) for slot in range(dates) for part in range(parts)]
    count = (len(refs) - 4) // 2
    near_ref, even_ref, odd_ref = refs[count : count + 3]
    sems = refs[-1]
    small = list(zip(refs[:count], refs[count + 3 : -1]))
    whole = [(x_ref.at[image], near_ref.at[image]) for image in images]
    copies = [
        pltpu.make_async_copy(source, target, sems.at[number])
        for number, (source, target) in enumerate(whole + small)
    ]
    for copy in copies:
        copy.start()
    forward = lax.axis_index("range") % 2 == 0
    for number, (slot, part) in enumerate(images):
        copies[number].wait()
        for parity, last_ref, first_ref in (
            (forward, even_ref, odd_ref),
            (jnp.logical_not(forward), odd_ref, even_ref),
        ):

            @pl.when(parity)
            def _():
                for half in range(2):
                    rows = slice(half * (lines // 2), (half + 1) * (lines // 2))
                    start = (half * len(images) + number) * MARGIN
                    spot = slice(start, start + MARGIN)
                    last_ref[:, spot] = near_ref[slot, part, rows, columns - MARGIN :]
                    first_ref[:, spot] = near_ref[slot, part, rows, :MARGIN]

    for copy in copies[len(images) :]:
        copy.wait()


def pool_matrix(columns, lanes):
    row, col = iotas(columns, lanes)
    return jnp.where(row // LOOK_RG == col, 1.0, 0.0).astype(jnp.bfloat16)


def taps_kernel(
    az_whole,
    az_part,
    rg_whole,
    rg_part,
    sweeps,
    x_ref,
    inner_ref,
    low_ref,
    high_ref,
    line_ref,
):
    dates, parts, lines, columns = x_ref.shape
    edge_rows = low_ref.shape[0]
    centre = TAPS // 2 - 1
    present = [lax.axis_index("date") * dates + slot for slot in range(dates)]
    table = weight_rows([rg_part[d] for d in present] + [az_part[d] for d in present])
    for slot, date in enumerate(present):
        shift = centre - rg_whole[date]
        weights = table[slot : slot + 1]
        row, col = iotas(columns, columns)
        own = banded(row - col + shift, weights).astype(jnp.bfloat16)
        for part in range(parts):
            inner_ref[slot, part] = jnp.dot(
                x_ref[slot, part], own, preferred_element_type=jnp.float32
            )
        row, col = iotas(edge_rows, LANES)
        low = banded(row % MARGIN - MARGIN - col + shift, weights)
        high = banded(row % MARGIN + LANES - col + shift, weights)
        for part in range(parts):
            image = slot * parts + part
            held = row // MARGIN == image
            spot = slice(image * LANES, (image + 1) * LANES)
            low_ref[:, spot] = jnp.where(held, low, 0.0).astype(jnp.bfloat16)
            high_ref[:, spot] = jnp.where(held, high, 0.0).astype(jnp.bfloat16)
        row, col = iotas(lines, lines)
        weights = table[dates + slot : dates + slot + 1]
        band = banded(col - row + (centre - az_whole[date]), weights)
        usable = row < sweeps[date] * (lines // MAX_SWEEPS)
        line_ref[slot] = jnp.where(usable, band, 0.0).astype(jnp.bfloat16)


def main_kernel(
    az_whole,
    az_part,
    rg_whole,
    rg_part,
    sweeps,
    x_ref,
    line_ref,
    inner_ref,
    low_ref,
    high_ref,
    pool_ref,
    *outs,
):
    dates, parts, lines, columns = x_ref.shape
    edge_rows = low_ref.shape[0]
    tile_lines = lines // len(outs)
    centre = TAPS // 2 - 1
    pool_ref[...] = pool_matrix(*pool_ref.shape)
    present = [lax.axis_index("date") * dates + slot for slot in range(dates)]
    table = weight_rows([rg_part[d] for d in present] + [az_part[d] for d in present])
    lows, highs = [], []
    for slot, date in enumerate(present):
        shift = centre - rg_whole[date]
        weights = table[slot : slot + 1]
        row, col = iotas(lines, lines)
        row = tile_order(row // tile_lines) * tile_lines + row % tile_lines
        band = banded(
            col - row + (centre - az_whole[date]), table[dates + slot : dates + slot + 1]
        )
        usable = row < sweeps[date] * (lines // MAX_SWEEPS)
        line = jnp.where(usable, band, 0.0).astype(jnp.bfloat16)
        line_ref[slot] = line
        row, col = iotas(columns, columns)
        own = banded(row - col + shift, weights).astype(jnp.bfloat16)
        for part in range(parts):
            inner = jnp.dot(x_ref[slot, part], own, preferred_element_type=jnp.float32)
            start = (slot * parts + part) * 2 * MARGIN
            inner_ref[:, start : start + MARGIN] = inner[:, :MARGIN]
            inner_ref[:, start + MARGIN : start + 2 * MARGIN] = inner[:, columns - MARGIN :]
            moved = jnp.dot(
                line, inner.astype(jnp.bfloat16), preferred_element_type=jnp.float32
            ).astype(jnp.bfloat16)
            for group, out_ref in enumerate(outs):
                out_ref[slot, part] = moved[group * tile_lines : (group + 1) * tile_lines]
        row, col = iotas(edge_rows, LANES)
        offset = row % MARGIN - col % MARGIN + shift
        lows.append(banded(offset - MARGIN, weights))
        highs.append(banded(offset + MARGIN, weights))
    row, col = iotas(edge_rows, LANES)
    same = row // MARGIN == col // (2 * MARGIN)
    upper = (col // MARGIN) % 2 == 1
    first = col < LANES // 2
    low = jnp.where(first, lows[0], lows[1])
    high = jnp.where(first, highs[0], highs[1])
    low_ref[...] = jnp.where(same & jnp.logical_not(upper), low, 0.0).astype(jnp.bfloat16)
    high_ref[...] = jnp.where(same & upper, high, 0.0).astype(jnp.bfloat16)


def spread_edges(even_ref, odd_ref, edges):
    backward = lax.axis_index("range") % 2
    height, width = even_ref.shape
    for half in range(2):
        rows = slice(half * height, (half + 1) * height)
        spot = slice(half * (width // 2), (half + 1) * (width // 2))
        edges[1 - backward, rows, :] = even_ref[:, spot]
        edges[backward, rows, :] = odd_ref[:, spot]


def patched(tile, border, image):
    start = image * 2 * MARGIN
    lane = lax.broadcasted_iota(jnp.int32, border.shape, 1)
    low = pltpu.roll(border, (LANES - start) % LANES, 1) if start else border
    high = pltpu.roll(border, (LANES - 2 * MARGIN - start) % LANES, 1)
    return (
        jnp.where(lane < MARGIN, low, tile[:, :LANES]),
        jnp.where(lane >= LANES - MARGIN, high, tile[:, LANES:]),
    )


def border_kernel(inner_ref, even_ref, odd_ref, low_ref, high_ref, line_ref, *refs):
    *refs, edges = refs
    tiles, wholes, outs = refs[: CHIPS // 2], refs[CHIPS // 2 : CHIPS], refs[CHIPS:]
    spread_edges(even_ref, odd_ref, edges)
    ranged = inner_ref[...]
    ranged += jnp.dot(edges[0], low_ref[...], preferred_element_type=jnp.float32)
    ranged += jnp.dot(edges[1], high_ref[...], preferred_element_type=jnp.float32)
    ranged = ranged.astype(jnp.bfloat16)
    moved = [
        jnp.dot(line_ref[slot], ranged, preferred_element_type=jnp.float32) for slot in range(2)
    ]
    lane = lax.broadcasted_iota(jnp.int32, moved[0].shape, 1)
    border = jnp.where(lane < LANES // 2, moved[0], moved[1])
    dates, parts, height, _ = wholes[0].shape
    for group, (tile_ref, whole_ref) in enumerate(zip(tiles, wholes)):
        own = border[group * height : (group + 1) * height]
        for slot in range(dates):
            for part in range(parts):
                tile = tile_ref[slot, part].astype(jnp.float32)
                low, high = patched(tile, own, slot * parts + part)
                whole_ref[slot, part, :, :LANES] = low.astype(jnp.bfloat16)
                whole_ref[slot, part, :, LANES:] = high.astype(jnp.bfloat16)
    for group, out_ref in enumerate(outs):
        start = (CHIPS // 2 + group) * height
        out_ref[...] = border[start : start + height].astype(jnp.bfloat16)


def bundle_kernel(*refs):
    *pieces, out_ref = refs
    for number, piece_ref in enumerate(pieces):
        out_ref[number] = piece_ref[...]


def resample_kernel(split, inner_ref, even_ref, odd_ref, low_ref, high_ref, line_ref, *refs):
    out_ref, edges = refs
    dates, parts, _, columns = inner_ref.shape
    line_groups, column_groups, tile_lines, tile_columns = split
    spread_edges(even_ref, odd_ref, edges)
    low = jnp.dot(edges[0], low_ref[...], preferred_element_type=jnp.float32)
    high = jnp.dot(edges[1], high_ref[...], preferred_element_type=jnp.float32)
    for slot in range(dates):
        for part in range(parts):
            spot = slice((slot * parts + part) * LANES, (slot * parts + part + 1) * LANES)
            pieces = [
                inner_ref[slot, part, :, start : start + LANES]
                for start in range(0, columns, LANES)
            ]
            pieces[0] += low[:, spot]
            pieces[-1] += high[:, spot]
            ranged = jnp.concatenate(pieces, axis=1)
            moved = jnp.dot(
                line_ref[slot], ranged.astype(jnp.bfloat16), preferred_element_type=jnp.float32
            ).astype(jnp.bfloat16)
            for i in range(line_groups):
                for j in range(column_groups):
                    tile = moved[
                        i * tile_lines : (i + 1) * tile_lines,
                        j * tile_columns : (j + 1) * tile_columns,
                    ]
                    out_ref[i * column_groups + j, slot, part] = tile


def partners(date, gap_ref, total):
    ahead = date + gap_ref[0, date]
    later = jnp.where(ahead < total, ahead, date - gap_ref[0, date])
    back = date - gap_ref[1, date]
    earlier = jnp.where(back >= 0, back, date + gap_ref[1, date])
    return (later, earlier)


def row_sums(values):
    row = lax.broadcasted_iota(jnp.int32, values[0].shape, 0)
    order = (3, 2, 1, 0, 7, 6, 5, 4)
    values = [values[number] for number in order]
    upper = row < 4
    values = [
        jnp.where(upper, a, b) + pltpu.roll(jnp.where(upper, b, a), 4, 0)
        for a, b in zip(values[:4], values[4:])
    ]
    for step, kept in ((2, row % 4 >= 2), (1, row % 2 == 1)):
        values = [
            jnp.where(kept, a + pltpu.roll(a, step, 0), b + pltpu.roll(b, 8 - step, 0))
            for a, b in zip(values[:step], values[step:])
        ]
    return values[0]


def pool_columns(sums, pool):
    coarse = sums.astype(jnp.bfloat16)
    fine = (sums - coarse.astype(jnp.float32)).astype(jnp.bfloat16)
    return jnp.dot(coarse, pool, preferred_element_type=jnp.float32) + jnp.dot(
        fine, pool, preferred_element_type=jnp.float32
    )


def looks_kernel(root_ref, gap_ref, tiles_ref, out_ref, stack, sums, pooled, powers):
    total, _, tile_lines, tile_columns = stack.shape
    owners, per_owner, lanes = out_ref.shape
    dates = per_owner // CHANNELS
    line_looks = tile_lines // LOOK_AZ
    unroll = total if total <= 16 else 1

    def widen(owner, carry):
        stack[pl.ds(owner * dates, dates)] = tiles_ref[owner].astype(jnp.float32)
        return carry

    lax.fori_loop(0, owners, widen, 0)

    def partner_of(kind, date):
        return partners(date, gap_ref, total)[kind - 1] if kind else root_ref[0]

    def collect(date, carry):
        left0, left1 = stack[date, 0], stack[date, 1]
        values = []
        for kind in range(KINDS):
            partner = partner_of(kind, date)
            right0, right1 = stack[partner, 0], stack[partner, 1]
            values += [left0 * right0 + left1 * right1, left1 * right0 - left0 * right1]
        values.append(left0 * left0 + left1 * left1)
        values.append(jnp.zeros_like(left0))
        rows = pl.ds(pl.multiple_of(date * QUANTITIES, QUANTITIES), QUANTITIES)
        for look in range(line_looks):
            start = look * LOOK_AZ
            sums[rows, look * tile_columns : (look + 1) * tile_columns] = row_sums(
                [value[start : start + 8] + value[start + 8 : start + 16] for value in values]
            )
        return carry

    lax.fori_loop(0, total, collect, 0, unroll=unroll)
    pooled[...] = pool_columns(sums[...], pool_matrix(sums.shape[1], lanes))

    def gather(date, carry):
        for kind in range(KINDS):
            power = partner_of(kind, date) * QUANTITIES + 2 * KINDS
            powers[kind, pl.ds(date, 1), :] = pooled[pl.ds(power, 1), :]
        return carry

    lax.fori_loop(0, total, gather, 0, unroll=unroll)
    scale = 1.0 / (LOOK_AZ * LOOK_RG) ** 0.5

    for slot in range(dates):

        def every(number):
            return pooled[pl.ds(slot * QUANTITIES + number, owners, stride=dates * QUANTITIES), :]

        power_left = every(2 * KINDS)
        for kind in range(KINDS):
            real, imag = every(2 * kind), every(2 * kind + 1)
            power_right = powers[kind, pl.ds(slot, owners, stride=dates), :]
            out_ref[:, slot * CHANNELS + 2 * kind, :] = real * scale
            out_ref[:, slot * CHANNELS + 2 * kind + 1, :] = imag * scale
            out_ref[:, slot * CHANNELS + 2 * KINDS + kind, :] = jnp.sqrt(
                real * real + imag * imag
            ) / jnp.sqrt(power_left * power_right + 1e-06)


def chip_looks_kernel(positions, root_ref, gap_ref, pool_ref, *refs):
    count = CHIPS * CORES
    tiles, refs = refs[:count], refs[count:]
    half = CHIPS // 2
    borders, (passed_ref, *outs), (stack, sums, pooled) = refs[:half], refs[half:-3], refs[-3:]
    dates, parts, _, columns = tiles[0].shape
    me = lax.axis_index("date")
    total = len(tiles) * dates
    scale = 1.0 / (LOOK_AZ * LOOK_RG) ** 0.5
    for position, tile_ref in zip(positions, tiles):
        chip = position // CORES - half
        if chip < 0:
            stack[position * dates : (position + 1) * dates] = tile_ref[...].astype(jnp.float32)
            continue
        border = (passed_ref[chip] if position % CORES else borders[chip][...]).astype(jnp.float32)
        for slot in range(dates):
            for number in range(parts):
                tile = tile_ref[slot, number].astype(jnp.float32)
                low, high = patched(tile, border, slot * parts + number)
                stack[position * dates + slot, number, :, :LANES] = low
                stack[position * dates + slot, number, :, LANES:] = high

    def partner_of(kind, date):
        partner = partners(date, gap_ref, total)[kind - 1] if kind else root_ref[0]
        return lax.div(partner, dates) ^ me, lax.rem(partner, dates)

    def part(spot, number, look):
        return stack[spot, number, look * LOOK_AZ : (look + 1) * LOOK_AZ, :]

    def folded(value):
        return value[: LOOK_AZ // 2] + value[LOOK_AZ // 2 :]

    block = QUANTITIES * CHIP_LOOKS
    for chip in range(CHIPS):
        for slot in range(dates):
            own = CORES * chip * dates + slot
            others = []
            for kind in range(KINDS):
                position, number = partner_of(kind, (me ^ (CORES * chip)) * dates + slot)
                others.append(position * dates + number)
            for look in range(CHIP_LOOKS):
                left0, left1 = part(own, 0, look), part(own, 1, look)
                values = []
                for other in others:
                    right0, right1 = part(other, 0, look), part(other, 1, look)
                    values.append(folded(left0 * right0 + left1 * right1))
                    values.append(folded(left1 * right0 - left0 * right1))
                values.append(folded(left0 * left0 + left1 * left1))
                right0, right1 = part(own + dates, 0, look), part(own + dates, 1, look)
                values.append(folded(right0 * right0 + right1 * right1))
                start = chip * block + look * QUANTITIES
                sums[start : start + QUANTITIES, slot * columns : (slot + 1) * columns] = (
                    row_sums(values)
                )
        rows = slice(chip * block, (chip + 1) * block)
        pooled[rows] = pool_columns(sums[rows], pool_ref[...])

    def every_look(start):
        return pooled[pl.ds(start, CHIP_LOOKS, stride=QUANTITIES), :]

    first = lax.broadcasted_iota(jnp.int32, (CHIP_LOOKS, LANES), 1) < LANES // 2
    for chip in range(CHIPS):
        base = chip * block
        power_left = every_look(base + 2 * KINDS)
        for kind in range(KINDS):
            halves = []
            for slot in range(dates):
                position, number = partner_of(kind, (me ^ (CORES * chip)) * dates + slot)
                start = lax.div(position, CORES) * block + 2 * KINDS + lax.rem(position, CORES)
                halves.append(pltpu.roll(every_look(start), LANES // 2 * (number ^ slot), 1))
            power = power_left * jnp.where(first, halves[0], halves[1])
            real, imag = every_look(base + 2 * kind), every_look(base + 2 * kind + 1)
            for channel, value in (
                (2 * kind, real * scale),
                (2 * kind + 1, imag * scale),
                (2 * KINDS + kind, jnp.sqrt(real * real + imag * imag) / jnp.sqrt(power + 1e-06)),
            ):
                outs[chip][channel * CHIP_LOOKS : (channel + 1) * CHIP_LOOKS, :] = value


def chip_place_kernel(positions, *refs):
    pieces, (ifg_ref, coh_ref) = refs[:CHIPS], refs[CHIPS:]
    dates, _, _, columns = ifg_ref.shape
    mine = lax.axis_index("date") // CORES
    for chip in range(CHIPS):

        @pl.when(mine == chip)
        def _():
            for position, piece_ref in zip(positions, pieces):
                start = (chip ^ position) * CHIP_LOOKS
                where = slice(start, start + CHIP_LOOKS)
                for channel in range(CHANNELS):
                    rows = piece_ref[channel * CHIP_LOOKS : (channel + 1) * CHIP_LOOKS, :]
                    for slot in range(dates):
                        part = rows[:, slot * columns : (slot + 1) * columns]
                        if channel < 2 * KINDS:
                            ifg_ref[slot, channel, where, :] = part
                        else:
                            coh_ref[slot, channel - 2 * KINDS, where, :] = part


def place_kernel(x_ref, ifg_ref, coh_ref):
    sources, rows, lanes = x_ref.shape
    dates, _, lines, columns = ifg_ref.shape
    looks = lanes // columns
    for slot in range(dates):
        for channel in range(CHANNELS):
            values = x_ref[:, slot * CHANNELS + channel, :]
            for look in range(looks):
                part = values[:, look * columns : (look + 1) * columns]
                where = pl.ds(look, sources, stride=looks)
                if channel < 2 * KINDS:
                    ifg_ref[slot, channel, where, :] = part
                else:
                    coh_ref[slot, channel - 2 * KINDS, where, :] = part


def body(
    epoch_tiles_quadrature,
    along_track_whole_displacement,
    along_track_subpixel_weights,
    slant_whole_displacement,
    slant_subpixel_weights,
    sweeps_each_epoch,
    baseline_companion_gap,
    master_epoch_image,
):
    block = epoch_tiles_quadrature
    dates, parts, lines, columns = block.shape
    owners = lax.axis_size("date")
    total = owners * dates
    images = dates * parts
    chips = by_chips(block, owners)
    line_groups = CHIPS if chips else min(owners, lines // LOOK_AZ)
    column_groups = 1 if chips else owners // line_groups
    tile_lines, tile_columns = lines // line_groups, columns // column_groups
    line_looks, column_looks = tile_lines // LOOK_AZ, tile_columns // LOOK_RG
    lanes = line_looks * column_looks

    arguments = (
        block,
        along_track_whole_displacement,
        along_track_subpixel_weights,
        slant_whole_displacement,
        slant_subpixel_weights,
        sweeps_each_epoch,
        baseline_companion_gap.T,
    )
    block, even, odd, *small = pl.pallas_call(
        start_kernel,
        out_shape=(
            pltpu.VMEM(block.shape, block.dtype),
            pltpu.VMEM((lines // 2, 2 * images * MARGIN), jnp.bfloat16),
            pltpu.VMEM((lines // 2, 2 * images * MARGIN), jnp.bfloat16),
            *[pltpu.SMEM(array.shape, array.dtype) for array in arguments[1:]],
        ),
        in_specs=[pl.BlockSpec(memory_space=pltpu.HBM)] * len(arguments),
        out_specs=(VMEM,) * 3 + (SMEM,) * (len(arguments) - 1),
        scratch_shapes=[pltpu.SemaphoreType.DMA((images + len(arguments) - 1,))],
        name="start",
        compiler_params=pltpu.CompilerParams(vmem_limit_bytes=GRANT),
    )(*[pltpu.with_memory_space_constraint(array, pltpu.HBM) for array in arguments])
    *small, gap = [pltpu.with_memory_space_constraint(array, pltpu.SMEM) for array in small]
    width = lax.axis_size("range")
    odd = exchanged(odd, "range", [(j, j + 1) for j in range(1, width - 1, 2)])
    even = exchanged(even, "range", [(j, j + 1) for j in range(0, width - 1, 2)])

    tile = (dates, parts, tile_lines, tile_columns)
    rows, cols = lines // LOOK_AZ, columns // LOOK_RG
    out_shape = (
        jax.ShapeDtypeStruct((dates, 2 * KINDS, rows, cols), jnp.float32),
        jax.ShapeDtypeStruct((dates, KINDS, rows, cols), jnp.float32),
    )
    if chips:

        def swapped(array, bits):
            pairs = [(i, i ^ bits) for i in range(owners) if i < i ^ bits]
            return exchanged(array, "date", pairs)

        line_taps, inner, low_taps, high_taps, pool, *tiles = pl.pallas_call(
            main_kernel,
            out_shape=(
                pltpu.VMEM((dates, lines, lines), jnp.bfloat16),
                pltpu.VMEM((lines, LANES), jnp.float32),
                pltpu.VMEM((images * MARGIN, LANES), jnp.bfloat16),
                pltpu.VMEM((images * MARGIN, LANES), jnp.bfloat16),
                pltpu.VMEM((dates * columns, LANES), jnp.bfloat16),
                *[pltpu.VMEM(tile, jnp.bfloat16)] * CHIPS,
            ),
            in_specs=[SMEM] * len(small) + [VMEM],
            out_specs=(VMEM,) * (5 + CHIPS),
            cost_estimate=pl.CostEstimate(
                flops=400000000, bytes_accessed=2000000, transcendentals=0
            ),
            name="main",
            compiler_params=pltpu.CompilerParams(vmem_limit_bytes=GRANT),
        )(*small, near(block))
        half = CHIPS // 2
        tiles[0], tiles[1], *borders = pl.pallas_call(
            border_kernel,
            out_shape=(pltpu.VMEM(tile, jnp.bfloat16),) * half
            + (pltpu.VMEM((tile_lines, LANES), jnp.bfloat16),) * half,
            in_specs=[VMEM] * (6 + half),
            out_specs=(VMEM,) * CHIPS,
            scratch_shapes=[pltpu.VMEM((2, lines, images * MARGIN), jnp.bfloat16)],
            name="border",
            compiler_params=pltpu.CompilerParams(vmem_limit_bytes=GRANT),
        )(
            *[near(array) for array in (inner, even, odd, low_taps, high_taps, line_taps)],
            *[near(array) for array in tiles[:half]],
        )
        order = [3, 2, 1]
        own = tiles[0]
        direct = {number: swapped(tiles[number], CORES * number) for number in order}
        borders = [swapped(borders[n], CORES * (half + n)) for n in range(half)]
        other = swapped(own, 1)
        direct[1], *borders = lax.optimization_barrier((direct[1], *borders))
        passed = {number: swapped(direct[number], 1) for number in order}
        held, positions = [own, other], [0, 1]
        for number in order:
            held += [direct[number], passed[number]]
            positions += [CORES * number, CORES * number + 1]
        bundle = pl.pallas_call(
            bundle_kernel,
            out_shape=pltpu.VMEM((half, tile_lines, LANES), jnp.bfloat16),
            in_specs=[VMEM] * half,
            out_specs=VMEM,
            name="bundle",
            compiler_params=pltpu.CompilerParams(vmem_limit_bytes=GRANT),
        )(*[near(border) for border in borders])
        held += borders + [swapped(bundle, 1)]
        results = pl.pallas_call(
            functools.partial(chip_looks_kernel, positions),
            out_shape=(pltpu.VMEM((CHANNELS * CHIP_LOOKS, LANES), jnp.float32),) * CHIPS,
            in_specs=[SMEM] * 2 + [VMEM] * (1 + len(held)),
            out_specs=(VMEM,) * CHIPS,
            scratch_shapes=[
                pltpu.VMEM((total, parts, tile_lines, tile_columns), jnp.float32),
                pltpu.VMEM((CHIPS * QUANTITIES * CHIP_LOOKS, dates * columns), jnp.float32),
                pltpu.VMEM((CHIPS * QUANTITIES * CHIP_LOOKS, LANES), jnp.float32),
            ],
            name="looks",
            compiler_params=pltpu.CompilerParams(vmem_limit_bytes=GRANT),
        )(master_epoch_image, gap, near(pool), *[near(tile) for tile in held])
        back = {number: swapped(results[number], CORES * number) for number in order}
        last = [3, 2, 1]
        pieces = [results[0]] + [back[number] for number in last]
        return pl.pallas_call(
            functools.partial(chip_place_kernel, [0] + last),
            out_shape=out_shape,
            in_specs=[VMEM] * CHIPS,
            out_specs=(VMEM, VMEM),
            name="place",
            compiler_params=pltpu.CompilerParams(vmem_limit_bytes=GRANT),
        )(*[near(piece) for piece in pieces])

    inner, low_taps, high_taps, line_taps = pl.pallas_call(
        taps_kernel,
        out_shape=(
            pltpu.VMEM(block.shape, jnp.float32),
            pltpu.VMEM((images * MARGIN, images * LANES), jnp.bfloat16),
            pltpu.VMEM((images * MARGIN, images * LANES), jnp.bfloat16),
            pltpu.VMEM((dates, lines, lines), jnp.bfloat16),
        ),
        in_specs=[SMEM] * len(small) + [VMEM],
        out_specs=(VMEM,) * 4,
        cost_estimate=pl.CostEstimate(flops=4000000, bytes_accessed=800000, transcendentals=0),
        name="taps",
        compiler_params=pltpu.CompilerParams(vmem_limit_bytes=GRANT),
    )(*small, near(block))
    tiles = pl.pallas_call(
        functools.partial(
            resample_kernel, (line_groups, column_groups, tile_lines, tile_columns)
        ),
        out_shape=pltpu.VMEM((owners,) + tile, jnp.bfloat16),
        in_specs=[VMEM] * 6,
        out_specs=VMEM,
        scratch_shapes=[pltpu.VMEM((2, lines, images * MARGIN), jnp.bfloat16)],
        name="resample",
        compiler_params=pltpu.CompilerParams(vmem_limit_bytes=GRANT),
    )(*[near(array) for array in (inner, even, odd, low_taps, high_taps, line_taps)])

    tiles = lax.all_to_all(tiles, "date", 0, 0)
    results = pl.pallas_call(
        looks_kernel,
        out_shape=pltpu.VMEM((owners, dates * CHANNELS, lanes), jnp.float32),
        in_specs=[SMEM] * 2 + [VMEM],
        out_specs=VMEM,
        scratch_shapes=[
            pltpu.VMEM((total, parts, tile_lines, tile_columns), jnp.float32),
            pltpu.VMEM((total * QUANTITIES, line_looks * tile_columns), jnp.float32),
            pltpu.VMEM((total * QUANTITIES, lanes), jnp.float32),
            pltpu.VMEM((KINDS, total, lanes), jnp.float32),
        ],
        name="looks",
        compiler_params=pltpu.CompilerParams(vmem_limit_bytes=GRANT),
    )(master_epoch_image, gap, near(tiles))
    results = lax.all_to_all(results, "date", 0, 0)

    if column_groups == 1:
        return pl.pallas_call(
            place_kernel,
            out_shape=out_shape,
            in_specs=[VMEM],
            out_specs=(VMEM, VMEM),
            name="place",
            compiler_params=pltpu.CompilerParams(vmem_limit_bytes=GRANT),
        )(near(results))
    whole = results.reshape(
        line_groups, column_groups, dates, CHANNELS, line_looks, column_looks
    )
    whole = jnp.transpose(whole, (2, 3, 0, 4, 1, 5)).reshape(dates, CHANNELS, rows, cols)
    return (whole[:, : 2 * KINDS], whole[:, 2 * KINDS :])


def solution(mesh):
    in_specs = (P("date", None, None, "range"), P(), P(), P(), P(), P(), P(), P())
    out_specs = (P("date", None, None, "range"), P("date", None, None, "range"))
    return jax.shard_map(body, mesh=mesh, in_specs=in_specs, out_specs=out_specs, check_vma=False)
```

```python
import functools

import jax
import jax.numpy as jnp
from jax import lax
from jax.experimental import pallas as pl
from jax.experimental.pallas import tpu as pltpu
from jax.sharding import PartitionSpec as P

MAX_SWEEPS = 4
TAPS = 8
FRACTIONS = 16
MARGIN = 16
LOOK_AZ = 16
LOOK_RG = 4
QUANTITIES = 8
KINDS = 3
CHANNELS = 9
LANES = 128
GRANT = 24 * 2**20
CORES = 2
CHIPS = 4
CHIP_LOOKS = 4

SMEM = pl.BlockSpec(memory_space=pltpu.SMEM)
VMEM = pl.BlockSpec(memory_space=pltpu.VMEM)


def exchanged(array, axis, pairs):
    return lax.ppermute(array, axis, [route for a, b in pairs for route in ((a, b), (b, a))])


def near(array):
    return pltpu.with_memory_space_constraint(array, pltpu.VMEM)


def iotas(rows, cols):
    return (
        lax.broadcasted_iota(jnp.int32, (rows, cols), 0),
        lax.broadcasted_iota(jnp.int32, (rows, cols), 1),
    )


def weight_rows(fractions):
    row, lane = iotas(8, LANES)
    spot = jnp.zeros((8, LANES), jnp.float32)
    for number, fraction in enumerate(fractions):
        spot = jnp.where(row == number, fraction.astype(jnp.float32), spot)
    spacing = (lane - 1 - (TAPS // 2 - 1)).astype(jnp.float32) - spot / FRACTIONS
    angle = jnp.pi * spacing
    sinc = jnp.where(spacing == 0.0, 1.0, jnp.sin(angle) / jnp.where(spacing == 0.0, 1.0, angle))
    weights = sinc * jnp.cos(angle / (TAPS + 1)) ** 2
    weights = jnp.where((lane >= 1) & (lane <= TAPS), weights, 0.0)
    weights = weights / jnp.sum(weights, axis=1, keepdims=True)
    return weights.astype(jnp.bfloat16).astype(jnp.float32)


def by_chips(block, owners):
    dates, parts, lines, columns = block.shape
    return (
        owners == CHIPS * CORES
        and (dates, parts) == (2, 2)
        and lines == CHIPS * CHIP_LOOKS * LOOK_AZ
        and columns == 2 * LANES
    )


def tile_order(position, chips):
    return position ^ (lax.axis_index("date") // CORES) if chips else position


def banded(offsets, weights):
    rows, cols = offsets.shape
    lanes = jnp.broadcast_to(weights, (rows, LANES))
    spots = jnp.clip(offsets + 1, 0, TAPS + 1)
    return jnp.concatenate(
        [
            jnp.take_along_axis(lanes, spots[:, start : start + LANES], axis=1)
            for start in range(0, cols, LANES)
        ],
        axis=1,
    )


def start_kernel(x_ref, *refs):
    dates, parts, lines, columns = x_ref.shape
    images = [(slot, part) for slot in range(dates) for part in range(parts)]
    count = (len(refs) - 4) // 2
    near_ref, even_ref, odd_ref = refs[count : count + 3]
    sems = refs[-1]
    small = list(zip(refs[:count], refs[count + 3 : -1]))
    whole = [(x_ref.at[image], near_ref.at[image]) for image in images]
    copies = [
        pltpu.make_async_copy(source, target, sems.at[number])
        for number, (source, target) in enumerate(whole + small)
    ]
    for copy in copies:
        copy.start()
    forward = lax.axis_index("range") % 2 == 0
    for number, (slot, part) in enumerate(images):
        copies[number].wait()
        for parity, last_ref, first_ref in (
            (forward, even_ref, odd_ref),
            (jnp.logical_not(forward), odd_ref, even_ref),
        ):

            @pl.when(parity)
            def _():
                for half in range(2):
                    rows = slice(half * (lines // 2), (half + 1) * (lines // 2))
                    start = (half * len(images) + number) * MARGIN
                    spot = slice(start, start + MARGIN)
                    last_ref[:, spot] = near_ref[slot, part, rows, columns - MARGIN :]
                    first_ref[:, spot] = near_ref[slot, part, rows, :MARGIN]

    for copy in copies[len(images) :]:
        copy.wait()


def pool_matrix(columns, lanes):
    row, col = iotas(columns, lanes)
    return jnp.where(row // LOOK_RG == col, 1.0, 0.0).astype(jnp.bfloat16)


def taps_kernel(
    chips,
    tile_lines,
    az_whole,
    az_part,
    rg_whole,
    rg_part,
    sweeps,
    x_ref,
    inner_ref,
    low_ref,
    high_ref,
    line_ref,
    pool_ref,
):
    dates, parts, lines, columns = x_ref.shape
    pool_ref[...] = pool_matrix(*pool_ref.shape)
    edge_rows = low_ref.shape[0]
    centre = TAPS // 2 - 1
    present = [lax.axis_index("date") * dates + slot for slot in range(dates)]
    table = weight_rows([rg_part[d] for d in present] + [az_part[d] for d in present])
    for slot, date in enumerate(present):
        shift = centre - rg_whole[date]
        weights = table[slot : slot + 1]
        row, col = iotas(columns, columns)
        own = banded(row - col + shift, weights).astype(jnp.bfloat16)
        for part in range(parts):
            inner_ref[slot, part] = jnp.dot(
                x_ref[slot, part], own, preferred_element_type=jnp.float32
            )
        row, col = iotas(edge_rows, LANES)
        low = banded(row % MARGIN - MARGIN - col + shift, weights)
        high = banded(row % MARGIN + LANES - col + shift, weights)
        for part in range(parts):
            image = slot * parts + part
            held = row // MARGIN == image
            spot = slice(image * LANES, (image + 1) * LANES)
            low_ref[:, spot] = jnp.where(held, low, 0.0).astype(jnp.bfloat16)
            high_ref[:, spot] = jnp.where(held, high, 0.0).astype(jnp.bfloat16)
        row, col = iotas(lines, lines)
        row = tile_order(row // tile_lines, chips) * tile_lines + row % tile_lines
        weights = table[dates + slot : dates + slot + 1]
        band = banded(col - row + (centre - az_whole[date]), weights)
        usable = row < sweeps[date] * (lines // MAX_SWEEPS)
        line_ref[slot] = jnp.where(usable, band, 0.0).astype(jnp.bfloat16)


def resample_kernel(split, inner_ref, even_ref, odd_ref, low_ref, high_ref, line_ref, *refs):
    *outs, edges = refs
    dates, parts, _, columns = inner_ref.shape
    line_groups, column_groups, tile_lines, tile_columns = split
    backward = lax.axis_index("range") % 2
    height, width = even_ref.shape
    for half in range(2):
        rows = slice(half * height, (half + 1) * height)
        spot = slice(half * (width // 2), (half + 1) * (width // 2))
        edges[1 - backward, rows, :] = even_ref[:, spot]
        edges[backward, rows, :] = odd_ref[:, spot]
    low = jnp.dot(edges[0], low_ref[...], preferred_element_type=jnp.float32)
    high = jnp.dot(edges[1], high_ref[...], preferred_element_type=jnp.float32)
    for slot in range(dates):
        for part in range(parts):
            spot = slice((slot * parts + part) * LANES, (slot * parts + part + 1) * LANES)
            pieces = [
                inner_ref[slot, part, :, start : start + LANES]
                for start in range(0, columns, LANES)
            ]
            pieces[0] += low[:, spot]
            pieces[-1] += high[:, spot]
            ranged = jnp.concatenate(pieces, axis=1)
            moved = jnp.dot(
                line_ref[slot], ranged.astype(jnp.bfloat16), preferred_element_type=jnp.float32
            ).astype(jnp.bfloat16)
            for i in range(line_groups):
                for j in range(column_groups):
                    tile = moved[
                        i * tile_lines : (i + 1) * tile_lines,
                        j * tile_columns : (j + 1) * tile_columns,
                    ]
                    if len(outs) == 1:
                        outs[0][i * column_groups + j, slot, part] = tile
                    else:
                        outs[i][slot, part] = tile


def partners(date, gap_ref, total):
    ahead = date + gap_ref[0, date]
    later = jnp.where(ahead < total, ahead, date - gap_ref[0, date])
    back = date - gap_ref[1, date]
    earlier = jnp.where(back >= 0, back, date + gap_ref[1, date])
    return (later, earlier)


def row_sums(values):
    row = lax.broadcasted_iota(jnp.int32, values[0].shape, 0)
    order = (3, 2, 1, 0, 7, 6, 5, 4)
    values = [values[number] for number in order]
    upper = row < 4
    values = [
        jnp.where(upper, a, b) + pltpu.roll(jnp.where(upper, b, a), 4, 0)
        for a, b in zip(values[:4], values[4:])
    ]
    for step, kept in ((2, row % 4 >= 2), (1, row % 2 == 1)):
        values = [
            jnp.where(kept, a + pltpu.roll(a, step, 0), b + pltpu.roll(b, 8 - step, 0))
            for a, b in zip(values[:step], values[step:])
        ]
    return values[0]


def pool_columns(sums, pool):
    coarse = sums.astype(jnp.bfloat16)
    fine = (sums - coarse.astype(jnp.float32)).astype(jnp.bfloat16)
    return jnp.dot(coarse, pool, preferred_element_type=jnp.float32) + jnp.dot(
        fine, pool, preferred_element_type=jnp.float32
    )


def looks_kernel(root_ref, gap_ref, tiles_ref, out_ref, stack, sums, pooled, powers):
    total, _, tile_lines, tile_columns = stack.shape
    owners, per_owner, lanes = out_ref.shape
    dates = per_owner // CHANNELS
    line_looks = tile_lines // LOOK_AZ
    unroll = total if total <= 16 else 1

    def widen(owner, carry):
        stack[pl.ds(owner * dates, dates)] = tiles_ref[owner].astype(jnp.float32)
        return carry

    lax.fori_loop(0, owners, widen, 0)

    def partner_of(kind, date):
        return partners(date, gap_ref, total)[kind - 1] if kind else root_ref[0]

    def collect(date, carry):
        left0, left1 = stack[date, 0], stack[date, 1]
        values = []
        for kind in range(KINDS):
            partner = partner_of(kind, date)
            right0, right1 = stack[partner, 0], stack[partner, 1]
            values += [left0 * right0 + left1 * right1, left1 * right0 - left0 * right1]
        values.append(left0 * left0 + left1 * left1)
        values.append(jnp.zeros_like(left0))
        rows = pl.ds(pl.multiple_of(date * QUANTITIES, QUANTITIES), QUANTITIES)
        for look in range(line_looks):
            start = look * LOOK_AZ
            sums[rows, look * tile_columns : (look + 1) * tile_columns] = row_sums(
                [value[start : start + 8] + value[start + 8 : start + 16] for value in values]
            )
        return carry

    lax.fori_loop(0, total, collect, 0, unroll=unroll)
    pooled[...] = pool_columns(sums[...], pool_matrix(sums.shape[1], lanes))

    def gather(date, carry):
        for kind in range(KINDS):
            power = partner_of(kind, date) * QUANTITIES + 2 * KINDS
            powers[kind, pl.ds(date, 1), :] = pooled[pl.ds(power, 1), :]
        return carry

    lax.fori_loop(0, total, gather, 0, unroll=unroll)
    scale = 1.0 / (LOOK_AZ * LOOK_RG) ** 0.5

    for slot in range(dates):

        def every(number):
            return pooled[pl.ds(slot * QUANTITIES + number, owners, stride=dates * QUANTITIES), :]

        power_left = every(2 * KINDS)
        for kind in range(KINDS):
            real, imag = every(2 * kind), every(2 * kind + 1)
            power_right = powers[kind, pl.ds(slot, owners, stride=dates), :]
            out_ref[:, slot * CHANNELS + 2 * kind, :] = real * scale
            out_ref[:, slot * CHANNELS + 2 * kind + 1, :] = imag * scale
            out_ref[:, slot * CHANNELS + 2 * KINDS + kind, :] = jnp.sqrt(
                real * real + imag * imag
            ) / jnp.sqrt(power_left * power_right + 1e-06)


def chip_looks_kernel(positions, root_ref, gap_ref, pool_ref, *refs):
    tiles, outs, (stack, sums, pooled) = refs[: CHIPS * CORES], refs[CHIPS * CORES : -3], refs[-3:]
    dates, _, _, columns = tiles[0].shape
    me = lax.axis_index("date")
    total = len(tiles) * dates
    scale = 1.0 / (LOOK_AZ * LOOK_RG) ** 0.5
    for position, tile_ref in zip(positions, tiles):
        stack[position * dates : (position + 1) * dates] = tile_ref[...].astype(jnp.float32)

    def partner_of(kind, date):
        partner = partners(date, gap_ref, total)[kind - 1] if kind else root_ref[0]
        return lax.div(partner, dates) ^ me, lax.rem(partner, dates)

    def part(spot, number, look):
        return stack[spot, number, look * LOOK_AZ : (look + 1) * LOOK_AZ, :]

    def folded(value):
        return value[: LOOK_AZ // 2] + value[LOOK_AZ // 2 :]

    block = QUANTITIES * CHIP_LOOKS
    for chip in range(CHIPS):
        for slot in range(dates):
            own = CORES * chip * dates + slot
            others = []
            for kind in range(KINDS):
                position, number = partner_of(kind, (me ^ (CORES * chip)) * dates + slot)
                others.append(position * dates + number)
            for look in range(CHIP_LOOKS):
                left0, left1 = part(own, 0, look), part(own, 1, look)
                values = []
                for other in others:
                    right0, right1 = part(other, 0, look), part(other, 1, look)
                    values.append(folded(left0 * right0 + left1 * right1))
                    values.append(folded(left1 * right0 - left0 * right1))
                values.append(folded(left0 * left0 + left1 * left1))
                right0, right1 = part(own + dates, 0, look), part(own + dates, 1, look)
                values.append(folded(right0 * right0 + right1 * right1))
                start = chip * block + look * QUANTITIES
                sums[start : start + QUANTITIES, slot * columns : (slot + 1) * columns] = (
                    row_sums(values)
                )
        rows = slice(chip * block, (chip + 1) * block)
        pooled[rows] = pool_columns(sums[rows], pool_ref[...])

    def every_look(start):
        return pooled[pl.ds(start, CHIP_LOOKS, stride=QUANTITIES), :]

    first = lax.broadcasted_iota(jnp.int32, (CHIP_LOOKS, LANES), 1) < LANES // 2
    for chip in range(CHIPS):
        base = chip * block
        power_left = every_look(base + 2 * KINDS)
        for kind in range(KINDS):
            halves = []
            for slot in range(dates):
                position, number = partner_of(kind, (me ^ (CORES * chip)) * dates + slot)
                start = lax.div(position, CORES) * block + 2 * KINDS + lax.rem(position, CORES)
                halves.append(pltpu.roll(every_look(start), LANES // 2 * (number ^ slot), 1))
            power = power_left * jnp.where(first, halves[0], halves[1])
            real, imag = every_look(base + 2 * kind), every_look(base + 2 * kind + 1)
            for channel, value in (
                (2 * kind, real * scale),
                (2 * kind + 1, imag * scale),
                (2 * KINDS + kind, jnp.sqrt((real * real + imag * imag) / (power + 1e-06))),
            ):
                outs[chip][channel * CHIP_LOOKS : (channel + 1) * CHIP_LOOKS, :] = value


def chip_place_kernel(positions, *refs):
    pieces, (ifg_ref, coh_ref) = refs[:CHIPS], refs[CHIPS:]
    dates, _, _, columns = ifg_ref.shape
    mine = lax.axis_index("date") // CORES
    for chip in range(CHIPS):

        @pl.when(mine == chip)
        def _():
            for position, piece_ref in zip(positions, pieces):
                start = (chip ^ position) * CHIP_LOOKS
                where = slice(start, start + CHIP_LOOKS)
                for channel in range(CHANNELS):
                    rows = piece_ref[channel * CHIP_LOOKS : (channel + 1) * CHIP_LOOKS, :]
                    for slot in range(dates):
                        part = rows[:, slot * columns : (slot + 1) * columns]
                        if channel < 2 * KINDS:
                            ifg_ref[slot, channel, where, :] = part
                        else:
                            coh_ref[slot, channel - 2 * KINDS, where, :] = part


def place_kernel(x_ref, ifg_ref, coh_ref):
    sources, rows, lanes = x_ref.shape
    dates, _, lines, columns = ifg_ref.shape
    looks = lanes // columns
    for slot in range(dates):
        for channel in range(CHANNELS):
            values = x_ref[:, slot * CHANNELS + channel, :]
            for look in range(looks):
                part = values[:, look * columns : (look + 1) * columns]
                where = pl.ds(look, sources, stride=looks)
                if channel < 2 * KINDS:
                    ifg_ref[slot, channel, where, :] = part
                else:
                    coh_ref[slot, channel - 2 * KINDS, where, :] = part


def body(
    epoch_tiles_quadrature,
    along_track_whole_displacement,
    along_track_subpixel_weights,
    slant_whole_displacement,
    slant_subpixel_weights,
    sweeps_each_epoch,
    baseline_companion_gap,
    master_epoch_image,
):
    block = epoch_tiles_quadrature
    dates, parts, lines, columns = block.shape
    owners = lax.axis_size("date")
    total = owners * dates
    images = dates * parts
    chips = by_chips(block, owners)
    line_groups = CHIPS if chips else min(owners, lines // LOOK_AZ)
    column_groups = 1 if chips else owners // line_groups
    tile_lines, tile_columns = lines // line_groups, columns // column_groups
    line_looks, column_looks = tile_lines // LOOK_AZ, tile_columns // LOOK_RG
    lanes = line_looks * column_looks

    arguments = (
        block,
        along_track_whole_displacement,
        along_track_subpixel_weights,
        slant_whole_displacement,
        slant_subpixel_weights,
        sweeps_each_epoch,
        baseline_companion_gap.T,
    )
    block, even, odd, *small = pl.pallas_call(
        start_kernel,
        out_shape=(
            pltpu.VMEM(block.shape, block.dtype),
            pltpu.VMEM((lines // 2, 2 * images * MARGIN), jnp.bfloat16),
            pltpu.VMEM((lines // 2, 2 * images * MARGIN), jnp.bfloat16),
            *[pltpu.SMEM(array.shape, array.dtype) for array in arguments[1:]],
        ),
        in_specs=[pl.BlockSpec(memory_space=pltpu.HBM)] * len(arguments),
        out_specs=(VMEM,) * 3 + (SMEM,) * (len(arguments) - 1),
        scratch_shapes=[pltpu.SemaphoreType.DMA((images + len(arguments) - 1,))],
        name="start",
        compiler_params=pltpu.CompilerParams(vmem_limit_bytes=GRANT),
    )(*[pltpu.with_memory_space_constraint(array, pltpu.HBM) for array in arguments])
    *small, gap = [pltpu.with_memory_space_constraint(array, pltpu.SMEM) for array in small]
    width = lax.axis_size("range")
    odd = exchanged(odd, "range", [(j, j + 1) for j in range(1, width - 1, 2)])
    even = exchanged(even, "range", [(j, j + 1) for j in range(0, width - 1, 2)])

    inner, low_taps, high_taps, line_taps, pool = pl.pallas_call(
        functools.partial(taps_kernel, chips, tile_lines),
        out_shape=(
            pltpu.VMEM(block.shape, jnp.float32),
            pltpu.VMEM((images * MARGIN, images * LANES), jnp.bfloat16),
            pltpu.VMEM((images * MARGIN, images * LANES), jnp.bfloat16),
            pltpu.VMEM((dates, lines, lines), jnp.bfloat16),
            pltpu.VMEM((dates * columns, LANES), jnp.bfloat16),
        ),
        in_specs=[SMEM] * len(small) + [VMEM],
        out_specs=(VMEM,) * 5,
        cost_estimate=pl.CostEstimate(flops=4000000, bytes_accessed=800000, transcendentals=0),
        name="taps",
        compiler_params=pltpu.CompilerParams(vmem_limit_bytes=GRANT),
    )(*small, near(block))
    tile = (dates, parts, tile_lines, tile_columns)
    if chips:
        out_shape = (pltpu.VMEM(tile, jnp.bfloat16),) * CHIPS
    else:
        out_shape = (pltpu.VMEM((owners,) + tile, jnp.bfloat16),)
    tiles = pl.pallas_call(
        functools.partial(
            resample_kernel, (line_groups, column_groups, tile_lines, tile_columns)
        ),
        out_shape=out_shape,
        in_specs=[VMEM] * 6,
        out_specs=(VMEM,) * len(out_shape),
        scratch_shapes=[pltpu.VMEM((2, lines, images * MARGIN), jnp.bfloat16)],
        name="resample",
        compiler_params=pltpu.CompilerParams(vmem_limit_bytes=GRANT),
    )(*[near(array) for array in (inner, even, odd, low_taps, high_taps, line_taps)])

    rows, cols = lines // LOOK_AZ, columns // LOOK_RG
    out_shape = (
        jax.ShapeDtypeStruct((dates, 2 * KINDS, rows, cols), jnp.float32),
        jax.ShapeDtypeStruct((dates, KINDS, rows, cols), jnp.float32),
    )
    if chips:

        def swapped(array, bits):
            pairs = [(i, i ^ bits) for i in range(owners) if i < i ^ bits]
            return exchanged(array, "date", pairs)

        order = [3, 2, 1]
        own = tiles[0]
        direct = {number: swapped(tiles[number], CORES * number) for number in order}
        other = swapped(own, 1)
        passed = {number: swapped(direct[number], 1) for number in order}
        held, positions = [own, other], [0, 1]
        for number in order:
            held += [direct[number], passed[number]]
            positions += [CORES * number, CORES * number + 1]
        results = pl.pallas_call(
            functools.partial(chip_looks_kernel, positions),
            out_shape=(pltpu.VMEM((CHANNELS * CHIP_LOOKS, LANES), jnp.float32),) * CHIPS,
            in_specs=[SMEM] * 2 + [VMEM] * (1 + len(held)),
            out_specs=(VMEM,) * CHIPS,
            scratch_shapes=[
                pltpu.VMEM((total, parts, tile_lines, tile_columns), jnp.float32),
                pltpu.VMEM((CHIPS * QUANTITIES * CHIP_LOOKS, dates * columns), jnp.float32),
                pltpu.VMEM(((CHIPS + 1) * QUANTITIES * CHIP_LOOKS, LANES), jnp.float32),
            ],
            name="looks",
            compiler_params=pltpu.CompilerParams(vmem_limit_bytes=GRANT),
        )(master_epoch_image, gap, near(pool), *[near(tile) for tile in held])
        back = {number: swapped(results[number], CORES * number) for number in order}
        last = [1, 3, 2]
        pieces = [results[0]] + [back[number] for number in last]
        return pl.pallas_call(
            functools.partial(chip_place_kernel, [0] + last),
            out_shape=out_shape,
            in_specs=[VMEM] * CHIPS,
            out_specs=(VMEM, VMEM),
            name="place",
            compiler_params=pltpu.CompilerParams(vmem_limit_bytes=GRANT),
        )(*[near(piece) for piece in pieces])

    tiles = lax.all_to_all(tiles[0], "date", 0, 0)
    results = pl.pallas_call(
        looks_kernel,
        out_shape=pltpu.VMEM((owners, dates * CHANNELS, lanes), jnp.float32),
        in_specs=[SMEM] * 2 + [VMEM],
        out_specs=VMEM,
        scratch_shapes=[
            pltpu.VMEM((total, parts, tile_lines, tile_columns), jnp.float32),
            pltpu.VMEM((total * QUANTITIES, line_looks * tile_columns), jnp.float32),
            pltpu.VMEM((total * QUANTITIES, lanes), jnp.float32),
            pltpu.VMEM((KINDS, total, lanes), jnp.float32),
        ],
        name="looks",
        compiler_params=pltpu.CompilerParams(vmem_limit_bytes=GRANT),
    )(master_epoch_image, gap, near(tiles))
    results = lax.all_to_all(results, "date", 0, 0)

    if column_groups == 1:
        return pl.pallas_call(
            place_kernel,
            out_shape=out_shape,
            in_specs=[VMEM],
            out_specs=(VMEM, VMEM),
            name="place",
            compiler_params=pltpu.CompilerParams(vmem_limit_bytes=GRANT),
        )(near(results))
    whole = results.reshape(
        line_groups, column_groups, dates, CHANNELS, line_looks, column_looks
    )
    whole = jnp.transpose(whole, (2, 3, 0, 4, 1, 5)).reshape(dates, CHANNELS, rows, cols)
    return (whole[:, : 2 * KINDS], whole[:, 2 * KINDS :])


def solution(mesh):
    in_specs = (P("date", None, None, "range"), P(), P(), P(), P(), P(), P(), P())
    out_specs = (P("date", None, None, "range"), P("date", None, None, "range"))
    return jax.shard_map(body, mesh=mesh, in_specs=in_specs, out_specs=out_specs, check_vma=False)
```

```python
import functools

import jax
import jax.numpy as jnp
from jax import lax
from jax.experimental import pallas as pl
from jax.experimental.pallas import tpu as pltpu
from jax.sharding import PartitionSpec as P

MAX_SWEEPS = 4
TAPS = 8
FRACTIONS = 16
MARGIN = 16
LOOK_AZ = 16
LOOK_RG = 4
QUANTITIES = 8
KINDS = 3
CHANNELS = 9
LANES = 128
GRANT = 24 * 2**20
CORES = 2
CHIPS = 4
CHIP_LOOKS = 4

SMEM = pl.BlockSpec(memory_space=pltpu.SMEM)
VMEM = pl.BlockSpec(memory_space=pltpu.VMEM)


def exchanged(array, axis, pairs):
    return lax.ppermute(array, axis, [route for a, b in pairs for route in ((a, b), (b, a))])


def near(array):
    return pltpu.with_memory_space_constraint(array, pltpu.VMEM)


def iotas(rows, cols):
    return (
        lax.broadcasted_iota(jnp.int32, (rows, cols), 0),
        lax.broadcasted_iota(jnp.int32, (rows, cols), 1),
    )


def weight_rows(fractions):
    row, lane = iotas(8, LANES)
    spot = jnp.zeros((8, LANES), jnp.float32)
    for number, fraction in enumerate(fractions):
        spot = jnp.where(row == number, fraction.astype(jnp.float32), spot)
    spacing = (lane - 1 - (TAPS // 2 - 1)).astype(jnp.float32) - spot / FRACTIONS
    angle = jnp.pi * spacing
    sinc = jnp.where(spacing == 0.0, 1.0, jnp.sin(angle) / jnp.where(spacing == 0.0, 1.0, angle))
    weights = sinc * jnp.cos(angle / (TAPS + 1)) ** 2
    weights = jnp.where((lane >= 1) & (lane <= TAPS), weights, 0.0)
    weights = weights / jnp.sum(weights, axis=1, keepdims=True)
    return weights.astype(jnp.bfloat16).astype(jnp.float32)


def by_chips(block, owners):
    dates, parts, lines, columns = block.shape
    return (
        owners == CHIPS * CORES
        and (dates, parts) == (2, 2)
        and lines == CHIPS * CHIP_LOOKS * LOOK_AZ
        and columns == 2 * LANES
    )


def tile_order(position, chips):
    return position ^ (lax.axis_index("date") // CORES) if chips else position


def banded(offsets, weights):
    rows, cols = offsets.shape
    lanes = jnp.broadcast_to(weights, (rows, LANES))
    spots = jnp.clip(offsets + 1, 0, TAPS + 1)
    return jnp.concatenate(
        [
            jnp.take_along_axis(lanes, spots[:, start : start + LANES], axis=1)
            for start in range(0, cols, LANES)
        ],
        axis=1,
    )


def start_kernel(x_ref, *refs):
    dates, parts, lines, columns = x_ref.shape
    images = [(slot, part) for slot in range(dates) for part in range(parts)]
    count = (len(refs) - 4) // 2
    near_ref, even_ref, odd_ref = refs[count : count + 3]
    sems = refs[-1]
    small = list(zip(refs[:count], refs[count + 3 : -1]))
    whole = [(x_ref.at[image], near_ref.at[image]) for image in images]
    copies = [
        pltpu.make_async_copy(source, target, sems.at[number])
        for number, (source, target) in enumerate(whole + small)
    ]
    for copy in copies:
        copy.start()
    forward = lax.axis_index("range") % 2 == 0
    for number, (slot, part) in enumerate(images):
        copies[number].wait()
        for parity, last_ref, first_ref in (
            (forward, even_ref, odd_ref),
            (jnp.logical_not(forward), odd_ref, even_ref),
        ):

            @pl.when(parity)
            def _():
                for half in range(2):
                    rows = slice(half * (lines // 2), (half + 1) * (lines // 2))
                    start = (half * len(images) + number) * MARGIN
                    spot = slice(start, start + MARGIN)
                    last_ref[:, spot] = near_ref[slot, part, rows, columns - MARGIN :]
                    first_ref[:, spot] = near_ref[slot, part, rows, :MARGIN]

    for copy in copies[len(images) :]:
        copy.wait()


def pool_matrix(columns, lanes):
    row, col = iotas(columns, lanes)
    return jnp.where(row // LOOK_RG == col, 1.0, 0.0).astype(jnp.bfloat16)


def taps_kernel(
    chips,
    tile_lines,
    az_whole,
    az_part,
    rg_whole,
    rg_part,
    sweeps,
    x_ref,
    inner_ref,
    low_ref,
    high_ref,
    line_ref,
    pool_ref,
):
    dates, parts, lines, columns = x_ref.shape
    pool_ref[...] = pool_matrix(*pool_ref.shape)
    edge_rows = low_ref.shape[0]
    centre = TAPS // 2 - 1
    present = [lax.axis_index("date") * dates + slot for slot in range(dates)]
    table = weight_rows([rg_part[d] for d in present] + [az_part[d] for d in present])
    for slot, date in enumerate(present):
        shift = centre - rg_whole[date]
        weights = table[slot : slot + 1]
        row, col = iotas(columns, columns)
        own = banded(row - col + shift, weights).astype(jnp.bfloat16)
        for part in range(parts):
            inner_ref[slot, part] = jnp.dot(
                x_ref[slot, part], own, preferred_element_type=jnp.float32
            )
        row, col = iotas(edge_rows, LANES)
        low = banded(row % MARGIN - MARGIN - col + shift, weights)
        high = banded(row % MARGIN + LANES - col + shift, weights)
        for part in range(parts):
            image = slot * parts + part
            held = row // MARGIN == image
            spot = slice(image * LANES, (image + 1) * LANES)
            low_ref[:, spot] = jnp.where(held, low, 0.0).astype(jnp.bfloat16)
            high_ref[:, spot] = jnp.where(held, high, 0.0).astype(jnp.bfloat16)
        row, col = iotas(lines, lines)
        row = tile_order(row // tile_lines, chips) * tile_lines + row % tile_lines
        weights = table[dates + slot : dates + slot + 1]
        band = banded(col - row + (centre - az_whole[date]), weights)
        usable = row < sweeps[date] * (lines // MAX_SWEEPS)
        line_ref[slot] = jnp.where(usable, band, 0.0).astype(jnp.bfloat16)


def resample_kernel(split, inner_ref, even_ref, odd_ref, low_ref, high_ref, line_ref, *refs):
    *outs, edges = refs
    dates, parts, _, columns = inner_ref.shape
    line_groups, column_groups, tile_lines, tile_columns = split
    backward = lax.axis_index("range") % 2
    height, width = even_ref.shape
    for half in range(2):
        rows = slice(half * height, (half + 1) * height)
        spot = slice(half * (width // 2), (half + 1) * (width // 2))
        edges[1 - backward, rows, :] = even_ref[:, spot]
        edges[backward, rows, :] = odd_ref[:, spot]
    low = jnp.dot(edges[0], low_ref[...], preferred_element_type=jnp.float32)
    high = jnp.dot(edges[1], high_ref[...], preferred_element_type=jnp.float32)
    for slot in range(dates):
        for part in range(parts):
            spot = slice((slot * parts + part) * LANES, (slot * parts + part + 1) * LANES)
            pieces = [
                inner_ref[slot, part, :, start : start + LANES]
                for start in range(0, columns, LANES)
            ]
            pieces[0] += low[:, spot]
            pieces[-1] += high[:, spot]
            ranged = jnp.concatenate(pieces, axis=1)
            moved = jnp.dot(
                line_ref[slot], ranged.astype(jnp.bfloat16), preferred_element_type=jnp.float32
            ).astype(jnp.bfloat16)
            for i in range(line_groups):
                for j in range(column_groups):
                    tile = moved[
                        i * tile_lines : (i + 1) * tile_lines,
                        j * tile_columns : (j + 1) * tile_columns,
                    ]
                    if len(outs) == 1:
                        outs[0][i * column_groups + j, slot, part] = tile
                    else:
                        outs[i][slot, part] = tile


def partners(date, gap_ref, total):
    ahead = date + gap_ref[0, date]
    later = jnp.where(ahead < total, ahead, date - gap_ref[0, date])
    back = date - gap_ref[1, date]
    earlier = jnp.where(back >= 0, back, date + gap_ref[1, date])
    return (later, earlier)


def row_sums(values):
    row = lax.broadcasted_iota(jnp.int32, values[0].shape, 0)
    order = (3, 2, 1, 0, 7, 6, 5, 4)
    values = [values[number] for number in order]
    upper = row < 4
    values = [
        jnp.where(upper, a, b) + pltpu.roll(jnp.where(upper, b, a), 4, 0)
        for a, b in zip(values[:4], values[4:])
    ]
    for step, kept in ((2, row % 4 >= 2), (1, row % 2 == 1)):
        values = [
            jnp.where(kept, a + pltpu.roll(a, step, 0), b + pltpu.roll(b, 8 - step, 0))
            for a, b in zip(values[:step], values[step:])
        ]
    return values[0]


def pool_columns(sums, pool):
    coarse = sums.astype(jnp.bfloat16)
    fine = (sums - coarse.astype(jnp.float32)).astype(jnp.bfloat16)
    return jnp.dot(coarse, pool, preferred_element_type=jnp.float32) + jnp.dot(
        fine, pool, preferred_element_type=jnp.float32
    )


def looks_kernel(root_ref, gap_ref, tiles_ref, out_ref, stack, sums, pooled, powers):
    total, _, tile_lines, tile_columns = stack.shape
    owners, per_owner, lanes = out_ref.shape
    dates = per_owner // CHANNELS
    line_looks = tile_lines // LOOK_AZ
    unroll = total if total <= 16 else 1

    def widen(owner, carry):
        stack[pl.ds(owner * dates, dates)] = tiles_ref[owner].astype(jnp.float32)
        return carry

    lax.fori_loop(0, owners, widen, 0)

    def partner_of(kind, date):
        return partners(date, gap_ref, total)[kind - 1] if kind else root_ref[0]

    def collect(date, carry):
        left0, left1 = stack[date, 0], stack[date, 1]
        values = []
        for kind in range(KINDS):
            partner = partner_of(kind, date)
            right0, right1 = stack[partner, 0], stack[partner, 1]
            values += [left0 * right0 + left1 * right1, left1 * right0 - left0 * right1]
        values.append(left0 * left0 + left1 * left1)
        values.append(jnp.zeros_like(left0))
        rows = pl.ds(pl.multiple_of(date * QUANTITIES, QUANTITIES), QUANTITIES)
        for look in range(line_looks):
            start = look * LOOK_AZ
            sums[rows, look * tile_columns : (look + 1) * tile_columns] = row_sums(
                [value[start : start + 8] + value[start + 8 : start + 16] for value in values]
            )
        return carry

    lax.fori_loop(0, total, collect, 0, unroll=unroll)
    pooled[...] = pool_columns(sums[...], pool_matrix(sums.shape[1], lanes))

    def gather(date, carry):
        for kind in range(KINDS):
            power = partner_of(kind, date) * QUANTITIES + 2 * KINDS
            powers[kind, pl.ds(date, 1), :] = pooled[pl.ds(power, 1), :]
        return carry

    lax.fori_loop(0, total, gather, 0, unroll=unroll)
    scale = 1.0 / (LOOK_AZ * LOOK_RG) ** 0.5

    for slot in range(dates):

        def every(number):
            return pooled[pl.ds(slot * QUANTITIES + number, owners, stride=dates * QUANTITIES), :]

        power_left = every(2 * KINDS)
        for kind in range(KINDS):
            real, imag = every(2 * kind), every(2 * kind + 1)
            power_right = powers[kind, pl.ds(slot, owners, stride=dates), :]
            out_ref[:, slot * CHANNELS + 2 * kind, :] = real * scale
            out_ref[:, slot * CHANNELS + 2 * kind + 1, :] = imag * scale
            out_ref[:, slot * CHANNELS + 2 * KINDS + kind, :] = jnp.sqrt(
                real * real + imag * imag
            ) / jnp.sqrt(power_left * power_right + 1e-06)


def chip_looks_kernel(positions, root_ref, gap_ref, pool_ref, *refs):
    tiles, outs, (stack, sums, pooled) = refs[: CHIPS * CORES], refs[CHIPS * CORES : -3], refs[-3:]
    dates, _, _, columns = tiles[0].shape
    me = lax.axis_index("date")
    total = len(tiles) * dates
    scale = 1.0 / (LOOK_AZ * LOOK_RG) ** 0.5
    for position, tile_ref in zip(positions, tiles):
        stack[position * dates : (position + 1) * dates] = tile_ref[...].astype(jnp.float32)

    def partner_of(kind, date):
        partner = partners(date, gap_ref, total)[kind - 1] if kind else root_ref[0]
        return lax.div(partner, dates) ^ me, lax.rem(partner, dates)

    def part(spot, number, look):
        return stack[spot, number, look * LOOK_AZ : (look + 1) * LOOK_AZ, :]

    def folded(value):
        return value[: LOOK_AZ // 2] + value[LOOK_AZ // 2 :]

    block = QUANTITIES * CHIP_LOOKS
    for chip in range(CHIPS):
        for slot in range(dates):
            own = CORES * chip * dates + slot
            others = []
            for kind in range(KINDS):
                position, number = partner_of(kind, (me ^ (CORES * chip)) * dates + slot)
                others.append(position * dates + number)
            for look in range(CHIP_LOOKS):
                left0, left1 = part(own, 0, look), part(own, 1, look)
                values = []
                for other in others:
                    right0, right1 = part(other, 0, look), part(other, 1, look)
                    values.append(folded(left0 * right0 + left1 * right1))
                    values.append(folded(left1 * right0 - left0 * right1))
                values.append(folded(left0 * left0 + left1 * left1))
                right0, right1 = part(own + dates, 0, look), part(own + dates, 1, look)
                values.append(folded(right0 * right0 + right1 * right1))
                start = chip * block + look * QUANTITIES
                sums[start : start + QUANTITIES, slot * columns : (slot + 1) * columns] = (
                    row_sums(values)
                )
        rows = slice(chip * block, (chip + 1) * block)
        pooled[rows] = pool_columns(sums[rows], pool_ref[...])

    def every_look(start):
        return pooled[pl.ds(start, CHIP_LOOKS, stride=QUANTITIES), :]

    first = lax.broadcasted_iota(jnp.int32, (CHIP_LOOKS, LANES), 1) < LANES // 2
    for chip in range(CHIPS):
        base = chip * block
        power_left = every_look(base + 2 * KINDS)
        for kind in range(KINDS):
            halves = []
            for slot in range(dates):
                position, number = partner_of(kind, (me ^ (CORES * chip)) * dates + slot)
                start = lax.div(position, CORES) * block + 2 * KINDS + lax.rem(position, CORES)
                halves.append(pltpu.roll(every_look(start), LANES // 2 * (number ^ slot), 1))
            power = power_left * jnp.where(first, halves[0], halves[1])
            real, imag = every_look(base + 2 * kind), every_look(base + 2 * kind + 1)
            for channel, value in (
                (2 * kind, real * scale),
                (2 * kind + 1, imag * scale),
                (2 * KINDS + kind, jnp.sqrt((real * real + imag * imag) / (power + 1e-06))),
            ):
                outs[chip][channel * CHIP_LOOKS : (channel + 1) * CHIP_LOOKS, :] = value


def chip_place_kernel(positions, *refs):
    pieces, (ifg_ref, coh_ref) = refs[:CHIPS], refs[CHIPS:]
    dates, _, _, columns = ifg_ref.shape
    mine = lax.axis_index("date") // CORES
    for chip in range(CHIPS):

        @pl.when(mine == chip)
        def _():
            for position, piece_ref in zip(positions, pieces):
                start = (chip ^ position) * CHIP_LOOKS
                where = slice(start, start + CHIP_LOOKS)
                for channel in range(CHANNELS):
                    rows = piece_ref[channel * CHIP_LOOKS : (channel + 1) * CHIP_LOOKS, :]
                    for slot in range(dates):
                        part = rows[:, slot * columns : (slot + 1) * columns]
                        if channel < 2 * KINDS:
                            ifg_ref[slot, channel, where, :] = part
                        else:
                            coh_ref[slot, channel - 2 * KINDS, where, :] = part


def place_kernel(x_ref, ifg_ref, coh_ref):
    sources, rows, lanes = x_ref.shape
    dates, _, lines, columns = ifg_ref.shape
    looks = lanes // columns
    for slot in range(dates):
        for channel in range(CHANNELS):
            values = x_ref[:, slot * CHANNELS + channel, :]
            for look in range(looks):
                part = values[:, look * columns : (look + 1) * columns]
                where = pl.ds(look, sources, stride=looks)
                if channel < 2 * KINDS:
                    ifg_ref[slot, channel, where, :] = part
                else:
                    coh_ref[slot, channel - 2 * KINDS, where, :] = part


def body(
    epoch_tiles_quadrature,
    along_track_whole_displacement,
    along_track_subpixel_weights,
    slant_whole_displacement,
    slant_subpixel_weights,
    sweeps_each_epoch,
    baseline_companion_gap,
    master_epoch_image,
):
    block = epoch_tiles_quadrature
    dates, parts, lines, columns = block.shape
    owners = lax.axis_size("date")
    total = owners * dates
    images = dates * parts
    chips = by_chips(block, owners)
    line_groups = CHIPS if chips else min(owners, lines // LOOK_AZ)
    column_groups = 1 if chips else owners // line_groups
    tile_lines, tile_columns = lines // line_groups, columns // column_groups
    line_looks, column_looks = tile_lines // LOOK_AZ, tile_columns // LOOK_RG
    lanes = line_looks * column_looks

    arguments = (
        block,
        along_track_whole_displacement,
        along_track_subpixel_weights,
        slant_whole_displacement,
        slant_subpixel_weights,
        sweeps_each_epoch,
        baseline_companion_gap.T,
    )
    block, even, odd, *small = pl.pallas_call(
        start_kernel,
        out_shape=(
            pltpu.VMEM(block.shape, block.dtype),
            pltpu.VMEM((lines // 2, 2 * images * MARGIN), jnp.bfloat16),
            pltpu.VMEM((lines // 2, 2 * images * MARGIN), jnp.bfloat16),
            *[pltpu.SMEM(array.shape, array.dtype) for array in arguments[1:]],
        ),
        in_specs=[pl.BlockSpec(memory_space=pltpu.HBM)] * len(arguments),
        out_specs=(VMEM,) * 3 + (SMEM,) * (len(arguments) - 1),
        scratch_shapes=[pltpu.SemaphoreType.DMA((images + len(arguments) - 1,))],
        name="start",
        compiler_params=pltpu.CompilerParams(vmem_limit_bytes=GRANT),
    )(*[pltpu.with_memory_space_constraint(array, pltpu.HBM) for array in arguments])
    *small, gap = [pltpu.with_memory_space_constraint(array, pltpu.SMEM) for array in small]
    width = lax.axis_size("range")
    odd = exchanged(odd, "range", [(j, j + 1) for j in range(1, width - 1, 2)])
    even = exchanged(even, "range", [(j, j + 1) for j in range(0, width - 1, 2)])

    inner, low_taps, high_taps, line_taps, pool = pl.pallas_call(
        functools.partial(taps_kernel, chips, tile_lines),
        out_shape=(
            pltpu.VMEM(block.shape, jnp.float32),
            pltpu.VMEM((images * MARGIN, images * LANES), jnp.bfloat16),
            pltpu.VMEM((images * MARGIN, images * LANES), jnp.bfloat16),
            pltpu.VMEM((dates, lines, lines), jnp.bfloat16),
            pltpu.VMEM((dates * columns, LANES), jnp.bfloat16),
        ),
        in_specs=[SMEM] * len(small) + [VMEM],
        out_specs=(VMEM,) * 5,
        cost_estimate=pl.CostEstimate(flops=4000000, bytes_accessed=800000, transcendentals=0),
        name="taps",
        compiler_params=pltpu.CompilerParams(vmem_limit_bytes=GRANT),
    )(*small, near(block))
    tile = (dates, parts, tile_lines, tile_columns)
    if chips:
        out_shape = (pltpu.VMEM(tile, jnp.bfloat16),) * CHIPS
    else:
        out_shape = (pltpu.VMEM((owners,) + tile, jnp.bfloat16),)
    tiles = pl.pallas_call(
        functools.partial(
            resample_kernel, (line_groups, column_groups, tile_lines, tile_columns)
        ),
        out_shape=out_shape,
        in_specs=[VMEM] * 6,
        out_specs=(VMEM,) * len(out_shape),
        scratch_shapes=[pltpu.VMEM((2, lines, images * MARGIN), jnp.bfloat16)],
        name="resample",
        compiler_params=pltpu.CompilerParams(vmem_limit_bytes=GRANT),
    )(*[near(array) for array in (inner, even, odd, low_taps, high_taps, line_taps)])

    rows, cols = lines // LOOK_AZ, columns // LOOK_RG
    out_shape = (
        jax.ShapeDtypeStruct((dates, 2 * KINDS, rows, cols), jnp.float32),
        jax.ShapeDtypeStruct((dates, KINDS, rows, cols), jnp.float32),
    )
    if chips:

        def swapped(array, bits):
            pairs = [(i, i ^ bits) for i in range(owners) if i < i ^ bits]
            return exchanged(array, "date", pairs)

        order = [3, 1, 2]
        own = tiles[0]
        direct = {number: swapped(tiles[number], CORES * number) for number in order}
        other = swapped(own, 1)
        passed = {number: swapped(direct[number], 1) for number in order}
        held, positions = [own, other], [0, 1]
        for number in order:
            held += [direct[number], passed[number]]
            positions += [CORES * number, CORES * number + 1]
        results = pl.pallas_call(
            functools.partial(chip_looks_kernel, positions),
            out_shape=(pltpu.VMEM((CHANNELS * CHIP_LOOKS, LANES), jnp.float32),) * CHIPS,
            in_specs=[SMEM] * 2 + [VMEM] * (1 + len(held)),
            out_specs=(VMEM,) * CHIPS,
            scratch_shapes=[
                pltpu.VMEM((total, parts, tile_lines, tile_columns), jnp.float32),
                pltpu.VMEM((CHIPS * QUANTITIES * CHIP_LOOKS, dates * columns), jnp.float32),
                pltpu.VMEM(((CHIPS + 1) * QUANTITIES * CHIP_LOOKS, LANES), jnp.float32),
            ],
            name="looks",
            compiler_params=pltpu.CompilerParams(vmem_limit_bytes=GRANT),
        )(master_epoch_image, gap, near(pool), *[near(tile) for tile in held])
        back = {number: swapped(results[number], CORES * number) for number in order}
        last = [1, 3, 2]
        pieces = [results[0]] + [back[number] for number in last]
        return pl.pallas_call(
            functools.partial(chip_place_kernel, [0] + last),
            out_shape=out_shape,
            in_specs=[VMEM] * CHIPS,
            out_specs=(VMEM, VMEM),
            name="place",
            compiler_params=pltpu.CompilerParams(vmem_limit_bytes=GRANT),
        )(*[near(piece) for piece in pieces])

    tiles = lax.all_to_all(tiles[0], "date", 0, 0)
    results = pl.pallas_call(
        looks_kernel,
        out_shape=pltpu.VMEM((owners, dates * CHANNELS, lanes), jnp.float32),
        in_specs=[SMEM] * 2 + [VMEM],
        out_specs=VMEM,
        scratch_shapes=[
            pltpu.VMEM((total, parts, tile_lines, tile_columns), jnp.float32),
            pltpu.VMEM((total * QUANTITIES, line_looks * tile_columns), jnp.float32),
            pltpu.VMEM((total * QUANTITIES, lanes), jnp.float32),
            pltpu.VMEM((KINDS, total, lanes), jnp.float32),
        ],
        name="looks",
        compiler_params=pltpu.CompilerParams(vmem_limit_bytes=GRANT),
    )(master_epoch_image, gap, near(tiles))
    results = lax.all_to_all(results, "date", 0, 0)

    if column_groups == 1:
        return pl.pallas_call(
            place_kernel,
            out_shape=out_shape,
            in_specs=[VMEM],
            out_specs=(VMEM, VMEM),
            name="place",
            compiler_params=pltpu.CompilerParams(vmem_limit_bytes=GRANT),
        )(near(results))
    whole = results.reshape(
        line_groups, column_groups, dates, CHANNELS, line_looks, column_looks
    )
    whole = jnp.transpose(whole, (2, 3, 0, 4, 1, 5)).reshape(dates, CHANNELS, rows, cols)
    return (whole[:, : 2 * KINDS], whole[:, 2 * KINDS :])


def solution(mesh):
    in_specs = (P("date", None, None, "range"), P(), P(), P(), P(), P(), P(), P())
    out_specs = (P("date", None, None, "range"), P("date", None, None, "range"))
    return jax.shard_map(body, mesh=mesh, in_specs=in_specs, out_specs=out_specs, check_vma=False)
```

```python
import functools

import jax
import jax.numpy as jnp
from jax import lax
from jax.experimental import pallas as pl
from jax.experimental.pallas import tpu as pltpu
from jax.sharding import PartitionSpec as P

MAX_SWEEPS = 4
TAPS = 8
FRACTIONS = 16
MARGIN = 16
LOOK_AZ = 16
LOOK_RG = 4
QUANTITIES = 8
KINDS = 3
CHANNELS = 9
LANES = 128
GRANT = 24 * 2**20
CORES = 2
CHIPS = 4
CHIP_LOOKS = 4

SMEM = pl.BlockSpec(memory_space=pltpu.SMEM)
VMEM = pl.BlockSpec(memory_space=pltpu.VMEM)


def exchanged(array, axis, pairs):
    return lax.ppermute(array, axis, [route for a, b in pairs for route in ((a, b), (b, a))])


def near(array):
    return pltpu.with_memory_space_constraint(array, pltpu.VMEM)


def iotas(rows, cols):
    return (
        lax.broadcasted_iota(jnp.int32, (rows, cols), 0),
        lax.broadcasted_iota(jnp.int32, (rows, cols), 1),
    )


def weight_rows(fractions):
    row, lane = iotas(8, LANES)
    spot = jnp.zeros((8, LANES), jnp.float32)
    for number, fraction in enumerate(fractions):
        spot = jnp.where(row == number, fraction.astype(jnp.float32), spot)
    spacing = (lane - 1 - (TAPS // 2 - 1)).astype(jnp.float32) - spot / FRACTIONS
    angle = jnp.pi * spacing
    sinc = jnp.where(spacing == 0.0, 1.0, jnp.sin(angle) / jnp.where(spacing == 0.0, 1.0, angle))
    weights = sinc * jnp.cos(angle / (TAPS + 1)) ** 2
    weights = jnp.where((lane >= 1) & (lane <= TAPS), weights, 0.0)
    weights = weights / jnp.sum(weights, axis=1, keepdims=True)
    return weights.astype(jnp.bfloat16).astype(jnp.float32)


def by_chips(block, owners):
    dates, parts, lines, columns = block.shape
    return (
        owners == CHIPS * CORES
        and (dates, parts) == (2, 2)
        and lines == CHIPS * CHIP_LOOKS * LOOK_AZ
        and columns == 2 * LANES
    )


def tile_order(position, chips):
    return position ^ (lax.axis_index("date") // CORES) if chips else position


def banded(offsets, weights):
    rows, cols = offsets.shape
    lanes = jnp.broadcast_to(weights, (rows, LANES))
    spots = jnp.clip(offsets + 1, 0, TAPS + 1)
    return jnp.concatenate(
        [
            jnp.take_along_axis(lanes, spots[:, start : start + LANES], axis=1)
            for start in range(0, cols, LANES)
        ],
        axis=1,
    )


def start_kernel(x_ref, *refs):
    dates, parts, lines, columns = x_ref.shape
    images = [(slot, part) for slot in range(dates) for part in range(parts)]
    count = (len(refs) - 4) // 2
    near_ref, even_ref, odd_ref = refs[count : count + 3]
    sems = refs[-1]
    small = list(zip(refs[:count], refs[count + 3 : -1]))
    whole = [(x_ref.at[image], near_ref.at[image]) for image in images]
    copies = [
        pltpu.make_async_copy(source, target, sems.at[number])
        for number, (source, target) in enumerate(whole + small)
    ]
    for copy in copies:
        copy.start()
    forward = lax.axis_index("range") % 2 == 0
    for number, (slot, part) in enumerate(images):
        copies[number].wait()
        for parity, last_ref, first_ref in (
            (forward, even_ref, odd_ref),
            (jnp.logical_not(forward), odd_ref, even_ref),
        ):

            @pl.when(parity)
            def _():
                for half in range(2):
                    rows = slice(half * (lines // 2), (half + 1) * (lines // 2))
                    start = (half * len(images) + number) * MARGIN
                    spot = slice(start, start + MARGIN)
                    last_ref[:, spot] = near_ref[slot, part, rows, columns - MARGIN :]
                    first_ref[:, spot] = near_ref[slot, part, rows, :MARGIN]

    for copy in copies[len(images) :]:
        copy.wait()


def pool_matrix(columns, lanes):
    row, col = iotas(columns, lanes)
    return jnp.where(row // LOOK_RG == col, 1.0, 0.0).astype(jnp.bfloat16)


def taps_kernel(
    chips,
    tile_lines,
    az_whole,
    az_part,
    rg_whole,
    rg_part,
    sweeps,
    x_ref,
    inner_ref,
    low_ref,
    high_ref,
    line_ref,
    pool_ref,
):
    dates, parts, lines, columns = x_ref.shape
    pool_ref[...] = pool_matrix(*pool_ref.shape)
    edge_rows = low_ref.shape[0]
    centre = TAPS // 2 - 1
    present = [lax.axis_index("date") * dates + slot for slot in range(dates)]
    table = weight_rows([rg_part[d] for d in present] + [az_part[d] for d in present])
    for slot, date in enumerate(present):
        shift = centre - rg_whole[date]
        weights = table[slot : slot + 1]
        row, col = iotas(columns, columns)
        own = banded(row - col + shift, weights).astype(jnp.bfloat16)
        for part in range(parts):
            inner_ref[slot, part] = jnp.dot(
                x_ref[slot, part], own, preferred_element_type=jnp.float32
            )
        row, col = iotas(edge_rows, LANES)
        low = banded(row % MARGIN - MARGIN - col + shift, weights)
        high = banded(row % MARGIN + LANES - col + shift, weights)
        for part in range(parts):
            image = slot * parts + part
            held = row // MARGIN == image
            spot = slice(image * LANES, (image + 1) * LANES)
            low_ref[:, spot] = jnp.where(held, low, 0.0).astype(jnp.bfloat16)
            high_ref[:, spot] = jnp.where(held, high, 0.0).astype(jnp.bfloat16)
        row, col = iotas(lines, lines)
        row = tile_order(row // tile_lines, chips) * tile_lines + row % tile_lines
        weights = table[dates + slot : dates + slot + 1]
        band = banded(col - row + (centre - az_whole[date]), weights)
        usable = row < sweeps[date] * (lines // MAX_SWEEPS)
        line_ref[slot] = jnp.where(usable, band, 0.0).astype(jnp.bfloat16)


def resample_kernel(split, inner_ref, even_ref, odd_ref, low_ref, high_ref, line_ref, *refs):
    *outs, edges = refs
    dates, parts, _, columns = inner_ref.shape
    line_groups, column_groups, tile_lines, tile_columns = split
    backward = lax.axis_index("range") % 2
    height, width = even_ref.shape
    for half in range(2):
        rows = slice(half * height, (half + 1) * height)
        spot = slice(half * (width // 2), (half + 1) * (width // 2))
        edges[1 - backward, rows, :] = even_ref[:, spot]
        edges[backward, rows, :] = odd_ref[:, spot]
    low = jnp.dot(edges[0], low_ref[...], preferred_element_type=jnp.float32)
    high = jnp.dot(edges[1], high_ref[...], preferred_element_type=jnp.float32)
    for slot in range(dates):
        for part in range(parts):
            spot = slice((slot * parts + part) * LANES, (slot * parts + part + 1) * LANES)
            pieces = [
                inner_ref[slot, part, :, start : start + LANES]
                for start in range(0, columns, LANES)
            ]
            pieces[0] += low[:, spot]
            pieces[-1] += high[:, spot]
            ranged = jnp.concatenate(pieces, axis=1)
            moved = jnp.dot(
                line_ref[slot], ranged.astype(jnp.bfloat16), preferred_element_type=jnp.float32
            ).astype(jnp.bfloat16)
            for i in range(line_groups):
                for j in range(column_groups):
                    tile = moved[
                        i * tile_lines : (i + 1) * tile_lines,
                        j * tile_columns : (j + 1) * tile_columns,
                    ]
                    if len(outs) == 1:
                        outs[0][i * column_groups + j, slot, part] = tile
                    else:
                        outs[i][slot, part] = tile


def partners(date, gap_ref, total):
    ahead = date + gap_ref[0, date]
    later = jnp.where(ahead < total, ahead, date - gap_ref[0, date])
    back = date - gap_ref[1, date]
    earlier = jnp.where(back >= 0, back, date + gap_ref[1, date])
    return (later, earlier)


def row_sums(values):
    row = lax.broadcasted_iota(jnp.int32, values[0].shape, 0)
    order = (3, 2, 1, 0, 7, 6, 5, 4)
    values = [values[number] for number in order]
    upper = row < 4
    values = [
        jnp.where(upper, a, b) + pltpu.roll(jnp.where(upper, b, a), 4, 0)
        for a, b in zip(values[:4], values[4:])
    ]
    for step, kept in ((2, row % 4 >= 2), (1, row % 2 == 1)):
        values = [
            jnp.where(kept, a + pltpu.roll(a, step, 0), b + pltpu.roll(b, 8 - step, 0))
            for a, b in zip(values[:step], values[step:])
        ]
    return values[0]


def pool_columns(sums, pool):
    coarse = sums.astype(jnp.bfloat16)
    fine = (sums - coarse.astype(jnp.float32)).astype(jnp.bfloat16)
    return jnp.dot(coarse, pool, preferred_element_type=jnp.float32) + jnp.dot(
        fine, pool, preferred_element_type=jnp.float32
    )


def looks_kernel(root_ref, gap_ref, tiles_ref, out_ref, stack, sums, pooled, powers):
    total, _, tile_lines, tile_columns = stack.shape
    owners, per_owner, lanes = out_ref.shape
    dates = per_owner // CHANNELS
    line_looks = tile_lines // LOOK_AZ
    unroll = total if total <= 16 else 1

    def widen(owner, carry):
        stack[pl.ds(owner * dates, dates)] = tiles_ref[owner].astype(jnp.float32)
        return carry

    lax.fori_loop(0, owners, widen, 0)

    def partner_of(kind, date):
        return partners(date, gap_ref, total)[kind - 1] if kind else root_ref[0]

    def collect(date, carry):
        left0, left1 = stack[date, 0], stack[date, 1]
        values = []
        for kind in range(KINDS):
            partner = partner_of(kind, date)
            right0, right1 = stack[partner, 0], stack[partner, 1]
            values += [left0 * right0 + left1 * right1, left1 * right0 - left0 * right1]
        values.append(left0 * left0 + left1 * left1)
        values.append(jnp.zeros_like(left0))
        rows = pl.ds(pl.multiple_of(date * QUANTITIES, QUANTITIES), QUANTITIES)
        for look in range(line_looks):
            start = look * LOOK_AZ
            sums[rows, look * tile_columns : (look + 1) * tile_columns] = row_sums(
                [value[start : start + 8] + value[start + 8 : start + 16] for value in values]
            )
        return carry

    lax.fori_loop(0, total, collect, 0, unroll=unroll)
    pooled[...] = pool_columns(sums[...], pool_matrix(sums.shape[1], lanes))

    def gather(date, carry):
        for kind in range(KINDS):
            power = partner_of(kind, date) * QUANTITIES + 2 * KINDS
            powers[kind, pl.ds(date, 1), :] = pooled[pl.ds(power, 1), :]
        return carry

    lax.fori_loop(0, total, gather, 0, unroll=unroll)
    scale = 1.0 / (LOOK_AZ * LOOK_RG) ** 0.5

    for slot in range(dates):

        def every(number):
            return pooled[pl.ds(slot * QUANTITIES + number, owners, stride=dates * QUANTITIES), :]

        power_left = every(2 * KINDS)
        for kind in range(KINDS):
            real, imag = every(2 * kind), every(2 * kind + 1)
            power_right = powers[kind, pl.ds(slot, owners, stride=dates), :]
            out_ref[:, slot * CHANNELS + 2 * kind, :] = real * scale
            out_ref[:, slot * CHANNELS + 2 * kind + 1, :] = imag * scale
            out_ref[:, slot * CHANNELS + 2 * KINDS + kind, :] = jnp.sqrt(
                real * real + imag * imag
            ) / jnp.sqrt(power_left * power_right + 1e-06)


def chip_looks_kernel(positions, root_ref, gap_ref, pool_ref, *refs):
    tiles, outs, (stack, sums, pooled) = refs[: CHIPS * CORES], refs[CHIPS * CORES : -3], refs[-3:]
    dates, _, _, columns = tiles[0].shape
    me = lax.axis_index("date")
    total = len(tiles) * dates
    scale = 1.0 / (LOOK_AZ * LOOK_RG) ** 0.5
    for position, tile_ref in zip(positions, tiles):
        stack[position * dates : (position + 1) * dates] = tile_ref[...].astype(jnp.float32)

    def partner_of(kind, date):
        partner = partners(date, gap_ref, total)[kind - 1] if kind else root_ref[0]
        return lax.div(partner, dates) ^ me, lax.rem(partner, dates)

    def part(spot, number, look):
        return stack[spot, number, look * LOOK_AZ : (look + 1) * LOOK_AZ, :]

    def folded(value):
        return value[: LOOK_AZ // 2] + value[LOOK_AZ // 2 :]

    block = QUANTITIES * CHIP_LOOKS
    for chip in range(CHIPS):
        for slot in range(dates):
            own = CORES * chip * dates + slot
            others = []
            for kind in range(KINDS):
                position, number = partner_of(kind, (me ^ (CORES * chip)) * dates + slot)
                others.append(position * dates + number)
            for look in range(CHIP_LOOKS):
                left0, left1 = part(own, 0, look), part(own, 1, look)
                values = []
                for other in others:
                    right0, right1 = part(other, 0, look), part(other, 1, look)
                    values.append(folded(left0 * right0 + left1 * right1))
                    values.append(folded(left1 * right0 - left0 * right1))
                values.append(folded(left0 * left0 + left1 * left1))
                right0, right1 = part(own + dates, 0, look), part(own + dates, 1, look)
                values.append(folded(right0 * right0 + right1 * right1))
                start = chip * block + look * QUANTITIES
                sums[start : start + QUANTITIES, slot * columns : (slot + 1) * columns] = (
                    row_sums(values)
                )
        rows = slice(chip * block, (chip + 1) * block)
        pooled[rows] = pool_columns(sums[rows], pool_ref[...])

    def every_look(start):
        return pooled[pl.ds(start, CHIP_LOOKS, stride=QUANTITIES), :]

    first = lax.broadcasted_iota(jnp.int32, (CHIP_LOOKS, LANES), 1) < LANES // 2
    for chip in range(CHIPS):
        base = chip * block
        power_left = every_look(base + 2 * KINDS)
        for kind in range(KINDS):
            halves = []
            for slot in range(dates):
                position, number = partner_of(kind, (me ^ (CORES * chip)) * dates + slot)
                start = lax.div(position, CORES) * block + 2 * KINDS + lax.rem(position, CORES)
                halves.append(pltpu.roll(every_look(start), LANES // 2 * (number ^ slot), 1))
            power = power_left * jnp.where(first, halves[0], halves[1])
            real, imag = every_look(base + 2 * kind), every_look(base + 2 * kind + 1)
            for channel, value in (
                (2 * kind, real * scale),
                (2 * kind + 1, imag * scale),
                (2 * KINDS + kind, jnp.sqrt((real * real + imag * imag) / (power + 1e-06))),
            ):
                outs[chip][channel * CHIP_LOOKS : (channel + 1) * CHIP_LOOKS, :] = value


def chip_place_kernel(positions, *refs):
    pieces, (ifg_ref, coh_ref) = refs[:CHIPS], refs[CHIPS:]
    dates, _, _, columns = ifg_ref.shape
    mine = lax.axis_index("date") // CORES
    for chip in range(CHIPS):

        @pl.when(mine == chip)
        def _():
            for position, piece_ref in zip(positions, pieces):
                start = (chip ^ position) * CHIP_LOOKS
                where = slice(start, start + CHIP_LOOKS)
                for channel in range(CHANNELS):
                    rows = piece_ref[channel * CHIP_LOOKS : (channel + 1) * CHIP_LOOKS, :]
                    for slot in range(dates):
                        part = rows[:, slot * columns : (slot + 1) * columns]
                        if channel < 2 * KINDS:
                            ifg_ref[slot, channel, where, :] = part
                        else:
                            coh_ref[slot, channel - 2 * KINDS, where, :] = part


def place_kernel(x_ref, ifg_ref, coh_ref):
    sources, rows, lanes = x_ref.shape
    dates, _, lines, columns = ifg_ref.shape
    looks = lanes // columns
    for slot in range(dates):
        for channel in range(CHANNELS):
            values = x_ref[:, slot * CHANNELS + channel, :]
            for look in range(looks):
                part = values[:, look * columns : (look + 1) * columns]
                where = pl.ds(look, sources, stride=looks)
                if channel < 2 * KINDS:
                    ifg_ref[slot, channel, where, :] = part
                else:
                    coh_ref[slot, channel - 2 * KINDS, where, :] = part


def body(
    epoch_tiles_quadrature,
    along_track_whole_displacement,
    along_track_subpixel_weights,
    slant_whole_displacement,
    slant_subpixel_weights,
    sweeps_each_epoch,
    baseline_companion_gap,
    master_epoch_image,
):
    block = epoch_tiles_quadrature
    dates, parts, lines, columns = block.shape
    owners = lax.axis_size("date")
    total = owners * dates
    images = dates * parts
    chips = by_chips(block, owners)
    line_groups = CHIPS if chips else min(owners, lines // LOOK_AZ)
    column_groups = 1 if chips else owners // line_groups
    tile_lines, tile_columns = lines // line_groups, columns // column_groups
    line_looks, column_looks = tile_lines // LOOK_AZ, tile_columns // LOOK_RG
    lanes = line_looks * column_looks

    arguments = (
        block,
        along_track_whole_displacement,
        along_track_subpixel_weights,
        slant_whole_displacement,
        slant_subpixel_weights,
        sweeps_each_epoch,
        baseline_companion_gap.T,
    )
    block, even, odd, *small = pl.pallas_call(
        start_kernel,
        out_shape=(
            pltpu.VMEM(block.shape, block.dtype),
            pltpu.VMEM((lines // 2, 2 * images * MARGIN), jnp.bfloat16),
            pltpu.VMEM((lines // 2, 2 * images * MARGIN), jnp.bfloat16),
            *[pltpu.SMEM(array.shape, array.dtype) for array in arguments[1:]],
        ),
        in_specs=[pl.BlockSpec(memory_space=pltpu.HBM)] * len(arguments),
        out_specs=(VMEM,) * 3 + (SMEM,) * (len(arguments) - 1),
        scratch_shapes=[pltpu.SemaphoreType.DMA((images + len(arguments) - 1,))],
        name="start",
        compiler_params=pltpu.CompilerParams(vmem_limit_bytes=GRANT),
    )(*[pltpu.with_memory_space_constraint(array, pltpu.HBM) for array in arguments])
    *small, gap = [pltpu.with_memory_space_constraint(array, pltpu.SMEM) for array in small]
    width = lax.axis_size("range")
    odd = exchanged(odd, "range", [(j, j + 1) for j in range(1, width - 1, 2)])
    even = exchanged(even, "range", [(j, j + 1) for j in range(0, width - 1, 2)])

    inner, low_taps, high_taps, line_taps, pool = pl.pallas_call(
        functools.partial(taps_kernel, chips, tile_lines),
        out_shape=(
            pltpu.VMEM(block.shape, jnp.float32),
            pltpu.VMEM((images * MARGIN, images * LANES), jnp.bfloat16),
            pltpu.VMEM((images * MARGIN, images * LANES), jnp.bfloat16),
            pltpu.VMEM((dates, lines, lines), jnp.bfloat16),
            pltpu.VMEM((dates * columns, LANES), jnp.bfloat16),
        ),
        in_specs=[SMEM] * len(small) + [VMEM],
        out_specs=(VMEM,) * 5,
        cost_estimate=pl.CostEstimate(flops=4000000, bytes_accessed=800000, transcendentals=0),
        name="taps",
        compiler_params=pltpu.CompilerParams(vmem_limit_bytes=GRANT),
    )(*small, near(block))
    tile = (dates, parts, tile_lines, tile_columns)
    if chips:
        out_shape = (pltpu.VMEM(tile, jnp.bfloat16),) * CHIPS
    else:
        out_shape = (pltpu.VMEM((owners,) + tile, jnp.bfloat16),)
    tiles = pl.pallas_call(
        functools.partial(
            resample_kernel, (line_groups, column_groups, tile_lines, tile_columns)
        ),
        out_shape=out_shape,
        in_specs=[VMEM] * 6,
        out_specs=(VMEM,) * len(out_shape),
        scratch_shapes=[pltpu.VMEM((2, lines, images * MARGIN), jnp.bfloat16)],
        name="resample",
        compiler_params=pltpu.CompilerParams(vmem_limit_bytes=GRANT),
    )(*[near(array) for array in (inner, even, odd, low_taps, high_taps, line_taps)])

    rows, cols = lines // LOOK_AZ, columns // LOOK_RG
    out_shape = (
        jax.ShapeDtypeStruct((dates, 2 * KINDS, rows, cols), jnp.float32),
        jax.ShapeDtypeStruct((dates, KINDS, rows, cols), jnp.float32),
    )
    if chips:

        def swapped(array, bits):
            pairs = [(i, i ^ bits) for i in range(owners) if i < i ^ bits]
            return exchanged(array, "date", pairs)

        order = [3, 2, 1]
        own = tiles[0]
        direct = {number: swapped(tiles[number], CORES * number) for number in order}
        other = swapped(own, 1)
        passed = {number: swapped(direct[number], 1) for number in order}
        held, positions = [own, other], [0, 1]
        for number in order:
            held += [direct[number], passed[number]]
            positions += [CORES * number, CORES * number + 1]
        results = pl.pallas_call(
            functools.partial(chip_looks_kernel, positions),
            out_shape=(pltpu.VMEM((CHANNELS * CHIP_LOOKS, LANES), jnp.float32),) * CHIPS,
            in_specs=[SMEM] * 2 + [VMEM] * (1 + len(held)),
            out_specs=(VMEM,) * CHIPS,
            scratch_shapes=[
                pltpu.VMEM((total, parts, tile_lines, tile_columns), jnp.float32),
                pltpu.VMEM((CHIPS * QUANTITIES * CHIP_LOOKS, dates * columns), jnp.float32),
                pltpu.VMEM(((CHIPS + 1) * QUANTITIES * CHIP_LOOKS, LANES), jnp.float32),
            ],
            name="looks",
            compiler_params=pltpu.CompilerParams(vmem_limit_bytes=GRANT),
        )(master_epoch_image, gap, near(pool), *[near(tile) for tile in held])
        back = {number: swapped(results[number], CORES * number) for number in order}
        last = [2, 3, 1]
        pieces = [results[0]] + [back[number] for number in last]
        return pl.pallas_call(
            functools.partial(chip_place_kernel, [0] + last),
            out_shape=out_shape,
            in_specs=[VMEM] * CHIPS,
            out_specs=(VMEM, VMEM),
            name="place",
            compiler_params=pltpu.CompilerParams(vmem_limit_bytes=GRANT),
        )(*[near(piece) for piece in pieces])

    tiles = lax.all_to_all(tiles[0], "date", 0, 0)
    results = pl.pallas_call(
        looks_kernel,
        out_shape=pltpu.VMEM((owners, dates * CHANNELS, lanes), jnp.float32),
        in_specs=[SMEM] * 2 + [VMEM],
        out_specs=VMEM,
        scratch_shapes=[
            pltpu.VMEM((total, parts, tile_lines, tile_columns), jnp.float32),
            pltpu.VMEM((total * QUANTITIES, line_looks * tile_columns), jnp.float32),
            pltpu.VMEM((total * QUANTITIES, lanes), jnp.float32),
            pltpu.VMEM((KINDS, total, lanes), jnp.float32),
        ],
        name="looks",
        compiler_params=pltpu.CompilerParams(vmem_limit_bytes=GRANT),
    )(master_epoch_image, gap, near(tiles))
    results = lax.all_to_all(results, "date", 0, 0)

    if column_groups == 1:
        return pl.pallas_call(
            place_kernel,
            out_shape=out_shape,
            in_specs=[VMEM],
            out_specs=(VMEM, VMEM),
            name="place",
            compiler_params=pltpu.CompilerParams(vmem_limit_bytes=GRANT),
        )(near(results))
    whole = results.reshape(
        line_groups, column_groups, dates, CHANNELS, line_looks, column_looks
    )
    whole = jnp.transpose(whole, (2, 3, 0, 4, 1, 5)).reshape(dates, CHANNELS, rows, cols)
    return (whole[:, : 2 * KINDS], whole[:, 2 * KINDS :])


def solution(mesh):
    in_specs = (P("date", None, None, "range"), P(), P(), P(), P(), P(), P(), P())
    out_specs = (P("date", None, None, "range"), P("date", None, None, "range"))
    return jax.shard_map(body, mesh=mesh, in_specs=in_specs, out_specs=out_specs, check_vma=False)
```

```python
import functools

import jax
import jax.numpy as jnp
from jax import lax
from jax.experimental import pallas as pl
from jax.experimental.pallas import tpu as pltpu
from jax.sharding import PartitionSpec as P

MAX_SWEEPS = 4
TAPS = 8
FRACTIONS = 16
MARGIN = 16
LOOK_AZ = 16
LOOK_RG = 4
QUANTITIES = 8
KINDS = 3
CHANNELS = 9
LANES = 128
GRANT = 24 * 2**20
CORES = 2
CHIPS = 4
CHIP_LOOKS = 4

SMEM = pl.BlockSpec(memory_space=pltpu.SMEM)
VMEM = pl.BlockSpec(memory_space=pltpu.VMEM)


def exchanged(array, axis, pairs):
    return lax.ppermute(array, axis, [route for a, b in pairs for route in ((a, b), (b, a))])


def near(array):
    return pltpu.with_memory_space_constraint(array, pltpu.VMEM)


def iotas(rows, cols):
    return (
        lax.broadcasted_iota(jnp.int32, (rows, cols), 0),
        lax.broadcasted_iota(jnp.int32, (rows, cols), 1),
    )


def weight_rows(fractions):
    row, lane = iotas(8, LANES)
    spot = jnp.zeros((8, LANES), jnp.float32)
    for number, fraction in enumerate(fractions):
        spot = jnp.where(row == number, fraction.astype(jnp.float32), spot)
    spacing = (lane - 1 - (TAPS // 2 - 1)).astype(jnp.float32) - spot / FRACTIONS
    angle = jnp.pi * spacing
    sinc = jnp.where(spacing == 0.0, 1.0, jnp.sin(angle) / jnp.where(spacing == 0.0, 1.0, angle))
    weights = sinc * jnp.cos(angle / (TAPS + 1)) ** 2
    weights = jnp.where((lane >= 1) & (lane <= TAPS), weights, 0.0)
    weights = weights / jnp.sum(weights, axis=1, keepdims=True)
    return weights.astype(jnp.bfloat16).astype(jnp.float32)


def by_chips(block, owners):
    dates, parts, lines, columns = block.shape
    return (
        owners == CHIPS * CORES
        and (dates, parts) == (2, 2)
        and lines == CHIPS * CHIP_LOOKS * LOOK_AZ
        and columns == 2 * LANES
    )


def tile_order(position, chips):
    return position ^ (lax.axis_index("date") // CORES) if chips else position


def banded(offsets, weights):
    rows, cols = offsets.shape
    lanes = jnp.broadcast_to(weights, (rows, LANES))
    spots = jnp.clip(offsets + 1, 0, TAPS + 1)
    return jnp.concatenate(
        [
            jnp.take_along_axis(lanes, spots[:, start : start + LANES], axis=1)
            for start in range(0, cols, LANES)
        ],
        axis=1,
    )


def start_kernel(x_ref, *refs):
    dates, parts, lines, columns = x_ref.shape
    images = [(slot, part) for slot in range(dates) for part in range(parts)]
    count = (len(refs) - 4) // 2
    near_ref, even_ref, odd_ref = refs[count : count + 3]
    sems = refs[-1]
    small = list(zip(refs[:count], refs[count + 3 : -1]))
    whole = [(x_ref.at[image], near_ref.at[image]) for image in images]
    copies = [
        pltpu.make_async_copy(source, target, sems.at[number])
        for number, (source, target) in enumerate(whole + small)
    ]
    for copy in copies:
        copy.start()
    forward = lax.axis_index("range") % 2 == 0
    for number, (slot, part) in enumerate(images):
        copies[number].wait()
        for parity, last_ref, first_ref in (
            (forward, even_ref, odd_ref),
            (jnp.logical_not(forward), odd_ref, even_ref),
        ):

            @pl.when(parity)
            def _():
                for half in range(2):
                    rows = slice(half * (lines // 2), (half + 1) * (lines // 2))
                    start = (half * len(images) + number) * MARGIN
                    spot = slice(start, start + MARGIN)
                    last_ref[:, spot] = near_ref[slot, part, rows, columns - MARGIN :]
                    first_ref[:, spot] = near_ref[slot, part, rows, :MARGIN]

    for copy in copies[len(images) :]:
        copy.wait()


def pool_matrix(columns, lanes):
    row, col = iotas(columns, lanes)
    return jnp.where(row // LOOK_RG == col, 1.0, 0.0).astype(jnp.bfloat16)


def taps_kernel(
    chips,
    tile_lines,
    az_whole,
    az_part,
    rg_whole,
    rg_part,
    sweeps,
    x_ref,
    inner_ref,
    low_ref,
    high_ref,
    line_ref,
    pool_ref,
):
    dates, parts, lines, columns = x_ref.shape
    pool_ref[...] = pool_matrix(*pool_ref.shape)
    edge_rows = low_ref.shape[0]
    centre = TAPS // 2 - 1
    present = [lax.axis_index("date") * dates + slot for slot in range(dates)]
    table = weight_rows([rg_part[d] for d in present] + [az_part[d] for d in present])
    for slot, date in enumerate(present):
        shift = centre - rg_whole[date]
        weights = table[slot : slot + 1]
        row, col = iotas(columns, columns)
        own = banded(row - col + shift, weights).astype(jnp.bfloat16)
        for part in range(parts):
            inner_ref[slot, part] = jnp.dot(
                x_ref[slot, part], own, preferred_element_type=jnp.float32
            )
        row, col = iotas(edge_rows, LANES)
        low = banded(row % MARGIN - MARGIN - col + shift, weights)
        high = banded(row % MARGIN + LANES - col + shift, weights)
        for part in range(parts):
            image = slot * parts + part
            held = row // MARGIN == image
            spot = slice(image * LANES, (image + 1) * LANES)
            low_ref[:, spot] = jnp.where(held, low, 0.0).astype(jnp.bfloat16)
            high_ref[:, spot] = jnp.where(held, high, 0.0).astype(jnp.bfloat16)
        row, col = iotas(lines, lines)
        row = tile_order(row // tile_lines, chips) * tile_lines + row % tile_lines
        weights = table[dates + slot : dates + slot + 1]
        band = banded(col - row + (centre - az_whole[date]), weights)
        usable = row < sweeps[date] * (lines // MAX_SWEEPS)
        line_ref[slot] = jnp.where(usable, band, 0.0).astype(jnp.bfloat16)


def resample_kernel(split, inner_ref, even_ref, odd_ref, low_ref, high_ref, line_ref, *refs):
    *outs, edges = refs
    dates, parts, _, columns = inner_ref.shape
    line_groups, column_groups, tile_lines, tile_columns = split
    backward = lax.axis_index("range") % 2
    height, width = even_ref.shape
    for half in range(2):
        rows = slice(half * height, (half + 1) * height)
        spot = slice(half * (width // 2), (half + 1) * (width // 2))
        edges[1 - backward, rows, :] = even_ref[:, spot]
        edges[backward, rows, :] = odd_ref[:, spot]
    low = jnp.dot(edges[0], low_ref[...], preferred_element_type=jnp.float32)
    high = jnp.dot(edges[1], high_ref[...], preferred_element_type=jnp.float32)
    for slot in range(dates):
        pieces = []
        for part in range(parts):
            spot = slice((slot * parts + part) * LANES, (slot * parts + part + 1) * LANES)
            ranged = [
                inner_ref[slot, part, :, start : start + LANES]
                for start in range(0, columns, LANES)
            ]
            ranged[0] += low[:, spot]
            ranged[-1] += high[:, spot]
            pieces += [piece.astype(jnp.bfloat16) for piece in ranged]
        both = jnp.dot(
            line_ref[slot], jnp.concatenate(pieces, axis=1), preferred_element_type=jnp.float32
        ).astype(jnp.bfloat16)
        for part in range(parts):
            moved = both[:, part * columns : (part + 1) * columns]
            for i in range(line_groups):
                for j in range(column_groups):
                    tile = moved[
                        i * tile_lines : (i + 1) * tile_lines,
                        j * tile_columns : (j + 1) * tile_columns,
                    ]
                    if len(outs) == 1:
                        outs[0][i * column_groups + j, slot, part] = tile
                    else:
                        outs[i][slot, part] = tile


def partners(date, gap_ref, total):
    ahead = date + gap_ref[0, date]
    later = jnp.where(ahead < total, ahead, date - gap_ref[0, date])
    back = date - gap_ref[1, date]
    earlier = jnp.where(back >= 0, back, date + gap_ref[1, date])
    return (later, earlier)


def row_sums(values):
    row = lax.broadcasted_iota(jnp.int32, values[0].shape, 0)
    order = (3, 2, 1, 0, 7, 6, 5, 4)
    values = [values[number] for number in order]
    upper = row < 4
    values = [
        jnp.where(upper, a, b) + pltpu.roll(jnp.where(upper, b, a), 4, 0)
        for a, b in zip(values[:4], values[4:])
    ]
    for step, kept in ((2, row % 4 >= 2), (1, row % 2 == 1)):
        values = [
            jnp.where(kept, a + pltpu.roll(a, step, 0), b + pltpu.roll(b, 8 - step, 0))
            for a, b in zip(values[:step], values[step:])
        ]
    return values[0]


def pool_columns(sums, pool):
    coarse = sums.astype(jnp.bfloat16)
    fine = (sums - coarse.astype(jnp.float32)).astype(jnp.bfloat16)
    return jnp.dot(coarse, pool, preferred_element_type=jnp.float32) + jnp.dot(
        fine, pool, preferred_element_type=jnp.float32
    )


def looks_kernel(root_ref, gap_ref, tiles_ref, out_ref, stack, sums, pooled, powers):
    total, _, tile_lines, tile_columns = stack.shape
    owners, per_owner, lanes = out_ref.shape
    dates = per_owner // CHANNELS
    line_looks = tile_lines // LOOK_AZ
    unroll = total if total <= 16 else 1

    def widen(owner, carry):
        stack[pl.ds(owner * dates, dates)] = tiles_ref[owner].astype(jnp.float32)
        return carry

    lax.fori_loop(0, owners, widen, 0)

    def partner_of(kind, date):
        return partners(date, gap_ref, total)[kind - 1] if kind else root_ref[0]

    def collect(date, carry):
        left0, left1 = stack[date, 0], stack[date, 1]
        values = []
        for kind in range(KINDS):
            partner = partner_of(kind, date)
            right0, right1 = stack[partner, 0], stack[partner, 1]
            values += [left0 * right0 + left1 * right1, left1 * right0 - left0 * right1]
        values.append(left0 * left0 + left1 * left1)
        values.append(jnp.zeros_like(left0))
        rows = pl.ds(pl.multiple_of(date * QUANTITIES, QUANTITIES), QUANTITIES)
        for look in range(line_looks):
            start = look * LOOK_AZ
            sums[rows, look * tile_columns : (look + 1) * tile_columns] = row_sums(
                [value[start : start + 8] + value[start + 8 : start + 16] for value in values]
            )
        return carry

    lax.fori_loop(0, total, collect, 0, unroll=unroll)
    pooled[...] = pool_columns(sums[...], pool_matrix(sums.shape[1], lanes))

    def gather(date, carry):
        for kind in range(KINDS):
            power = partner_of(kind, date) * QUANTITIES + 2 * KINDS
            powers[kind, pl.ds(date, 1), :] = pooled[pl.ds(power, 1), :]
        return carry

    lax.fori_loop(0, total, gather, 0, unroll=unroll)
    scale = 1.0 / (LOOK_AZ * LOOK_RG) ** 0.5

    for slot in range(dates):

        def every(number):
            return pooled[pl.ds(slot * QUANTITIES + number, owners, stride=dates * QUANTITIES), :]

        power_left = every(2 * KINDS)
        for kind in range(KINDS):
            real, imag = every(2 * kind), every(2 * kind + 1)
            power_right = powers[kind, pl.ds(slot, owners, stride=dates), :]
            out_ref[:, slot * CHANNELS + 2 * kind, :] = real * scale
            out_ref[:, slot * CHANNELS + 2 * kind + 1, :] = imag * scale
            out_ref[:, slot * CHANNELS + 2 * KINDS + kind, :] = jnp.sqrt(
                real * real + imag * imag
            ) / jnp.sqrt(power_left * power_right + 1e-06)


def chip_looks_kernel(positions, root_ref, gap_ref, pool_ref, *refs):
    tiles, outs, (stack, sums, pooled) = refs[: CHIPS * CORES], refs[CHIPS * CORES : -3], refs[-3:]
    dates, _, _, columns = tiles[0].shape
    me = lax.axis_index("date")
    total = len(tiles) * dates
    scale = 1.0 / (LOOK_AZ * LOOK_RG) ** 0.5
    for position, tile_ref in zip(positions, tiles):
        stack[position * dates : (position + 1) * dates] = tile_ref[...].astype(jnp.float32)

    def partner_of(kind, date):
        partner = partners(date, gap_ref, total)[kind - 1] if kind else root_ref[0]
        return lax.div(partner, dates) ^ me, lax.rem(partner, dates)

    def part(spot, number, look):
        return stack[spot, number, look * LOOK_AZ : (look + 1) * LOOK_AZ, :]

    def folded(value):
        return value[: LOOK_AZ // 2] + value[LOOK_AZ // 2 :]

    block = QUANTITIES * CHIP_LOOKS
    for chip in range(CHIPS):
        for slot in range(dates):
            own = CORES * chip * dates + slot
            others = []
            for kind in range(KINDS):
                position, number = partner_of(kind, (me ^ (CORES * chip)) * dates + slot)
                others.append(position * dates + number)
            for look in range(CHIP_LOOKS):
                left0, left1 = part(own, 0, look), part(own, 1, look)
                values = []
                for other in others:
                    right0, right1 = part(other, 0, look), part(other, 1, look)
                    values.append(folded(left0 * right0 + left1 * right1))
                    values.append(folded(left1 * right0 - left0 * right1))
                values.append(folded(left0 * left0 + left1 * left1))
                right0, right1 = part(own + dates, 0, look), part(own + dates, 1, look)
                values.append(folded(right0 * right0 + right1 * right1))
                start = chip * block + look * QUANTITIES
                sums[start : start + QUANTITIES, slot * columns : (slot + 1) * columns] = (
                    row_sums(values)
                )
        rows = slice(chip * block, (chip + 1) * block)
        pooled[rows] = pool_columns(sums[rows], pool_ref[...])

    def every_look(start):
        return pooled[pl.ds(start, CHIP_LOOKS, stride=QUANTITIES), :]

    first = lax.broadcasted_iota(jnp.int32, (CHIP_LOOKS, LANES), 1) < LANES // 2
    for chip in range(CHIPS):
        base = chip * block
        power_left = every_look(base + 2 * KINDS)
        for kind in range(KINDS):
            halves = []
            for slot in range(dates):
                position, number = partner_of(kind, (me ^ (CORES * chip)) * dates + slot)
                start = lax.div(position, CORES) * block + 2 * KINDS + lax.rem(position, CORES)
                halves.append(pltpu.roll(every_look(start), LANES // 2 * (number ^ slot), 1))
            power = power_left * jnp.where(first, halves[0], halves[1])
            real, imag = every_look(base + 2 * kind), every_look(base + 2 * kind + 1)
            for channel, value in (
                (2 * kind, real * scale),
                (2 * kind + 1, imag * scale),
                (2 * KINDS + kind, jnp.sqrt((real * real + imag * imag) / (power + 1e-06))),
            ):
                outs[chip][channel * CHIP_LOOKS : (channel + 1) * CHIP_LOOKS, :] = value


def chip_place_kernel(positions, *refs):
    pieces, (ifg_ref, coh_ref) = refs[:CHIPS], refs[CHIPS:]
    dates, _, _, columns = ifg_ref.shape
    mine = lax.axis_index("date") // CORES
    for chip in range(CHIPS):

        @pl.when(mine == chip)
        def _():
            for position, piece_ref in zip(positions, pieces):
                start = (chip ^ position) * CHIP_LOOKS
                where = slice(start, start + CHIP_LOOKS)
                for channel in range(CHANNELS):
                    rows = piece_ref[channel * CHIP_LOOKS : (channel + 1) * CHIP_LOOKS, :]
                    for slot in range(dates):
                        part = rows[:, slot * columns : (slot + 1) * columns]
                        if channel < 2 * KINDS:
                            ifg_ref[slot, channel, where, :] = part
                        else:
                            coh_ref[slot, channel - 2 * KINDS, where, :] = part


def place_kernel(x_ref, ifg_ref, coh_ref):
    sources, rows, lanes = x_ref.shape
    dates, _, lines, columns = ifg_ref.shape
    looks = lanes // columns
    for slot in range(dates):
        for channel in range(CHANNELS):
            values = x_ref[:, slot * CHANNELS + channel, :]
            for look in range(looks):
                part = values[:, look * columns : (look + 1) * columns]
                where = pl.ds(look, sources, stride=looks)
                if channel < 2 * KINDS:
                    ifg_ref[slot, channel, where, :] = part
                else:
                    coh_ref[slot, channel - 2 * KINDS, where, :] = part


def body(
    epoch_tiles_quadrature,
    along_track_whole_displacement,
    along_track_subpixel_weights,
    slant_whole_displacement,
    slant_subpixel_weights,
    sweeps_each_epoch,
    baseline_companion_gap,
    master_epoch_image,
):
    block = epoch_tiles_quadrature
    dates, parts, lines, columns = block.shape
    owners = lax.axis_size("date")
    total = owners * dates
    images = dates * parts
    chips = by_chips(block, owners)
    line_groups = CHIPS if chips else min(owners, lines // LOOK_AZ)
    column_groups = 1 if chips else owners // line_groups
    tile_lines, tile_columns = lines // line_groups, columns // column_groups
    line_looks, column_looks = tile_lines // LOOK_AZ, tile_columns // LOOK_RG
    lanes = line_looks * column_looks

    arguments = (
        block,
        along_track_whole_displacement,
        along_track_subpixel_weights,
        slant_whole_displacement,
        slant_subpixel_weights,
        sweeps_each_epoch,
        baseline_companion_gap.T,
    )
    block, even, odd, *small = pl.pallas_call(
        start_kernel,
        out_shape=(
            pltpu.VMEM(block.shape, block.dtype),
            pltpu.VMEM((lines // 2, 2 * images * MARGIN), jnp.bfloat16),
            pltpu.VMEM((lines // 2, 2 * images * MARGIN), jnp.bfloat16),
            *[pltpu.SMEM(array.shape, array.dtype) for array in arguments[1:]],
        ),
        in_specs=[pl.BlockSpec(memory_space=pltpu.HBM)] * len(arguments),
        out_specs=(VMEM,) * 3 + (SMEM,) * (len(arguments) - 1),
        scratch_shapes=[pltpu.SemaphoreType.DMA((images + len(arguments) - 1,))],
        name="start",
        compiler_params=pltpu.CompilerParams(vmem_limit_bytes=GRANT),
    )(*[pltpu.with_memory_space_constraint(array, pltpu.HBM) for array in arguments])
    *small, gap = [pltpu.with_memory_space_constraint(array, pltpu.SMEM) for array in small]
    width = lax.axis_size("range")
    odd = exchanged(odd, "range", [(j, j + 1) for j in range(1, width - 1, 2)])
    even = exchanged(even, "range", [(j, j + 1) for j in range(0, width - 1, 2)])

    inner, low_taps, high_taps, line_taps, pool = pl.pallas_call(
        functools.partial(taps_kernel, chips, tile_lines),
        out_shape=(
            pltpu.VMEM(block.shape, jnp.float32),
            pltpu.VMEM((images * MARGIN, images * LANES), jnp.bfloat16),
            pltpu.VMEM((images * MARGIN, images * LANES), jnp.bfloat16),
            pltpu.VMEM((dates, lines, lines), jnp.bfloat16),
            pltpu.VMEM((dates * columns, LANES), jnp.bfloat16),
        ),
        in_specs=[SMEM] * len(small) + [VMEM],
        out_specs=(VMEM,) * 5,
        cost_estimate=pl.CostEstimate(flops=4000000, bytes_accessed=800000, transcendentals=0),
        name="taps",
        compiler_params=pltpu.CompilerParams(vmem_limit_bytes=GRANT),
    )(*small, near(block))
    tile = (dates, parts, tile_lines, tile_columns)
    if chips:
        out_shape = (pltpu.VMEM(tile, jnp.bfloat16),) * CHIPS
    else:
        out_shape = (pltpu.VMEM((owners,) + tile, jnp.bfloat16),)
    tiles = pl.pallas_call(
        functools.partial(
            resample_kernel, (line_groups, column_groups, tile_lines, tile_columns)
        ),
        out_shape=out_shape,
        in_specs=[VMEM] * 6,
        out_specs=(VMEM,) * len(out_shape),
        scratch_shapes=[pltpu.VMEM((2, lines, images * MARGIN), jnp.bfloat16)],
        name="resample",
        compiler_params=pltpu.CompilerParams(vmem_limit_bytes=GRANT),
    )(*[near(array) for array in (inner, even, odd, low_taps, high_taps, line_taps)])

    rows, cols = lines // LOOK_AZ, columns // LOOK_RG
    out_shape = (
        jax.ShapeDtypeStruct((dates, 2 * KINDS, rows, cols), jnp.float32),
        jax.ShapeDtypeStruct((dates, KINDS, rows, cols), jnp.float32),
    )
    if chips:

        def swapped(array, bits):
            pairs = [(i, i ^ bits) for i in range(owners) if i < i ^ bits]
            return exchanged(array, "date", pairs)

        order = [3, 2, 1]
        own = tiles[0]
        direct = {number: swapped(tiles[number], CORES * number) for number in order}
        other = swapped(own, 1)
        passed = {number: swapped(direct[number], 1) for number in order}
        held, positions = [own, other], [0, 1]
        for number in order:
            held += [direct[number], passed[number]]
            positions += [CORES * number, CORES * number + 1]
        results = pl.pallas_call(
            functools.partial(chip_looks_kernel, positions),
            out_shape=(pltpu.VMEM((CHANNELS * CHIP_LOOKS, LANES), jnp.float32),) * CHIPS,
            in_specs=[SMEM] * 2 + [VMEM] * (1 + len(held)),
            out_specs=(VMEM,) * CHIPS,
            scratch_shapes=[
                pltpu.VMEM((total, parts, tile_lines, tile_columns), jnp.float32),
                pltpu.VMEM((CHIPS * QUANTITIES * CHIP_LOOKS, dates * columns), jnp.float32),
                pltpu.VMEM(((CHIPS + 1) * QUANTITIES * CHIP_LOOKS, LANES), jnp.float32),
            ],
            name="looks",
            compiler_params=pltpu.CompilerParams(vmem_limit_bytes=GRANT),
        )(master_epoch_image, gap, near(pool), *[near(tile) for tile in held])
        back = {number: swapped(results[number], CORES * number) for number in order}
        last = [1, 3, 2]
        pieces = [results[0]] + [back[number] for number in last]
        return pl.pallas_call(
            functools.partial(chip_place_kernel, [0] + last),
            out_shape=out_shape,
            in_specs=[VMEM] * CHIPS,
            out_specs=(VMEM, VMEM),
            name="place",
            compiler_params=pltpu.CompilerParams(vmem_limit_bytes=GRANT),
        )(*[near(piece) for piece in pieces])

    tiles = lax.all_to_all(tiles[0], "date", 0, 0)
    results = pl.pallas_call(
        looks_kernel,
        out_shape=pltpu.VMEM((owners, dates * CHANNELS, lanes), jnp.float32),
        in_specs=[SMEM] * 2 + [VMEM],
        out_specs=VMEM,
        scratch_shapes=[
            pltpu.VMEM((total, parts, tile_lines, tile_columns), jnp.float32),
            pltpu.VMEM((total * QUANTITIES, line_looks * tile_columns), jnp.float32),
            pltpu.VMEM((total * QUANTITIES, lanes), jnp.float32),
            pltpu.VMEM((KINDS, total, lanes), jnp.float32),
        ],
        name="looks",
        compiler_params=pltpu.CompilerParams(vmem_limit_bytes=GRANT),
    )(master_epoch_image, gap, near(tiles))
    results = lax.all_to_all(results, "date", 0, 0)

    if column_groups == 1:
        return pl.pallas_call(
            place_kernel,
            out_shape=out_shape,
            in_specs=[VMEM],
            out_specs=(VMEM, VMEM),
            name="place",
            compiler_params=pltpu.CompilerParams(vmem_limit_bytes=GRANT),
        )(near(results))
    whole = results.reshape(
        line_groups, column_groups, dates, CHANNELS, line_looks, column_looks
    )
    whole = jnp.transpose(whole, (2, 3, 0, 4, 1, 5)).reshape(dates, CHANNELS, rows, cols)
    return (whole[:, : 2 * KINDS], whole[:, 2 * KINDS :])


def solution(mesh):
    in_specs = (P("date", None, None, "range"), P(), P(), P(), P(), P(), P(), P())
    out_specs = (P("date", None, None, "range"), P("date", None, None, "range"))
    return jax.shard_map(body, mesh=mesh, in_specs=in_specs, out_specs=out_specs, check_vma=False)
```
